32 devices in a mesh: dp: 16 (over z, y, core), tensor: 2 (over x).
Axes of the slice: x: 2, y: 2, z: 4, core: 2. Of those that a mesh axis runs over, the one named last changes fastest.
Arguments:
- inputs: bfloat16 [2, 4096, 2048], P(None, ('dp', 'tensor')), may hold values from -6 to 6
- out_grad: bfloat16 [2, 4096, 2048], P(None, ('dp', 'tensor')), may hold values from -6 to 6
- deal_order: int32 [2, 4096], replicated, may hold values from 0 to 4095, as said below
- segment: int32 [2, 4096], P(None, 'dp'), may hold values from 0 to 2, as said below
- query_weight: bfloat16 [2048, 1024], P('dp', 'tensor'), may hold values from -0.125 to 0.125
- key_weight: bfloat16 [2048, 256], P('dp', 'tensor'), may hold values from -0.125 to 0.125
- value_weight: bfloat16 [2048, 256], P('dp', 'tensor'), may hold values from -0.125 to 0.125
- attention_out: bfloat16 [2048, 1024], P('dp', 'tensor'), may hold values from -0.75 to 0.75
- mamba_gate: bfloat16 [2048, 3072], P('dp', 'tensor'), may hold values from -0.125 to 0.125
- mamba_input: bfloat16 [2048, 3072], P('dp', 'tensor'), may hold values from -0.125 to 0.125
- step_weight: bfloat16 [2048, 48], P('dp', 'tensor'), may hold values from -0.125 to 0.125
- state_weight: bfloat16 [2048, 512], P('dp'), may hold values from -0.125 to 0.125
- mamba_out: bfloat16 [2048, 3072], P('dp', 'tensor'), may hold values from -0.109375 to 0.109375
- feed_gate: bfloat16 [2048, 4096], P('dp', 'tensor'), may hold values from -0.125 to 0.125
- feed_up: bfloat16 [2048, 4096], P('dp', 'tensor'), may hold values from -0.125 to 0.125
- feed_down: bfloat16 [2048, 4096], P('dp', 'tensor'), may hold values from -0.09375 to 0.09375
- gain_input: float32 [2048], replicated, may hold values from 0.5 to 1.5
- gain_middle: float32 [2048], replicated, may hold values from 0.5 to 1.5
- kernel_inner: float32 [5, 3072], P(None, 'tensor'), may hold values from -0.5 to 0.5
- kernel_state: float32 [5, 512], replicated, may hold values from -0.5 to 0.5
- mixer_gain: float32 [3072], P('tensor'), may hold values from 0.5 to 1.5
- step_bias: float32 [48], P('tensor'), may hold values from -6 to -2
- log_rate: float32 [48], P('tensor'), may hold values from -1 to 2
- skip_gain: float32 [48], P('tensor'), may hold values from 0.5 to 1.5
Outputs:
- block_out: bfloat16 [2, 4096, 2048], P(None, ('dp', 'tensor'))
- grad_input: bfloat16 [2, 4096, 2048], P(None, ('dp', 'tensor'))
- grad_query_weight: float32 [2048, 1024], P('dp', 'tensor')
- grad_key_weight: float32 [2048, 256], P('dp', 'tensor')
- grad_value_weight: float32 [2048, 256], P('dp', 'tensor')
- grad_attention_out: float32 [2048, 1024], P('dp', 'tensor')
- grad_mamba_gate: float32 [2048, 3072], P('dp', 'tensor')
- grad_mamba_input: float32 [2048, 3072], P('dp', 'tensor')
- grad_step_weight: float32 [2048, 48], P('dp', 'tensor')
- grad_state_weight: float32 [2048, 512], P(('dp', 'tensor'))
- grad_mamba_out: float32 [2048, 3072], P('dp', 'tensor')
- grad_feed_gate: float32 [2048, 4096], P('dp', 'tensor')
- grad_feed_up: float32 [2048, 4096], P('dp', 'tensor')
- grad_feed_down: float32 [2048, 4096], P('dp', 'tensor')
- grad_gain_input: float32 [2048], replicated
- grad_gain_middle: float32 [2048], replicated
- grad_kernel_inner: float32 [5, 3072], replicated
- grad_kernel_state: float32 [5, 512], replicated
- grad_mixer_gain: float32 [3072], replicated
- grad_step_bias: float32 [48], replicated
- grad_log_rate: float32 [48], replicated
- grad_skip_gain: float32 [48], replicated
The draws below stay inside these ranges and needn't reach their ends.
Inputs may be any that keep to these rules, and one draw needn't show every extreme that they name: For each micro-batch a permutation of its rows: initial row r becomes dealt row deal_order[m, r]. The rows that device (i, t) holds in the initial order go to rows of devices (j, t) in the dealt order, exactly 8 to each j. `segment`: within each aligned block of 256 dealt rows the ids start at 0 and never fall.
All inputs are finite; a program needn't handle non-finite values.
Results may differ from the reference program's by a relative error of at most 0.017.
Values may be sent and summed in bfloat16 or wider, within the bound.
No kernel may reach another device: no remote copies, remote signals or barrier semaphores. Data moves between devices by JAX's collectives and lax.ppermute only.
A program may use at most 256 MiB of HBM per device.

```python
import math
import jax
import jax.numpy as jnp
from jax import lax

D = 2048
FF = 4096
QH = 8
HEAD = 128
KVH = 2
SH = 48
SHD = 64
NS = 256
CONV = 4
TOK_DEV = 128
MICRO = 2
GROUP_ROWS = 256
TOKENS_MB = 4096
N_DP = 16
N_TENSOR = 2


def draw_deal_order(key, part):
    device_count = N_DP * N_TENSOR
    per_group = TOK_DEV // N_DP
    total_rows = device_count * TOK_DEV

    def one_micro(micro_key):
        source_key, target_key = jax.random.split(micro_key)
        source_keys = jax.random.split(source_key, device_count)
        target_keys = jax.random.split(target_key, device_count)
        source_rank = jax.vmap(lambda inner_key: jax.random.permutation(inner_key, TOK_DEV))(source_keys)
        target_rank = jax.vmap(lambda inner_key: jax.random.permutation(inner_key, TOK_DEV))(target_keys)
        source_dev = jnp.arange(device_count, dtype=jnp.int32)[:, None]
        pair_index = jnp.arange(TOK_DEV, dtype=jnp.int32)[None, :]
        group_index = pair_index // per_group
        copy_index = pair_index % per_group
        lane_index = source_dev % N_TENSOR
        anchor_group = source_dev // N_TENSOR
        target_dev = group_index * N_TENSOR + lane_index
        slot_index = target_rank[target_dev, anchor_group * per_group + copy_index]
        dealt_row = (target_dev * TOK_DEV + slot_index).astype(jnp.int32)
        source_row = (source_dev * TOK_DEV + source_rank[source_dev, jnp.broadcast_to(pair_index, (device_count, TOK_DEV))]).astype(jnp.int32)
        return jnp.zeros((total_rows,), jnp.int32).at[source_row.reshape(-1)].set(dealt_row.reshape(-1))
    return jax.vmap(one_micro)(jax.random.split(key, MICRO))


def draw_segment(key, part):
    block_count = MICRO * N_DP
    cut_points = jax.random.randint(key, (block_count, 2), GROUP_ROWS // 8, GROUP_ROWS - GROUP_ROWS // 8)
    first_cut = jnp.min(cut_points, axis=1)
    second_cut = jnp.max(cut_points, axis=1)
    places = jnp.arange(GROUP_ROWS, dtype=jnp.int32)[None, :]
    labels = (places >= first_cut[:, None]).astype(jnp.int32) + (places >= second_cut[:, None]).astype(jnp.int32)
    return labels.reshape(MICRO, N_DP * GROUP_ROWS)


def block_levels(key, dims, cuts, low, high):
    def one(dim, shards_of):
        draws = jax.random.uniform(jax.random.fold_in(jax.random.fold_in(key, 6), dim), (shards_of,), jnp.float32, low / len(cuts), high / len(cuts))
        return jnp.repeat(jnp.exp(draws), dims[dim] // shards_of).reshape((-1,) + (1,) * (len(dims) - dim - 1))

    level = one(*cuts[0])
    for cut in cuts[1:]:
        level = level * one(*cut)
    return level


def normal_values(own_key, extent, deviation, most, cuts=(), kind=jnp.bfloat16):
    values = jax.random.normal(own_key, extent, jnp.float32) * deviation
    if len(cuts) > 0:
        values = block_levels(own_key, extent, cuts, -0.22, 0.18) * values
    return jnp.clip(values, min=-most, max=most).astype(kind)


def setup_inputs(seed: int = 0) -> dict:
    key_of = jax.random.split(jax.random.key(seed), 25)
    return {
        "inputs": normal_values(key_of[0], (MICRO, TOKENS_MB, D), 1.0, 6.0, ((1, 32),)),
        "out_grad": normal_values(key_of[1], (MICRO, TOKENS_MB, D), 1.0, 6.0, ((1, 32),)),
        "deal_order": draw_deal_order(jax.random.fold_in(key_of[24], 71), 0),
        "segment": draw_segment(jax.random.fold_in(key_of[24], 71), 0),
        "query_weight": normal_values(key_of[4], (D, QH * HEAD), D ** -0.5, 0.125, ((0, 16), (1, 2))),
        "key_weight": normal_values(key_of[5], (D, KVH * HEAD), D ** -0.5, 0.125, ((0, 16), (1, 2))),
        "value_weight": normal_values(key_of[6], (D, KVH * HEAD), D ** -0.5, 0.125, ((0, 16), (1, 2))),
        "attention_out": normal_values(key_of[7], (D, QH * HEAD), (QH * HEAD // 16) ** -0.5, 0.75, ((0, 16), (1, 2))),
        "mamba_gate": normal_values(key_of[8], (D, SH * SHD), D ** -0.5, 0.125, ((0, 16), (1, 2))),
        "mamba_input": normal_values(key_of[9], (D, SH * SHD), D ** -0.5, 0.125, ((0, 16), (1, 2))),
        "step_weight": normal_values(key_of[10], (D, SH), D ** -0.5, 0.125, ((0, 16), (1, 2))),
        "state_weight": normal_values(key_of[11], (D, 2 * NS), D ** -0.5, 0.125, ((0, 16),)),
        "mamba_out": normal_values(key_of[12], (D, SH * SHD), (SH * SHD) ** -0.5, 0.109375, ((0, 16), (1, 2))),
        "feed_gate": normal_values(key_of[13], (D, FF), D ** -0.5, 0.125, ((0, 16), (1, 2))),
        "feed_up": normal_values(key_of[14], (D, FF), D ** -0.5, 0.125, ((0, 16), (1, 2))),
        "feed_down": normal_values(key_of[15], (D, FF), FF ** -0.5, 0.09375, ((0, 16), (1, 2))),
        "gain_input": jnp.clip(1.0 + 0.1 * jax.random.normal(key_of[16], (D,), jnp.float32), 0.5, 1.5),
        "gain_middle": jnp.clip(1.0 + 0.1 * jax.random.normal(key_of[17], (D,), jnp.float32), 0.5, 1.5),
        "kernel_inner": jnp.clip(jax.random.uniform(key_of[18], (CONV + 1, SH * SHD), jnp.float32, -0.5, 0.5) * block_levels(key_of[18], (CONV + 1, SH * SHD), ((1, 2),), -0.4, 0.0), -0.5, 0.5),
        "kernel_state": jnp.clip(jax.random.uniform(key_of[19], (CONV + 1, 2 * NS), jnp.float32, -0.5, 0.5), -0.5, 0.5),
        "mixer_gain": jnp.clip(1.0 + 0.1 * jax.random.normal(key_of[20], (SH * SHD,), jnp.float32), 0.5, 1.5),
        "step_bias": jnp.clip(-6.0 + 4.0 * jax.random.uniform(key_of[21], (SH,), jnp.float32) ** block_levels(key_of[21], (SH,), ((0, 2),), -0.2, 0.2), -6.0, -2.0),
        "log_rate": jnp.clip(-1.0 + 3.0 * jax.random.uniform(key_of[22], (SH,), jnp.float32) ** block_levels(key_of[22], (SH,), ((0, 2),), -0.2, 0.2), -1.0, 2.0),
        "skip_gain": jnp.clip(0.5 + 1.0 * jax.random.uniform(key_of[23], (SH,), jnp.float32) ** block_levels(key_of[23], (SH,), ((0, 2),), -0.2, 0.2), 0.5, 1.5),
    }


@jax.custom_vjp
def low(v):
    return lax.optimization_barrier(v.astype(jnp.bfloat16)).astype(jnp.float32)

@jax.custom_vjp
def low_back(v):
    return v

def low_keep(v):
    return (low(v), None)

def low_pass(kept, grad):
    return (grad,)

def back_keep(v):
    return (v, None)

def back_low(kept, grad):
    return (low(grad),)
low.defvjp(low_keep, low_pass)
low_back.defvjp(back_keep, back_low)
epsilon = 1e-05
rope_base = 100000000000.0
highest = lax.Precision.HIGHEST

def product(left, right):
    return jnp.dot(left, right, precision=highest, preferred_element_type=jnp.float32)

def product_back(left, right):
    return lax.dot_general(left, right, (((1,), (1,)), ((), ())), precision=highest, preferred_element_type=jnp.float32)

def rms_norm(values, gain):
    return values * lax.rsqrt(lax.optimization_barrier(jnp.mean(values * values, axis=-1, keepdims=True)) + epsilon) * gain

def seq_layout(segment):
    row_count = segment.shape[0]
    before = lax.optimization_barrier(jnp.sum((segment[None, :] < segment[:, None]).astype(jnp.int32), axis=1))
    places = jnp.arange(row_count, dtype=jnp.int32)
    allowed = (segment[:, None] == segment[None, :]) & (places[None, :] <= places[:, None])
    return (places - before, allowed)

def rotate(values, position):
    half_size = values.shape[-1] // 2
    frequency = jnp.exp(jnp.arange(half_size, dtype=jnp.float32) * (-2.0 * math.log(rope_base) / values.shape[-1]))
    angles = position.astype(jnp.float32)[:, None] * frequency[None, :]
    cosine = jnp.cos(angles)[:, None, :]
    sine_val = jnp.sin(angles)[:, None, :]
    first_half = values[..., :half_size]
    second = values[..., half_size:]
    return jnp.concatenate([first_half * cosine - second * sine_val, second * cosine + first_half * sine_val], axis=-1)

def conv_act(signal, kernel, position):
    summed = kernel[CONV][None, :] + signal * kernel[0][None, :]
    for shift_by in range(1, CONV):
        shifted = jnp.concatenate([jnp.zeros((shift_by, signal.shape[1]), signal.dtype), signal[:-shift_by]], axis=0)
        summed = summed + jnp.where((position >= shift_by)[:, None], shifted, 0.0) * kernel[shift_by][None, :]
    return jax.nn.silu(summed)

def decay_scores(state_inner, raw_step, step_bias, log_rate, allowed):
    step_size = jax.nn.softplus(raw_step + step_bias)
    running = jnp.cumsum(step_size * -jnp.exp(log_rate), axis=0).T
    spread = running[:, :, None] - running[:, None, :]
    decayed = jnp.exp(jnp.where(allowed[None], spread, -jnp.inf))
    return state_inner[None] * decayed * step_size.T[:, None, :]

def layer(params, rows_in, segment):
    query_weight, key_weight, value_weight, attention_out, mamba_gate, mamba_input, step_weight, state_weight, mamba_out, feed_gate, feed_up, feed_down, gain_input, gain_middle, kernel_inner, kernel_state, mixer_gain, step_bias, log_rate, skip_gain = params
    row_count = rows_in.shape[0]
    position, allowed = seq_layout(segment)
    normed = low(rms_norm(rows_in, gain_input))
    gate_z = low_back(product(normed, mamba_gate))
    ssm_in = low_back(product(normed, mamba_input))
    raw_step = low_back(product(normed, step_weight))
    ssm_cols = conv_act(ssm_in, kernel_inner, position)
    set_heads = SH // N_TENSOR
    pieces = []
    for set_index in range(N_TENSOR):
        head_range = slice(set_index * set_heads, (set_index + 1) * set_heads)
        columns = slice(set_index * set_heads * SHD, (set_index + 1) * set_heads * SHD)
        state_act = conv_act(low_back(product(normed, state_weight)), kernel_state, position)
        state_inner = low_back(product_back(low(state_act[:, NS:]), low(state_act[:, :NS])))
        mixing = low(decay_scores(state_inner, raw_step[:, head_range], step_bias[head_range], log_rate[head_range], allowed))
        ssm_heads = ssm_cols[:, columns].reshape(row_count, set_heads, SHD)
        mixed_out = jnp.einsum('hij,jhd->ihd', mixing, low(ssm_heads), precision=highest)
        pieces.append((low_back(mixed_out) + skip_gain[head_range][None, :, None] * ssm_heads).reshape(row_count, set_heads * SHD))
    ssm_out = jnp.concatenate(pieces, axis=1)
    gated = ssm_out * jax.nn.silu(gate_z)
    gated_norm = low(rms_norm(gated, mixer_gain))
    mix_out = product_back(gated_norm, mamba_out)
    query = low(rotate(low_back(product(normed, query_weight)).reshape(row_count, QH, HEAD), position))
    keys_all = low(rotate(low_back(product(normed, key_weight)).reshape(row_count, KVH, HEAD), position))
    values_all = low(low_back(product(normed, value_weight)).reshape(row_count, KVH, HEAD))
    group_size = QH // KVH
    query_grouped = query.reshape(row_count, KVH, group_size, HEAD)
    scores = low_back(jnp.einsum('igkd,jgd->gkij', query_grouped, keys_all, precision=highest) * HEAD ** (-0.5))
    scores = jnp.where(allowed[None, None], scores, -jnp.inf)
    attention_weights = low(jax.nn.softmax(scores, axis=-1))
    attended = low(low_back(jnp.einsum('gkij,jgd->igkd', attention_weights, values_all, precision=highest)))
    attn_branch = product_back(attended.reshape(row_count, QH * HEAD), attention_out)
    branch = low_back(mix_out + attn_branch)
    middle = low(rows_in + branch)
    normed_mid = low(rms_norm(middle, gain_middle))
    gate_ff = low_back(product(normed_mid, feed_gate))
    up_ff = low_back(product(normed_mid, feed_up))
    hidden = low(jax.nn.silu(gate_ff) * up_ff)
    return middle + low_back(product_back(hidden, feed_down))

def reference(inputs, out_grad, deal_order, segment, query_weight, key_weight, value_weight, attention_out, mamba_gate, mamba_input, step_weight, state_weight, mamba_out, feed_gate, feed_up, feed_down, gain_input, gain_middle, kernel_inner, kernel_state, mixer_gain, step_bias, log_rate, skip_gain):
    weights32 = tuple((item.astype(jnp.float32) for item in (query_weight, key_weight, value_weight, attention_out, mamba_gate, mamba_input, step_weight, state_weight, mamba_out, feed_gate, feed_up, feed_down, gain_input, gain_middle, kernel_inner, kernel_state, mixer_gain, step_bias, log_rate, skip_gain)))
    micro_count = inputs.shape[0]
    total_rows = inputs.shape[1]

    def deal_rows(source, target_rows):
        return jnp.zeros_like(source).at[target_rows].set(source)
    dealt_in = jax.vmap(deal_rows)(inputs.astype(jnp.float32), deal_order)
    dealt_grad = jax.vmap(deal_rows)(out_grad.astype(jnp.float32), deal_order)
    block_count = micro_count * (total_rows // GROUP_ROWS)
    stacked_in = dealt_in.reshape(block_count, GROUP_ROWS, -1)
    stacked_grad = dealt_grad.reshape(block_count, GROUP_ROWS, -1)
    stacked_seg = segment.reshape(block_count, GROUP_ROWS)

    def run_group(running_sum, batch_item):
        rows_in, cot_rows, seg_rows = batch_item

        def forward(prm, rows_value):
            return layer(prm, rows_value, seg_rows)
        result, pull = jax.vjp(forward, weights32, rows_in)
        grad_params, grad_rows = pull(cot_rows)
        return (jax.tree.map(jnp.add, running_sum, grad_params), (result, grad_rows))
    zero_sums = jax.tree.map(jnp.zeros_like, weights32)
    totals, (results, row_grads) = lax.scan(run_group, zero_sums, (stacked_in, stacked_grad, stacked_seg))
    results = results.reshape(micro_count, total_rows, -1)
    row_grads = row_grads.reshape(micro_count, total_rows, -1)

    def take_rows(source, target_rows):
        return source[target_rows]
    block_out = jax.vmap(take_rows)(results, deal_order).astype(jnp.bfloat16)
    grad_input = jax.vmap(take_rows)(row_grads, deal_order).astype(jnp.bfloat16)
    return (block_out, grad_input, totals[0], totals[1], totals[2], totals[3], totals[4], totals[5], totals[6], totals[7], totals[8], totals[9], totals[10], totals[11], totals[12], totals[13], totals[14], totals[15], totals[16], totals[17], totals[18], totals[19])
```

```python
import math

import jax
import jax.numpy as jnp
from jax import lax
from jax.sharding import PartitionSpec as P

HEAD = 128
SH = 48
SHD = 64
NS = 256
CONV = 4
STEP_PAD = 128

epsilon = 1e-05
rope_base = 100000000000.0
f32 = jnp.float32
bf16 = jnp.bfloat16


def project(left, right):
    return jnp.dot(left, right, preferred_element_type=f32)


def project_back(left, right):
    return lax.dot_general(left, right, (((1,), (1,)), ((), ())), preferred_element_type=f32)


def outer_sum(left, right):
    return lax.dot_general(left, right, (((0,), (0,)), ((), ())), preferred_element_type=f32)


def rms_scale(values):
    return lax.rsqrt(jnp.mean(values * values, axis=-1, keepdims=True) + epsilon)


def rms_back(grad, values, scale, gain):
    weighted = grad * gain
    inner = jnp.sum(weighted * values, axis=-1, keepdims=True)
    return scale * weighted - values * (scale * scale * scale * inner / values.shape[-1])


def shift_down(values, count):
    return jnp.concatenate([jnp.zeros((count, values.shape[1]), values.dtype), values[:-count]], axis=0)


def shift_up(values, count):
    return jnp.concatenate([values[count:], jnp.zeros((count, values.shape[1]), values.dtype)], axis=0)


def conv_sum(signal, kernel, position):
    summed = kernel[CONV][None, :] + signal * kernel[0][None, :]
    for tap in range(1, CONV):
        moved = jnp.where(position >= tap, shift_down(signal, tap), 0.0)
        summed = summed + moved * kernel[tap][None, :]
    return summed


def silu_back(values):
    sig = jax.nn.sigmoid(values)
    return sig * (1.0 + values * (1.0 - sig))


def conv_back(grad, signal, kernel, position):
    grad_sum = grad * silu_back(conv_sum(signal, kernel, position))
    grad_signal = grad_sum * kernel[0][None, :]
    grad_taps = [jnp.sum(grad_sum * signal, axis=0)]
    for tap in range(1, CONV):
        kept = jnp.where(position >= tap, grad_sum, 0.0)
        grad_signal = grad_signal + shift_up(kept, tap) * kernel[tap][None, :]
        grad_taps.append(jnp.sum(kept * shift_down(signal, tap), axis=0))
    grad_taps.append(jnp.sum(grad_sum, axis=0))
    return grad_signal, jnp.stack(grad_taps)


def rope_tables(position):
    half_size = HEAD // 2
    frequency = jnp.exp(jnp.arange(half_size, dtype=f32) * (-2.0 * math.log(rope_base) / HEAD))
    angles = position.astype(f32) * frequency[None, :]
    return jnp.cos(angles)[:, None, :], jnp.sin(angles)[:, None, :]


def rotate(values, cosine, sine):
    half_size = HEAD // 2
    first, second = values[..., :half_size], values[..., half_size:]
    return jnp.concatenate([first * cosine - second * sine, second * cosine + first * sine], axis=-1)


def rotate_back(values, cosine, sine):
    return rotate(values, cosine, -sine)


def local(
    inputs,
    out_grad,
    deal_order,
    segment,
    query_weight,
    key_weight,
    value_weight,
    attention_out,
    mamba_gate,
    mamba_input,
    step_weight,
    state_weight,
    mamba_out,
    feed_gate,
    feed_up,
    feed_down,
    gain_input,
    gain_middle,
    kernel_inner,
    kernel_state,
    mixer_gain,
    step_bias,
    log_rate,
    skip_gain,
):
    micro, own, width = inputs.shape
    groups = lax.axis_size("dp")
    lanes = lax.axis_size("tensor")
    lane = lax.axis_index("tensor")
    group = lax.axis_index("dp")
    device = group * lanes + lane
    per = own // groups
    rows = own * lanes
    total = micro * rows
    inner_width = SH * SHD
    scale_factor = HEAD ** (-0.5)
    outer_count = groups // 4
    shard = width // groups

    swap_lane = [(0, 1), (1, 0)]

    def other_lane(values):
        return lax.ppermute(values, "tensor", swap_lane)

    def other_group(values, bits):
        return lax.ppermute(values, "dp", [(i, i ^ bits) for i in range(groups)])

    step_padded = jnp.pad(step_weight, ((0, 0), (0, STEP_PAD - step_weight.shape[1])))
    early = [mamba_gate, mamba_input, state_weight, step_padded, query_weight, key_weight, value_weight, mamba_out, attention_out]
    late = [feed_gate, feed_up, feed_down]

    def gather(pieces):
        whole = lax.all_gather(jnp.concatenate(pieces, axis=1), "dp", axis=0, tiled=True)
        found, start = [], 0
        for piece in pieces:
            found.append(whole[:, start : start + piece.shape[1]])
            start += piece.shape[1]
        return found

    full_gate, full_input, full_state, full_step, full_query, full_key, full_value, full_mix, full_attn = gather(early)
    full_fgate, full_fup, full_fdown = gather(late)

    own_places = jnp.arange(own, dtype=jnp.int32)
    own_order = lax.dynamic_slice_in_dim(deal_order, device * own, own, 1)
    micro_index = jnp.arange(micro, dtype=jnp.int32)[:, None]

    def buffer_place(destination, rank):
        return destination * (micro * per) + micro_index * per + rank

    send_rank = jnp.sum((own_order[:, None, :] < own_order[:, :, None]).astype(jnp.int32), axis=2)
    send_place = buffer_place(send_rank // per, send_rank % per).reshape(-1)
    lane_order = lax.dynamic_index_in_dim(deal_order.reshape(micro, groups, lanes, own), lane, 2, keepdims=False)
    slots = device * own + own_places
    found = lane_order[:, None, :, :] == slots[None, :, None, None]
    source = jnp.sum(
        jnp.where(found, jnp.arange(groups, dtype=jnp.int32)[None, None, :, None], 0), axis=(2, 3)
    )
    recv_rank = jnp.sum(
        ((source[:, None, :] == source[:, :, None]) & (own_places[None, None, :] < own_places[None, :, None])).astype(jnp.int32),
        axis=2,
    )
    recv_place = buffer_place(source, recv_rank).reshape(-1)
    buffer_places = jnp.arange(micro * own, dtype=jnp.int32)
    send_pick = (buffer_places[:, None] == send_place[None, :]).astype(bf16)
    recv_pick = (recv_place[:, None] == buffer_places[None, :]).astype(bf16)

    def exchange(buffer):
        return lax.all_to_all(
            buffer.reshape(groups, micro * per, width), "dp", split_axis=0, concat_axis=0, tiled=True
        ).reshape(micro * own, width)

    def deal(values):
        sent = project(send_pick, values.reshape(micro * own, width)).astype(bf16)
        return project(recv_pick, exchange(sent)).astype(bf16)

    def deal_back(values):
        sent = outer_sum(recv_pick, values).astype(bf16)
        return outer_sum(send_pick, exchange(sent)).astype(bf16).reshape(micro, own, width)

    def join_lanes(values):
        mine = values.reshape(micro, 1, own, -1)
        theirs = other_lane(values).reshape(micro, 1, own, -1)
        low = jnp.where(lane == 0, mine, theirs)
        high = jnp.where(lane == 0, theirs, mine)
        return jnp.concatenate([low, high], axis=1).reshape(total, -1)

    def lane_rows(values, which):
        return lax.dynamic_index_in_dim(
            values.reshape(micro, lanes, own, -1), which, 1, keepdims=False
        ).reshape(micro * own, -1)

    own_in = deal(inputs)
    own_grad = deal(out_grad)
    whole_in = join_lanes(own_in)
    whole_grad = join_lanes(own_grad)

    before = jnp.sum((segment[:, None, :] < segment[:, :, None]).astype(jnp.int32), axis=2)
    places = jnp.arange(rows, dtype=jnp.int32)
    allowed = (segment[:, :, None] == segment[:, None, :]) & (places[None, None, :] <= places[None, :, None])
    position = (places[None, :] - before).reshape(total, 1)

    core_bit = group & 1
    y_bit = (group >> 1) & 1
    outer_index = group >> 2

    def split_left(left):
        blocks = left.reshape(left.shape[0], outer_count, 2, 2, shard)

        def part(core, y):
            picked = lax.dynamic_index_in_dim(blocks, core, 3, keepdims=False)
            picked = lax.dynamic_index_in_dim(picked, y, 2, keepdims=False)
            return picked.reshape(left.shape[0], outer_count * shard)

        send = jnp.concatenate([part(1 - core_bit, 1 - y_bit), part(1 - core_bit, y_bit)], axis=1)
        return send, part(core_bit, 1 - y_bit), part(core_bit, y_bit)

    quarter = outer_count * shard

    def reduce_weight(left_parts, right):
        send, keep_send, keep = left_parts
        from_core = other_group(outer_sum(send, right).astype(bf16), 1)
        to_y = (outer_sum(keep_send, right) + from_core[:quarter].astype(f32)).astype(bf16)
        from_y = other_group(to_y, 2).reshape(outer_count, shard, -1)
        mine = (outer_sum(keep, right) + from_core[quarter:].astype(f32)).astype(bf16).reshape(outer_count, shard, -1)

        def pair_sum(index):
            a = lax.dynamic_index_in_dim(mine, index, 0, keepdims=False).astype(f32)
            b = lax.dynamic_index_in_dim(from_y, index, 0, keepdims=False).astype(f32)
            return a + b

        result = pair_sum(outer_index)
        for step in range(1, outer_count):
            got = other_group(pair_sum(outer_index ^ step).astype(bf16), step << 2)
            result = result + got.astype(f32)
        return result

    in32 = whole_in.astype(f32)
    in_scale = rms_scale(in32)
    normed_low = (in32 * in_scale * gain_input).astype(bf16)
    gate_z = project(normed_low, full_gate)
    ssm_in = project(normed_low, full_input)
    state_raw = project(normed_low, full_state)
    heads = step_weight.shape[1]
    raw_step = project(normed_low, full_step)[:, :heads]
    ssm_cols = jax.nn.silu(conv_sum(ssm_in, kernel_inner, position))
    state_act = jax.nn.silu(conv_sum(state_raw, kernel_state, position)).astype(bf16)
    b_state = state_act[:, :NS].reshape(micro, rows, NS)
    c_state = state_act[:, NS:].reshape(micro, rows, NS)
    state_inner = jnp.einsum("mis,mjs->mij", c_state, b_state, preferred_element_type=f32)
    rate = -jnp.exp(log_rate)
    step_size = jax.nn.softplus(raw_step + step_bias)
    step_heads = step_size.reshape(micro, rows, heads).transpose(0, 2, 1)
    lower = (places[None, :] <= places[:, None]).astype(f32)
    running = jnp.einsum(
        "mhj,ij->mhi", step_heads * rate[None, :, None], lower, precision=lax.Precision.HIGHEST, preferred_element_type=f32
    )
    decay = jnp.exp(jnp.where(allowed[:, None], running[:, :, :, None] - running[:, :, None, :], -jnp.inf))
    mixing_low = (state_inner[:, None] * decay * step_heads[:, :, None, :]).astype(bf16)
    ssm_heads = ssm_cols.reshape(micro, rows, heads, SHD)
    heads_low = ssm_heads.astype(bf16)
    skip_wide = jnp.repeat(skip_gain, SHD)[None, :]
    ssm_out = (
        jnp.einsum("mhij,mjhd->mihd", mixing_low, heads_low, preferred_element_type=f32).reshape(total, -1)
        + skip_wide * ssm_cols
    )
    silu_z = jax.nn.silu(gate_z)
    gated = ssm_out * silu_z
    square_own = jnp.sum(gated * gated, axis=1)
    square_sum = square_own + other_lane(square_own)
    inv_rms = lax.rsqrt(square_sum / inner_width + epsilon)[:, None]
    gated_low = (gated * inv_rms * mixer_gain).astype(bf16)

    cosine, sine = rope_tables(position)
    query_low = rotate(project(normed_low, full_query).reshape(total, -1, HEAD), cosine, sine).astype(bf16)
    key_low = rotate(project(normed_low, full_key).reshape(total, -1, HEAD), cosine, sine).astype(bf16)
    value_low = project(normed_low, full_value).astype(bf16)
    kv_here = key_low.shape[1]
    query_low = query_low.reshape(micro, rows, kv_here, -1, HEAD)
    key_low = key_low.reshape(micro, rows, kv_here, HEAD)
    value_low = value_low.reshape(micro, rows, kv_here, HEAD)
    logits = jnp.einsum("migkd,mjgd->mgkij", query_low, key_low, preferred_element_type=f32) * scale_factor
    logits = jnp.where(allowed[:, None, None], logits, -jnp.inf)
    exp_scores = jnp.exp(logits - jnp.max(logits, axis=-1, keepdims=True))
    probs = exp_scores / jnp.sum(exp_scores, axis=-1, keepdims=True)
    probs_low = probs.astype(bf16)
    attended_low = (
        jnp.einsum("mgkij,mjgd->migkd", probs_low, value_low, preferred_element_type=f32).astype(bf16).reshape(total, -1)
    )
    branch_part = (project_back(gated_low, full_mix) + project_back(attended_low, full_attn)).astype(bf16)
    branch = branch_part.astype(f32) + other_lane(branch_part).astype(f32)
    whole_mid = (in32 + branch).astype(bf16)
    mid32 = whole_mid.astype(f32)
    mid_scale = rms_scale(mid32)
    mid_low = (mid32 * mid_scale * gain_middle).astype(bf16)
    gate_ff = project(mid_low, full_fgate)
    up_ff = project(mid_low, full_fup)
    sig_ff = jax.nn.sigmoid(gate_ff)
    hidden_low = (gate_ff * sig_ff * up_ff).astype(bf16)

    grad_left = split_left(whole_grad)
    mid_left = split_left(mid_low)
    total_fdown = reduce_weight(grad_left, hidden_low)
    grad_hidden = project(whole_grad, full_fdown)
    gate_ff_low = (grad_hidden * up_ff * (sig_ff * (1.0 + gate_ff * (1.0 - sig_ff)))).astype(bf16)
    up_ff_low = (grad_hidden * (gate_ff * sig_ff)).astype(bf16)
    total_fgate = reduce_weight(mid_left, gate_ff_low)
    total_fup = reduce_weight(mid_left, up_ff_low)
    grad_mid_norm = project_back(gate_ff_low, full_fgate) + project_back(up_ff_low, full_fup)
    grad_gain_mid = jnp.sum(grad_mid_norm * mid32 * mid_scale, axis=0)
    mid_part = rms_back(grad_mid_norm, mid32, mid_scale, gain_middle).astype(bf16)
    grad_middle = whole_grad.astype(f32) + (mid_part.astype(f32) + other_lane(mid_part).astype(f32))
    whole_branch = grad_middle.astype(bf16)

    ffn_part = project_back(hidden_low, full_fdown).astype(bf16)
    ffn_out = lane_rows(ffn_part, lane).astype(f32) + other_lane(lane_rows(ffn_part, 1 - lane)).astype(f32)
    out_rows = (lane_rows(whole_mid, lane).astype(f32) + ffn_out).astype(bf16)
    block_out = deal_back(out_rows)

    branch_left = split_left(whole_branch)
    total_mix = reduce_weight(branch_left, gated_low)
    total_attn = reduce_weight(branch_left, attended_low)
    grad_gated_norm = project(whole_branch, full_mix)
    scaled_grad = grad_gated_norm * mixer_gain
    grad_mixer = jnp.sum(grad_gated_norm * gated * inv_rms, axis=0)
    cross_own = jnp.sum(scaled_grad * gated, axis=1)
    cross_sum = cross_own + other_lane(cross_own)
    grad_gated = inv_rms * scaled_grad - gated * (inv_rms**3 * cross_sum[:, None] / inner_width)
    grad_ssm_out = grad_gated * silu_z
    gate_low = (grad_gated * ssm_out * silu_back(gate_z)).astype(bf16)
    normed_left = split_left(normed_low)
    total_gate = reduce_weight(normed_left, gate_low)

    grad_attended = project(whole_branch, full_attn).astype(bf16).reshape(micro, rows, kv_here, -1, HEAD)
    grad_probs = jnp.einsum("migkd,mjgd->mgkij", grad_attended, value_low, preferred_element_type=f32)
    grad_value = jnp.einsum("mgkij,migkd->mjgd", probs_low, grad_attended, preferred_element_type=f32)
    weighted_sum = jnp.sum(probs * grad_probs, axis=-1, keepdims=True)
    grad_logits = (probs * (grad_probs - weighted_sum)).astype(bf16)
    grad_query_rot = jnp.einsum("mgkij,mjgd->migkd", grad_logits, key_low, preferred_element_type=f32) * scale_factor
    grad_key_rot = jnp.einsum("mgkij,migkd->mjgd", grad_logits, query_low, preferred_element_type=f32) * scale_factor
    query_grad_low = rotate_back(grad_query_rot.reshape(total, -1, HEAD), cosine, sine).astype(bf16).reshape(total, -1)
    key_grad_low = rotate_back(grad_key_rot.reshape(total, -1, HEAD), cosine, sine).astype(bf16).reshape(total, -1)
    value_grad_low = grad_value.astype(bf16).reshape(total, -1)
    qkv_low = jnp.concatenate([query_grad_low, key_grad_low, value_grad_low], axis=1)
    total_qkv = reduce_weight(normed_left, qkv_low)

    grad_heads_low = grad_ssm_out.astype(bf16).reshape(micro, rows, heads, SHD)
    grad_ssm_cols = (
        jnp.einsum("mhij,mihd->mjhd", mixing_low, grad_heads_low, preferred_element_type=f32).reshape(total, -1)
        + skip_wide * grad_ssm_out
    )
    grad_skip = jnp.sum((grad_ssm_out * ssm_cols).reshape(total, heads, SHD), axis=(0, 2))
    grad_mixing = jnp.einsum("mihd,mjhd->mhij", grad_heads_low, heads_low, preferred_element_type=f32)
    grad_decay = grad_mixing * decay
    inner_low = jnp.sum(grad_decay * step_heads[:, :, None, :], axis=1).astype(bf16)
    grad_direct = jnp.sum(grad_decay * state_inner[:, None], axis=2)
    grad_rows = jnp.sum(grad_decay * state_inner[:, None] * step_heads[:, :, None, :], axis=3)
    grad_running = grad_rows - step_heads * grad_direct
    grad_product = jnp.einsum(
        "mhi,ij->mhj", grad_running, lower, precision=lax.Precision.HIGHEST, preferred_element_type=f32
    )
    grad_step = (grad_direct + grad_product * rate[None, :, None]).transpose(0, 2, 1).reshape(total, heads)
    grad_rate = jnp.sum(grad_product * step_heads, axis=(0, 2)) * rate
    grad_raw_step = grad_step * jax.nn.sigmoid(raw_step + step_bias)
    grad_bias = jnp.sum(grad_raw_step, axis=0)
    grad_c = jnp.einsum("mij,mjs->mis", inner_low, b_state, preferred_element_type=f32)
    grad_b = jnp.einsum("mij,mis->mjs", inner_low, c_state, preferred_element_type=f32)
    grad_state_act = jnp.concatenate([grad_b, grad_c], axis=2).reshape(total, 2 * NS)
    grad_state_raw, grad_kernel_state = conv_back(grad_state_act, state_raw, kernel_state, position)
    grad_ssm_in, grad_kernel_inner = conv_back(grad_ssm_cols, ssm_in, kernel_inner, position)
    input_low = grad_ssm_in.astype(bf16)
    step_low = jnp.pad(grad_raw_step.astype(bf16), ((0, 0), (0, STEP_PAD - heads)))
    state_low = jnp.concatenate([grad_state_raw.astype(bf16), step_low], axis=1)
    total_input = reduce_weight(normed_left, input_low)
    total_state = reduce_weight(normed_left, state_low)

    grad_normed = project_back(gate_low, full_gate) + project_back(query_grad_low, full_query)
    grad_normed = grad_normed + project_back(key_grad_low, full_key) + project_back(value_grad_low, full_value)
    grad_normed = grad_normed + project_back(input_low, full_input)
    grad_normed = grad_normed + project_back(state_low[:, : 2 * NS], full_state) + project_back(step_low, full_step)
    grad_gain_in = jnp.sum(grad_normed * in32 * in_scale, axis=0)
    in_part = rms_back(grad_normed, in32, in_scale, gain_input).astype(bf16)
    in_sum = lane_rows(in_part, lane).astype(f32) + other_lane(lane_rows(in_part, 1 - lane)).astype(f32)
    in_grad_rows = (in_sum + lane_rows(grad_middle, lane)).astype(bf16)
    grad_input = deal_back(in_grad_rows)

    shared = [grad_gain_in, grad_gain_mid, grad_kernel_state.reshape(-1)]
    split = [grad_kernel_inner.reshape(-1), grad_mixer, grad_bias, grad_rate, grad_skip]
    both_flat = jnp.concatenate(shared + split)
    flat_size = both_flat.shape[0]
    padded = -(-flat_size // 1024) * 1024
    flat = jnp.pad(both_flat, (0, padded - flat_size)).reshape(padded // 128, 128)
    bits = 1
    while bits < groups:
        flat = flat + other_group(flat, bits)
        bits *= 2
    theirs = other_lane(flat).reshape(-1)
    flat = flat.reshape(-1)
    pieces = []
    start = 0
    for item in shared:
        pieces.append(flat[start : start + item.shape[0]] + theirs[start : start + item.shape[0]])
        start += item.shape[0]
    for item in split:
        mine, other = flat[start : start + item.shape[0]], theirs[start : start + item.shape[0]]
        pieces.append((jnp.where(lane == 0, mine, other), jnp.where(lane == 0, other, mine)))
        start += item.shape[0]
    sum_gin, sum_gmid, sum_kst = pieces[0], pieces[1], pieces[2].reshape(CONV + 1, -1)
    sum_kin = jnp.concatenate([half.reshape(CONV + 1, -1) for half in pieces[3]], axis=1)
    sum_mix, sum_bias, sum_rate, sum_skip = [jnp.concatenate(pair) for pair in pieces[4:]]

    query_cols = query_weight.shape[1]
    key_cols = key_weight.shape[1]
    total_query = total_qkv[:, :query_cols]
    total_key = total_qkv[:, query_cols : query_cols + key_cols]
    total_value = total_qkv[:, query_cols + key_cols :]
    total_step = total_state[:, 2 * NS : 2 * NS + heads]
    state_rows = total_state[:, : 2 * NS].reshape(lanes, shard // lanes, 2 * NS)
    state_own = lax.dynamic_index_in_dim(state_rows, lane, 0, keepdims=False)
    state_send = lax.dynamic_index_in_dim(state_rows, 1 - lane, 0, keepdims=False)
    state_lane = state_own + other_lane(state_send)
    return (
        block_out,
        grad_input,
        total_query,
        total_key,
        total_value,
        total_attn,
        total_gate,
        total_input,
        total_step,
        state_lane,
        total_mix,
        total_fgate,
        total_fup,
        total_fdown,
        sum_gin,
        sum_gmid,
        sum_kin,
        sum_kst,
        sum_mix,
        sum_bias,
        sum_rate,
        sum_skip,
    )


def solution(mesh):
    both = P("dp", "tensor")
    in_specs = (
        P(None, ("dp", "tensor"), None),
        P(None, ("dp", "tensor"), None),
        P(),
        P(None, "dp"),
        both,
        both,
        both,
        both,
        both,
        both,
        both,
        P("dp", None),
        both,
        both,
        both,
        both,
        P(),
        P(),
        P(None, "tensor"),
        P(),
        P("tensor"),
        P("tensor"),
        P("tensor"),
        P("tensor"),
    )
    out_specs = (
        P(None, ("dp", "tensor"), None),
        P(None, ("dp", "tensor"), None),
        both,
        both,
        both,
        both,
        both,
        both,
        both,
        P(("dp", "tensor"), None),
        both,
        both,
        both,
        both,
        P(),
        P(),
        P(),
        P(),
        P(),
        P(),
        P(),
        P(),
    )
    return jax.shard_map(local, mesh=mesh, in_specs=in_specs, out_specs=out_specs, check_vma=False)
```

```python
import math

import jax
import jax.numpy as jnp
from jax import lax
from jax.experimental import pallas as pl
from jax.experimental.pallas import tpu as pltpu
from jax.sharding import PartitionSpec as P

HEAD = 128
SH = 48
SHD = 64
NS = 256
CONV = 4
STEP_PAD = 128

epsilon = 1e-05
rope_base = 100000000000.0
f32 = jnp.float32
bf16 = jnp.bfloat16


def project(left, right):
    return jnp.dot(left, right, preferred_element_type=f32)


def project_back(left, right):
    return lax.dot_general(left, right, (((1,), (1,)), ((), ())), preferred_element_type=f32)


def outer_sum(left, right):
    return lax.dot_general(left, right, (((0,), (0,)), ((), ())), preferred_element_type=f32)


def rms_scale(values):
    return lax.rsqrt(jnp.mean(values * values, axis=-1, keepdims=True) + epsilon)


def rms_back(grad, values, scale, gain):
    weighted = grad * gain
    inner = jnp.sum(weighted * values, axis=-1, keepdims=True)
    return scale * weighted - values * (scale * scale * scale * inner / values.shape[-1])


def shift_down(values, count):
    return jnp.concatenate([jnp.zeros((count, values.shape[1]), values.dtype), values[:-count]], axis=0)


def shift_up(values, count):
    return jnp.concatenate([values[count:], jnp.zeros((count, values.shape[1]), values.dtype)], axis=0)


def conv_sum(signal, kernel, position):
    summed = kernel[CONV][None, :] + signal * kernel[0][None, :]
    for tap in range(1, CONV):
        moved = jnp.where(position >= tap, shift_down(signal, tap), 0.0)
        summed = summed + moved * kernel[tap][None, :]
    return summed


def silu_back(values):
    sig = jax.nn.sigmoid(values)
    return sig * (1.0 + values * (1.0 - sig))


def conv_back(grad, signal, kernel, position):
    grad_sum = grad * silu_back(conv_sum(signal, kernel, position))
    grad_signal = grad_sum * kernel[0][None, :]
    grad_taps = [jnp.sum(grad_sum * signal, axis=0)]
    for tap in range(1, CONV):
        kept = jnp.where(position >= tap, grad_sum, 0.0)
        grad_signal = grad_signal + shift_up(kept, tap) * kernel[tap][None, :]
        grad_taps.append(jnp.sum(kept * shift_down(signal, tap), axis=0))
    grad_taps.append(jnp.sum(grad_sum, axis=0))
    return grad_signal, jnp.stack(grad_taps)


def rope_tables(position):
    half_size = HEAD // 2
    frequency = jnp.exp(jnp.arange(half_size, dtype=f32) * (-2.0 * math.log(rope_base) / HEAD))
    angles = position.astype(f32) * frequency[None, :]
    return jnp.cos(angles)[:, None, :], jnp.sin(angles)[:, None, :]


def rotate(values, cosine, sine):
    half_size = HEAD // 2
    first, second = values[..., :half_size], values[..., half_size:]
    return jnp.concatenate([first * cosine - second * sine, second * cosine + first * sine], axis=-1)


def copy_block(order_ref, source_ref, target_ref):
    target_ref[...] = source_ref[...]


def pick_blocks(values, order, block):
    height, width = values.shape
    if block % 128:
        return jnp.take(values.reshape(height, -1, block), order, axis=1).reshape(height, width)
    return pl.pallas_call(
        copy_block,
        out_shape=jax.ShapeDtypeStruct(values.shape, values.dtype),
        grid_spec=pltpu.PrefetchScalarGridSpec(
            num_scalar_prefetch=1,
            grid=(width // block,),
            in_specs=[pl.BlockSpec((height, block), lambda i, order: (0, order[i]))],
            out_specs=pl.BlockSpec((height, block), lambda i, order: (0, i)),
        ),
        cost_estimate=pl.CostEstimate(flops=0, transcendentals=0, bytes_accessed=4 * height * width),
    )(order, values)


def rotate_back(values, cosine, sine):
    return rotate(values, cosine, -sine)


NEGATIVE = -1e30


def sigmoid_of(values):
    return 1.0 / (1.0 + jnp.exp(-values))


def block_mask(rows, segment_col, segment_row):
    row_index = lax.broadcasted_iota(jnp.int32, (rows, rows), 0)
    col_index = lax.broadcasted_iota(jnp.int32, (rows, rows), 1)
    return jnp.where((segment_col == segment_row) & (col_index <= row_index), 0.0, NEGATIVE)


def conv_block(signal, taps_ref, position):
    summed = taps_ref[CONV : CONV + 1, :] + signal * taps_ref[0:1, :]
    moved = []
    for tap in range(1, CONV):
        shifted = jnp.where(position >= tap, pltpu.roll(signal, tap, 0), 0.0)
        moved.append(shifted)
        summed = summed + shifted * taps_ref[tap : tap + 1, :]
    return summed, moved


def mixing_block(inner, mask, run_col, run_row, step_row):
    decay = jnp.exp(run_col - run_row + mask)
    return decay, (inner * decay * step_row).astype(bf16)


def state_forward_kernel(
    signal_ref, gate_ref, taps_ref, skip_ref, state_ref, seg_col_ref, seg_row_ref, position_ref,
    run_row_ref, run_col_ref, step_ref, out_ref, square_ref, inner_ref, mask_ref,
):
    rows = signal_ref.shape[0]

    @pl.when(pl.program_id(1) == 0)
    def _():
        inner_ref[...] = lax.dot_general(
            state_ref[:, NS:], state_ref[:, :NS], (((1,), (1,)), ((), ())), preferred_element_type=f32
        )
        mask_ref[...] = block_mask(rows, seg_col_ref[...], seg_row_ref[0])
        square_ref[...] = jnp.zeros_like(square_ref)

    summed, _ = conv_block(signal_ref[...], taps_ref, position_ref[...])
    cols = summed * sigmoid_of(summed)
    cols_low = cols.astype(bf16)
    mixed = []
    for head in range(2):
        _, mixing = mixing_block(
            inner_ref[...], mask_ref[...], run_col_ref[0, 0, :, head : head + 1],
            run_row_ref[0, 0, head : head + 1, :], step_ref[0, 0, head : head + 1, :],
        )
        mixed.append(jnp.dot(mixing, cols_low, preferred_element_type=f32))
    lanes = lax.broadcasted_iota(jnp.int32, cols.shape, 1)
    out = jnp.where(lanes < SHD, mixed[0], mixed[1]) + skip_ref[...] * cols
    out_ref[...] = out
    gate = gate_ref[...]
    gated = out * (gate * sigmoid_of(gate))
    square_ref[...] += gated * gated


def state_backward_kernel(
    grad_ref, out_ref, gate_ref, signal_ref, taps_ref, skip_ref, gain_ref, scale_ref, cross_ref, state_ref,
    seg_col_ref, seg_row_ref, position_ref, run_row_ref, run_col_ref, step_ref,
    gate_low_ref, input_low_ref, sums_ref, direct_ref, along_ref, state_grad_ref, inner_ref, mask_ref, grad_inner_ref,
):
    rows = signal_ref.shape[0]

    @pl.when(pl.program_id(1) == 0)
    def _():
        inner_ref[...] = lax.dot_general(
            state_ref[:, NS:], state_ref[:, :NS], (((1,), (1,)), ((), ())), preferred_element_type=f32
        )
        mask_ref[...] = block_mask(rows, seg_col_ref[...], seg_row_ref[0])
        grad_inner_ref[...] = jnp.zeros_like(grad_inner_ref)

    grad, out, gate, signal = grad_ref[...], out_ref[...], gate_ref[...], signal_ref[...]
    position = position_ref[...]
    sig = sigmoid_of(gate)
    silu = gate * sig
    gated = out * silu
    scaled = grad * scale_ref[...]
    grad_gated = scaled * gain_ref[...] - gated * cross_ref[...]
    grad_out = grad_gated * silu
    gate_low_ref[...] = (grad_gated * out * (sig * (1.0 + gate * (1.0 - sig)))).astype(bf16)
    summed, moved = conv_block(signal, taps_ref, position)
    sig = sigmoid_of(summed)
    cols = summed * sig
    cols_low = cols.astype(bf16)
    grad_low = grad_out.astype(bf16)
    lanes = lax.broadcasted_iota(jnp.int32, cols.shape, 1)
    zero = jnp.zeros_like(grad_low)
    grad_cols = []
    for head in range(2):
        step_row = step_ref[0, 0, head : head + 1, :]
        inner = inner_ref[...]
        decay, mixing = mixing_block(
            inner, mask_ref[...], run_col_ref[0, 0, :, head : head + 1], run_row_ref[0, 0, head : head + 1, :], step_row
        )
        grad_cols.append(
            lax.dot_general(mixing, grad_low, (((0,), (0,)), ((), ())), preferred_element_type=f32)
        )
        grad_head = jnp.where((lanes < SHD) == (head == 0), grad_low, zero)
        grad_decay = lax.dot_general(
            grad_head, cols_low, (((1,), (1,)), ((), ())), preferred_element_type=f32
        ) * decay
        stepped = grad_decay * step_row
        grad_inner_ref[...] += stepped
        direct_ref[0, 0, head : head + 1, :] = jnp.sum(grad_decay * inner, axis=0, keepdims=True)
        along_ref[0, 0, :, head : head + 1] = jnp.sum(stepped * inner, axis=1, keepdims=True)
    grad_cols = jnp.where(lanes < SHD, grad_cols[0], grad_cols[1]) + skip_ref[...] * grad_out
    grad_sum = grad_cols * (sig * (1.0 + summed * (1.0 - sig)))
    grad_signal = grad_sum * taps_ref[0:1, :]
    sums_ref[0, 0:1, :] = jnp.sum(grad_sum * signal, axis=0, keepdims=True)
    for tap in range(1, CONV):
        kept = jnp.where(position >= tap, grad_sum, 0.0)
        grad_signal = grad_signal + pltpu.roll(kept, rows - tap, 0) * taps_ref[tap : tap + 1, :]
        sums_ref[0, tap : tap + 1, :] = jnp.sum(grad_sum * moved[tap - 1], axis=0, keepdims=True)
    sums_ref[0, CONV : CONV + 1, :] = jnp.sum(grad_sum, axis=0, keepdims=True)
    sums_ref[0, CONV + 1 : CONV + 2, :] = jnp.sum(scaled * gated, axis=0, keepdims=True)
    sums_ref[0, CONV + 2 : CONV + 3, :] = jnp.sum(grad_out * cols, axis=0, keepdims=True)
    sums_ref[0, CONV + 3 : CONV + 4, :] = jnp.zeros((1, cols.shape[1]), f32)
    input_low_ref[...] = grad_signal.astype(bf16)

    @pl.when(pl.program_id(1) == pl.num_programs(1) - 1)
    def _():
        inner_low = grad_inner_ref[...].astype(bf16)
        state_grad_ref[:, :NS] = lax.dot_general(
            inner_low, state_ref[:, NS:], (((0,), (0,)), ((), ())), preferred_element_type=f32
        )
        state_grad_ref[:, NS:] = jnp.dot(inner_low, state_ref[:, :NS], preferred_element_type=f32)


def state_specs(rows, pairs):
    block = pl.BlockSpec((rows, 2 * SHD), lambda m, p: (m, p))
    return {
        "block": block,
        "taps": pl.BlockSpec((CONV + 1, 2 * SHD), lambda m, p: (0, p)),
        "vector": pl.BlockSpec((1, 2 * SHD), lambda m, p: (0, p)),
        "state": pl.BlockSpec((rows, 2 * NS), lambda m, p: (m, 0)),
        "column": pl.BlockSpec((rows, 1), lambda m, p: (m, 0)),
        "row": pl.BlockSpec((1, 1, rows), lambda m, p: (m, 0, 0)),
        "head_row": pl.BlockSpec((1, 1, 2, rows), lambda m, p: (m, p, 0, 0)),
        "head_col": pl.BlockSpec((1, 1, rows, 2), lambda m, p: (m, p, 0, 0)),
    }


def state_forward(signal, gate, taps, skip, state, seg_col, seg_row, position, run_row, run_col, step):
    micro, pairs, _, rows = run_row.shape
    spec = state_specs(rows, pairs)
    total, width = signal.shape
    return pl.pallas_call(
        state_forward_kernel,
        out_shape=(jax.ShapeDtypeStruct((total, width), f32), jax.ShapeDtypeStruct((total, 2 * SHD), f32)),
        grid=(micro, pairs),
        in_specs=[spec[name] for name in (
            "block", "block", "taps", "vector", "state", "column", "row", "column", "head_row", "head_col", "head_row")],
        out_specs=(spec["block"], pl.BlockSpec((rows, 2 * SHD), lambda m, p: (m, 0))),
        scratch_shapes=[pltpu.VMEM((rows, rows), f32), pltpu.VMEM((rows, rows), f32)],
        cost_estimate=pl.CostEstimate(
            flops=8 * total * rows * width // SHD * SHD, transcendentals=total * rows * width // SHD, bytes_accessed=12 * total * width
        ),
        name="state_forward",
    )(signal, gate, taps, skip, state, seg_col, seg_row, position, run_row, run_col, step)


def state_backward(grad, out, gate, signal, taps, skip, gain, scale, cross, state, seg_col, seg_row, position, run_row, run_col, step):
    micro, pairs, _, rows = run_row.shape
    spec = state_specs(rows, pairs)
    total, width = signal.shape
    return pl.pallas_call(
        state_backward_kernel,
        out_shape=(
            jax.ShapeDtypeStruct((total, width), bf16),
            jax.ShapeDtypeStruct((total, width), bf16),
            jax.ShapeDtypeStruct((micro, 8, width), f32),
            jax.ShapeDtypeStruct(run_row.shape, f32),
            jax.ShapeDtypeStruct(run_col.shape, f32),
            jax.ShapeDtypeStruct((total, 2 * NS), f32),
        ),
        grid=(micro, pairs),
        in_specs=[spec[name] for name in (
            "block", "block", "block", "block", "taps", "vector", "vector", "column", "column", "state",
            "column", "row", "column", "head_row", "head_col", "head_row")],
        out_specs=(
            spec["block"], spec["block"], pl.BlockSpec((1, 8, 2 * SHD), lambda m, p: (m, 0, p)),
            spec["head_row"], spec["head_col"], spec["state"],
        ),
        scratch_shapes=[pltpu.VMEM((rows, rows), f32)] * 3,
        cost_estimate=pl.CostEstimate(
            flops=20 * total * rows * width, transcendentals=total * rows * width // SHD, bytes_accessed=20 * total * width
        ),
        name="state_backward",
    )(grad, out, gate, signal, taps, skip, gain, scale, cross, state, seg_col, seg_row, position, run_row, run_col, step)


def local(
    inputs,
    out_grad,
    deal_order,
    segment,
    query_weight,
    key_weight,
    value_weight,
    attention_out,
    mamba_gate,
    mamba_input,
    step_weight,
    state_weight,
    mamba_out,
    feed_gate,
    feed_up,
    feed_down,
    gain_input,
    gain_middle,
    kernel_inner,
    kernel_state,
    mixer_gain,
    step_bias,
    log_rate,
    skip_gain,
):
    micro, own, width = inputs.shape
    groups = lax.axis_size("dp")
    lanes = lax.axis_size("tensor")
    lane = lax.axis_index("tensor")
    group = lax.axis_index("dp")
    device = group * lanes + lane
    per = own // groups
    rows = own * lanes
    total = micro * rows
    inner_width = SH * SHD
    scale_factor = HEAD ** (-0.5)
    outer_count = groups // 4
    shard = width // groups

    swap_lane = [(0, 1), (1, 0)]

    def other_lane(values):
        return lax.ppermute(values, "tensor", swap_lane)

    def other_group(values, bits):
        return lax.ppermute(values, "dp", [(i, i ^ bits) for i in range(groups)])

    step_padded = jnp.pad(step_weight, ((0, 0), (0, STEP_PAD - step_weight.shape[1])))
    early = [mamba_gate, mamba_input, state_weight, step_padded, query_weight, key_weight, value_weight, mamba_out, attention_out]
    late = [feed_gate, feed_up, feed_down]

    def gather(pieces):
        whole = lax.all_gather(jnp.concatenate(pieces, axis=1), "dp", axis=0, tiled=True)
        found, start = [], 0
        for piece in pieces:
            found.append(whole[:, start : start + piece.shape[1]])
            start += piece.shape[1]
        return found

    full_gate, full_input, full_state, full_step, full_query, full_key, full_value, full_mix, full_attn = gather(early)
    full_fgate, full_fup, full_fdown = gather(late)

    own_places = jnp.arange(own, dtype=jnp.int32)
    own_order = lax.dynamic_slice_in_dim(deal_order, device * own, own, 1)
    micro_index = jnp.arange(micro, dtype=jnp.int32)[:, None]

    def buffer_place(destination, rank):
        return destination * (micro * per) + micro_index * per + rank

    send_rank = jnp.sum((own_order[:, None, :] < own_order[:, :, None]).astype(jnp.int32), axis=2)
    send_place = buffer_place(send_rank // per, send_rank % per).reshape(-1)
    lane_order = lax.dynamic_index_in_dim(deal_order.reshape(micro, groups, lanes, own), lane, 2, keepdims=False)
    slots = device * own + own_places
    found = lane_order[:, None, :, :] == slots[None, :, None, None]
    source = jnp.sum(
        jnp.where(found, jnp.arange(groups, dtype=jnp.int32)[None, None, :, None], 0), axis=(2, 3)
    )
    recv_rank = jnp.sum(
        ((source[:, None, :] == source[:, :, None]) & (own_places[None, None, :] < own_places[None, :, None])).astype(jnp.int32),
        axis=2,
    )
    recv_place = buffer_place(source, recv_rank).reshape(-1)
    buffer_places = jnp.arange(micro * own, dtype=jnp.int32)
    send_pick = (buffer_places[:, None] == send_place[None, :]).astype(bf16)
    recv_pick = (recv_place[:, None] == buffer_places[None, :]).astype(bf16)

    def exchange(buffer):
        return lax.all_to_all(
            buffer.reshape(groups, micro * per, width), "dp", split_axis=0, concat_axis=0, tiled=True
        ).reshape(micro * own, width)

    def deal(values):
        sent = project(send_pick, values.reshape(micro * own, width)).astype(bf16)
        return project(recv_pick, exchange(sent)).astype(bf16)

    def deal_order_rows(values):
        return outer_sum(recv_pick, values).astype(bf16)

    def deal_take(moved):
        return outer_sum(send_pick, moved).astype(bf16).reshape(micro, own, width)

    def join_lanes(values):
        mine = values.reshape(micro, 1, own, -1)
        theirs = other_lane(values).reshape(micro, 1, own, -1)
        low = jnp.where(lane == 0, mine, theirs)
        high = jnp.where(lane == 0, theirs, mine)
        return jnp.concatenate([low, high], axis=1).reshape(total, -1)

    def lane_rows(values, which):
        return lax.dynamic_index_in_dim(
            values.reshape(micro, lanes, own, -1), which, 1, keepdims=False
        ).reshape(micro * own, -1)

    own_in = deal(inputs)
    own_grad = deal(out_grad)
    whole_in = join_lanes(own_in)
    whole_grad = join_lanes(own_grad)

    before = jnp.sum((segment[:, None, :] < segment[:, :, None]).astype(jnp.int32), axis=2)
    places = jnp.arange(rows, dtype=jnp.int32)
    allowed = (segment[:, :, None] == segment[:, None, :]) & (places[None, None, :] <= places[None, :, None])
    position = (places[None, :] - before).reshape(total, 1)

    masks = [1, 2] + [4, 12][: max(0, groups.bit_length() - 3)]
    while 1 << len(masks) < groups:
        masks.append(1 << len(masks))
    relative = []
    for block in range(groups):
        flip = 0
        for place, mask in enumerate(masks):
            if block >> (len(masks) - 1 - place) & 1:
                flip ^= mask
        relative.append(flip)
    block_order = jnp.bitwise_xor(group.astype(jnp.int32), jnp.array(relative, jnp.int32))
    half_width = width // 2

    def split_left(left):
        mixed = pick_blocks(left, block_order, shard)
        return mixed[:, :half_width], mixed[:, half_width:]

    inner_places = list(range(1, len(masks)))

    def core_send(left_parts, right):
        return outer_sum(left_parts[1], right).astype(bf16)

    def halve(kept, place):
        return (
            lax.slice_in_dim(kept, 1, 2, axis=place - 1).reshape(-1, kept.shape[-1]),
            lax.slice_in_dim(kept, 0, 1, axis=place - 1),
        )

    class Reduction:
        def __init__(self, first):
            self.places = [place for place in first if place in inner_places]
            self.places += [place for place in inner_places if place not in first]
            self.stage = 0

        def move(self, send, kept):
            self.came = other_group(send, masks[self.places[self.stage]])
            self.kept = kept
            self.stage += 1

        def first(self, left_parts, right, from_core):
            kept = (outer_sum(left_parts[0], right) + from_core.astype(f32)).astype(bf16)
            kept = kept.reshape((2,) * len(inner_places) + (shard, -1))
            return halve(kept, self.places[0])

        def added(self):
            return self.kept.astype(f32) + self.came.reshape(self.kept.shape).astype(f32)

        def next(self):
            return halve(self.added().astype(bf16), self.places[self.stage])

        def last(self):
            return self.added().reshape(shard, -1)

        def step(self):
            return self.next() if self.stage < len(self.places) else self.last()

    def advance(reductions, *others):
        steps, results = unit(lambda: ([red.step() for red in reductions], [work() for work in others]))
        for red, step in zip(reductions, steps):
            if red.stage < len(red.places):
                red.move(*step)
            else:
                red.result = step
        return results

    order = [deal_order[0, 0] >= 0]

    def unit(work):
        shapes = jax.eval_shape(work)
        results = lax.cond(
            order[0], work, lambda: jax.tree.map(lambda leaf: jnp.zeros(leaf.shape, leaf.dtype), shapes)
        )
        results, order[0] = lax.optimization_barrier((results, order[0]))
        return results

    in32 = whole_in.astype(f32)
    in_scale = rms_scale(in32)
    normed_low = (in32 * in_scale * gain_input).astype(bf16)
    gate_z = project(normed_low, full_gate)
    ssm_in = project(normed_low, full_input)
    state_raw = project(normed_low, full_state)
    heads = step_weight.shape[1]
    raw_step = project(normed_low, full_step)[:, :heads]
    state_low = jax.nn.silu(conv_sum(state_raw, kernel_state, position)).astype(bf16)
    rate = -jnp.exp(log_rate)
    step_size = jax.nn.softplus(raw_step + step_bias)
    step_heads = step_size.reshape(micro, rows, heads).transpose(0, 2, 1)
    lower = (places[None, :] <= places[:, None]).astype(f32)
    running = jnp.einsum(
        "mhj,ij->mhi", step_heads * rate[None, :, None], lower, precision=lax.Precision.HIGHEST, preferred_element_type=f32
    )
    pairs = heads // 2
    run_row = running.reshape(micro, pairs, 2, rows)
    run_col = run_row.transpose(0, 1, 3, 2)
    step_row = step_heads.reshape(micro, pairs, 2, rows)
    skip_wide = jnp.repeat(skip_gain, SHD)[None, :]
    layout = (state_low, segment.reshape(total, 1), segment.reshape(micro, 1, rows), position, run_row, run_col, step_row)
    ssm_out, squares = state_forward(ssm_in, gate_z, kernel_inner, skip_wide, *layout)
    square_own = jnp.sum(squares, axis=1)
    square_sum = square_own + other_lane(square_own)
    inv_rms = lax.rsqrt(square_sum / inner_width + epsilon)[:, None]
    gated_low = (ssm_out * jax.nn.silu(gate_z) * inv_rms * mixer_gain).astype(bf16)

    cosine, sine = rope_tables(position)
    query_low = rotate(project(normed_low, full_query).reshape(total, -1, HEAD), cosine, sine).astype(bf16)
    key_low = rotate(project(normed_low, full_key).reshape(total, -1, HEAD), cosine, sine).astype(bf16)
    value_low = project(normed_low, full_value).astype(bf16)
    kv_here = key_low.shape[1]
    query_low = query_low.reshape(micro, rows, kv_here, -1, HEAD)
    key_low = key_low.reshape(micro, rows, kv_here, HEAD)
    value_low = value_low.reshape(micro, rows, kv_here, HEAD)
    logits = jnp.einsum("migkd,mjgd->mgkij", query_low, key_low, preferred_element_type=f32) * scale_factor
    logits = jnp.where(allowed[:, None, None], logits, -jnp.inf)
    exp_scores = jnp.exp(logits - jnp.max(logits, axis=-1, keepdims=True))
    probs = exp_scores / jnp.sum(exp_scores, axis=-1, keepdims=True)
    probs_low = probs.astype(bf16)
    attended_low = (
        jnp.einsum("mgkij,mjgd->migkd", probs_low, value_low, preferred_element_type=f32).astype(bf16).reshape(total, -1)
    )
    branch_part = (project_back(gated_low, full_mix) + project_back(attended_low, full_attn)).astype(bf16)
    branch = branch_part.astype(f32) + other_lane(branch_part).astype(f32)
    whole_mid = (in32 + branch).astype(bf16)
    mid32 = whole_mid.astype(f32)
    mid_scale = rms_scale(mid32)
    mid_low = (mid32 * mid_scale * gain_middle).astype(bf16)
    grad_left = split_left(whole_grad)
    mid_left = split_left(mid_low)
    normed_left = split_left(normed_low)
    red_down, red_fgate, red_fup, red_branch, red_gate, red_input, red_rest = [
        Reduction(order) for order in ((1, 2, 3), (2, 3, 1), (3, 2, 1), (1, 3, 2), (2, 3, 1), (3, 2, 1), (1, 3, 2))
    ]
    ff_cols = feed_gate.shape[1]
    gate_cols = mamba_gate.shape[1]

    def feed_forward():
        gate_ff = project(mid_low, full_fgate)
        up_ff = project(mid_low, full_fup)
        sig_ff = jax.nn.sigmoid(gate_ff)
        hidden_low = (gate_ff * sig_ff * up_ff).astype(bf16)
        grad_hidden = project(whole_grad, full_fdown)
        gate_ff_low = (grad_hidden * up_ff * (sig_ff * (1.0 + gate_ff * (1.0 - sig_ff)))).astype(bf16)
        up_ff_low = (grad_hidden * (gate_ff * sig_ff)).astype(bf16)
        grad_mid_norm = project_back(gate_ff_low, full_fgate) + project_back(up_ff_low, full_fup)
        grad_gain_mid = jnp.sum(grad_mid_norm * mid32 * mid_scale, axis=0)
        mid_part = rms_back(grad_mid_norm, mid32, mid_scale, gain_middle).astype(bf16)
        return hidden_low, gate_ff_low, up_ff_low, mid_part, grad_gain_mid, core_send(grad_left, hidden_low)

    hidden_low, gate_ff_low, up_ff_low, mid_part, grad_gain_mid, send_down = unit(feed_forward)
    mid_other = other_lane(mid_part)
    from_core_down = other_group(send_down, 1)

    def feed_sends():
        ffn_part = project_back(hidden_low, full_fdown).astype(bf16)
        send = jnp.concatenate([core_send(mid_left, gate_ff_low), core_send(mid_left, up_ff_low)], axis=1)
        return lane_rows(ffn_part, lane), lane_rows(ffn_part, 1 - lane), send

    ffn_own, ffn_send, send_feed = unit(feed_sends)
    from_core_feed = other_group(send_feed, 1)
    red_down.move(*unit(lambda: red_down.first(grad_left, hidden_low, from_core_down)))
    moves = unit(
        lambda: (
            red_fgate.first(mid_left, gate_ff_low, from_core_feed[:, :ff_cols]),
            red_fup.first(mid_left, up_ff_low, from_core_feed[:, ff_cols:]),
        )
    )
    red_fgate.move(*moves[0])
    red_fup.move(*moves[1])

    def branch_start():
        grad_middle = whole_grad.astype(f32) + (mid_part.astype(f32) + mid_other.astype(f32))
        whole_branch = grad_middle.astype(bf16)
        grad_gated_norm = project(whole_branch, full_mix)
        cross_own = jnp.sum(grad_gated_norm * mixer_gain * (ssm_out * jax.nn.silu(gate_z)), axis=1)
        return lane_rows(grad_middle, lane), whole_branch, grad_gated_norm, cross_own

    grad_middle_own, whole_branch, grad_gated_norm, cross_own = unit(branch_start)
    cross_other = other_lane(cross_own)
    ffn_other = other_lane(ffn_send)

    def attention_backward():
        branch_left = split_left(whole_branch)
        branch_right = jnp.concatenate([gated_low, attended_low], axis=1)
        grad_attended = project(whole_branch, full_attn).astype(bf16).reshape(micro, rows, kv_here, -1, HEAD)
        grad_probs = jnp.einsum("migkd,mjgd->mgkij", grad_attended, value_low, preferred_element_type=f32)
        grad_value = jnp.einsum("mgkij,migkd->mjgd", probs_low, grad_attended, preferred_element_type=f32)
        weighted_sum = jnp.sum(probs * grad_probs, axis=-1, keepdims=True)
        grad_logits = (probs * (grad_probs - weighted_sum)).astype(bf16)
        grad_query_rot = jnp.einsum("mgkij,mjgd->migkd", grad_logits, key_low, preferred_element_type=f32) * scale_factor
        grad_key_rot = jnp.einsum("mgkij,migkd->mjgd", grad_logits, query_low, preferred_element_type=f32) * scale_factor
        query_grad_low = rotate_back(grad_query_rot.reshape(total, -1, HEAD), cosine, sine).astype(bf16).reshape(total, -1)
        key_grad_low = rotate_back(grad_key_rot.reshape(total, -1, HEAD), cosine, sine).astype(bf16).reshape(total, -1)
        value_grad_low = grad_value.astype(bf16).reshape(total, -1)
        return (
            branch_left, branch_right, core_send(branch_left, branch_right), query_grad_low, key_grad_low, value_grad_low
        )

    branch_left, branch_right, send_branch, query_grad_low, key_grad_low, value_grad_low = unit(attention_backward)
    from_core_branch = other_group(send_branch, 1)

    def state_space_backward():
        cross = (inv_rms**3) * ((cross_own + cross_other)[:, None] / inner_width)
        gate_low, input_low, column_sums, direct, along, grad_state_act = state_backward(
            grad_gated_norm, ssm_out, gate_z, ssm_in, kernel_inner, skip_wide, mixer_gain[None, :], inv_rms, cross, *layout
        )
        column_sums = jnp.sum(column_sums, axis=0)
        grad_kernel_inner = column_sums[: CONV + 1]
        grad_mixer = column_sums[CONV + 1]
        grad_skip = jnp.sum(column_sums[CONV + 2].reshape(heads, SHD), axis=1)
        grad_direct = direct.reshape(micro, heads, rows)
        grad_running = along.transpose(0, 1, 3, 2).reshape(micro, heads, rows) - step_heads * grad_direct
        grad_product = jnp.einsum(
            "mhi,ij->mhj", grad_running, lower, precision=lax.Precision.HIGHEST, preferred_element_type=f32
        )
        grad_step = (grad_direct + grad_product * rate[None, :, None]).transpose(0, 2, 1).reshape(total, heads)
        grad_rate = jnp.sum(grad_product * step_heads, axis=(0, 2)) * rate
        grad_raw_step = grad_step * jax.nn.sigmoid(raw_step + step_bias)
        grad_bias = jnp.sum(grad_raw_step, axis=0)
        grad_state_raw, grad_kernel_state = conv_back(grad_state_act, state_raw, kernel_state, position)
        step_low = jnp.pad(grad_raw_step.astype(bf16), ((0, 0), (0, STEP_PAD - heads)))
        rest_low = jnp.concatenate(
            [grad_state_raw.astype(bf16), step_low, query_grad_low, key_grad_low, value_grad_low], axis=1
        )
        send = jnp.concatenate([core_send(normed_left, part) for part in (gate_low, input_low, rest_low)], axis=1)
        small = (grad_kernel_state, grad_kernel_inner, grad_mixer, grad_bias, grad_rate, grad_skip)
        return gate_low, input_low, rest_low, send, small

    gate_low, input_low, rest_low, send_first, small = unit(state_space_backward)
    grad_kernel_state, grad_kernel_inner, grad_mixer, grad_bias, grad_rate, grad_skip = small
    from_core_first = other_group(send_first, 1)

    def middle_moves():
        ffn_out = ffn_own.astype(f32) + ffn_other.astype(f32)
        out_rows = (lane_rows(whole_mid, lane).astype(f32) + ffn_out).astype(bf16)
        return (
            red_branch.first(branch_left, branch_right, from_core_branch),
            red_down.next(), red_fgate.next(), red_fup.next(), deal_order_rows(out_rows),
        )

    moves = unit(middle_moves)
    for red, move in zip((red_branch, red_down, red_fgate, red_fup), moves):
        red.move(*move)
    out_moved = exchange(moves[4])

    def input_gradient():
        grad_normed = project_back(gate_low, full_gate) + project_back(input_low, full_input)
        columns = [2 * NS, STEP_PAD, query_weight.shape[1], key_weight.shape[1], value_weight.shape[1]]
        start = 0
        for size, weight in zip(columns, (full_state, full_step, full_query, full_key, full_value)):
            grad_normed = grad_normed + project_back(rest_low[:, start : start + size], weight)
            start += size
        grad_gain_in = jnp.sum(grad_normed * in32 * in_scale, axis=0)
        in_part = rms_back(grad_normed, in32, in_scale, gain_input).astype(bf16)
        return grad_gain_in, lane_rows(in_part, lane), lane_rows(in_part, 1 - lane)

    grad_gain_in, in_own, in_send = unit(input_gradient)
    in_other = other_lane(in_send)

    advance([red_down, red_fgate, red_fup])
    moves = unit(
        lambda: (
            red_gate.first(normed_left, gate_low, from_core_first[:, :gate_cols]),
            red_input.first(normed_left, input_low, from_core_first[:, gate_cols : 2 * gate_cols]),
            red_rest.first(normed_left, rest_low, from_core_first[:, 2 * gate_cols :]),
        )
    )
    early = [red_down, red_fgate, red_fup, red_branch]
    late = [red_gate, red_input, red_rest]
    for red, move in zip(late, moves):
        red.move(*move)


    shared = [grad_gain_in, grad_gain_mid, grad_kernel_state.reshape(-1)]
    split = [grad_kernel_inner.reshape(-1), grad_mixer, grad_bias, grad_rate, grad_skip]
    used = sum(item.shape[0] for item in shared + split)
    padded = -(-used // 1024) * 1024

    def send_input():
        in_sum = in_own.astype(f32) + in_other.astype(f32)
        return deal_order_rows((in_sum + grad_middle_own).astype(bf16))

    in_sent, flat = advance(
        early,
        send_input,
        lambda: jnp.pad(jnp.concatenate(shared + split), (0, padded - used)).reshape(padded // 128, 128),
    )
    in_moved = exchange(in_sent)
    flat_moved = other_group(flat, masks[0])
    flat, block_out = advance(late, lambda: flat + flat_moved, lambda: deal_take(out_moved))
    pending = early + late
    bits = 1
    pending = [red for red in pending if not hasattr(red, "result")]
    while pending:
        work = []
        if bits < len(masks):
            flat_moved = other_group(flat, masks[bits])
            work.append(lambda: flat + flat_moved)
        results = advance(pending, *work)
        if bits < len(masks):
            flat = results[0]
            bits += 1
        pending = [red for red in pending if not hasattr(red, "result")]
    while bits < len(masks):
        flat = flat + other_group(flat, masks[bits])
        bits += 1
    grad_input = deal_take(in_moved)
    theirs = other_lane(flat).reshape(-1)
    flat = flat.reshape(-1)
    pieces = []
    start = 0
    for item in shared:
        pieces.append(flat[start : start + item.shape[0]] + theirs[start : start + item.shape[0]])
        start += item.shape[0]
    for item in split:
        mine, other = flat[start : start + item.shape[0]], theirs[start : start + item.shape[0]]
        pieces.append((jnp.where(lane == 0, mine, other), jnp.where(lane == 0, other, mine)))
        start += item.shape[0]
    sum_gin, sum_gmid, sum_kst = pieces[0], pieces[1], pieces[2].reshape(CONV + 1, -1)
    sum_kin = jnp.concatenate([half.reshape(CONV + 1, -1) for half in pieces[3]], axis=1)
    sum_mix, sum_bias, sum_rate, sum_skip = [jnp.concatenate(pair) for pair in pieces[4:]]

    query_cols, key_cols = query_weight.shape[1], key_weight.shape[1]
    total_fdown, total_fgate, total_fup = red_down.result, red_fgate.result, red_fup.result
    total_mix, total_attn = red_branch.result[:, :gate_cols], red_branch.result[:, gate_cols:]
    total_gate, total_input = red_gate.result, red_input.result
    rest = red_rest.result
    total_step = rest[:, 2 * NS : 2 * NS + heads]
    start = 2 * NS + STEP_PAD
    total_query = rest[:, start : start + query_cols]
    total_key = rest[:, start + query_cols : start + query_cols + key_cols]
    total_value = rest[:, start + query_cols + key_cols :]
    state_rows = rest[:, : 2 * NS].reshape(lanes, shard // lanes, 2 * NS)
    state_own = lax.dynamic_index_in_dim(state_rows, lane, 0, keepdims=False)
    state_send = lax.dynamic_index_in_dim(state_rows, 1 - lane, 0, keepdims=False)
    state_lane = state_own + other_lane(state_send)
    return (
        block_out,
        grad_input,
        total_query,
        total_key,
        total_value,
        total_attn,
        total_gate,
        total_input,
        total_step,
        state_lane,
        total_mix,
        total_fgate,
        total_fup,
        total_fdown,
        sum_gin,
        sum_gmid,
        sum_kin,
        sum_kst,
        sum_mix,
        sum_bias,
        sum_rate,
        sum_skip,
    )


def solution(mesh):
    both = P("dp", "tensor")
    in_specs = (
        P(None, ("dp", "tensor"), None),
        P(None, ("dp", "tensor"), None),
        P(),
        P(None, "dp"),
        both,
        both,
        both,
        both,
        both,
        both,
        both,
        P("dp", None),
        both,
        both,
        both,
        both,
        P(),
        P(),
        P(None, "tensor"),
        P(),
        P("tensor"),
        P("tensor"),
        P("tensor"),
        P("tensor"),
    )
    out_specs = (
        P(None, ("dp", "tensor"), None),
        P(None, ("dp", "tensor"), None),
        both,
        both,
        both,
        both,
        both,
        both,
        both,
        P(("dp", "tensor"), None),
        both,
        both,
        both,
        both,
        P(),
        P(),
        P(),
        P(),
        P(),
        P(),
        P(),
        P(),
    )
    return jax.shard_map(local, mesh=mesh, in_specs=in_specs, out_specs=out_specs, check_vma=False)
```

```python
import math

import jax
import jax.numpy as jnp
from jax import lax
from jax.experimental import pallas as pl
from jax.experimental.pallas import tpu as pltpu
from jax.sharding import PartitionSpec as P

HEAD = 128
SH = 48
SHD = 64
NS = 256
CONV = 4
STEP_PAD = 128

epsilon = 1e-05
rope_base = 100000000000.0
f32 = jnp.float32
bf16 = jnp.bfloat16


def project(left, right):
    return jnp.dot(left, right, preferred_element_type=f32)


def project_back(left, right):
    return lax.dot_general(left, right, (((1,), (1,)), ((), ())), preferred_element_type=f32)


def outer_sum(left, right):
    return lax.dot_general(left, right, (((0,), (0,)), ((), ())), preferred_element_type=f32)


def rms_scale(values):
    return lax.rsqrt(jnp.mean(values * values, axis=-1, keepdims=True) + epsilon)


def rms_back(grad, values, scale, gain):
    weighted = grad * gain
    inner = jnp.sum(weighted * values, axis=-1, keepdims=True)
    return scale * weighted - values * (scale * scale * scale * inner / values.shape[-1])


def shift_down(values, count):
    return jnp.concatenate([jnp.zeros((count, values.shape[1]), values.dtype), values[:-count]], axis=0)


def shift_up(values, count):
    return jnp.concatenate([values[count:], jnp.zeros((count, values.shape[1]), values.dtype)], axis=0)


def conv_sum(signal, kernel, position):
    summed = kernel[CONV][None, :] + signal * kernel[0][None, :]
    for tap in range(1, CONV):
        moved = jnp.where(position >= tap, shift_down(signal, tap), 0.0)
        summed = summed + moved * kernel[tap][None, :]
    return summed


def silu_back(values):
    sig = jax.nn.sigmoid(values)
    return sig * (1.0 + values * (1.0 - sig))


def conv_back(grad, signal, kernel, position):
    grad_sum = grad * silu_back(conv_sum(signal, kernel, position))
    grad_signal = grad_sum * kernel[0][None, :]
    grad_taps = [jnp.sum(grad_sum * signal, axis=0)]
    for tap in range(1, CONV):
        kept = jnp.where(position >= tap, grad_sum, 0.0)
        grad_signal = grad_signal + shift_up(kept, tap) * kernel[tap][None, :]
        grad_taps.append(jnp.sum(kept * shift_down(signal, tap), axis=0))
    grad_taps.append(jnp.sum(grad_sum, axis=0))
    return grad_signal, jnp.stack(grad_taps)


def rope_tables(position):
    half_size = HEAD // 2
    frequency = jnp.exp(jnp.arange(half_size, dtype=f32) * (-2.0 * math.log(rope_base) / HEAD))
    angles = position.astype(f32) * frequency[None, :]
    return jnp.cos(angles)[:, None, :], jnp.sin(angles)[:, None, :]


def rotate(values, cosine, sine):
    half_size = HEAD // 2
    first, second = values[..., :half_size], values[..., half_size:]
    return jnp.concatenate([first * cosine - second * sine, second * cosine + first * sine], axis=-1)


def copy_blocks(order_ref, first_ref, second_ref, first_out_ref, second_out_ref):
    first_out_ref[...] = first_ref[...]
    second_out_ref[...] = second_ref[...]


def pick_halves(values, order, block):
    height, width = values.shape
    count = width // block // 2
    if block % 128:
        mixed = jnp.take(values.reshape(height, -1, block), order, axis=1).reshape(height, width)
        return mixed[:, : width // 2], mixed[:, width // 2 :]
    half = jax.ShapeDtypeStruct((height, width // 2), values.dtype)
    out_spec = pl.BlockSpec((height, block), lambda i, order: (0, i))
    return pl.pallas_call(
        copy_blocks,
        out_shape=(half, half),
        grid_spec=pltpu.PrefetchScalarGridSpec(
            num_scalar_prefetch=1,
            grid=(count,),
            in_specs=[
                pl.BlockSpec((height, block), lambda i, order: (0, order[i])),
                pl.BlockSpec((height, block), lambda i, order: (0, order[i + count])),
            ],
            out_specs=(out_spec, out_spec),
        ),
        cost_estimate=pl.CostEstimate(flops=0, transcendentals=0, bytes_accessed=4 * height * width),
        name="pick_halves",
    )(order, values, values)


def rotate_back(values, cosine, sine):
    return rotate(values, cosine, -sine)


NEGATIVE = -1e30


def sigmoid_of(values):
    return 1.0 / (1.0 + jnp.exp(-values))


def block_mask(rows, segment_col, segment_row):
    row_index = lax.broadcasted_iota(jnp.int32, (rows, rows), 0)
    col_index = lax.broadcasted_iota(jnp.int32, (rows, rows), 1)
    return jnp.where((segment_col == segment_row) & (col_index <= row_index), 0.0, NEGATIVE)


def conv_block(signal, taps_ref, position):
    summed = taps_ref[CONV : CONV + 1, :] + signal * taps_ref[0:1, :]
    moved = []
    for tap in range(1, CONV):
        shifted = jnp.where(position >= tap, pltpu.roll(signal, tap, 0), 0.0)
        moved.append(shifted)
        summed = summed + shifted * taps_ref[tap : tap + 1, :]
    return summed, moved


def mixing_block(inner, mask, run_col, run_row, step_row):
    decay = jnp.exp(run_col - run_row + mask)
    return decay, (inner * decay * step_row).astype(bf16)


def state_forward_kernel(
    signal_ref, gate_ref, taps_ref, skip_ref, state_ref, seg_col_ref, seg_row_ref, position_ref,
    run_row_ref, run_col_ref, step_ref, out_ref, square_ref, inner_ref, mask_ref,
):
    rows = signal_ref.shape[0]

    @pl.when(pl.program_id(1) == 0)
    def _():
        inner_ref[...] = lax.dot_general(
            state_ref[:, NS:], state_ref[:, :NS], (((1,), (1,)), ((), ())), preferred_element_type=f32
        )
        mask_ref[...] = block_mask(rows, seg_col_ref[...], seg_row_ref[0])
        square_ref[...] = jnp.zeros_like(square_ref)

    summed, _ = conv_block(signal_ref[...], taps_ref, position_ref[...])
    cols = summed * sigmoid_of(summed)
    cols_low = cols.astype(bf16)
    mixed = []
    for head in range(2):
        _, mixing = mixing_block(
            inner_ref[...], mask_ref[...], run_col_ref[0, 0, :, head : head + 1],
            run_row_ref[0, 0, head : head + 1, :], step_ref[0, 0, head : head + 1, :],
        )
        mixed.append(jnp.dot(mixing, cols_low, preferred_element_type=f32))
    lanes = lax.broadcasted_iota(jnp.int32, cols.shape, 1)
    out = jnp.where(lanes < SHD, mixed[0], mixed[1]) + skip_ref[...] * cols
    out_ref[...] = out
    gate = gate_ref[...]
    gated = out * (gate * sigmoid_of(gate))
    square_ref[...] += gated * gated


def state_backward_kernel(
    grad_ref, out_ref, gate_ref, signal_ref, taps_ref, skip_ref, gain_ref, scale_ref, cross_ref, state_ref,
    seg_col_ref, seg_row_ref, position_ref, run_row_ref, run_col_ref, step_ref,
    gate_low_ref, input_low_ref, sums_ref, direct_ref, along_ref, state_grad_ref, inner_ref, mask_ref, grad_inner_ref,
):
    rows = signal_ref.shape[0]

    @pl.when(pl.program_id(1) == 0)
    def _():
        inner_ref[...] = lax.dot_general(
            state_ref[:, NS:], state_ref[:, :NS], (((1,), (1,)), ((), ())), preferred_element_type=f32
        )
        mask_ref[...] = block_mask(rows, seg_col_ref[...], seg_row_ref[0])
        grad_inner_ref[...] = jnp.zeros_like(grad_inner_ref)

    grad, out, gate, signal = grad_ref[...], out_ref[...], gate_ref[...], signal_ref[...]
    position = position_ref[...]
    sig = sigmoid_of(gate)
    silu = gate * sig
    gated = out * silu
    scaled = grad * scale_ref[...]
    grad_gated = scaled * gain_ref[...] - gated * cross_ref[...]
    grad_out = grad_gated * silu
    gate_low_ref[...] = (grad_gated * out * (sig * (1.0 + gate * (1.0 - sig)))).astype(bf16)
    summed, moved = conv_block(signal, taps_ref, position)
    sig = sigmoid_of(summed)
    cols = summed * sig
    cols_low = cols.astype(bf16)
    grad_low = grad_out.astype(bf16)
    lanes = lax.broadcasted_iota(jnp.int32, cols.shape, 1)
    zero = jnp.zeros_like(grad_low)
    grad_cols = []
    for head in range(2):
        step_row = step_ref[0, 0, head : head + 1, :]
        inner = inner_ref[...]
        decay, mixing = mixing_block(
            inner, mask_ref[...], run_col_ref[0, 0, :, head : head + 1], run_row_ref[0, 0, head : head + 1, :], step_row
        )
        grad_cols.append(
            lax.dot_general(mixing, grad_low, (((0,), (0,)), ((), ())), preferred_element_type=f32)
        )
        grad_head = jnp.where((lanes < SHD) == (head == 0), grad_low, zero)
        grad_decay = lax.dot_general(
            grad_head, cols_low, (((1,), (1,)), ((), ())), preferred_element_type=f32
        ) * decay
        stepped = grad_decay * step_row
        grad_inner_ref[...] += stepped
        direct_ref[0, 0, head : head + 1, :] = jnp.sum(grad_decay * inner, axis=0, keepdims=True)
        along_ref[0, 0, :, head : head + 1] = jnp.sum(stepped * inner, axis=1, keepdims=True)
    grad_cols = jnp.where(lanes < SHD, grad_cols[0], grad_cols[1]) + skip_ref[...] * grad_out
    grad_sum = grad_cols * (sig * (1.0 + summed * (1.0 - sig)))
    grad_signal = grad_sum * taps_ref[0:1, :]
    sums_ref[0, 0:1, :] = jnp.sum(grad_sum * signal, axis=0, keepdims=True)
    for tap in range(1, CONV):
        kept = jnp.where(position >= tap, grad_sum, 0.0)
        grad_signal = grad_signal + pltpu.roll(kept, rows - tap, 0) * taps_ref[tap : tap + 1, :]
        sums_ref[0, tap : tap + 1, :] = jnp.sum(grad_sum * moved[tap - 1], axis=0, keepdims=True)
    sums_ref[0, CONV : CONV + 1, :] = jnp.sum(grad_sum, axis=0, keepdims=True)
    sums_ref[0, CONV + 1 : CONV + 2, :] = jnp.sum(scaled * gated, axis=0, keepdims=True)
    sums_ref[0, CONV + 2 : CONV + 3, :] = jnp.sum(grad_out * cols, axis=0, keepdims=True)
    sums_ref[0, CONV + 3 : CONV + 4, :] = jnp.zeros((1, cols.shape[1]), f32)
    input_low_ref[...] = grad_signal.astype(bf16)

    @pl.when(pl.program_id(1) == pl.num_programs(1) - 1)
    def _():
        inner_low = grad_inner_ref[...].astype(bf16)
        state_grad_ref[:, :NS] = lax.dot_general(
            inner_low, state_ref[:, NS:], (((0,), (0,)), ((), ())), preferred_element_type=f32
        )
        state_grad_ref[:, NS:] = jnp.dot(inner_low, state_ref[:, :NS], preferred_element_type=f32)


def state_specs(rows, pairs):
    block = pl.BlockSpec((rows, 2 * SHD), lambda m, p: (m, p))
    return {
        "block": block,
        "taps": pl.BlockSpec((CONV + 1, 2 * SHD), lambda m, p: (0, p)),
        "vector": pl.BlockSpec((1, 2 * SHD), lambda m, p: (0, p)),
        "state": pl.BlockSpec((rows, 2 * NS), lambda m, p: (m, 0)),
        "column": pl.BlockSpec((rows, 1), lambda m, p: (m, 0)),
        "row": pl.BlockSpec((1, 1, rows), lambda m, p: (m, 0, 0)),
        "head_row": pl.BlockSpec((1, 1, 2, rows), lambda m, p: (m, p, 0, 0)),
        "head_col": pl.BlockSpec((1, 1, rows, 2), lambda m, p: (m, p, 0, 0)),
    }


def state_forward(signal, gate, taps, skip, state, seg_col, seg_row, position, run_row, run_col, step):
    micro, pairs, _, rows = run_row.shape
    spec = state_specs(rows, pairs)
    total, width = signal.shape
    return pl.pallas_call(
        state_forward_kernel,
        out_shape=(jax.ShapeDtypeStruct((total, width), f32), jax.ShapeDtypeStruct((total, 2 * SHD), f32)),
        grid=(micro, pairs),
        in_specs=[spec[name] for name in (
            "block", "block", "taps", "vector", "state", "column", "row", "column", "head_row", "head_col", "head_row")],
        out_specs=(spec["block"], pl.BlockSpec((rows, 2 * SHD), lambda m, p: (m, 0))),
        scratch_shapes=[pltpu.VMEM((rows, rows), f32), pltpu.VMEM((rows, rows), f32)],
        cost_estimate=pl.CostEstimate(
            flops=8 * total * rows * width // SHD * SHD, transcendentals=total * rows * width // SHD, bytes_accessed=12 * total * width
        ),
        name="state_forward",
    )(signal, gate, taps, skip, state, seg_col, seg_row, position, run_row, run_col, step)


def state_backward(grad, out, gate, signal, taps, skip, gain, scale, cross, state, seg_col, seg_row, position, run_row, run_col, step):
    micro, pairs, _, rows = run_row.shape
    spec = state_specs(rows, pairs)
    total, width = signal.shape
    return pl.pallas_call(
        state_backward_kernel,
        out_shape=(
            jax.ShapeDtypeStruct((total, width), bf16),
            jax.ShapeDtypeStruct((total, width), bf16),
            jax.ShapeDtypeStruct((micro, 8, width), f32),
            jax.ShapeDtypeStruct(run_row.shape, f32),
            jax.ShapeDtypeStruct(run_col.shape, f32),
            jax.ShapeDtypeStruct((total, 2 * NS), f32),
        ),
        grid=(micro, pairs),
        in_specs=[spec[name] for name in (
            "block", "block", "block", "block", "taps", "vector", "vector", "column", "column", "state",
            "column", "row", "column", "head_row", "head_col", "head_row")],
        out_specs=(
            spec["block"], spec["block"], pl.BlockSpec((1, 8, 2 * SHD), lambda m, p: (m, 0, p)),
            spec["head_row"], spec["head_col"], spec["state"],
        ),
        scratch_shapes=[pltpu.VMEM((rows, rows), f32)] * 3,
        cost_estimate=pl.CostEstimate(
            flops=20 * total * rows * width, transcendentals=total * rows * width // SHD, bytes_accessed=20 * total * width
        ),
        name="state_backward",
    )(grad, out, gate, signal, taps, skip, gain, scale, cross, state, seg_col, seg_row, position, run_row, run_col, step)


def local(
    inputs,
    out_grad,
    deal_order,
    segment,
    query_weight,
    key_weight,
    value_weight,
    attention_out,
    mamba_gate,
    mamba_input,
    step_weight,
    state_weight,
    mamba_out,
    feed_gate,
    feed_up,
    feed_down,
    gain_input,
    gain_middle,
    kernel_inner,
    kernel_state,
    mixer_gain,
    step_bias,
    log_rate,
    skip_gain,
):
    micro, own, width = inputs.shape
    groups = lax.axis_size("dp")
    lanes = lax.axis_size("tensor")
    lane = lax.axis_index("tensor")
    group = lax.axis_index("dp")
    device = group * lanes + lane
    per = own // groups
    rows = own * lanes
    total = micro * rows
    inner_width = SH * SHD
    scale_factor = HEAD ** (-0.5)
    outer_count = groups // 4
    shard = width // groups

    swap_lane = [(0, 1), (1, 0)]

    def other_lane(values):
        return lax.ppermute(values, "tensor", swap_lane)

    def other_group(values, bits):
        return lax.ppermute(values, "dp", [(i, i ^ bits) for i in range(groups)])

    step_padded = jnp.pad(step_weight, ((0, 0), (0, STEP_PAD - step_weight.shape[1])))
    early = [mamba_gate, mamba_input, state_weight, step_padded, query_weight, key_weight, value_weight, mamba_out, attention_out]
    late = [feed_gate, feed_up, feed_down]

    def gather(pieces):
        whole = lax.all_gather(jnp.concatenate(pieces, axis=1), "dp", axis=0, tiled=True)
        found, start = [], 0
        for piece in pieces:
            found.append(whole[:, start : start + piece.shape[1]])
            start += piece.shape[1]
        return found

    full_gate, full_input, full_state, full_step, full_query, full_key, full_value, full_mix, full_attn = gather(early)
    full_fgate, full_fup, full_fdown = gather(late)

    own_places = jnp.arange(own, dtype=jnp.int32)
    own_order = lax.dynamic_slice_in_dim(deal_order, device * own, own, 1)
    micro_index = jnp.arange(micro, dtype=jnp.int32)[:, None]

    def buffer_place(destination, rank):
        return destination * (micro * per) + micro_index * per + rank

    send_rank = jnp.sum((own_order[:, None, :] < own_order[:, :, None]).astype(jnp.int32), axis=2)
    send_place = buffer_place(send_rank // per, send_rank % per).reshape(-1)
    lane_order = lax.dynamic_index_in_dim(deal_order.reshape(micro, groups, lanes, own), lane, 2, keepdims=False)
    slots = device * own + own_places
    found = lane_order[:, None, :, :] == slots[None, :, None, None]
    source = jnp.sum(
        jnp.where(found, jnp.arange(groups, dtype=jnp.int32)[None, None, :, None], 0), axis=(2, 3)
    )
    recv_rank = jnp.sum(
        ((source[:, None, :] == source[:, :, None]) & (own_places[None, None, :] < own_places[None, :, None])).astype(jnp.int32),
        axis=2,
    )
    recv_place = buffer_place(source, recv_rank).reshape(-1)
    buffer_places = jnp.arange(micro * own, dtype=jnp.int32)
    send_pick = (buffer_places[:, None] == send_place[None, :]).astype(bf16)
    recv_pick = (recv_place[:, None] == buffer_places[None, :]).astype(bf16)

    def exchange(buffer):
        return lax.all_to_all(
            buffer.reshape(groups, micro * per, width), "dp", split_axis=0, concat_axis=0, tiled=True
        ).reshape(micro * own, width)

    def deal(values):
        sent = project(send_pick, values.reshape(micro * own, width)).astype(bf16)
        return project(recv_pick, exchange(sent)).astype(bf16)

    def deal_order_rows(values):
        return outer_sum(recv_pick, values).astype(bf16)

    def deal_take(moved):
        return outer_sum(send_pick, moved).astype(bf16).reshape(micro, own, width)

    def join_lanes(values):
        mine = values.reshape(micro, 1, own, -1)
        theirs = other_lane(values).reshape(micro, 1, own, -1)
        low = jnp.where(lane == 0, mine, theirs)
        high = jnp.where(lane == 0, theirs, mine)
        return jnp.concatenate([low, high], axis=1).reshape(total, -1)

    def lane_rows(values, which):
        return lax.dynamic_index_in_dim(
            values.reshape(micro, lanes, own, -1), which, 1, keepdims=False
        ).reshape(micro * own, -1)

    own_in = deal(inputs)
    own_grad = deal(out_grad)
    whole_in = join_lanes(own_in)
    whole_grad = join_lanes(own_grad)

    before = jnp.sum((segment[:, None, :] < segment[:, :, None]).astype(jnp.int32), axis=2)
    places = jnp.arange(rows, dtype=jnp.int32)
    allowed = (segment[:, :, None] == segment[:, None, :]) & (places[None, None, :] <= places[None, :, None])
    position = (places[None, :] - before).reshape(total, 1)

    masks = [1, 2] + [4, 12][: max(0, groups.bit_length() - 3)]
    while 1 << len(masks) < groups:
        masks.append(1 << len(masks))
    relative = []
    for block in range(groups):
        flip = 0
        for place, mask in enumerate(masks):
            if block >> (len(masks) - 1 - place) & 1:
                flip ^= mask
        relative.append(flip)
    block_order = jnp.bitwise_xor(group.astype(jnp.int32), jnp.array(relative, jnp.int32))

    def split_left(left):
        return pick_halves(left, block_order, shard)

    inner_places = list(range(1, len(masks)))

    def core_send(left_parts, right):
        return outer_sum(left_parts[1], right).astype(bf16)

    def halve(kept, place):
        return (
            lax.slice_in_dim(kept, 1, 2, axis=place - 1).reshape(-1, kept.shape[-1]),
            lax.slice_in_dim(kept, 0, 1, axis=place - 1),
        )

    class Reduction:
        def __init__(self, first):
            self.places = [place for place in first if place in inner_places]
            self.places += [place for place in inner_places if place not in first]
            self.stage = 0

        def move(self, send, kept):
            self.came = other_group(send, masks[self.places[self.stage]])
            self.kept = kept
            self.stage += 1

        def first(self, left_parts, right, from_core):
            kept = (outer_sum(left_parts[0], right) + from_core.astype(f32)).astype(bf16)
            kept = kept.reshape((2,) * len(inner_places) + (shard, -1))
            return halve(kept, self.places[0])

        def added(self):
            return self.kept.astype(f32) + self.came.reshape(self.kept.shape).astype(f32)

        def next(self):
            return halve(self.added().astype(bf16), self.places[self.stage])

        def last(self):
            return self.added().reshape(shard, -1)

        def step(self):
            return self.next() if self.stage < len(self.places) else self.last()

    order = [deal_order[0, 0] >= 0]

    def unit(work):
        shapes = jax.eval_shape(work)
        results = lax.cond(
            order[0], work, lambda: jax.tree.map(lambda leaf: jnp.zeros(leaf.shape, leaf.dtype), shapes)
        )
        leaves, form = jax.tree.flatten(results)
        least = min(range(len(leaves)), key=lambda place: leaves[place].size)
        leaves[least], order[0] = lax.optimization_barrier((leaves[least], order[0]))
        return jax.tree.unflatten(form, leaves)

    def after(value, *others):
        return lax.optimization_barrier((value, others))[0]

    in32 = whole_in.astype(f32)
    in_scale = rms_scale(in32)
    normed_low = (in32 * in_scale * gain_input).astype(bf16)
    grad_left = split_left(whole_grad)
    normed_left = split_left(normed_low)
    full_gate = after(full_gate, whole_grad, grad_left, normed_left)
    gate_z = project(normed_low, full_gate)
    ssm_in = project(normed_low, full_input)
    state_raw = project(normed_low, full_state)
    heads = step_weight.shape[1]
    raw_step = project(normed_low, full_step)[:, :heads]
    state_low = jax.nn.silu(conv_sum(state_raw, kernel_state, position)).astype(bf16)
    rate = -jnp.exp(log_rate)
    step_size = jax.nn.softplus(raw_step + step_bias)
    step_heads = step_size.reshape(micro, rows, heads).transpose(0, 2, 1)
    lower = (places[None, :] <= places[:, None]).astype(f32)
    running = jnp.einsum(
        "mhj,ij->mhi", step_heads * rate[None, :, None], lower, precision=lax.Precision.HIGHEST, preferred_element_type=f32
    )
    pairs = heads // 2
    run_row = running.reshape(micro, pairs, 2, rows)
    run_col = run_row.transpose(0, 1, 3, 2)
    step_row = step_heads.reshape(micro, pairs, 2, rows)
    skip_wide = jnp.repeat(skip_gain, SHD)[None, :]
    layout = (state_low, segment.reshape(total, 1), segment.reshape(micro, 1, rows), position, run_row, run_col, step_row)
    ssm_out, squares = state_forward(ssm_in, gate_z, kernel_inner, skip_wide, *layout)
    square_own = jnp.sum(squares, axis=1)
    square_sum = square_own + other_lane(square_own)
    inv_rms = lax.rsqrt(square_sum / inner_width + epsilon)[:, None]
    gated_low = (ssm_out * jax.nn.silu(gate_z) * inv_rms * mixer_gain).astype(bf16)

    cosine, sine = rope_tables(position)
    query_low = rotate(project(normed_low, full_query).reshape(total, -1, HEAD), cosine, sine).astype(bf16)
    key_low = rotate(project(normed_low, full_key).reshape(total, -1, HEAD), cosine, sine).astype(bf16)
    value_low = project(normed_low, full_value).astype(bf16)
    kv_here = key_low.shape[1]
    query_low = query_low.reshape(micro, rows, kv_here, -1, HEAD)
    key_low = key_low.reshape(micro, rows, kv_here, HEAD)
    value_low = value_low.reshape(micro, rows, kv_here, HEAD)
    logits = jnp.einsum("migkd,mjgd->mgkij", query_low, key_low, preferred_element_type=f32) * scale_factor
    logits = jnp.where(allowed[:, None, None], logits, -jnp.inf)
    exp_scores = jnp.exp(logits - jnp.max(logits, axis=-1, keepdims=True))
    probs = exp_scores / jnp.sum(exp_scores, axis=-1, keepdims=True)
    probs_low = probs.astype(bf16)
    attended_low = (
        jnp.einsum("mgkij,mjgd->migkd", probs_low, value_low, preferred_element_type=f32).astype(bf16).reshape(total, -1)
    )
    branch_part = (project_back(gated_low, full_mix) + project_back(attended_low, full_attn)).astype(bf16)
    branch = branch_part.astype(f32) + other_lane(branch_part).astype(f32)
    whole_mid = (in32 + branch).astype(bf16)
    mid32 = whole_mid.astype(f32)
    mid_scale = rms_scale(mid32)
    mid_low = (mid32 * mid_scale * gain_middle).astype(bf16)
    red_down, red_fgate, red_fup, red_branch, red_gate, red_input, red_rest = [
        Reduction(places) for places in ((1, 2, 3), (2, 3, 1), (3, 1, 2), (1, 3, 2), (2, 3, 1), (3, 1, 2), (1, 2, 3))
    ]
    gate_cols = mamba_gate.shape[1]
    rest_cols = 2 * NS + STEP_PAD + query_weight.shape[1] + key_weight.shape[1] + value_weight.shape[1]

    def feed_forward():
        mid_left = split_left(mid_low)
        gate_ff = project(mid_low, full_fgate)
        up_ff = project(mid_low, full_fup)
        sig_ff = jax.nn.sigmoid(gate_ff)
        hidden_low = (gate_ff * sig_ff * up_ff).astype(bf16)
        grad_hidden = project(whole_grad, full_fdown)
        gate_ff_low = (grad_hidden * up_ff * (sig_ff * (1.0 + gate_ff * (1.0 - sig_ff)))).astype(bf16)
        up_ff_low = (grad_hidden * (gate_ff * sig_ff)).astype(bf16)
        grad_mid_norm = project_back(gate_ff_low, full_fgate) + project_back(up_ff_low, full_fup)
        grad_gain_mid = jnp.sum(grad_mid_norm * mid32 * mid_scale, axis=0)
        mid_part = rms_back(grad_mid_norm, mid32, mid_scale, gain_middle).astype(bf16)
        rights = (hidden_low, gate_ff_low, up_ff_low)
        sends = [core_send(left, right) for left, right in zip((grad_left, mid_left, mid_left), rights)]
        return grad_gain_mid, mid_part, mid_left, rights, sends

    grad_gain_mid, mid_part, mid_left, feed_rights, sends = unit(feed_forward)
    hidden_low = feed_rights[0]
    mid_other = other_lane(mid_part)
    feed_lefts = (grad_left, mid_left, mid_left)
    feed_came = [other_group(send, 1) for send in sends]
    feeds = (red_down, red_fgate, red_fup)

    def feed_output():
        ffn_part = project_back(hidden_low, full_fdown).astype(bf16)
        return lane_rows(ffn_part, lane), lane_rows(ffn_part, 1 - lane)

    ffn_own, ffn_send = unit(feed_output)
    moves = unit(lambda: [red.first(*given) for red, *given in zip(feeds, feed_lefts, feed_rights, feed_came)])
    for red, move in zip(feeds, moves):
        red.move(*move)

    def branch_backward():
        grad_middle = whole_grad.astype(f32) + (mid_part.astype(f32) + mid_other.astype(f32))
        whole_branch = grad_middle.astype(bf16)
        grad_gated_norm = project(whole_branch, full_mix)
        cross_own = jnp.sum(grad_gated_norm * mixer_gain * (ssm_out * jax.nn.silu(gate_z)), axis=1)
        grad_attended = project(whole_branch, full_attn).astype(bf16).reshape(micro, rows, kv_here, -1, HEAD)
        grad_probs = jnp.einsum("migkd,mjgd->mgkij", grad_attended, value_low, preferred_element_type=f32)
        grad_value = jnp.einsum("mgkij,migkd->mjgd", probs_low, grad_attended, preferred_element_type=f32)
        weighted_sum = jnp.sum(probs * grad_probs, axis=-1, keepdims=True)
        grad_logits = (probs * (grad_probs - weighted_sum)).astype(bf16)
        grad_query_rot = jnp.einsum("mgkij,mjgd->migkd", grad_logits, key_low, preferred_element_type=f32) * scale_factor
        grad_key_rot = jnp.einsum("mgkij,migkd->mjgd", grad_logits, query_low, preferred_element_type=f32) * scale_factor
        query_grad_low = rotate_back(grad_query_rot.reshape(total, -1, HEAD), cosine, sine).astype(bf16).reshape(total, -1)
        key_grad_low = rotate_back(grad_key_rot.reshape(total, -1, HEAD), cosine, sine).astype(bf16).reshape(total, -1)
        value_grad_low = grad_value.astype(bf16).reshape(total, -1)
        branch_right = jnp.concatenate([gated_low, attended_low], axis=1)
        return (
            cross_own, lane_rows(grad_middle, lane), grad_gated_norm, split_left(whole_branch), branch_right,
            (query_grad_low, key_grad_low, value_grad_low),
        )

    cross_own, grad_middle_own, grad_gated_norm, branch_left, branch_right, qkv_low = unit(branch_backward)

    def second_moves():
        return core_send(branch_left, branch_right), [red.next() for red in feeds], lax.optimization_barrier(ffn_send)

    cross_other = other_lane(cross_own)
    send_branch, moves, ffn_send = unit(second_moves)
    branch_came = other_group(send_branch, 1)
    ffn_other = other_lane(ffn_send)
    for red, move in zip(feeds, moves):
        red.move(*move)

    def state_space_backward():
        cross = (inv_rms**3) * ((cross_own + cross_other)[:, None] / inner_width)
        gate_low, input_low, column_sums, direct, along, grad_state_act = state_backward(
            grad_gated_norm, ssm_out, gate_z, ssm_in, kernel_inner, skip_wide, mixer_gain[None, :], inv_rms, cross, *layout
        )
        column_sums = jnp.sum(column_sums, axis=0)
        grad_kernel_inner = column_sums[: CONV + 1]
        grad_mixer = column_sums[CONV + 1]
        grad_skip = jnp.sum(column_sums[CONV + 2].reshape(heads, SHD), axis=1)
        grad_direct = direct.reshape(micro, heads, rows)
        grad_running = along.transpose(0, 1, 3, 2).reshape(micro, heads, rows) - step_heads * grad_direct
        grad_product = jnp.einsum(
            "mhi,ij->mhj", grad_running, lower, precision=lax.Precision.HIGHEST, preferred_element_type=f32
        )
        grad_step = (grad_direct + grad_product * rate[None, :, None]).transpose(0, 2, 1).reshape(total, heads)
        grad_rate = jnp.sum(grad_product * step_heads, axis=(0, 2)) * rate
        grad_raw_step = grad_step * jax.nn.sigmoid(raw_step + step_bias)
        grad_bias = jnp.sum(grad_raw_step, axis=0)
        grad_state_raw, grad_kernel_state = conv_back(grad_state_act, state_raw, kernel_state, position)
        step_low = jnp.pad(grad_raw_step.astype(bf16), ((0, 0), (0, STEP_PAD - heads)))
        first_right = jnp.concatenate([gate_low, input_low, grad_state_raw.astype(bf16), step_low, *qkv_low], axis=1)
        small = (grad_kernel_state, grad_kernel_inner, grad_mixer, grad_bias, grad_rate, grad_skip)
        return small, first_right

    small, first_right = unit(state_space_backward)
    grad_kernel_state, grad_kernel_inner, grad_mixer, grad_bias, grad_rate, grad_skip = small

    def third_moves():
        ffn_out = ffn_own.astype(f32) + ffn_other.astype(f32)
        out_rows = (lane_rows(whole_mid, lane).astype(f32) + ffn_out).astype(bf16)
        return (
            core_send(normed_left, first_right),
            red_branch.first(branch_left, branch_right, branch_came),
            [red.step() for red in feeds],
            deal_order_rows(out_rows),
        )

    def settle(reductions, steps):
        for red, step in zip(reductions, steps):
            if red.stage < len(red.places):
                red.move(*step)
            else:
                red.result = step

    send_first, move, moves, out_sent = unit(third_moves)
    first_came = other_group(send_first, 1)
    red_branch.move(*move)
    settle(feeds, moves)
    out_moved = exchange(out_sent)

    def input_gradient():
        weights = (full_gate, full_input, full_state, full_step, full_query, full_key, full_value)
        grad_normed, start = 0.0, 0
        for weight in weights:
            grad_normed = grad_normed + project_back(first_right[:, start : start + weight.shape[1]], weight)
            start += weight.shape[1]
        grad_gain_in = jnp.sum(grad_normed * in32 * in_scale, axis=0)
        in_part = rms_back(grad_normed, in32, in_scale, gain_input).astype(bf16)
        return grad_gain_in, lane_rows(in_part, lane), lane_rows(in_part, 1 - lane)

    grad_gain_in, in_own, in_send = unit(input_gradient)

    shared = [grad_gain_in, grad_gain_mid, grad_kernel_state.reshape(-1)]
    split = [grad_kernel_inner.reshape(-1), grad_mixer, grad_bias, grad_rate, grad_skip]
    used = sum(item.shape[0] for item in shared) + lanes * sum(item.shape[0] for item in split)
    padded = -(-used // 1024) * 1024
    firsts = (red_gate, red_input, red_rest)

    def first_moves():
        kept = (outer_sum(normed_left[0], first_right) + first_came.astype(f32)).astype(bf16)
        kept = kept.reshape((2,) * len(inner_places) + (shard, -1))
        moves, start = [], 0
        for red, size in zip(firsts, (gate_cols, gate_cols, rest_cols)):
            moves.append(halve(kept[..., start : start + size], red.places[0]))
            start += size
        return moves, lax.optimization_barrier(in_send), [red.step() for red in feeds if not hasattr(red, "result")]

    moves, in_send, steps = unit(first_moves)
    for red, move in zip(firsts, moves):
        red.move(*move)
    settle([red for red in feeds if not hasattr(red, "result")], steps)
    in_other = other_lane(in_send)
    block_out = unit(lambda: deal_take(out_moved))

    def send_input():
        in_sum = in_own.astype(f32) + in_other.astype(f32)
        zero = [jnp.zeros_like(item) for item in split]
        low = [jnp.where(lane == 0, item, none) for item, none in zip(split, zero)]
        high = [jnp.where(lane == 0, none, item) for item, none in zip(split, zero)]
        flat = jnp.pad(jnp.concatenate(shared + low + high), (0, padded - used)).reshape(padded // 128, 128)
        return deal_order_rows((in_sum + grad_middle_own).astype(bf16)), flat

    everything = [*feeds, red_branch, *firsts]
    in_moved = None
    def small_sums():
        pieces, start = [], 0
        for item in shared + split + split:
            pieces.append(flat.reshape(-1)[start : start + item.shape[0]])
            start += item.shape[0]
        halves = list(zip(pieces[3 : 3 + len(split)], pieces[3 + len(split) :]))
        return (
            pieces[0], pieces[1], pieces[2].reshape(CONV + 1, -1),
            jnp.concatenate([half.reshape(CONV + 1, -1) for half in halves[0]], axis=1),
            *[jnp.concatenate(pair) for pair in halves[1:]],
        )

    while pending := [red for red in everything if not hasattr(red, "result")]:
        last = all(red.stage == len(red.places) for red in pending)
        steps, other = unit(
            lambda: (
                [red.step() for red in pending],
                (deal_take(in_moved), small_sums()) if last else send_input() if in_moved is None else (),
            )
        )
        settle(pending, steps)
        if in_moved is None:
            in_moved = exchange(other[0])
            flat = lax.psum(other[1], ("dp", "tensor"))
    grad_input, (sum_gin, sum_gmid, sum_kst, sum_kin, sum_mix, sum_bias, sum_rate, sum_skip) = other

    query_cols, key_cols = query_weight.shape[1], key_weight.shape[1]
    total_fdown, total_fgate, total_fup = red_down.result, red_fgate.result, red_fup.result
    total_mix, total_attn = red_branch.result[:, :gate_cols], red_branch.result[:, gate_cols:]
    total_gate, total_input = red_gate.result, red_input.result
    rest = red_rest.result
    total_step = rest[:, 2 * NS : 2 * NS + heads]
    start = 2 * NS + STEP_PAD
    total_query = rest[:, start : start + query_cols]
    total_key = rest[:, start + query_cols : start + query_cols + key_cols]
    total_value = rest[:, start + query_cols + key_cols :]
    state_rows = rest[:, : 2 * NS].reshape(lanes, shard // lanes, 2 * NS)
    state_own = lax.dynamic_index_in_dim(state_rows, lane, 0, keepdims=False)
    state_send = lax.dynamic_index_in_dim(state_rows, 1 - lane, 0, keepdims=False)
    state_lane = state_own + other_lane(state_send)
    return (
        block_out,
        grad_input,
        total_query,
        total_key,
        total_value,
        total_attn,
        total_gate,
        total_input,
        total_step,
        state_lane,
        total_mix,
        total_fgate,
        total_fup,
        total_fdown,
        sum_gin,
        sum_gmid,
        sum_kin,
        sum_kst,
        sum_mix,
        sum_bias,
        sum_rate,
        sum_skip,
    )


def solution(mesh):
    both = P("dp", "tensor")
    in_specs = (
        P(None, ("dp", "tensor"), None),
        P(None, ("dp", "tensor"), None),
        P(),
        P(None, "dp"),
        both,
        both,
        both,
        both,
        both,
        both,
        both,
        P("dp", None),
        both,
        both,
        both,
        both,
        P(),
        P(),
        P(None, "tensor"),
        P(),
        P("tensor"),
        P("tensor"),
        P("tensor"),
        P("tensor"),
    )
    out_specs = (
        P(None, ("dp", "tensor"), None),
        P(None, ("dp", "tensor"), None),
        both,
        both,
        both,
        both,
        both,
        both,
        both,
        P(("dp", "tensor"), None),
        both,
        both,
        both,
        both,
        P(),
        P(),
        P(),
        P(),
        P(),
        P(),
        P(),
        P(),
    )
    return jax.shard_map(local, mesh=mesh, in_specs=in_specs, out_specs=out_specs, check_vma=False)
```

```python
import math

import jax
import jax.numpy as jnp
from jax import lax
from jax.experimental import pallas as pl
from jax.experimental.pallas import tpu as pltpu
from jax.sharding import PartitionSpec as P

HEAD = 128
SH = 48
SHD = 64
NS = 256
CONV = 4
STEP_PAD = 128

epsilon = 1e-05
rope_base = 100000000000.0
f32 = jnp.float32
bf16 = jnp.bfloat16


def project(left, right):
    return jnp.dot(left, right, preferred_element_type=f32)


def project_back(left, right):
    return lax.dot_general(left, right, (((1,), (1,)), ((), ())), preferred_element_type=f32)


def outer_sum(left, right):
    return lax.dot_general(left, right, (((0,), (0,)), ((), ())), preferred_element_type=f32)


def rms_scale(values):
    return lax.rsqrt(jnp.mean(values * values, axis=-1, keepdims=True) + epsilon)


def rms_back(grad, values, scale, gain):
    weighted = grad * gain
    inner = jnp.sum(weighted * values, axis=-1, keepdims=True)
    return scale * weighted - values * (scale * scale * scale * inner / values.shape[-1])


def shift_down(values, count):
    return jnp.concatenate([jnp.zeros((count, values.shape[1]), values.dtype), values[:-count]], axis=0)


def shift_up(values, count):
    return jnp.concatenate([values[count:], jnp.zeros((count, values.shape[1]), values.dtype)], axis=0)


def conv_sum(signal, kernel, position):
    summed = kernel[CONV][None, :] + signal * kernel[0][None, :]
    for tap in range(1, CONV):
        moved = jnp.where(position >= tap, shift_down(signal, tap), 0.0)
        summed = summed + moved * kernel[tap][None, :]
    return summed


def silu_back(values):
    sig = jax.nn.sigmoid(values)
    return sig * (1.0 + values * (1.0 - sig))


def conv_back(grad, signal, kernel, position):
    grad_sum = grad * silu_back(conv_sum(signal, kernel, position))
    grad_signal = grad_sum * kernel[0][None, :]
    grad_taps = [jnp.sum(grad_sum * signal, axis=0)]
    for tap in range(1, CONV):
        kept = jnp.where(position >= tap, grad_sum, 0.0)
        grad_signal = grad_signal + shift_up(kept, tap) * kernel[tap][None, :]
        grad_taps.append(jnp.sum(kept * shift_down(signal, tap), axis=0))
    grad_taps.append(jnp.sum(grad_sum, axis=0))
    return grad_signal, jnp.stack(grad_taps)


def rope_tables(position):
    half_size = HEAD // 2
    frequency = jnp.exp(jnp.arange(half_size, dtype=f32) * (-2.0 * math.log(rope_base) / HEAD))
    angles = position.astype(f32) * frequency[None, :]
    return jnp.cos(angles)[:, None, :], jnp.sin(angles)[:, None, :]


def rotate(values, cosine, sine):
    half_size = HEAD // 2
    first, second = values[..., :half_size], values[..., half_size:]
    return jnp.concatenate([first * cosine - second * sine, second * cosine + first * sine], axis=-1)


def copy_blocks(order_ref, first_ref, second_ref, first_out_ref, second_out_ref):
    first_out_ref[...] = first_ref[...]
    second_out_ref[...] = second_ref[...]


def pick_halves(values, order, block):
    height, width = values.shape
    count = width // block // 2
    if block % 128:
        mixed = jnp.take(values.reshape(height, -1, block), order, axis=1).reshape(height, width)
        return mixed[:, : width // 2], mixed[:, width // 2 :]
    half = jax.ShapeDtypeStruct((height, width // 2), values.dtype)
    out_spec = pl.BlockSpec((height, block), lambda i, order: (0, i))
    return pl.pallas_call(
        copy_blocks,
        out_shape=(half, half),
        grid_spec=pltpu.PrefetchScalarGridSpec(
            num_scalar_prefetch=1,
            grid=(count,),
            in_specs=[
                pl.BlockSpec((height, block), lambda i, order: (0, order[i])),
                pl.BlockSpec((height, block), lambda i, order: (0, order[i + count])),
            ],
            out_specs=(out_spec, out_spec),
        ),
        cost_estimate=pl.CostEstimate(flops=0, transcendentals=0, bytes_accessed=4 * height * width),
        name="pick_halves",
    )(order, values, values)


def hand_over(values, microseconds):
    def idle(values_ref, out_ref):
        pass

    return pl.pallas_call(
        idle,
        out_shape=jax.ShapeDtypeStruct(values.shape, values.dtype),
        in_specs=[pl.BlockSpec(memory_space=pl.ANY)],
        out_specs=pl.BlockSpec(memory_space=pl.ANY),
        input_output_aliases={0: 0},
        cost_estimate=pl.CostEstimate(flops=microseconds * 1150000000, transcendentals=0, bytes_accessed=0),
        name="hand_over",
    )(values)


def rotate_back(values, cosine, sine):
    return rotate(values, cosine, -sine)


NEGATIVE = -1e30


def sigmoid_of(values):
    return 1.0 / (1.0 + jnp.exp(-values))


def block_mask(rows, segment_col, segment_row):
    row_index = lax.broadcasted_iota(jnp.int32, (rows, rows), 0)
    col_index = lax.broadcasted_iota(jnp.int32, (rows, rows), 1)
    return jnp.where((segment_col == segment_row) & (col_index <= row_index), 0.0, NEGATIVE)


def conv_block(signal, taps_ref, position):
    summed = taps_ref[CONV : CONV + 1, :] + signal * taps_ref[0:1, :]
    moved = []
    for tap in range(1, CONV):
        shifted = jnp.where(position >= tap, pltpu.roll(signal, tap, 0), 0.0)
        moved.append(shifted)
        summed = summed + shifted * taps_ref[tap : tap + 1, :]
    return summed, moved


def mixing_block(inner, mask, run_col, run_row, step_row):
    decay = jnp.exp(run_col - run_row + mask)
    return decay, (inner * decay * step_row).astype(bf16)


def state_forward_kernel(
    signal_ref, gate_ref, taps_ref, skip_ref, state_ref, seg_col_ref, seg_row_ref, position_ref,
    run_row_ref, run_col_ref, step_ref, out_ref, square_ref, inner_ref, mask_ref,
):
    rows = signal_ref.shape[0]

    @pl.when(pl.program_id(1) == 0)
    def _():
        inner_ref[...] = lax.dot_general(
            state_ref[:, NS:], state_ref[:, :NS], (((1,), (1,)), ((), ())), preferred_element_type=f32
        )
        mask_ref[...] = block_mask(rows, seg_col_ref[...], seg_row_ref[0])
        square_ref[...] = jnp.zeros_like(square_ref)

    summed, _ = conv_block(signal_ref[...], taps_ref, position_ref[...])
    cols = summed * sigmoid_of(summed)
    cols_low = cols.astype(bf16)
    mixed = []
    for head in range(2):
        _, mixing = mixing_block(
            inner_ref[...], mask_ref[...], run_col_ref[0, 0, :, head : head + 1],
            run_row_ref[0, 0, head : head + 1, :], step_ref[0, 0, head : head + 1, :],
        )
        mixed.append(jnp.dot(mixing, cols_low, preferred_element_type=f32))
    lanes = lax.broadcasted_iota(jnp.int32, cols.shape, 1)
    out = jnp.where(lanes < SHD, mixed[0], mixed[1]) + skip_ref[...] * cols
    out_ref[...] = out
    gate = gate_ref[...]
    gated = out * (gate * sigmoid_of(gate))
    square_ref[...] += gated * gated


def state_backward_kernel(
    grad_ref, out_ref, gate_ref, signal_ref, taps_ref, skip_ref, gain_ref, scale_ref, cross_ref, state_ref,
    seg_col_ref, seg_row_ref, position_ref, run_row_ref, run_col_ref, step_ref,
    gate_low_ref, input_low_ref, sums_ref, direct_ref, along_ref, state_grad_ref, inner_ref, mask_ref, grad_inner_ref,
):
    rows = signal_ref.shape[0]

    @pl.when(pl.program_id(1) == 0)
    def _():
        inner_ref[...] = lax.dot_general(
            state_ref[:, NS:], state_ref[:, :NS], (((1,), (1,)), ((), ())), preferred_element_type=f32
        )
        mask_ref[...] = block_mask(rows, seg_col_ref[...], seg_row_ref[0])
        grad_inner_ref[...] = jnp.zeros_like(grad_inner_ref)

    grad, out, gate, signal = grad_ref[...], out_ref[...], gate_ref[...], signal_ref[...]
    position = position_ref[...]
    sig = sigmoid_of(gate)
    silu = gate * sig
    gated = out * silu
    scaled = grad * scale_ref[...]
    grad_gated = scaled * gain_ref[...] - gated * cross_ref[...]
    grad_out = grad_gated * silu
    gate_low_ref[...] = (grad_gated * out * (sig * (1.0 + gate * (1.0 - sig)))).astype(bf16)
    summed, moved = conv_block(signal, taps_ref, position)
    sig = sigmoid_of(summed)
    cols = summed * sig
    cols_low = cols.astype(bf16)
    grad_low = grad_out.astype(bf16)
    lanes = lax.broadcasted_iota(jnp.int32, cols.shape, 1)
    zero = jnp.zeros_like(grad_low)
    grad_cols = []
    for head in range(2):
        step_row = step_ref[0, 0, head : head + 1, :]
        inner = inner_ref[...]
        decay, mixing = mixing_block(
            inner, mask_ref[...], run_col_ref[0, 0, :, head : head + 1], run_row_ref[0, 0, head : head + 1, :], step_row
        )
        grad_cols.append(
            lax.dot_general(mixing, grad_low, (((0,), (0,)), ((), ())), preferred_element_type=f32)
        )
        grad_head = jnp.where((lanes < SHD) == (head == 0), grad_low, zero)
        grad_decay = lax.dot_general(
            grad_head, cols_low, (((1,), (1,)), ((), ())), preferred_element_type=f32
        ) * decay
        stepped = grad_decay * step_row
        grad_inner_ref[...] += stepped
        direct_ref[0, 0, head : head + 1, :] = jnp.sum(grad_decay * inner, axis=0, keepdims=True)
        along_ref[0, 0, :, head : head + 1] = jnp.sum(stepped * inner, axis=1, keepdims=True)
    grad_cols = jnp.where(lanes < SHD, grad_cols[0], grad_cols[1]) + skip_ref[...] * grad_out
    grad_sum = grad_cols * (sig * (1.0 + summed * (1.0 - sig)))
    grad_signal = grad_sum * taps_ref[0:1, :]
    sums_ref[0, 0:1, :] = jnp.sum(grad_sum * signal, axis=0, keepdims=True)
    for tap in range(1, CONV):
        kept = jnp.where(position >= tap, grad_sum, 0.0)
        grad_signal = grad_signal + pltpu.roll(kept, rows - tap, 0) * taps_ref[tap : tap + 1, :]
        sums_ref[0, tap : tap + 1, :] = jnp.sum(grad_sum * moved[tap - 1], axis=0, keepdims=True)
    sums_ref[0, CONV : CONV + 1, :] = jnp.sum(grad_sum, axis=0, keepdims=True)
    sums_ref[0, CONV + 1 : CONV + 2, :] = jnp.sum(scaled * gated, axis=0, keepdims=True)
    sums_ref[0, CONV + 2 : CONV + 3, :] = jnp.sum(grad_out * cols, axis=0, keepdims=True)
    sums_ref[0, CONV + 3 : CONV + 4, :] = jnp.zeros((1, cols.shape[1]), f32)
    input_low_ref[...] = grad_signal.astype(bf16)

    @pl.when(pl.program_id(1) == pl.num_programs(1) - 1)
    def _():
        inner_low = grad_inner_ref[...].astype(bf16)
        state_grad_ref[:, :NS] = lax.dot_general(
            inner_low, state_ref[:, NS:], (((0,), (0,)), ((), ())), preferred_element_type=f32
        )
        state_grad_ref[:, NS:] = jnp.dot(inner_low, state_ref[:, :NS], preferred_element_type=f32)


def state_specs(rows, pairs):
    block = pl.BlockSpec((rows, 2 * SHD), lambda m, p: (m, p))
    return {
        "block": block,
        "taps": pl.BlockSpec((CONV + 1, 2 * SHD), lambda m, p: (0, p)),
        "vector": pl.BlockSpec((1, 2 * SHD), lambda m, p: (0, p)),
        "state": pl.BlockSpec((rows, 2 * NS), lambda m, p: (m, 0)),
        "column": pl.BlockSpec((rows, 1), lambda m, p: (m, 0)),
        "row": pl.BlockSpec((1, 1, rows), lambda m, p: (m, 0, 0)),
        "head_row": pl.BlockSpec((1, 1, 2, rows), lambda m, p: (m, p, 0, 0)),
        "head_col": pl.BlockSpec((1, 1, rows, 2), lambda m, p: (m, p, 0, 0)),
    }


def state_forward(signal, gate, taps, skip, state, seg_col, seg_row, position, run_row, run_col, step):
    micro, pairs, _, rows = run_row.shape
    spec = state_specs(rows, pairs)
    total, width = signal.shape
    return pl.pallas_call(
        state_forward_kernel,
        out_shape=(jax.ShapeDtypeStruct((total, width), f32), jax.ShapeDtypeStruct((total, 2 * SHD), f32)),
        grid=(micro, pairs),
        in_specs=[spec[name] for name in (
            "block", "block", "taps", "vector", "state", "column", "row", "column", "head_row", "head_col", "head_row")],
        out_specs=(spec["block"], pl.BlockSpec((rows, 2 * SHD), lambda m, p: (m, 0))),
        scratch_shapes=[pltpu.VMEM((rows, rows), f32), pltpu.VMEM((rows, rows), f32)],
        cost_estimate=pl.CostEstimate(
            flops=8 * total * rows * width // SHD * SHD, transcendentals=total * rows * width // SHD, bytes_accessed=12 * total * width
        ),
        name="state_forward",
    )(signal, gate, taps, skip, state, seg_col, seg_row, position, run_row, run_col, step)


def state_backward(grad, out, gate, signal, taps, skip, gain, scale, cross, state, seg_col, seg_row, position, run_row, run_col, step):
    micro, pairs, _, rows = run_row.shape
    spec = state_specs(rows, pairs)
    total, width = signal.shape
    return pl.pallas_call(
        state_backward_kernel,
        out_shape=(
            jax.ShapeDtypeStruct((total, width), bf16),
            jax.ShapeDtypeStruct((total, width), bf16),
            jax.ShapeDtypeStruct((micro, 8, width), f32),
            jax.ShapeDtypeStruct(run_row.shape, f32),
            jax.ShapeDtypeStruct(run_col.shape, f32),
            jax.ShapeDtypeStruct((total, 2 * NS), f32),
        ),
        grid=(micro, pairs),
        in_specs=[spec[name] for name in (
            "block", "block", "block", "block", "taps", "vector", "vector", "column", "column", "state",
            "column", "row", "column", "head_row", "head_col", "head_row")],
        out_specs=(
            spec["block"], spec["block"], pl.BlockSpec((1, 8, 2 * SHD), lambda m, p: (m, 0, p)),
            spec["head_row"], spec["head_col"], spec["state"],
        ),
        scratch_shapes=[pltpu.VMEM((rows, rows), f32)] * 3,
        cost_estimate=pl.CostEstimate(
            flops=20 * total * rows * width, transcendentals=total * rows * width // SHD, bytes_accessed=20 * total * width
        ),
        name="state_backward",
    )(grad, out, gate, signal, taps, skip, gain, scale, cross, state, seg_col, seg_row, position, run_row, run_col, step)


def local(
    inputs,
    out_grad,
    deal_order,
    segment,
    query_weight,
    key_weight,
    value_weight,
    attention_out,
    mamba_gate,
    mamba_input,
    step_weight,
    state_weight,
    mamba_out,
    feed_gate,
    feed_up,
    feed_down,
    gain_input,
    gain_middle,
    kernel_inner,
    kernel_state,
    mixer_gain,
    step_bias,
    log_rate,
    skip_gain,
):
    micro, own, width = inputs.shape
    groups = lax.axis_size("dp")
    lanes = lax.axis_size("tensor")
    lane = lax.axis_index("tensor")
    group = lax.axis_index("dp")
    device = group * lanes + lane
    per = own // groups
    rows = own * lanes
    total = micro * rows
    inner_width = SH * SHD
    scale_factor = HEAD ** (-0.5)
    outer_count = groups // 4
    shard = width // groups

    swap_lane = [(0, 1), (1, 0)]

    def other_lane(values):
        return lax.ppermute(values, "tensor", swap_lane)

    def other_group(values, bits):
        return lax.ppermute(values, "dp", [(i, i ^ bits) for i in range(groups)])

    step_padded = jnp.pad(step_weight, ((0, 0), (0, STEP_PAD - step_weight.shape[1])))
    early = dict(
        gate=mamba_gate, input=mamba_input, state=state_weight, step=step_padded, query=query_weight, key=key_weight,
        value=value_weight, mix=mamba_out, attn=attention_out,
    )
    late = dict(fgate=feed_gate, fup=feed_up, fdown=feed_down)
    whole, places_of = {}, {}
    for label, group_weights in (("early", early), ("late", late)):
        start = 0
        for name, weight in group_weights.items():
            places_of[name] = (label, start, weight.shape[1])
            start += weight.shape[1]
        whole[label] = lax.all_gather(jnp.concatenate(list(group_weights.values()), axis=1), "dp", axis=0, tiled=True)

    def full(name):
        label, start, size = places_of[name]
        return lax.slice_in_dim(whole[label], start, start + size, axis=1)

    own_places = jnp.arange(own, dtype=jnp.int32)
    own_order = lax.dynamic_slice_in_dim(deal_order, device * own, own, 1)
    micro_index = jnp.arange(micro, dtype=jnp.int32)[:, None]

    def buffer_place(destination, rank):
        return destination * (micro * per) + micro_index * per + rank

    send_rank = jnp.sum((own_order[:, None, :] < own_order[:, :, None]).astype(jnp.int32), axis=2)
    send_place = buffer_place(send_rank // per, send_rank % per).reshape(-1)
    lane_order = lax.dynamic_index_in_dim(deal_order.reshape(micro, groups, lanes, own), lane, 2, keepdims=False)
    slots = device * own + own_places
    found = lane_order[:, None, :, :] == slots[None, :, None, None]
    source = jnp.sum(
        jnp.where(found, jnp.arange(groups, dtype=jnp.int32)[None, None, :, None], 0), axis=(2, 3)
    )
    recv_rank = jnp.sum(
        ((source[:, None, :] == source[:, :, None]) & (own_places[None, None, :] < own_places[None, :, None])).astype(jnp.int32),
        axis=2,
    )
    recv_place = buffer_place(source, recv_rank).reshape(-1)
    buffer_places = jnp.arange(micro * own, dtype=jnp.int32)
    send_pick = (buffer_places[:, None] == send_place[None, :]).astype(bf16)
    recv_pick = (recv_place[:, None] == buffer_places[None, :]).astype(bf16)

    def exchange(buffer):
        return lax.all_to_all(
            buffer.reshape(groups, micro * per, width), "dp", split_axis=0, concat_axis=0, tiled=True
        ).reshape(micro * own, width)

    def deal(values):
        sent = project(send_pick, values.reshape(micro * own, width)).astype(bf16)
        return project(recv_pick, exchange(sent)).astype(bf16)

    def deal_order_rows(values):
        return outer_sum(recv_pick, values).astype(bf16)

    def deal_take(moved):
        return outer_sum(send_pick, moved).astype(bf16).reshape(micro, own, width)

    def join_lanes(values):
        mine = values.reshape(micro, 1, own, -1)
        theirs = other_lane(values).reshape(micro, 1, own, -1)
        low = jnp.where(lane == 0, mine, theirs)
        high = jnp.where(lane == 0, theirs, mine)
        return jnp.concatenate([low, high], axis=1).reshape(total, -1)

    def lane_rows(values, which):
        return lax.dynamic_index_in_dim(
            values.reshape(micro, lanes, own, -1), which, 1, keepdims=False
        ).reshape(micro * own, -1)

    own_in = deal(inputs)
    own_grad = deal(out_grad)
    whole_in = join_lanes(own_in)
    whole_grad = join_lanes(own_grad)

    before = jnp.sum((segment[:, None, :] < segment[:, :, None]).astype(jnp.int32), axis=2)
    places = jnp.arange(rows, dtype=jnp.int32)
    allowed = (segment[:, :, None] == segment[:, None, :]) & (places[None, None, :] <= places[None, :, None])
    position = (places[None, :] - before).reshape(total, 1)

    masks = [1 << place for place in range(groups.bit_length() - 1)]
    relative = []
    for block in range(groups):
        flip = 0
        for place, mask in enumerate(masks):
            if block >> (len(masks) - 1 - place) & 1:
                flip ^= mask
        relative.append(flip)
    block_order = jnp.bitwise_xor(group.astype(jnp.int32), jnp.array(relative, jnp.int32))

    def split_left(left):
        return pick_halves(left, block_order, shard)

    inner_places = list(range(1, len(masks)))

    def core_send(left_parts, right):
        return outer_sum(left_parts[1], right).astype(bf16)

    def halve(kept, place):
        return (
            lax.slice_in_dim(kept, 1, 2, axis=place - 1).reshape(-1, kept.shape[-1]),
            lax.slice_in_dim(kept, 0, 1, axis=place - 1),
        )

    class Reduction:
        def __init__(self, first):
            self.places = [place for place in first if place in inner_places]
            self.places += [place for place in inner_places if place not in first]
            self.stage = 0

        def move(self, send, kept):
            self.came = other_group(send, masks[self.places[self.stage]])
            self.kept = kept
            self.stage += 1

        def first(self, left_parts, right, from_core):
            kept = (outer_sum(left_parts[0], right) + from_core.astype(f32)).astype(bf16)
            kept = kept.reshape((2,) * len(inner_places) + (shard, -1))
            return halve(kept, self.places[0])

        def added(self):
            return self.kept.astype(f32) + self.came.reshape(self.kept.shape).astype(f32)

        def next(self):
            return halve(self.added().astype(bf16), self.places[self.stage])

        def last(self):
            return self.added().reshape(shard, -1)

        def step(self):
            return self.next() if self.stage < len(self.places) else self.last()

    order = [deal_order[0, 0] >= 0]

    def unit(work):
        shapes = jax.eval_shape(work)
        results = lax.cond(
            order[0], work, lambda: jax.tree.map(lambda leaf: jnp.zeros(leaf.shape, leaf.dtype), shapes)
        )
        leaves, form = jax.tree.flatten(results)
        least = min(range(len(leaves)), key=lambda place: leaves[place].size)
        leaves[least], order[0] = lax.optimization_barrier((leaves[least], order[0]))
        return jax.tree.unflatten(form, leaves)

    def after(value, *others):
        return lax.optimization_barrier((value, others))[0]

    in32 = whole_in.astype(f32)
    in_scale = rms_scale(in32)
    normed_low = (in32 * in_scale * gain_input).astype(bf16)
    normed_left = split_left(normed_low)
    whole["early"] = after(whole["early"], whole_grad, normed_left)
    gate_z = project(normed_low, full("gate"))
    ssm_in = project(normed_low, full("input"))
    state_raw = project(normed_low, full("state"))
    heads = step_weight.shape[1]
    raw_step = project(normed_low, full("step"))[:, :heads]
    state_low = jax.nn.silu(conv_sum(state_raw, kernel_state, position)).astype(bf16)
    rate = -jnp.exp(log_rate)
    step_size = jax.nn.softplus(raw_step + step_bias)
    step_heads = step_size.reshape(micro, rows, heads).transpose(0, 2, 1)
    lower = (places[None, :] <= places[:, None]).astype(f32)
    running = jnp.einsum(
        "mhj,ij->mhi", step_heads * rate[None, :, None], lower, precision=lax.Precision.HIGHEST, preferred_element_type=f32
    )
    pairs = heads // 2
    run_row = running.reshape(micro, pairs, 2, rows)
    run_col = run_row.transpose(0, 1, 3, 2)
    step_row = step_heads.reshape(micro, pairs, 2, rows)
    skip_wide = jnp.repeat(skip_gain, SHD)[None, :]
    layout = (state_low, segment.reshape(total, 1), segment.reshape(micro, 1, rows), position, run_row, run_col, step_row)
    ssm_out, squares = state_forward(ssm_in, gate_z, kernel_inner, skip_wide, *layout)
    square_own = jnp.sum(squares, axis=1)
    square_sum = square_own + other_lane(square_own)
    inv_rms = lax.rsqrt(square_sum / inner_width + epsilon)[:, None]
    gated_low = (ssm_out * jax.nn.silu(gate_z) * inv_rms * mixer_gain).astype(bf16)

    cosine, sine = rope_tables(position)
    query_low = rotate(project(normed_low, full("query")).reshape(total, -1, HEAD), cosine, sine).astype(bf16)
    key_low = rotate(project(normed_low, full("key")).reshape(total, -1, HEAD), cosine, sine).astype(bf16)
    value_low = project(normed_low, full("value")).astype(bf16)
    kv_here = key_low.shape[1]
    query_low = query_low.reshape(micro, rows, kv_here, -1, HEAD)
    key_low = key_low.reshape(micro, rows, kv_here, HEAD)
    value_low = value_low.reshape(micro, rows, kv_here, HEAD)
    logits = jnp.einsum("migkd,mjgd->mgkij", query_low, key_low, preferred_element_type=f32) * scale_factor
    logits = jnp.where(allowed[:, None, None], logits, -jnp.inf)
    exp_scores = jnp.exp(logits - jnp.max(logits, axis=-1, keepdims=True))
    probs = exp_scores / jnp.sum(exp_scores, axis=-1, keepdims=True)
    probs_low = probs.astype(bf16)
    attended_low = (
        jnp.einsum("mgkij,mjgd->migkd", probs_low, value_low, preferred_element_type=f32).astype(bf16).reshape(total, -1)
    )
    branch_part = (project_back(gated_low, full("mix")) + project_back(attended_low, full("attn"))).astype(bf16)
    branch = branch_part.astype(f32) + other_lane(branch_part).astype(f32)
    whole_mid = (in32 + branch).astype(bf16)
    mid32 = whole_mid.astype(f32)
    mid_scale = rms_scale(mid32)
    mid_low = (mid32 * mid_scale * gain_middle).astype(bf16)
    red_fgate, red_fup, red_branch, red_low, red_high = [
        Reduction(places) for places in ((1, 2), (2, 1), (1, 2), (1, 2), (2, 1))
    ]
    feeds = (red_fgate, red_fup)
    ff_cols = feed_gate.shape[1]
    gate_cols = mamba_gate.shape[1]

    def feed_forward():
        gate_ff = project(mid_low, full("fgate"))
        up_ff = project(mid_low, full("fup"))
        sig_ff = jax.nn.sigmoid(gate_ff)
        hidden_low = (gate_ff * sig_ff * up_ff).astype(bf16)
        grad_hidden = project(whole_grad, full("fdown"))
        gate_ff_low = (grad_hidden * up_ff * (sig_ff * (1.0 + gate_ff * (1.0 - sig_ff)))).astype(bf16)
        up_ff_low = (grad_hidden * (gate_ff * sig_ff)).astype(bf16)
        grad_mid_norm = project_back(gate_ff_low, full("fgate")) + project_back(up_ff_low, full("fup"))
        grad_gain_mid = jnp.sum(grad_mid_norm * mid32 * mid_scale, axis=0)
        mid_part = rms_back(grad_mid_norm, mid32, mid_scale, gain_middle).astype(bf16)
        return grad_gain_mid, mid_part, hidden_low, jnp.concatenate([gate_ff_low, up_ff_low], axis=1)

    grad_gain_mid, mid_part, hidden_low, feed_low = unit(feed_forward)
    mid_other = hand_over(other_lane(mid_part), 3000)

    def feed_output():
        ffn_part = project_back(hidden_low, full("fdown")).astype(bf16)
        mid_left = split_left(mid_low)
        return (
            lane_rows(ffn_part, lane), lane_rows(ffn_part, 1 - lane), mid_left[0], core_send(mid_left, feed_low),
            outer_sum(whole_grad, hidden_low).astype(bf16),
        )

    ffn_own, ffn_send, mid_keep, send_feed, part_fdown = unit(feed_output)
    sum_fdown = lax.psum_scatter(part_fdown, "dp", scatter_dimension=0, tiled=True)
    feed_came = other_group(send_feed, 1)

    def keep_first(keep, right, came, reductions, sizes):
        kept = (outer_sum(keep, right) + came.astype(f32)).astype(bf16)
        kept = kept.reshape((2,) * len(inner_places) + (shard, -1))
        moves, start = [], 0
        for red, size in zip(reductions, sizes):
            moves.append(halve(kept[..., start : start + size], red.places[0]))
            start += size
        return moves

    def settle(reductions, steps):
        for red, step in zip(reductions, steps):
            if red.stage < len(red.places):
                red.move(*step)
            else:
                red.result = step

    mid_other, feed_came = lax.optimization_barrier((mid_other, feed_came))
    moves = unit(lambda: keep_first(mid_keep, feed_low, feed_came, feeds, (ff_cols, ff_cols)))
    for red, move in zip(feeds, moves):
        red.move(*move)

    def branch_backward():
        grad_middle = whole_grad.astype(f32) + (mid_part.astype(f32) + mid_other.astype(f32))
        whole_branch = grad_middle.astype(bf16)
        grad_gated_norm = project(whole_branch, full("mix"))
        cross_own = jnp.sum(grad_gated_norm * mixer_gain * (ssm_out * jax.nn.silu(gate_z)), axis=1)
        grad_attended = project(whole_branch, full("attn")).astype(bf16).reshape(micro, rows, kv_here, -1, HEAD)
        grad_probs = jnp.einsum("migkd,mjgd->mgkij", grad_attended, value_low, preferred_element_type=f32)
        grad_value = jnp.einsum("mgkij,migkd->mjgd", probs_low, grad_attended, preferred_element_type=f32)
        weighted_sum = jnp.sum(probs * grad_probs, axis=-1, keepdims=True)
        grad_logits = (probs * (grad_probs - weighted_sum)).astype(bf16)
        grad_query_rot = jnp.einsum("mgkij,mjgd->migkd", grad_logits, key_low, preferred_element_type=f32) * scale_factor
        grad_key_rot = jnp.einsum("mgkij,migkd->mjgd", grad_logits, query_low, preferred_element_type=f32) * scale_factor
        query_grad_low = rotate_back(grad_query_rot.reshape(total, -1, HEAD), cosine, sine).astype(bf16).reshape(total, -1)
        key_grad_low = rotate_back(grad_key_rot.reshape(total, -1, HEAD), cosine, sine).astype(bf16).reshape(total, -1)
        value_grad_low = grad_value.astype(bf16).reshape(total, -1)
        branch_right = jnp.concatenate([gated_low, attended_low], axis=1)
        branch_left = split_left(whole_branch)
        return (
            cross_own, lane_rows(grad_middle, lane), grad_gated_norm, branch_left, branch_right,
            (query_grad_low, key_grad_low, value_grad_low),
        )

    cross_own, grad_middle_own, grad_gated_norm, branch_left, branch_right, qkv_low = unit(branch_backward)

    cross_other = other_lane(cross_own)
    send_branch, steps = unit(lambda: (core_send(branch_left, branch_right), [red.step() for red in feeds]))
    branch_came = other_group(send_branch, 1)
    settle(feeds, steps)

    def state_space_backward():
        cross = (inv_rms**3) * ((cross_own + cross_other)[:, None] / inner_width)
        gate_low, input_low, column_sums, direct, along, grad_state_act = state_backward(
            grad_gated_norm, ssm_out, gate_z, ssm_in, kernel_inner, skip_wide, mixer_gain[None, :], inv_rms, cross, *layout
        )
        column_sums = jnp.sum(column_sums, axis=0)
        grad_kernel_inner = column_sums[: CONV + 1]
        grad_mixer = column_sums[CONV + 1]
        grad_skip = jnp.sum(column_sums[CONV + 2].reshape(heads, SHD), axis=1)
        grad_direct = direct.reshape(micro, heads, rows)
        grad_running = along.transpose(0, 1, 3, 2).reshape(micro, heads, rows) - step_heads * grad_direct
        grad_product = jnp.einsum(
            "mhi,ij->mhj", grad_running, lower, precision=lax.Precision.HIGHEST, preferred_element_type=f32
        )
        grad_step = (grad_direct + grad_product * rate[None, :, None]).transpose(0, 2, 1).reshape(total, heads)
        grad_rate = jnp.sum(grad_product * step_heads, axis=(0, 2)) * rate
        grad_raw_step = grad_step * jax.nn.sigmoid(raw_step + step_bias)
        grad_bias = jnp.sum(grad_raw_step, axis=0)
        grad_state_raw, grad_kernel_state = conv_back(grad_state_act, state_raw, kernel_state, position)
        step_low = jnp.pad(grad_raw_step.astype(bf16), ((0, 0), (0, STEP_PAD - heads)))
        first_right = jnp.concatenate([gate_low, input_low, grad_state_raw.astype(bf16), step_low, *qkv_low], axis=1)
        small = (grad_kernel_state, grad_kernel_inner, grad_mixer, grad_bias, grad_rate, grad_skip)
        return small, first_right

    small, first_right = unit(state_space_backward)
    grad_kernel_state, grad_kernel_inner, grad_mixer, grad_bias, grad_rate, grad_skip = small

    def third_moves():
        return (
            core_send(normed_left, first_right),
            red_branch.first(branch_left, branch_right, branch_came),
            lax.optimization_barrier(ffn_send),
            [red.step() for red in feeds],
            sum_fdown.astype(f32),
        )

    send_first, move, ffn_send, steps, total_fdown = unit(third_moves)
    settle(feeds, steps)
    first_came = other_group(send_first, 1)
    red_branch.move(*move)
    ffn_other = other_lane(ffn_send)

    def input_gradient():
        weights = [full(name) for name in ("gate", "input", "state", "step", "query", "key", "value")]
        grad_normed, start = 0.0, 0
        for weight in weights:
            grad_normed = grad_normed + project_back(first_right[:, start : start + weight.shape[1]], weight)
            start += weight.shape[1]
        grad_gain_in = jnp.sum(grad_normed * in32 * in_scale, axis=0)
        in_part = rms_back(grad_normed, in32, in_scale, gain_input).astype(bf16)
        return grad_gain_in, lane_rows(in_part, lane), lane_rows(in_part, 1 - lane)

    grad_gain_in, in_own, in_send = unit(input_gradient)

    shared = [grad_gain_in, grad_gain_mid, grad_kernel_state.reshape(-1)]
    split = [grad_kernel_inner.reshape(-1), grad_mixer, grad_bias, grad_rate, grad_skip]
    used = sum(item.shape[0] for item in shared + split)
    padded = -(-used // 1024) * 1024
    firsts = (red_low, red_high)
    first_sizes = (first_right.shape[1] // 256 * 128, first_right.shape[1] - first_right.shape[1] // 256 * 128)

    def first_moves():
        moves = keep_first(normed_left[0], first_right, first_came, firsts, first_sizes)
        flat = jnp.pad(jnp.concatenate(shared + split), (0, padded - used)).reshape(padded // 128, 128)
        ffn_out = ffn_own.astype(f32) + ffn_other.astype(f32)
        out_rows = (lane_rows(whole_mid, lane).astype(f32) + ffn_out).astype(bf16)
        return moves, lax.optimization_barrier(in_send), flat, deal_order_rows(out_rows), [red.step() for red in (*feeds, red_branch)]

    moves, in_send, flat, out_sent, steps = unit(first_moves)
    settle((*feeds, red_branch), steps)
    out_moved = exchange(out_sent)
    for red, move in zip(firsts, moves):
        red.move(*move)
    in_other = other_lane(in_send)
    flat_moved = other_group(flat, masks[0])
    flat = unit(lambda: flat + flat_moved)
    flat_moved = other_group(flat, masks[1])

    def send_input():
        in_sum = in_own.astype(f32) + in_other.astype(f32)
        return deal_order_rows((in_sum + grad_middle_own).astype(bf16))

    everything = [*feeds, red_branch, *firsts]
    in_moved = None
    bits = 2
    while pending := [red for red in everything if not hasattr(red, "result")]:
        last = all(red.stage == len(red.places) for red in pending)
        steps, flat, other = unit(
            lambda: (
                [red.step() for red in pending],
                flat + flat_moved if bits <= len(masks) else flat,
                (deal_take(in_moved), deal_take(out_moved)) if last else send_input() if in_moved is None else (),
            )
        )
        settle(pending, steps)
        if bits < len(masks):
            flat_moved = other_group(flat, masks[bits])
        bits += 1
        if in_moved is None:
            in_moved = exchange(other)
    grad_input, block_out = other
    theirs = other_lane(flat).reshape(-1)
    flat = flat.reshape(-1)
    pieces, start = [], 0
    for item in shared:
        pieces.append(flat[start : start + item.shape[0]] + theirs[start : start + item.shape[0]])
        start += item.shape[0]
    for item in split:
        mine, other = flat[start : start + item.shape[0]], theirs[start : start + item.shape[0]]
        pieces.append((jnp.where(lane == 0, mine, other), jnp.where(lane == 0, other, mine)))
        start += item.shape[0]
    sum_gin, sum_gmid, sum_kst = pieces[0], pieces[1], pieces[2].reshape(CONV + 1, -1)
    sum_kin = jnp.concatenate([half.reshape(CONV + 1, -1) for half in pieces[3]], axis=1)
    sum_mix, sum_bias, sum_rate, sum_skip = [jnp.concatenate(pair) for pair in pieces[4:]]

    query_cols, key_cols = query_weight.shape[1], key_weight.shape[1]
    total_fgate, total_fup = red_fgate.result, red_fup.result
    total_mix, total_attn = red_branch.result[:, :gate_cols], red_branch.result[:, gate_cols:]
    rest = jnp.concatenate([red.result for red in firsts], axis=1)
    total_gate, total_input, rest = rest[:, :gate_cols], rest[:, gate_cols : 2 * gate_cols], rest[:, 2 * gate_cols :]
    total_step = rest[:, 2 * NS : 2 * NS + heads]
    start = 2 * NS + STEP_PAD
    total_query = rest[:, start : start + query_cols]
    total_key = rest[:, start + query_cols : start + query_cols + key_cols]
    total_value = rest[:, start + query_cols + key_cols :]
    state_rows = rest[:, : 2 * NS].reshape(lanes, shard // lanes, 2 * NS)
    state_own = lax.dynamic_index_in_dim(state_rows, lane, 0, keepdims=False)
    state_send = lax.dynamic_index_in_dim(state_rows, 1 - lane, 0, keepdims=False)
    state_lane = state_own + other_lane(state_send)
    return (
        block_out,
        grad_input,
        total_query,
        total_key,
        total_value,
        total_attn,
        total_gate,
        total_input,
        total_step,
        state_lane,
        total_mix,
        total_fgate,
        total_fup,
        total_fdown,
        sum_gin,
        sum_gmid,
        sum_kin,
        sum_kst,
        sum_mix,
        sum_bias,
        sum_rate,
        sum_skip,
    )


def solution(mesh):
    both = P("dp", "tensor")
    in_specs = (
        P(None, ("dp", "tensor"), None),
        P(None, ("dp", "tensor"), None),
        P(),
        P(None, "dp"),
        both,
        both,
        both,
        both,
        both,
        both,
        both,
        P("dp", None),
        both,
        both,
        both,
        both,
        P(),
        P(),
        P(None, "tensor"),
        P(),
        P("tensor"),
        P("tensor"),
        P("tensor"),
        P("tensor"),
    )
    out_specs = (
        P(None, ("dp", "tensor"), None),
        P(None, ("dp", "tensor"), None),
        both,
        both,
        both,
        both,
        both,
        both,
        both,
        P(("dp", "tensor"), None),
        both,
        both,
        both,
        both,
        P(),
        P(),
        P(),
        P(),
        P(),
        P(),
        P(),
        P(),
    )
    return jax.shard_map(local, mesh=mesh, in_specs=in_specs, out_specs=out_specs, check_vma=False)
```

```python
import math

import jax
import jax.numpy as jnp
from jax import lax
from jax.experimental import pallas as pl
from jax.experimental.pallas import tpu as pltpu
from jax.sharding import PartitionSpec as P

HEAD = 128
SH = 48
SHD = 64
NS = 256
CONV = 4
STEP_PAD = 128

epsilon = 1e-05
rope_base = 100000000000.0
f32 = jnp.float32
bf16 = jnp.bfloat16


def project(left, right):
    return jnp.dot(left, right, preferred_element_type=f32)


def project_back(left, right):
    return lax.dot_general(left, right, (((1,), (1,)), ((), ())), preferred_element_type=f32)


def outer_sum(left, right):
    return lax.dot_general(left, right, (((0,), (0,)), ((), ())), preferred_element_type=f32)


def rms_scale(values):
    return lax.rsqrt(jnp.mean(values * values, axis=-1, keepdims=True) + epsilon)


def rms_back(grad, values, scale, gain):
    weighted = grad * gain
    inner = jnp.sum(weighted * values, axis=-1, keepdims=True)
    return scale * weighted - values * (scale * scale * scale * inner / values.shape[-1])


def shift_down(values, count):
    return jnp.concatenate([jnp.zeros((count, values.shape[1]), values.dtype), values[:-count]], axis=0)


def shift_up(values, count):
    return jnp.concatenate([values[count:], jnp.zeros((count, values.shape[1]), values.dtype)], axis=0)


def conv_sum(signal, kernel, position):
    summed = kernel[CONV][None, :] + signal * kernel[0][None, :]
    for tap in range(1, CONV):
        moved = jnp.where(position >= tap, shift_down(signal, tap), 0.0)
        summed = summed + moved * kernel[tap][None, :]
    return summed


def silu_back(values):
    sig = jax.nn.sigmoid(values)
    return sig * (1.0 + values * (1.0 - sig))


def conv_back(grad, signal, kernel, position):
    grad_sum = grad * silu_back(conv_sum(signal, kernel, position))
    grad_signal = grad_sum * kernel[0][None, :]
    grad_taps = [jnp.sum(grad_sum * signal, axis=0)]
    for tap in range(1, CONV):
        kept = jnp.where(position >= tap, grad_sum, 0.0)
        grad_signal = grad_signal + shift_up(kept, tap) * kernel[tap][None, :]
        grad_taps.append(jnp.sum(kept * shift_down(signal, tap), axis=0))
    grad_taps.append(jnp.sum(grad_sum, axis=0))
    return grad_signal, jnp.stack(grad_taps)


def rope_tables(position):
    half_size = HEAD // 2
    frequency = jnp.exp(jnp.arange(half_size, dtype=f32) * (-2.0 * math.log(rope_base) / HEAD))
    angles = position.astype(f32) * frequency[None, :]
    return jnp.cos(angles)[:, None, :], jnp.sin(angles)[:, None, :]


def rotate(values, cosine, sine):
    half_size = HEAD // 2
    first, second = values[..., :half_size], values[..., half_size:]
    return jnp.concatenate([first * cosine - second * sine, second * cosine + first * sine], axis=-1)


def copy_blocks(order_ref, first_ref, second_ref, first_out_ref, second_out_ref):
    first_out_ref[...] = first_ref[...]
    second_out_ref[...] = second_ref[...]


def pick_halves(values, order, block):
    height, width = values.shape
    count = width // block // 2
    if block % 128:
        mixed = jnp.take(values.reshape(height, -1, block), order, axis=1).reshape(height, width)
        return mixed[:, : width // 2], mixed[:, width // 2 :]
    half = jax.ShapeDtypeStruct((height, width // 2), values.dtype)
    out_spec = pl.BlockSpec((height, block), lambda i, order: (0, i))
    return pl.pallas_call(
        copy_blocks,
        out_shape=(half, half),
        grid_spec=pltpu.PrefetchScalarGridSpec(
            num_scalar_prefetch=1,
            grid=(count,),
            in_specs=[
                pl.BlockSpec((height, block), lambda i, order: (0, order[i])),
                pl.BlockSpec((height, block), lambda i, order: (0, order[i + count])),
            ],
            out_specs=(out_spec, out_spec),
        ),
        cost_estimate=pl.CostEstimate(flops=0, transcendentals=0, bytes_accessed=4 * height * width),
        name="pick_halves",
    )(order, values, values)


def hand_over(values, microseconds):
    def idle(values_ref, out_ref):
        pass

    return pl.pallas_call(
        idle,
        out_shape=jax.ShapeDtypeStruct(values.shape, values.dtype),
        in_specs=[pl.BlockSpec(memory_space=pl.ANY)],
        out_specs=pl.BlockSpec(memory_space=pl.ANY),
        input_output_aliases={0: 0},
        cost_estimate=pl.CostEstimate(flops=microseconds * 1150000000, transcendentals=0, bytes_accessed=0),
        name="hand_over",
    )(values)


def rotate_back(values, cosine, sine):
    return rotate(values, cosine, -sine)


NEGATIVE = -1e30


def sigmoid_of(values):
    return 1.0 / (1.0 + jnp.exp(-values))


def block_mask(rows, segment_col, segment_row):
    row_index = lax.broadcasted_iota(jnp.int32, (rows, rows), 0)
    col_index = lax.broadcasted_iota(jnp.int32, (rows, rows), 1)
    return jnp.where((segment_col == segment_row) & (col_index <= row_index), 0.0, NEGATIVE)


def conv_block(signal, taps_ref, position):
    summed = taps_ref[CONV : CONV + 1, :] + signal * taps_ref[0:1, :]
    moved = []
    for tap in range(1, CONV):
        shifted = jnp.where(position >= tap, pltpu.roll(signal, tap, 0), 0.0)
        moved.append(shifted)
        summed = summed + shifted * taps_ref[tap : tap + 1, :]
    return summed, moved


def conv_block_back(grad_sum, signal, moved, taps_ref, position, sums_ref):
    rows = signal.shape[0]
    grad_signal = grad_sum * taps_ref[0:1, :]
    sums_ref[0, 0:1, :] = jnp.sum(grad_sum * signal, axis=0, keepdims=True)
    for tap in range(1, CONV):
        kept = jnp.where(position >= tap, grad_sum, 0.0)
        grad_signal = grad_signal + pltpu.roll(kept, rows - tap, 0) * taps_ref[tap : tap + 1, :]
        sums_ref[0, tap : tap + 1, :] = jnp.sum(grad_sum * moved[tap - 1], axis=0, keepdims=True)
    sums_ref[0, CONV : CONV + 1, :] = jnp.sum(grad_sum, axis=0, keepdims=True)
    return grad_signal


def mixing_block(inner, mask, run_col, run_row, step_row):
    decay = jnp.exp(run_col - run_row + mask)
    return decay, (inner * decay * step_row).astype(bf16)


def state_forward_kernel(
    signal_ref, gate_ref, taps_ref, skip_ref, state_ref, seg_col_ref, seg_row_ref, position_ref,
    run_row_ref, run_col_ref, step_ref, out_ref, square_ref, inner_ref, mask_ref,
):
    rows = signal_ref.shape[0]

    @pl.when(pl.program_id(1) == 0)
    def _():
        inner_ref[...] = lax.dot_general(
            state_ref[:, NS:], state_ref[:, :NS], (((1,), (1,)), ((), ())), preferred_element_type=f32
        )
        mask_ref[...] = block_mask(rows, seg_col_ref[...], seg_row_ref[0])
        square_ref[...] = jnp.zeros_like(square_ref)

    summed, _ = conv_block(signal_ref[...], taps_ref, position_ref[...])
    cols = summed * sigmoid_of(summed)
    cols_low = cols.astype(bf16)
    mixed = []
    for head in range(2):
        _, mixing = mixing_block(
            inner_ref[...], mask_ref[...], run_col_ref[0, 0, :, head : head + 1],
            run_row_ref[0, 0, head : head + 1, :], step_ref[0, 0, head : head + 1, :],
        )
        mixed.append(jnp.dot(mixing, cols_low, preferred_element_type=f32))
    lanes = lax.broadcasted_iota(jnp.int32, cols.shape, 1)
    out = jnp.where(lanes < SHD, mixed[0], mixed[1]) + skip_ref[...] * cols
    out_ref[...] = out
    gate = gate_ref[...]
    gated = out * (gate * sigmoid_of(gate))
    square_ref[...] += gated * gated


def state_backward_kernel(
    grad_ref, out_ref, gate_ref, signal_ref, taps_ref, skip_ref, gain_ref, scale_ref, cross_ref, state_ref,
    seg_col_ref, seg_row_ref, position_ref, run_row_ref, run_col_ref, step_ref,
    state_raw_ref, state_taps_ref, step_all_ref, step_sig_ref, rate_ref,
    gate_low_ref, input_low_ref, sums_ref, rest_low_ref, state_sums_ref, head_sums_ref,
    inner_ref, mask_ref, grad_inner_ref, direct_ref, along_ref,
):
    rows = signal_ref.shape[0]
    pair = pl.program_id(1)

    @pl.when(pair == 0)
    def _():
        along_ref[...] = jnp.zeros_like(along_ref)
        inner_ref[...] = lax.dot_general(
            state_ref[:, NS:], state_ref[:, :NS], (((1,), (1,)), ((), ())), preferred_element_type=f32
        )
        mask_ref[...] = block_mask(rows, seg_col_ref[...], seg_row_ref[0])
        grad_inner_ref[...] = jnp.zeros_like(grad_inner_ref)

    grad, out, gate, signal = grad_ref[...], out_ref[...], gate_ref[...], signal_ref[...]
    position = position_ref[...]
    sig = sigmoid_of(gate)
    silu = gate * sig
    gated = out * silu
    scaled = grad * scale_ref[...]
    grad_gated = scaled * gain_ref[...] - gated * cross_ref[...]
    grad_out = grad_gated * silu
    gate_low_ref[...] = (grad_gated * out * (sig * (1.0 + gate * (1.0 - sig)))).astype(bf16)
    summed, moved = conv_block(signal, taps_ref, position)
    sig = sigmoid_of(summed)
    cols = summed * sig
    cols_low = cols.astype(bf16)
    grad_low = grad_out.astype(bf16)
    lanes = lax.broadcasted_iota(jnp.int32, cols.shape, 1)
    zero = jnp.zeros_like(grad_low)
    grad_cols = []
    for head in range(2):
        step_row = step_ref[0, 0, head : head + 1, :]
        inner = inner_ref[...]
        decay, mixing = mixing_block(
            inner, mask_ref[...], run_col_ref[0, 0, :, head : head + 1], run_row_ref[0, 0, head : head + 1, :], step_row
        )
        grad_cols.append(
            lax.dot_general(mixing, grad_low, (((0,), (0,)), ((), ())), preferred_element_type=f32)
        )
        grad_head = jnp.where((lanes < SHD) == (head == 0), grad_low, zero)
        grad_decay = lax.dot_general(
            grad_head, cols_low, (((1,), (1,)), ((), ())), preferred_element_type=f32
        ) * decay
        stepped = grad_decay * step_row
        grad_inner_ref[...] += stepped
        direct_ref[pl.ds(2 * pair + head, 1), :] = jnp.sum(grad_decay * inner, axis=0, keepdims=True)
        along = jnp.sum(stepped * inner, axis=1, keepdims=True)
        along_ref[...] = jnp.where(lanes == 2 * pair + head, along, along_ref[...])
    grad_cols = jnp.where(lanes < SHD, grad_cols[0], grad_cols[1]) + skip_ref[...] * grad_out
    grad_sum = grad_cols * (sig * (1.0 + summed * (1.0 - sig)))
    grad_signal = conv_block_back(grad_sum, signal, moved, taps_ref, position, sums_ref)
    sums_ref[0, CONV + 1 : CONV + 2, :] = jnp.sum(scaled * gated, axis=0, keepdims=True)
    sums_ref[0, CONV + 2 : CONV + 3, :] = jnp.sum(grad_out * cols, axis=0, keepdims=True)
    sums_ref[0, CONV + 3 : CONV + 4, :] = jnp.zeros((1, cols.shape[1]), f32)
    input_low_ref[...] = grad_signal.astype(bf16)

    @pl.when(pair == pl.num_programs(1) - 1)
    def _():
        inner_low = grad_inner_ref[...].astype(bf16)
        for part, (mine, other) in enumerate((((0, NS), (NS, 2 * NS)), ((NS, 2 * NS), (0, NS)))):
            raw = state_raw_ref[:, mine[0] : mine[1]]
            taps = state_taps_ref.at[:, mine[0] : mine[1]]
            summed, moved = conv_block(raw, taps, position)
            sig = sigmoid_of(summed)
            grad = lax.dot_general(
                inner_low, state_ref[:, other[0] : other[1]], (((part,), (0,)), ((), ())), preferred_element_type=f32
            )
            grad_sum = grad * (sig * (1.0 + summed * (1.0 - sig)))
            back = conv_block_back(grad_sum, raw, moved, taps, position, state_sums_ref.at[:, :, mine[0] : mine[1]])
            rest_low_ref[:, mine[0] : mine[1]] = back.astype(bf16)
        state_sums_ref[0, CONV + 1 :, :] = jnp.zeros((7 - CONV, 2 * NS), f32)
        heads = step_all_ref.shape[1]
        direct, step = direct_ref[...], step_all_ref[0]
        grad_running = along_ref[...].T[:heads] - step * direct
        row_index = lax.broadcasted_iota(jnp.int32, (rows, rows), 0)
        col_index = lax.broadcasted_iota(jnp.int32, (rows, rows), 1)
        lower = jnp.where(col_index <= row_index, 1.0, 0.0)
        grad_product = jnp.dot(
            grad_running, lower, precision=lax.Precision.HIGHEST, preferred_element_type=f32
        )
        grad_raw = (direct + grad_product * rate_ref[...]) * step_sig_ref[0]
        head_sums_ref[0, :, 0:1] = jnp.sum(grad_product * step, axis=1, keepdims=True)
        head_sums_ref[0, :, 1:2] = jnp.sum(grad_raw, axis=1, keepdims=True)
        wide = jnp.concatenate([grad_raw, jnp.zeros((STEP_PAD - heads, rows), f32)], axis=0)
        rest_low_ref[:, 2 * NS :] = wide.T.astype(bf16)


def state_specs(rows, pairs):
    block = pl.BlockSpec((rows, 2 * SHD), lambda m, p: (m, p))
    return {
        "block": block,
        "taps": pl.BlockSpec((CONV + 1, 2 * SHD), lambda m, p: (0, p)),
        "vector": pl.BlockSpec((1, 2 * SHD), lambda m, p: (0, p)),
        "state": pl.BlockSpec((rows, 2 * NS), lambda m, p: (m, 0)),
        "column": pl.BlockSpec((rows, 1), lambda m, p: (m, 0)),
        "row": pl.BlockSpec((1, 1, rows), lambda m, p: (m, 0, 0)),
        "head_row": pl.BlockSpec((1, 1, 2, rows), lambda m, p: (m, p, 0, 0)),
        "head_col": pl.BlockSpec((1, 1, rows, 2), lambda m, p: (m, p, 0, 0)),
    }


def state_forward(signal, gate, taps, skip, state, seg_col, seg_row, position, run_row, run_col, step):
    micro, pairs, _, rows = run_row.shape
    spec = state_specs(rows, pairs)
    total, width = signal.shape
    return pl.pallas_call(
        state_forward_kernel,
        out_shape=(jax.ShapeDtypeStruct((total, width), f32), jax.ShapeDtypeStruct((total, 2 * SHD), f32)),
        grid=(micro, pairs),
        in_specs=[spec[name] for name in (
            "block", "block", "taps", "vector", "state", "column", "row", "column", "head_row", "head_col", "head_row")],
        out_specs=(spec["block"], pl.BlockSpec((rows, 2 * SHD), lambda m, p: (m, 0))),
        scratch_shapes=[pltpu.VMEM((rows, rows), f32), pltpu.VMEM((rows, rows), f32)],
        cost_estimate=pl.CostEstimate(
            flops=8 * total * rows * width // SHD * SHD, transcendentals=total * rows * width // SHD, bytes_accessed=12 * total * width
        ),
        name="state_forward",
    )(signal, gate, taps, skip, state, seg_col, seg_row, position, run_row, run_col, step)


def state_backward(
    grad, out, gate, signal, taps, skip, gain, scale, cross, state, seg_col, seg_row, position, run_row, run_col, step,
    state_raw, state_taps, step_all, step_sig, rate,
):
    micro, pairs, _, rows = run_row.shape
    heads = 2 * pairs
    spec = state_specs(rows, pairs)
    total, width = signal.shape
    heads_block = pl.BlockSpec((1, heads, rows), lambda m, p: (m, 0, 0))
    return pl.pallas_call(
        state_backward_kernel,
        out_shape=(
            jax.ShapeDtypeStruct((total, width), bf16),
            jax.ShapeDtypeStruct((total, width), bf16),
            jax.ShapeDtypeStruct((micro, 8, width), f32),
            jax.ShapeDtypeStruct((total, 2 * NS + STEP_PAD), bf16),
            jax.ShapeDtypeStruct((micro, 8, 2 * NS), f32),
            jax.ShapeDtypeStruct((micro, heads, 2), f32),
        ),
        grid=(micro, pairs),
        in_specs=[spec[name] for name in (
            "block", "block", "block", "block", "taps", "vector", "vector", "column", "column", "state",
            "column", "row", "column", "head_row", "head_col", "head_row", "state")]
        + [
            pl.BlockSpec((CONV + 1, 2 * NS), lambda m, p: (0, 0)), heads_block, heads_block,
            pl.BlockSpec((heads, 1), lambda m, p: (0, 0)),
        ],
        out_specs=(
            spec["block"], spec["block"], pl.BlockSpec((1, 8, 2 * SHD), lambda m, p: (m, 0, p)),
            pl.BlockSpec((rows, 2 * NS + STEP_PAD), lambda m, p: (m, 0)),
            pl.BlockSpec((1, 8, 2 * NS), lambda m, p: (m, 0, 0)),
            pl.BlockSpec((1, heads, 2), lambda m, p: (m, 0, 0)),
        ),
        scratch_shapes=[pltpu.VMEM((rows, rows), f32)] * 3 + [pltpu.VMEM((heads, rows), f32), pltpu.VMEM((rows, 2 * SHD), f32)],
        cost_estimate=pl.CostEstimate(
            flops=20 * total * rows * width, transcendentals=total * rows * width // SHD, bytes_accessed=20 * total * width
        ),
        name="state_backward",
    )(
        grad, out, gate, signal, taps, skip, gain, scale, cross, state, seg_col, seg_row, position, run_row, run_col, step,
        state_raw, state_taps, step_all, step_sig, rate,
    )


def local(
    inputs,
    out_grad,
    deal_order,
    segment,
    query_weight,
    key_weight,
    value_weight,
    attention_out,
    mamba_gate,
    mamba_input,
    step_weight,
    state_weight,
    mamba_out,
    feed_gate,
    feed_up,
    feed_down,
    gain_input,
    gain_middle,
    kernel_inner,
    kernel_state,
    mixer_gain,
    step_bias,
    log_rate,
    skip_gain,
):
    micro, own, width = inputs.shape
    groups = lax.axis_size("dp")
    lanes = lax.axis_size("tensor")
    lane = lax.axis_index("tensor")
    group = lax.axis_index("dp")
    device = group * lanes + lane
    per = own // groups
    rows = own * lanes
    total = micro * rows
    inner_width = SH * SHD
    scale_factor = HEAD ** (-0.5)
    outer_count = groups // 4
    shard = width // groups

    swap_lane = [(0, 1), (1, 0)]

    def other_lane(values):
        return lax.ppermute(values, "tensor", swap_lane)

    def other_group(values, bits):
        return lax.ppermute(values, "dp", [(i, i ^ bits) for i in range(groups)])

    step_padded = jnp.pad(step_weight, ((0, 0), (0, STEP_PAD - step_weight.shape[1])))
    early = dict(
        gate=mamba_gate, input=mamba_input, state=state_weight, step=step_padded, query=query_weight, key=key_weight,
        value=value_weight, mix=mamba_out, attn=attention_out,
    )
    late = dict(fgate=feed_gate, fup=feed_up, fdown=feed_down)
    whole, places_of = {}, {}
    for label, group_weights in (("early", early), ("late", late)):
        start = 0
        for name, weight in group_weights.items():
            places_of[name] = (label, start, weight.shape[1])
            start += weight.shape[1]
        whole[label] = lax.all_gather(jnp.concatenate(list(group_weights.values()), axis=1), "dp", axis=0, tiled=True)

    def full(name):
        label, start, size = places_of[name]
        return lax.slice_in_dim(whole[label], start, start + size, axis=1)

    own_places = jnp.arange(own, dtype=jnp.int32)
    own_order = lax.dynamic_slice_in_dim(deal_order, device * own, own, 1)
    micro_index = jnp.arange(micro, dtype=jnp.int32)[:, None]

    def buffer_place(destination, rank):
        return destination * (micro * per) + micro_index * per + rank

    send_rank = jnp.sum((own_order[:, None, :] < own_order[:, :, None]).astype(jnp.int32), axis=2)
    send_place = buffer_place(send_rank // per, send_rank % per).reshape(-1)
    lane_order = lax.dynamic_index_in_dim(deal_order.reshape(micro, groups, lanes, own), lane, 2, keepdims=False)
    slots = device * own + own_places
    found = lane_order[:, None, :, :] == slots[None, :, None, None]
    source = jnp.sum(
        jnp.where(found, jnp.arange(groups, dtype=jnp.int32)[None, None, :, None], 0), axis=(2, 3)
    )
    recv_rank = jnp.sum(
        ((source[:, None, :] == source[:, :, None]) & (own_places[None, None, :] < own_places[None, :, None])).astype(jnp.int32),
        axis=2,
    )
    recv_place = buffer_place(source, recv_rank).reshape(-1)
    buffer_places = jnp.arange(micro * own, dtype=jnp.int32)
    send_pick = (buffer_places[:, None] == send_place[None, :]).astype(bf16)
    recv_pick = (recv_place[:, None] == buffer_places[None, :]).astype(bf16)

    def exchange(buffer):
        return lax.all_to_all(
            buffer.reshape(groups, micro * per, width), "dp", split_axis=0, concat_axis=0, tiled=True
        ).reshape(micro * own, width)

    def deal(values):
        sent = project(send_pick, values.reshape(micro * own, width)).astype(bf16)
        return project(recv_pick, exchange(sent)).astype(bf16)

    def deal_order_rows(values):
        return outer_sum(recv_pick, values).astype(bf16)

    def deal_take(moved):
        return outer_sum(send_pick, moved).astype(bf16).reshape(micro, own, width)

    def join_lanes(values):
        mine = values.reshape(micro, 1, own, -1)
        theirs = other_lane(values).reshape(micro, 1, own, -1)
        low = jnp.where(lane == 0, mine, theirs)
        high = jnp.where(lane == 0, theirs, mine)
        return jnp.concatenate([low, high], axis=1).reshape(total, -1)

    def lane_rows(values, which):
        return lax.dynamic_index_in_dim(
            values.reshape(micro, lanes, own, -1), which, 1, keepdims=False
        ).reshape(micro * own, -1)

    own_in = deal(inputs)
    own_grad = deal(out_grad)
    whole_in = join_lanes(own_in)
    whole_grad = join_lanes(own_grad)

    before = jnp.sum((segment[:, None, :] < segment[:, :, None]).astype(jnp.int32), axis=2)
    places = jnp.arange(rows, dtype=jnp.int32)
    allowed = (segment[:, :, None] == segment[:, None, :]) & (places[None, None, :] <= places[None, :, None])
    position = (places[None, :] - before).reshape(total, 1)

    masks = [1 << place for place in range(groups.bit_length() - 1)]
    relative = []
    for block in range(groups):
        flip = 0
        for place, mask in enumerate(masks):
            if block >> (len(masks) - 1 - place) & 1:
                flip ^= mask
        relative.append(flip)
    block_order = jnp.bitwise_xor(group.astype(jnp.int32), jnp.array(relative, jnp.int32))

    def split_left(left):
        return pick_halves(left, block_order, shard)

    inner_places = list(range(1, len(masks)))

    def core_send(left_parts, right):
        return outer_sum(left_parts[1], right).astype(bf16)

    def halve(kept, place):
        return (
            lax.slice_in_dim(kept, 1, 2, axis=place - 1).reshape(-1, kept.shape[-1]),
            lax.slice_in_dim(kept, 0, 1, axis=place - 1),
        )

    class Reduction:
        def __init__(self, first):
            self.places = [place for place in first if place in inner_places]
            self.places += [place for place in inner_places if place not in first]
            self.stage = 0

        def move(self, send, kept):
            self.came = other_group(send, masks[self.places[self.stage]])
            self.kept = kept
            self.stage += 1

        def first(self, left_parts, right, from_core):
            kept = (outer_sum(left_parts[0], right) + from_core.astype(f32)).astype(bf16)
            kept = kept.reshape((2,) * len(inner_places) + (shard, -1))
            return halve(kept, self.places[0])

        def added(self):
            return self.kept.astype(f32) + self.came.reshape(self.kept.shape).astype(f32)

        def next(self):
            return halve(self.added().astype(bf16), self.places[self.stage])

        def last(self):
            return self.added().reshape(shard, -1)

        def step(self):
            return self.next() if self.stage < len(self.places) else self.last()

    order = [deal_order[0, 0] >= 0]

    def unit(work):
        shapes = jax.eval_shape(work)
        results = lax.cond(
            order[0], work, lambda: jax.tree.map(lambda leaf: jnp.zeros(leaf.shape, leaf.dtype), shapes)
        )
        leaves, form = jax.tree.flatten(results)
        least = min(range(len(leaves)), key=lambda place: leaves[place].size)
        leaves[least], order[0] = lax.optimization_barrier((leaves[least], order[0]))
        return jax.tree.unflatten(form, leaves)

    def after(value, *others):
        return lax.optimization_barrier((value, others))[0]

    in32 = whole_in.astype(f32)
    in_scale = rms_scale(in32)
    normed_low = (in32 * in_scale * gain_input).astype(bf16)
    normed_left = split_left(normed_low)
    whole["early"] = after(whole["early"], whole_grad, normed_left)
    gate_z = project(normed_low, full("gate"))
    ssm_in = project(normed_low, full("input"))
    state_raw = project(normed_low, full("state"))
    heads = step_weight.shape[1]
    raw_step = project(normed_low, full("step"))[:, :heads]
    state_low = jax.nn.silu(conv_sum(state_raw, kernel_state, position)).astype(bf16)
    rate = -jnp.exp(log_rate)
    step_size = jax.nn.softplus(raw_step + step_bias)
    step_heads = step_size.reshape(micro, rows, heads).transpose(0, 2, 1)
    lower = (places[None, :] <= places[:, None]).astype(f32)
    running = jnp.einsum(
        "mhj,ij->mhi", step_heads * rate[None, :, None], lower, precision=lax.Precision.HIGHEST, preferred_element_type=f32
    )
    pairs = heads // 2
    run_row = running.reshape(micro, pairs, 2, rows)
    run_col = run_row.transpose(0, 1, 3, 2)
    step_row = step_heads.reshape(micro, pairs, 2, rows)
    skip_wide = jnp.repeat(skip_gain, SHD)[None, :]
    layout = (state_low, segment.reshape(total, 1), segment.reshape(micro, 1, rows), position, run_row, run_col, step_row)
    ssm_out, squares = state_forward(ssm_in, gate_z, kernel_inner, skip_wide, *layout)
    square_own = jnp.sum(squares, axis=1)
    square_sum = square_own + other_lane(square_own)
    inv_rms = lax.rsqrt(square_sum / inner_width + epsilon)[:, None]
    gated_low = (ssm_out * jax.nn.silu(gate_z) * inv_rms * mixer_gain).astype(bf16)

    cosine, sine = rope_tables(position)
    query_low = rotate(project(normed_low, full("query")).reshape(total, -1, HEAD), cosine, sine).astype(bf16)
    key_low = rotate(project(normed_low, full("key")).reshape(total, -1, HEAD), cosine, sine).astype(bf16)
    value_low = project(normed_low, full("value")).astype(bf16)
    kv_here = key_low.shape[1]
    query_low = query_low.reshape(micro, rows, kv_here, -1, HEAD)
    key_low = key_low.reshape(micro, rows, kv_here, HEAD)
    value_low = value_low.reshape(micro, rows, kv_here, HEAD)
    logits = jnp.einsum("migkd,mjgd->mgkij", query_low, key_low, preferred_element_type=f32) * scale_factor
    logits = jnp.where(allowed[:, None, None], logits, -jnp.inf)
    exp_scores = jnp.exp(logits - jnp.max(logits, axis=-1, keepdims=True))
    probs = exp_scores / jnp.sum(exp_scores, axis=-1, keepdims=True)
    probs_low = probs.astype(bf16)
    attended_low = (
        jnp.einsum("mgkij,mjgd->migkd", probs_low, value_low, preferred_element_type=f32).astype(bf16).reshape(total, -1)
    )
    branch_part = (project_back(gated_low, full("mix")) + project_back(attended_low, full("attn"))).astype(bf16)
    branch = branch_part.astype(f32) + other_lane(branch_part).astype(f32)
    whole_mid = (in32 + branch).astype(bf16)
    mid32 = whole_mid.astype(f32)
    mid_scale = rms_scale(mid32)
    mid_low = (mid32 * mid_scale * gain_middle).astype(bf16)
    red_fgate, red_fup, red_low, red_high = [Reduction(places) for places in ((1, 2), (2, 1), (1, 2), (2, 1))]
    feeds = (red_fgate, red_fup)
    ff_cols = feed_gate.shape[1]
    gate_cols = mamba_gate.shape[1]

    def feed_forward():
        gate_ff = project(mid_low, full("fgate"))
        up_ff = project(mid_low, full("fup"))
        sig_ff = jax.nn.sigmoid(gate_ff)
        hidden_low = (gate_ff * sig_ff * up_ff).astype(bf16)
        grad_hidden = project(whole_grad, full("fdown"))
        gate_ff_low = (grad_hidden * up_ff * (sig_ff * (1.0 + gate_ff * (1.0 - sig_ff)))).astype(bf16)
        up_ff_low = (grad_hidden * (gate_ff * sig_ff)).astype(bf16)
        grad_mid_norm = project_back(gate_ff_low, full("fgate")) + project_back(up_ff_low, full("fup"))
        grad_gain_mid = jnp.sum(grad_mid_norm * mid32 * mid_scale, axis=0)
        mid_part = rms_back(grad_mid_norm, mid32, mid_scale, gain_middle).astype(bf16)
        return grad_gain_mid, mid_part, hidden_low, jnp.concatenate([gate_ff_low, up_ff_low], axis=1)

    grad_gain_mid, mid_part, hidden_low, feed_low = unit(feed_forward)
    mid_other = hand_over(other_lane(mid_part), 3000)

    def feed_output():
        ffn_part = project_back(hidden_low, full("fdown")).astype(bf16)
        mid_left = split_left(mid_low)
        return (
            lane_rows(ffn_part, lane), lane_rows(ffn_part, 1 - lane), mid_left[0], core_send(mid_left, feed_low),
            outer_sum(whole_grad, hidden_low).astype(bf16),
        )

    ffn_own, ffn_send, mid_keep, send_feed, part_fdown = unit(feed_output)
    sum_fdown = lax.psum_scatter(part_fdown, "dp", scatter_dimension=0, tiled=True)
    feed_came = other_group(send_feed, 1)

    def keep_first(keep, right, came, reductions, sizes):
        kept = (outer_sum(keep, right) + came.astype(f32)).astype(bf16)
        kept = kept.reshape((2,) * len(inner_places) + (shard, -1))
        moves, start = [], 0
        for red, size in zip(reductions, sizes):
            moves.append(halve(kept[..., start : start + size], red.places[0]))
            start += size
        return moves

    def settle(reductions, steps):
        for red, step in zip(reductions, steps):
            if red.stage < len(red.places):
                red.move(*step)
            else:
                red.result = step

    def branch_backward():
        grad_middle = whole_grad.astype(f32) + (mid_part.astype(f32) + mid_other.astype(f32))
        whole_branch = grad_middle.astype(bf16)
        grad_gated_norm = project(whole_branch, full("mix"))
        cross_own = jnp.sum(grad_gated_norm * mixer_gain * (ssm_out * jax.nn.silu(gate_z)), axis=1)
        grad_attended = project(whole_branch, full("attn")).astype(bf16).reshape(micro, rows, kv_here, -1, HEAD)
        grad_probs = jnp.einsum("migkd,mjgd->mgkij", grad_attended, value_low, preferred_element_type=f32)
        grad_value = jnp.einsum("mgkij,migkd->mjgd", probs_low, grad_attended, preferred_element_type=f32)
        weighted_sum = jnp.sum(probs * grad_probs, axis=-1, keepdims=True)
        grad_logits = (probs * (grad_probs - weighted_sum)).astype(bf16)
        grad_query_rot = jnp.einsum("mgkij,mjgd->migkd", grad_logits, key_low, preferred_element_type=f32) * scale_factor
        grad_key_rot = jnp.einsum("mgkij,migkd->mjgd", grad_logits, query_low, preferred_element_type=f32) * scale_factor
        query_grad_low = rotate_back(grad_query_rot.reshape(total, -1, HEAD), cosine, sine).astype(bf16).reshape(total, -1)
        key_grad_low = rotate_back(grad_key_rot.reshape(total, -1, HEAD), cosine, sine).astype(bf16).reshape(total, -1)
        value_grad_low = grad_value.astype(bf16).reshape(total, -1)
        return (
            cross_own, lane_rows(grad_middle, lane), grad_gated_norm, whole_branch,
            (query_grad_low, key_grad_low, value_grad_low),
        )

    cross_own, grad_middle_own, grad_gated_norm, whole_branch, qkv_low = unit(branch_backward)
    cross_other = other_lane(cross_own)

    def second_moves():
        moves = keep_first(mid_keep, feed_low, feed_came, feeds, (ff_cols, ff_cols))
        branch_right = jnp.concatenate([gated_low, attended_low], axis=1)
        return moves, outer_sum(whole_branch, branch_right).astype(bf16)

    moves, part_branch = unit(second_moves)
    for red, move in zip(feeds, moves):
        red.move(*move)
    sum_branch = lax.psum_scatter(part_branch, "dp", scatter_dimension=0, tiled=True)

    def state_space_backward():
        cross = (inv_rms**3) * ((cross_own + cross_other)[:, None] / inner_width)
        step_sig = jax.nn.sigmoid(raw_step + step_bias).reshape(micro, rows, heads).transpose(0, 2, 1)
        gate_low, input_low, column_sums, rest_low, state_sums, head_sums = state_backward(
            grad_gated_norm, ssm_out, gate_z, ssm_in, kernel_inner, skip_wide, mixer_gain[None, :], inv_rms, cross, *layout,
            state_raw, kernel_state, step_heads, step_sig, rate[:, None],
        )
        return column_sums, state_sums, head_sums, jnp.concatenate([gate_low, input_low, rest_low, *qkv_low], axis=1)

    column_sums, state_sums, head_sums, first_right = unit(state_space_backward)

    def third_moves():
        return (
            core_send(normed_left, first_right),
            lax.optimization_barrier(ffn_send),
            [red.step() for red in feeds],
            sum_fdown.astype(f32),
        )

    send_first, ffn_send, steps, total_fdown = unit(third_moves)
    settle(feeds, steps)
    first_came = other_group(send_first, 1)
    ffn_other = other_lane(ffn_send)

    def input_gradient():
        grad_normed = project_back(first_right, lax.slice_in_dim(whole["early"], 0, first_right.shape[1], axis=1))
        grad_gain_in = jnp.sum(grad_normed * in32 * in_scale, axis=0)
        in_part = rms_back(grad_normed, in32, in_scale, gain_input).astype(bf16)
        return grad_gain_in, lane_rows(in_part, lane), lane_rows(in_part, 1 - lane)

    grad_gain_in, in_own, in_send = unit(input_gradient)

    small_sizes = (width, width, (CONV + 1) * 2 * NS, (CONV + 1) * inner_width // lanes, inner_width // lanes, heads, heads, heads)
    used = sum(small_sizes)
    padded = -(-used // 1024) * 1024
    firsts = (red_low, red_high)
    first_sizes = (first_right.shape[1] // 256 * 128, first_right.shape[1] - first_right.shape[1] // 256 * 128)

    def first_moves():
        moves = keep_first(normed_left[0], first_right, first_came, firsts, first_sizes)
        ffn_out = ffn_own.astype(f32) + ffn_other.astype(f32)
        out_rows = (lane_rows(whole_mid, lane).astype(f32) + ffn_out).astype(bf16)
        return moves, lax.optimization_barrier(in_send), deal_order_rows(out_rows), [red.step() for red in feeds]

    moves, in_send, out_sent, steps = unit(first_moves)
    settle(feeds, steps)
    out_moved = exchange(out_sent)
    for red, move in zip(firsts, moves):
        red.move(*move)
    in_other = other_lane(in_send)

    def small_flat():
        columns = jnp.sum(column_sums, axis=0)
        head_totals = jnp.sum(head_sums, axis=0)
        parts = (
            grad_gain_in, grad_gain_mid, jnp.sum(state_sums, axis=0)[: CONV + 1].reshape(-1), columns[: CONV + 1].reshape(-1),
            columns[CONV + 1], head_totals[:, 1], head_totals[:, 0] * rate,
            jnp.sum(columns[CONV + 2].reshape(heads, SHD), axis=1),
        )
        return jnp.pad(jnp.concatenate(parts), (0, padded - used)).reshape(padded // 128, 128)

    flat = unit(small_flat)
    flat_moved = other_group(flat, masks[0])

    def send_input():
        in_sum = in_own.astype(f32) + in_other.astype(f32)
        return deal_order_rows((in_sum + grad_middle_own).astype(bf16)), sum_branch.astype(f32)

    everything = [*feeds, *firsts]
    in_moved = None
    bits = 1
    while pending := [red for red in everything if not hasattr(red, "result")]:
        last = all(red.stage == len(red.places) for red in pending)
        steps, flat, other = unit(
            lambda: (
                [red.step() for red in pending],
                flat + flat_moved if bits <= len(masks) else flat,
                (deal_take(in_moved), deal_take(out_moved)) if last else send_input() if in_moved is None else (),
            )
        )
        settle(pending, steps)
        if bits < len(masks):
            flat_moved = other_group(flat, masks[bits])
        bits += 1
        if in_moved is None:
            in_moved = exchange(other[0])
            total_branch = other[1]
    grad_input, block_out = other
    while bits <= len(masks):
        flat = flat + flat_moved
        if bits < len(masks):
            flat_moved = other_group(flat, masks[bits])
        bits += 1
    theirs = other_lane(flat).reshape(-1)
    flat = flat.reshape(-1)
    pieces, start = [], 0
    for place, size in enumerate(small_sizes):
        mine, other = flat[start : start + size], theirs[start : start + size]
        pieces.append(mine + other if place < 3 else (jnp.where(lane == 0, mine, other), jnp.where(lane == 0, other, mine)))
        start += size
    sum_gin, sum_gmid, sum_kst = pieces[0], pieces[1], pieces[2].reshape(CONV + 1, -1)
    sum_kin = jnp.concatenate([half.reshape(CONV + 1, -1) for half in pieces[3]], axis=1)
    sum_mix, sum_bias, sum_rate, sum_skip = [jnp.concatenate(pair) for pair in pieces[4:]]

    query_cols, key_cols = query_weight.shape[1], key_weight.shape[1]
    total_fgate, total_fup = red_fgate.result, red_fup.result
    total_mix, total_attn = total_branch[:, :gate_cols], total_branch[:, gate_cols:]
    rest = jnp.concatenate([red.result for red in firsts], axis=1)
    total_gate, total_input, rest = rest[:, :gate_cols], rest[:, gate_cols : 2 * gate_cols], rest[:, 2 * gate_cols :]
    total_step = rest[:, 2 * NS : 2 * NS + heads]
    start = 2 * NS + STEP_PAD
    total_query = rest[:, start : start + query_cols]
    total_key = rest[:, start + query_cols : start + query_cols + key_cols]
    total_value = rest[:, start + query_cols + key_cols :]
    state_rows = rest[:, : 2 * NS].reshape(lanes, shard // lanes, 2 * NS)
    state_own = lax.dynamic_index_in_dim(state_rows, lane, 0, keepdims=False)
    state_send = lax.dynamic_index_in_dim(state_rows, 1 - lane, 0, keepdims=False)
    state_lane = state_own + other_lane(state_send)
    return (
        block_out,
        grad_input,
        total_query,
        total_key,
        total_value,
        total_attn,
        total_gate,
        total_input,
        total_step,
        state_lane,
        total_mix,
        total_fgate,
        total_fup,
        total_fdown,
        sum_gin,
        sum_gmid,
        sum_kin,
        sum_kst,
        sum_mix,
        sum_bias,
        sum_rate,
        sum_skip,
    )


def solution(mesh):
    both = P("dp", "tensor")
    in_specs = (
        P(None, ("dp", "tensor"), None),
        P(None, ("dp", "tensor"), None),
        P(),
        P(None, "dp"),
        both,
        both,
        both,
        both,
        both,
        both,
        both,
        P("dp", None),
        both,
        both,
        both,
        both,
        P(),
        P(),
        P(None, "tensor"),
        P(),
        P("tensor"),
        P("tensor"),
        P("tensor"),
        P("tensor"),
    )
    out_specs = (
        P(None, ("dp", "tensor"), None),
        P(None, ("dp", "tensor"), None),
        both,
        both,
        both,
        both,
        both,
        both,
        both,
        P(("dp", "tensor"), None),
        both,
        both,
        both,
        both,
        P(),
        P(),
        P(),
        P(),
        P(),
        P(),
        P(),
        P(),
    )
    return jax.shard_map(local, mesh=mesh, in_specs=in_specs, out_specs=out_specs, check_vma=False)
```

```python
import math

import jax
import jax.numpy as jnp
from jax import lax
from jax.experimental import pallas as pl
from jax.experimental.pallas import tpu as pltpu
from jax.sharding import PartitionSpec as P

HEAD = 128
SH = 48
SHD = 64
NS = 256
CONV = 4
STEP_PAD = 128

epsilon = 1e-05
rope_base = 100000000000.0
f32 = jnp.float32
bf16 = jnp.bfloat16


def project(left, right):
    return jnp.dot(left, right, preferred_element_type=f32)


def project_back(left, right):
    return lax.dot_general(left, right, (((1,), (1,)), ((), ())), preferred_element_type=f32)


def outer_sum(left, right):
    return lax.dot_general(left, right, (((0,), (0,)), ((), ())), preferred_element_type=f32)


def rms_scale(values):
    return lax.rsqrt(jnp.mean(values * values, axis=-1, keepdims=True) + epsilon)


def rms_back(grad, values, scale, gain):
    weighted = grad * gain
    inner = jnp.sum(weighted * values, axis=-1, keepdims=True)
    return scale * weighted - values * (scale * scale * scale * inner / values.shape[-1])


def shift_down(values, count):
    return jnp.concatenate([jnp.zeros((count, values.shape[1]), values.dtype), values[:-count]], axis=0)


def shift_up(values, count):
    return jnp.concatenate([values[count:], jnp.zeros((count, values.shape[1]), values.dtype)], axis=0)


def conv_sum(signal, kernel, position):
    summed = kernel[CONV][None, :] + signal * kernel[0][None, :]
    for tap in range(1, CONV):
        moved = jnp.where(position >= tap, shift_down(signal, tap), 0.0)
        summed = summed + moved * kernel[tap][None, :]
    return summed


def silu_back(values):
    sig = jax.nn.sigmoid(values)
    return sig * (1.0 + values * (1.0 - sig))


def conv_back(grad, signal, kernel, position):
    grad_sum = grad * silu_back(conv_sum(signal, kernel, position))
    grad_signal = grad_sum * kernel[0][None, :]
    grad_taps = [jnp.sum(grad_sum * signal, axis=0)]
    for tap in range(1, CONV):
        kept = jnp.where(position >= tap, grad_sum, 0.0)
        grad_signal = grad_signal + shift_up(kept, tap) * kernel[tap][None, :]
        grad_taps.append(jnp.sum(kept * shift_down(signal, tap), axis=0))
    grad_taps.append(jnp.sum(grad_sum, axis=0))
    return grad_signal, jnp.stack(grad_taps)


def rope_tables(position):
    half_size = HEAD // 2
    frequency = jnp.exp(jnp.arange(half_size, dtype=f32) * (-2.0 * math.log(rope_base) / HEAD))
    angles = position.astype(f32) * frequency[None, :]
    return jnp.cos(angles)[:, None, :], jnp.sin(angles)[:, None, :]


def rotate(values, cosine, sine):
    half_size = HEAD // 2
    first, second = values[..., :half_size], values[..., half_size:]
    return jnp.concatenate([first * cosine - second * sine, second * cosine + first * sine], axis=-1)


def copy_blocks(order_ref, first_ref, second_ref, first_out_ref, second_out_ref):
    first_out_ref[...] = first_ref[...]
    second_out_ref[...] = second_ref[...]


def pick_halves(values, order, block):
    height, width = values.shape
    count = width // block // 2
    if block % 128:
        mixed = jnp.take(values.reshape(height, -1, block), order, axis=1).reshape(height, width)
        return mixed[:, : width // 2], mixed[:, width // 2 :]
    half = jax.ShapeDtypeStruct((height, width // 2), values.dtype)
    out_spec = pl.BlockSpec((height, block), lambda i, order: (0, i))
    return pl.pallas_call(
        copy_blocks,
        out_shape=(half, half),
        grid_spec=pltpu.PrefetchScalarGridSpec(
            num_scalar_prefetch=1,
            grid=(count,),
            in_specs=[
                pl.BlockSpec((height, block), lambda i, order: (0, order[i])),
                pl.BlockSpec((height, block), lambda i, order: (0, order[i + count])),
            ],
            out_specs=(out_spec, out_spec),
        ),
        cost_estimate=pl.CostEstimate(flops=0, transcendentals=0, bytes_accessed=4 * height * width),
        name="pick_halves",
    )(order, values, values)


def hand_over(values, microseconds):
    def idle(values_ref, out_ref):
        pass

    return pl.pallas_call(
        idle,
        out_shape=jax.ShapeDtypeStruct(values.shape, values.dtype),
        in_specs=[pl.BlockSpec(memory_space=pl.ANY)],
        out_specs=pl.BlockSpec(memory_space=pl.ANY),
        input_output_aliases={0: 0},
        cost_estimate=pl.CostEstimate(flops=microseconds * 1150000000, transcendentals=0, bytes_accessed=0),
        name="hand_over",
    )(values)


def rotate_back(values, cosine, sine):
    return rotate(values, cosine, -sine)


NEGATIVE = -1e30


def sigmoid_of(values):
    return 1.0 / (1.0 + jnp.exp(-values))


def block_mask(rows, segment_col, segment_row):
    row_index = lax.broadcasted_iota(jnp.int32, (rows, rows), 0)
    col_index = lax.broadcasted_iota(jnp.int32, (rows, rows), 1)
    return jnp.where((segment_col == segment_row) & (col_index <= row_index), 0.0, NEGATIVE)


def conv_block(signal, taps_ref, position):
    summed = taps_ref[CONV : CONV + 1, :] + signal * taps_ref[0:1, :]
    moved = []
    for tap in range(1, CONV):
        shifted = jnp.where(position >= tap, pltpu.roll(signal, tap, 0), 0.0)
        moved.append(shifted)
        summed = summed + shifted * taps_ref[tap : tap + 1, :]
    return summed, moved


def conv_block_back(grad_sum, signal, moved, taps_ref, position, sums_ref):
    rows = signal.shape[0]
    grad_signal = grad_sum * taps_ref[0:1, :]
    sums_ref[0, 0:1, :] = jnp.sum(grad_sum * signal, axis=0, keepdims=True)
    for tap in range(1, CONV):
        kept = jnp.where(position >= tap, grad_sum, 0.0)
        grad_signal = grad_signal + pltpu.roll(kept, rows - tap, 0) * taps_ref[tap : tap + 1, :]
        sums_ref[0, tap : tap + 1, :] = jnp.sum(grad_sum * moved[tap - 1], axis=0, keepdims=True)
    sums_ref[0, CONV : CONV + 1, :] = jnp.sum(grad_sum, axis=0, keepdims=True)
    return grad_signal


def mixing_block(inner, mask, run_col, run_row, step_row):
    decay = jnp.exp(run_col - run_row + mask)
    return decay, (inner * decay * step_row).astype(bf16)


def state_forward_kernel(
    signal_ref, gate_ref, taps_ref, skip_ref, state_ref, seg_row_ref, run_row_ref, run_col_ref, step_ref, columns_ref,
    out_ref, square_ref, inner_ref, mask_ref,
):
    rows = signal_ref.shape[0]
    position = columns_ref[:, 1:2]

    @pl.when(pl.program_id(1) == 0)
    def _():
        inner_ref[...] = lax.dot_general(
            state_ref[:, NS:], state_ref[:, :NS], (((1,), (1,)), ((), ())), preferred_element_type=f32
        )
        mask_ref[...] = block_mask(rows, columns_ref[:, 0:1], seg_row_ref[0])
        square_ref[...] = jnp.zeros_like(square_ref)

    summed, _ = conv_block(signal_ref[...], taps_ref, position)
    cols = summed * sigmoid_of(summed)
    cols_low = cols.astype(bf16)
    mixed = []
    for head in range(2):
        _, mixing = mixing_block(
            inner_ref[...], mask_ref[...], run_col_ref[0, 0, :, head : head + 1],
            run_row_ref[0, 0, head : head + 1, :], step_ref[0, 0, head : head + 1, :],
        )
        mixed.append(jnp.dot(mixing, cols_low, preferred_element_type=f32))
    lanes = lax.broadcasted_iota(jnp.int32, cols.shape, 1)
    out = jnp.where(lanes < SHD, mixed[0], mixed[1]) + skip_ref[...] * cols
    out_ref[...] = out
    gate = gate_ref[...]
    gated = out * (gate * sigmoid_of(gate))
    square_ref[...] += gated * gated


def state_backward_kernel(
    grad_ref, out_ref, gate_ref, signal_ref, taps_ref, skip_ref, gain_ref, state_ref, seg_row_ref, run_row_ref, run_col_ref,
    step_ref, columns_ref, state_raw_ref, state_taps_ref, step_all_ref, step_sig_ref, rate_ref, others_ref,
    first_ref, sums_ref, state_sums_ref, head_sums_ref,
    inner_ref, mask_ref, grad_inner_ref, direct_ref, along_ref,
):
    rows = signal_ref.shape[0]
    pair = pl.program_id(1)

    @pl.when(pair == 0)
    def _():
        along_ref[...] = jnp.zeros_like(along_ref)
        inner_ref[...] = lax.dot_general(
            state_ref[:, NS:], state_ref[:, :NS], (((1,), (1,)), ((), ())), preferred_element_type=f32
        )
        mask_ref[...] = block_mask(rows, columns_ref[:, 0:1], seg_row_ref[0])
        grad_inner_ref[...] = jnp.zeros_like(grad_inner_ref)

    grad, out, gate, signal = grad_ref[...], out_ref[...], gate_ref[...], signal_ref[...]
    position, scale, cross = columns_ref[:, 1:2], columns_ref[:, 2:3], columns_ref[:, 3:4]
    gate_cols = pl.num_programs(1) * 2 * SHD
    here = pl.multiple_of(pair * 2 * SHD, 2 * SHD)
    rest = first_ref.shape[1] - others_ref.shape[1] - 2 * NS - STEP_PAD
    sig = sigmoid_of(gate)
    silu = gate * sig
    gated = out * silu
    scaled = grad * scale
    grad_gated = scaled * gain_ref[...] - gated * cross
    grad_out = grad_gated * silu
    first_ref[:, pl.ds(here, 2 * SHD)] = (grad_gated * out * (sig * (1.0 + gate * (1.0 - sig)))).astype(bf16)
    summed, moved = conv_block(signal, taps_ref, position)
    sig = sigmoid_of(summed)
    cols = summed * sig
    cols_low = cols.astype(bf16)
    grad_low = grad_out.astype(bf16)
    lanes = lax.broadcasted_iota(jnp.int32, cols.shape, 1)
    zero = jnp.zeros_like(grad_low)
    grad_cols = []
    for head in range(2):
        step_row = step_ref[0, 0, head : head + 1, :]
        inner = inner_ref[...]
        decay, mixing = mixing_block(
            inner, mask_ref[...], run_col_ref[0, 0, :, head : head + 1], run_row_ref[0, 0, head : head + 1, :], step_row
        )
        grad_cols.append(
            lax.dot_general(mixing, grad_low, (((0,), (0,)), ((), ())), preferred_element_type=f32)
        )
        grad_head = jnp.where((lanes < SHD) == (head == 0), grad_low, zero)
        grad_decay = lax.dot_general(
            grad_head, cols_low, (((1,), (1,)), ((), ())), preferred_element_type=f32
        ) * decay
        stepped = grad_decay * step_row
        grad_inner_ref[...] += stepped
        direct_ref[pl.ds(2 * pair + head, 1), :] = jnp.sum(grad_decay * inner, axis=0, keepdims=True)
        along = jnp.sum(stepped * inner, axis=1, keepdims=True)
        along_ref[...] = jnp.where(lanes == 2 * pair + head, along, along_ref[...])
    grad_cols = jnp.where(lanes < SHD, grad_cols[0], grad_cols[1]) + skip_ref[...] * grad_out
    grad_sum = grad_cols * (sig * (1.0 + summed * (1.0 - sig)))
    grad_signal = conv_block_back(grad_sum, signal, moved, taps_ref, position, sums_ref)
    sums_ref[0, CONV + 1 : CONV + 2, :] = jnp.sum(scaled * gated, axis=0, keepdims=True)
    sums_ref[0, CONV + 2 : CONV + 3, :] = jnp.sum(grad_out * cols, axis=0, keepdims=True)
    sums_ref[0, CONV + 3 : CONV + 4, :] = jnp.zeros((1, cols.shape[1]), f32)
    first_ref[:, pl.ds(pl.multiple_of(gate_cols + here, 2 * SHD), 2 * SHD)] = grad_signal.astype(bf16)

    @pl.when(pair == pl.num_programs(1) - 1)
    def _():
        inner_low = grad_inner_ref[...].astype(bf16)
        for part, (mine, other) in enumerate((((0, NS), (NS, 2 * NS)), ((NS, 2 * NS), (0, NS)))):
            raw = state_raw_ref[:, mine[0] : mine[1]]
            taps = state_taps_ref.at[:, mine[0] : mine[1]]
            summed, moved = conv_block(raw, taps, position)
            sig = sigmoid_of(summed)
            grad = lax.dot_general(
                inner_low, state_ref[:, other[0] : other[1]], (((part,), (0,)), ((), ())), preferred_element_type=f32
            )
            grad_sum = grad * (sig * (1.0 + summed * (1.0 - sig)))
            back = conv_block_back(grad_sum, raw, moved, taps, position, state_sums_ref.at[:, :, mine[0] : mine[1]])
            first_ref[:, rest + mine[0] : rest + mine[1]] = back.astype(bf16)
        state_sums_ref[0, CONV + 1 :, :] = jnp.zeros((7 - CONV, 2 * NS), f32)
        heads = step_all_ref.shape[1]
        direct, step = direct_ref[...], step_all_ref[0]
        grad_running = along_ref[...].T[:heads] - step * direct
        row_index = lax.broadcasted_iota(jnp.int32, (rows, rows), 0)
        col_index = lax.broadcasted_iota(jnp.int32, (rows, rows), 1)
        lower = jnp.where(col_index <= row_index, 1.0, 0.0)
        grad_product = jnp.dot(
            grad_running, lower, precision=lax.Precision.HIGHEST, preferred_element_type=f32
        )
        grad_raw = (direct + grad_product * rate_ref[...]) * step_sig_ref[0]
        head_sums_ref[0, :, 0:1] = jnp.sum(grad_product * step, axis=1, keepdims=True)
        head_sums_ref[0, :, 1:2] = jnp.sum(grad_raw, axis=1, keepdims=True)
        wide = jnp.concatenate([grad_raw, jnp.zeros((STEP_PAD - heads, rows), f32)], axis=0)
        first_ref[:, rest + 2 * NS : rest + 2 * NS + STEP_PAD] = wide.T.astype(bf16)
        first_ref[:, rest + 2 * NS + STEP_PAD :] = others_ref[...]


def state_specs(rows, pairs):
    block = pl.BlockSpec((rows, 2 * SHD), lambda m, p: (m, p))
    return {
        "block": block,
        "taps": pl.BlockSpec((CONV + 1, 2 * SHD), lambda m, p: (0, p)),
        "vector": pl.BlockSpec((1, 2 * SHD), lambda m, p: (0, p)),
        "state": pl.BlockSpec((rows, 2 * NS), lambda m, p: (m, 0)),
        "columns": pl.BlockSpec((rows, 8), lambda m, p: (m, 0)),
        "row": pl.BlockSpec((1, 1, rows), lambda m, p: (m, 0, 0)),
        "head_row": pl.BlockSpec((1, 1, 2, rows), lambda m, p: (m, p, 0, 0)),
        "head_col": pl.BlockSpec((1, 1, rows, 2), lambda m, p: (m, p, 0, 0)),
    }


def state_forward(signal, gate, taps, skip, state, seg_row, run_row, run_col, step, columns):
    micro, pairs, _, rows = run_row.shape
    spec = state_specs(rows, pairs)
    total, width = signal.shape
    return pl.pallas_call(
        state_forward_kernel,
        out_shape=(jax.ShapeDtypeStruct((total, width), f32), jax.ShapeDtypeStruct((total, 2 * SHD), f32)),
        grid=(micro, pairs),
        in_specs=[spec[name] for name in (
            "block", "block", "taps", "vector", "state", "row", "head_row", "head_col", "head_row", "columns")],
        out_specs=(spec["block"], pl.BlockSpec((rows, 2 * SHD), lambda m, p: (m, 0))),
        scratch_shapes=[pltpu.VMEM((rows, rows), f32), pltpu.VMEM((rows, rows), f32)],
        cost_estimate=pl.CostEstimate(
            flops=8 * total * rows * width // SHD * SHD, transcendentals=total * rows * width // SHD, bytes_accessed=12 * total * width
        ),
        name="state_forward",
    )(signal, gate, taps, skip, state, seg_row, run_row, run_col, step, columns)


def state_backward(
    grad, out, gate, signal, taps, skip, gain, state, seg_row, run_row, run_col, step, columns,
    state_raw, state_taps, step_all, step_sig, rate, others,
):
    micro, pairs, _, rows = run_row.shape
    heads = 2 * pairs
    spec = state_specs(rows, pairs)
    total, width = signal.shape
    joint = 2 * width + 2 * NS + STEP_PAD + others.shape[1]
    heads_block = pl.BlockSpec((1, heads, rows), lambda m, p: (m, 0, 0))
    return pl.pallas_call(
        state_backward_kernel,
        out_shape=(
            jax.ShapeDtypeStruct((total, joint), bf16),
            jax.ShapeDtypeStruct((micro, 8, width), f32),
            jax.ShapeDtypeStruct((micro, 8, 2 * NS), f32),
            jax.ShapeDtypeStruct((micro, heads, 2), f32),
        ),
        grid=(micro, pairs),
        in_specs=[spec[name] for name in (
            "block", "block", "block", "block", "taps", "vector", "vector", "state",
            "row", "head_row", "head_col", "head_row", "columns", "state")]
        + [
            pl.BlockSpec((CONV + 1, 2 * NS), lambda m, p: (0, 0)), heads_block, heads_block,
            pl.BlockSpec((heads, 1), lambda m, p: (0, 0)), pl.BlockSpec((rows, others.shape[1]), lambda m, p: (m, 0)),
        ],
        out_specs=(
            pl.BlockSpec((rows, joint), lambda m, p: (m, 0)), pl.BlockSpec((1, 8, 2 * SHD), lambda m, p: (m, 0, p)),
            pl.BlockSpec((1, 8, 2 * NS), lambda m, p: (m, 0, 0)),
            pl.BlockSpec((1, heads, 2), lambda m, p: (m, 0, 0)),
        ),
        scratch_shapes=[pltpu.VMEM((rows, rows), f32)] * 3 + [pltpu.VMEM((heads, rows), f32), pltpu.VMEM((rows, 2 * SHD), f32)],
        cost_estimate=pl.CostEstimate(
            flops=20 * total * rows * width, transcendentals=total * rows * width // SHD, bytes_accessed=20 * total * width
        ),
        name="state_backward",
    )(
        grad, out, gate, signal, taps, skip, gain, state, seg_row, run_row, run_col, step, columns,
        state_raw, state_taps, step_all, step_sig, rate, others,
    )


def local(
    inputs,
    out_grad,
    deal_order,
    segment,
    query_weight,
    key_weight,
    value_weight,
    attention_out,
    mamba_gate,
    mamba_input,
    step_weight,
    state_weight,
    mamba_out,
    feed_gate,
    feed_up,
    feed_down,
    gain_input,
    gain_middle,
    kernel_inner,
    kernel_state,
    mixer_gain,
    step_bias,
    log_rate,
    skip_gain,
):
    micro, own, width = inputs.shape
    groups = lax.axis_size("dp")
    lanes = lax.axis_size("tensor")
    lane = lax.axis_index("tensor")
    group = lax.axis_index("dp")
    device = group * lanes + lane
    per = own // groups
    rows = own * lanes
    total = micro * rows
    inner_width = SH * SHD
    scale_factor = HEAD ** (-0.5)
    outer_count = groups // 4
    shard = width // groups

    swap_lane = [(0, 1), (1, 0)]

    def other_lane(values):
        return lax.ppermute(values, "tensor", swap_lane)

    def other_group(values, bits):
        return lax.ppermute(values, "dp", [(i, i ^ bits) for i in range(groups)])

    step_padded = jnp.pad(step_weight, ((0, 0), (0, STEP_PAD - step_weight.shape[1])))
    early = dict(
        gate=mamba_gate, input=mamba_input, state=state_weight, step=step_padded, query=query_weight, key=key_weight,
        value=value_weight, mix=mamba_out, attn=attention_out,
    )
    late = dict(fgate=feed_gate, fup=feed_up, fdown=feed_down)
    whole, places_of = {}, {}
    for label, group_weights in (("early", early), ("late", late)):
        start = 0
        for name, weight in group_weights.items():
            places_of[name] = (label, start, weight.shape[1])
            start += weight.shape[1]
        whole[label] = lax.all_gather(jnp.concatenate(list(group_weights.values()), axis=1), "dp", axis=0, tiled=True)

    def full(name):
        label, start, size = places_of[name]
        return lax.slice_in_dim(whole[label], start, start + size, axis=1)

    own_places = jnp.arange(own, dtype=jnp.int32)
    own_order = lax.dynamic_slice_in_dim(deal_order, device * own, own, 1)
    micro_index = jnp.arange(micro, dtype=jnp.int32)[:, None]

    def buffer_place(destination, rank):
        return destination * (micro * per) + micro_index * per + rank

    send_rank = jnp.sum((own_order[:, None, :] < own_order[:, :, None]).astype(jnp.int32), axis=2)
    send_place = buffer_place(send_rank // per, send_rank % per).reshape(-1)
    lane_order = lax.dynamic_index_in_dim(deal_order.reshape(micro, groups, lanes, own), lane, 2, keepdims=False)
    slots = device * own + own_places
    found = lane_order[:, None, :, :] == slots[None, :, None, None]
    source = jnp.sum(
        jnp.where(found, jnp.arange(groups, dtype=jnp.int32)[None, None, :, None], 0), axis=(2, 3)
    )
    recv_rank = jnp.sum(
        ((source[:, None, :] == source[:, :, None]) & (own_places[None, None, :] < own_places[None, :, None])).astype(jnp.int32),
        axis=2,
    )
    recv_place = buffer_place(source, recv_rank).reshape(-1)
    buffer_places = jnp.arange(micro * own, dtype=jnp.int32)
    send_pick = (buffer_places[:, None] == send_place[None, :]).astype(bf16)
    recv_pick = (recv_place[:, None] == buffer_places[None, :]).astype(bf16)

    def exchange(buffer):
        return lax.all_to_all(
            buffer.reshape(groups, micro * per, width), "dp", split_axis=0, concat_axis=0, tiled=True
        ).reshape(micro * own, width)

    def deal(values):
        sent = project(send_pick, values.reshape(micro * own, width)).astype(bf16)
        return project(recv_pick, exchange(sent)).astype(bf16)

    def deal_order_rows(values):
        return outer_sum(recv_pick, values).astype(bf16)

    def deal_take(moved):
        return outer_sum(send_pick, moved).astype(bf16).reshape(micro, own, width)

    def join_lanes(values):
        mine = values.reshape(micro, 1, own, -1)
        theirs = other_lane(values).reshape(micro, 1, own, -1)
        low = jnp.where(lane == 0, mine, theirs)
        high = jnp.where(lane == 0, theirs, mine)
        return jnp.concatenate([low, high], axis=1).reshape(total, -1)

    def lane_rows(values, which):
        return lax.dynamic_index_in_dim(
            values.reshape(micro, lanes, own, -1), which, 1, keepdims=False
        ).reshape(micro * own, -1)

    own_in = deal(inputs)
    own_grad = deal(out_grad)
    whole_in = join_lanes(own_in)
    whole_grad = join_lanes(own_grad)

    before = jnp.sum((segment[:, None, :] < segment[:, :, None]).astype(jnp.int32), axis=2)
    places = jnp.arange(rows, dtype=jnp.int32)
    allowed = (segment[:, :, None] == segment[:, None, :]) & (places[None, None, :] <= places[None, :, None])
    position = (places[None, :] - before).reshape(total, 1)

    masks = [1 << place for place in range(groups.bit_length() - 1)]
    relative = []
    for block in range(groups):
        flip = 0
        for place, mask in enumerate(masks):
            if block >> (len(masks) - 1 - place) & 1:
                flip ^= mask
        relative.append(flip)
    block_order = jnp.bitwise_xor(group.astype(jnp.int32), jnp.array(relative, jnp.int32))

    def split_left(left):
        return pick_halves(left, block_order, shard)

    inner_places = list(range(1, len(masks)))

    def core_send(left_parts, right):
        return outer_sum(left_parts[1], right).astype(bf16)

    def halve(kept, place):
        return (
            lax.slice_in_dim(kept, 1, 2, axis=place - 1).reshape(-1, kept.shape[-1]),
            lax.slice_in_dim(kept, 0, 1, axis=place - 1),
        )

    class Reduction:
        def __init__(self, first):
            self.places = [place for place in first if place in inner_places]
            self.places += [place for place in inner_places if place not in first]
            self.stage = 0

        def move(self, send, kept):
            self.came = other_group(send, masks[self.places[self.stage]])
            self.kept = kept
            self.stage += 1

        def first(self, left_parts, right, from_core):
            kept = (outer_sum(left_parts[0], right) + from_core.astype(f32)).astype(bf16)
            kept = kept.reshape((2,) * len(inner_places) + (shard, -1))
            return halve(kept, self.places[0])

        def added(self):
            return self.kept.astype(f32) + self.came.reshape(self.kept.shape).astype(f32)

        def next(self):
            return halve(self.added().astype(bf16), self.places[self.stage])

        def last(self):
            return self.added().reshape(shard, -1)

        def step(self):
            return self.next() if self.stage < len(self.places) else self.last()

    order = [deal_order[0, 0] >= 0]

    def unit(work):
        shapes = jax.eval_shape(work)
        results = lax.cond(
            order[0], work, lambda: jax.tree.map(lambda leaf: jnp.zeros(leaf.shape, leaf.dtype), shapes)
        )
        leaves, form = jax.tree.flatten(results)
        least = min(range(len(leaves)), key=lambda place: leaves[place].size)
        leaves[least], order[0] = lax.optimization_barrier((leaves[least], order[0]))
        return jax.tree.unflatten(form, leaves)

    def after(value, *others):
        return lax.optimization_barrier((value, others))[0]

    in32 = whole_in.astype(f32)
    in_scale = rms_scale(in32)
    normed_low = (in32 * in_scale * gain_input).astype(bf16)
    normed_left = split_left(normed_low)
    whole["early"] = after(whole["early"], whole_grad, normed_left)
    gate_z = project(normed_low, full("gate"))
    ssm_in = project(normed_low, full("input"))
    state_raw = project(normed_low, full("state"))
    heads = step_weight.shape[1]
    raw_step = project(normed_low, full("step"))[:, :heads]
    state_low = jax.nn.silu(conv_sum(state_raw, kernel_state, position)).astype(bf16)
    rate = -jnp.exp(log_rate)
    step_size = jax.nn.softplus(raw_step + step_bias)
    step_heads = step_size.reshape(micro, rows, heads).transpose(0, 2, 1)
    lower = (places[None, :] <= places[:, None]).astype(f32)
    running = jnp.einsum(
        "mhj,ij->mhi", step_heads * rate[None, :, None], lower, precision=lax.Precision.HIGHEST, preferred_element_type=f32
    )
    pairs = heads // 2
    run_row = running.reshape(micro, pairs, 2, rows)
    run_col = run_row.transpose(0, 1, 3, 2)
    step_row = step_heads.reshape(micro, pairs, 2, rows)
    skip_wide = jnp.repeat(skip_gain, SHD)[None, :]
    layout = (state_low, segment.reshape(micro, 1, rows).astype(f32), run_row, run_col, step_row)
    row_facts = jnp.concatenate([segment.reshape(total, 1).astype(f32), position.astype(f32)], axis=1)
    ssm_out, squares = state_forward(ssm_in, gate_z, kernel_inner, skip_wide, *layout, jnp.pad(row_facts, ((0, 0), (0, 6))))
    square_own = jnp.sum(squares, axis=1)
    square_sum = square_own + other_lane(square_own)
    inv_rms = lax.rsqrt(square_sum / inner_width + epsilon)[:, None]
    gated_low = (ssm_out * jax.nn.silu(gate_z) * inv_rms * mixer_gain).astype(bf16)

    cosine, sine = rope_tables(position)
    query_low = rotate(project(normed_low, full("query")).reshape(total, -1, HEAD), cosine, sine).astype(bf16)
    key_low = rotate(project(normed_low, full("key")).reshape(total, -1, HEAD), cosine, sine).astype(bf16)
    value_low = project(normed_low, full("value")).astype(bf16)
    kv_here = key_low.shape[1]
    query_low = query_low.reshape(micro, rows, kv_here, -1, HEAD)
    key_low = key_low.reshape(micro, rows, kv_here, HEAD)
    value_low = value_low.reshape(micro, rows, kv_here, HEAD)
    logits = jnp.einsum("migkd,mjgd->mgkij", query_low, key_low, preferred_element_type=f32) * scale_factor
    logits = jnp.where(allowed[:, None, None], logits, -jnp.inf)
    exp_scores = jnp.exp(logits - jnp.max(logits, axis=-1, keepdims=True))
    probs = exp_scores / jnp.sum(exp_scores, axis=-1, keepdims=True)
    probs_low = probs.astype(bf16)
    attended_low = (
        jnp.einsum("mgkij,mjgd->migkd", probs_low, value_low, preferred_element_type=f32).astype(bf16).reshape(total, -1)
    )
    branch_part = (project_back(gated_low, full("mix")) + project_back(attended_low, full("attn"))).astype(bf16)
    branch = branch_part.astype(f32) + other_lane(branch_part).astype(f32)
    whole_mid = (in32 + branch).astype(bf16)
    mid32 = whole_mid.astype(f32)
    mid_scale = rms_scale(mid32)
    mid_low = (mid32 * mid_scale * gain_middle).astype(bf16)
    red_fgate, red_fup, red_low, red_high = [Reduction(places) for places in ((1, 2), (2, 1), (1, 2), (2, 1))]
    feeds = (red_fgate, red_fup)
    ff_cols = feed_gate.shape[1]
    gate_cols = mamba_gate.shape[1]

    def feed_forward():
        gate_ff = project(mid_low, full("fgate"))
        up_ff = project(mid_low, full("fup"))
        sig_ff = jax.nn.sigmoid(gate_ff)
        hidden_low = (gate_ff * sig_ff * up_ff).astype(bf16)
        grad_hidden = project(whole_grad, full("fdown"))
        gate_ff_low = (grad_hidden * up_ff * (sig_ff * (1.0 + gate_ff * (1.0 - sig_ff)))).astype(bf16)
        up_ff_low = (grad_hidden * (gate_ff * sig_ff)).astype(bf16)
        grad_mid_norm = project_back(gate_ff_low, full("fgate")) + project_back(up_ff_low, full("fup"))
        grad_gain_mid = jnp.sum(grad_mid_norm * mid32 * mid_scale, axis=0)
        mid_part = rms_back(grad_mid_norm, mid32, mid_scale, gain_middle).astype(bf16)
        return grad_gain_mid, mid_part, hidden_low, jnp.concatenate([gate_ff_low, up_ff_low], axis=1)

    grad_gain_mid, mid_part, hidden_low, feed_low = unit(feed_forward)
    mid_other = hand_over(other_lane(mid_part), 3000)

    def feed_output():
        ffn_part = project_back(hidden_low, full("fdown")).astype(bf16)
        mid_left = split_left(mid_low)
        return (
            lane_rows(ffn_part, lane), lane_rows(ffn_part, 1 - lane), mid_left[0], core_send(mid_left, feed_low),
            outer_sum(whole_grad, hidden_low).astype(bf16),
        )

    ffn_own, ffn_send, mid_keep, send_feed, part_fdown = unit(feed_output)
    sum_fdown = lax.psum_scatter(part_fdown, "dp", scatter_dimension=0, tiled=True)
    feed_came = other_group(send_feed, 1)

    def keep_first(keep, right, came, reductions, sizes):
        kept = (outer_sum(keep, right) + came.astype(f32)).astype(bf16)
        kept = kept.reshape((2,) * len(inner_places) + (shard, -1))
        moves, start = [], 0
        for red, size in zip(reductions, sizes):
            moves.append(halve(kept[..., start : start + size], red.places[0]))
            start += size
        return moves

    def settle(reductions, steps):
        for red, step in zip(reductions, steps):
            if red.stage < len(red.places):
                red.move(*step)
            else:
                red.result = step

    def branch_backward():
        grad_middle = whole_grad.astype(f32) + (mid_part.astype(f32) + mid_other.astype(f32))
        whole_branch = grad_middle.astype(bf16)
        grad_gated_norm = project(whole_branch, full("mix"))
        cross_own = jnp.sum(grad_gated_norm * mixer_gain * (ssm_out * jax.nn.silu(gate_z)), axis=1)
        grad_attended = project(whole_branch, full("attn")).astype(bf16).reshape(micro, rows, kv_here, -1, HEAD)
        grad_probs = jnp.einsum("migkd,mjgd->mgkij", grad_attended, value_low, preferred_element_type=f32)
        grad_value = jnp.einsum("mgkij,migkd->mjgd", probs_low, grad_attended, preferred_element_type=f32)
        weighted_sum = jnp.sum(probs * grad_probs, axis=-1, keepdims=True)
        grad_logits = (probs * (grad_probs - weighted_sum)).astype(bf16)
        grad_query_rot = jnp.einsum("mgkij,mjgd->migkd", grad_logits, key_low, preferred_element_type=f32) * scale_factor
        grad_key_rot = jnp.einsum("mgkij,migkd->mjgd", grad_logits, query_low, preferred_element_type=f32) * scale_factor
        query_grad_low = rotate_back(grad_query_rot.reshape(total, -1, HEAD), cosine, sine).astype(bf16).reshape(total, -1)
        key_grad_low = rotate_back(grad_key_rot.reshape(total, -1, HEAD), cosine, sine).astype(bf16).reshape(total, -1)
        value_grad_low = grad_value.astype(bf16).reshape(total, -1)
        return (
            cross_own, lane_rows(grad_middle, lane), grad_gated_norm, whole_branch,
            (query_grad_low, key_grad_low, value_grad_low),
        )

    cross_own, grad_middle_own, grad_gated_norm, whole_branch, qkv_low = unit(branch_backward)
    cross_other = other_lane(cross_own)

    def second_moves():
        moves = keep_first(mid_keep, feed_low, feed_came, feeds, (ff_cols, ff_cols))
        return moves

    moves = unit(second_moves)
    for red, move in zip(feeds, moves):
        red.move(*move)

    def state_space_backward():
        cross = (inv_rms**3) * ((cross_own + cross_other)[:, None] / inner_width)
        step_sig = jax.nn.sigmoid(raw_step + step_bias).reshape(micro, rows, heads).transpose(0, 2, 1)
        columns = jnp.pad(jnp.concatenate([row_facts, inv_rms, cross], axis=1), ((0, 0), (0, 4)))
        first_right, column_sums, state_sums, head_sums = state_backward(
            grad_gated_norm, ssm_out, gate_z, ssm_in, kernel_inner, skip_wide, mixer_gain[None, :], *layout, columns,
            state_raw, kernel_state, step_heads, step_sig, rate[:, None], jnp.concatenate(qkv_low, axis=1),
        )
        return column_sums, state_sums, head_sums, first_right

    column_sums, state_sums, head_sums, first_right = unit(state_space_backward)

    def third_moves():
        return (
            core_send(normed_left, first_right),
            lax.optimization_barrier(ffn_send),
            [red.step() for red in feeds],
            sum_fdown.astype(f32),
            outer_sum(whole_branch, jnp.concatenate([gated_low, attended_low], axis=1)).astype(bf16),
        )

    send_first, ffn_send, steps, total_fdown, part_branch = unit(third_moves)
    sum_branch = lax.psum_scatter(part_branch, "dp", scatter_dimension=0, tiled=True)
    settle(feeds, steps)
    first_came = other_group(send_first, 1)
    ffn_other = other_lane(ffn_send)

    def input_gradient():
        grad_normed = project_back(first_right, lax.slice_in_dim(whole["early"], 0, first_right.shape[1], axis=1))
        grad_gain_in = jnp.sum(grad_normed * in32 * in_scale, axis=0)
        in_part = rms_back(grad_normed, in32, in_scale, gain_input).astype(bf16)
        return grad_gain_in, lane_rows(in_part, lane), lane_rows(in_part, 1 - lane)

    grad_gain_in, in_own, in_send = unit(input_gradient)

    firsts = (red_low, red_high)
    first_sizes = (first_right.shape[1] // 256 * 128, first_right.shape[1] - first_right.shape[1] // 256 * 128)

    def first_moves():
        moves = keep_first(normed_left[0], first_right, first_came, firsts, first_sizes)
        ffn_out = ffn_own.astype(f32) + ffn_other.astype(f32)
        out_rows = (lane_rows(whole_mid, lane).astype(f32) + ffn_out).astype(bf16)
        head_row = (jnp.sum(head_sums, axis=0).T * jnp.stack([rate, jnp.ones_like(rate)])).reshape(1, -1)
        flat = jnp.concatenate(
            [
                jnp.concatenate([jnp.sum(column_sums, axis=0), jnp.sum(state_sums, axis=0)], axis=1),
                grad_gain_in[None, :], grad_gain_mid[None, :], jnp.pad(head_row, ((0, 5), (0, width - head_row.shape[1]))),
            ]
        )
        return moves, lax.optimization_barrier(in_send), deal_order_rows(out_rows), [red.step() for red in feeds], flat

    moves, in_send, out_sent, steps, flat = unit(first_moves)
    flat_moved = other_group(flat, masks[0])
    settle(feeds, steps)
    out_moved = exchange(out_sent)
    for red, move in zip(firsts, moves):
        red.move(*move)
    in_other = other_lane(in_send)

    def send_input():
        in_sum = in_own.astype(f32) + in_other.astype(f32)
        return deal_order_rows((in_sum + grad_middle_own).astype(bf16))

    everything = [*feeds, *firsts]
    in_moved = None
    bits = 1
    while pending := [red for red in everything if not hasattr(red, "result")]:
        last = all(red.stage == len(red.places) for red in pending)
        steps, flat, other = unit(
            lambda: (
                [red.step() for red in pending],
                flat + flat_moved if bits <= len(masks) else flat,
                (deal_take(in_moved), deal_take(out_moved), sum_branch.astype(f32)) if last else send_input() if in_moved is None else (),
            )
        )
        settle(pending, steps)
        if bits < len(masks):
            flat_moved = other_group(flat, masks[bits])
        bits += 1
        if in_moved is None:
            in_moved = exchange(other)
    grad_input, block_out, total_branch = other
    while bits <= len(masks):
        flat = flat + flat_moved
        if bits < len(masks):
            flat_moved = other_group(flat, masks[bits])
        bits += 1
    theirs = other_lane(flat)
    low, high = jnp.where(lane == 0, flat, theirs), jnp.where(lane == 0, theirs, flat)
    both = flat + theirs

    def joined(row, start, count):
        return jnp.concatenate([low[row, start : start + count], high[row, start : start + count]])

    gate_width = mamba_gate.shape[1]
    sum_gin, sum_gmid = both[8], both[9]
    sum_kst = both[: CONV + 1, gate_width : gate_width + 2 * NS]
    sum_kin = jnp.concatenate([low[: CONV + 1, :gate_width], high[: CONV + 1, :gate_width]], axis=1)
    sum_mix = joined(CONV + 1, 0, gate_width)
    sum_skip = jnp.sum(joined(CONV + 2, 0, gate_width).reshape(SH, SHD), axis=1)
    sum_bias = joined(10, heads, heads)
    sum_rate = joined(10, 0, heads)

    query_cols, key_cols = query_weight.shape[1], key_weight.shape[1]
    total_fgate, total_fup = red_fgate.result, red_fup.result
    total_mix, total_attn = total_branch[:, :gate_cols], total_branch[:, gate_cols:]
    rest = jnp.concatenate([red.result for red in firsts], axis=1)
    total_gate, total_input, rest = rest[:, :gate_cols], rest[:, gate_cols : 2 * gate_cols], rest[:, 2 * gate_cols :]
    total_step = rest[:, 2 * NS : 2 * NS + heads]
    start = 2 * NS + STEP_PAD
    total_query = rest[:, start : start + query_cols]
    total_key = rest[:, start + query_cols : start + query_cols + key_cols]
    total_value = rest[:, start + query_cols + key_cols :]
    state_rows = rest[:, : 2 * NS].reshape(lanes, shard // lanes, 2 * NS)
    state_own = lax.dynamic_index_in_dim(state_rows, lane, 0, keepdims=False)
    state_send = lax.dynamic_index_in_dim(state_rows, 1 - lane, 0, keepdims=False)
    state_lane = state_own + other_lane(state_send)
    return (
        block_out,
        grad_input,
        total_query,
        total_key,
        total_value,
        total_attn,
        total_gate,
        total_input,
        total_step,
        state_lane,
        total_mix,
        total_fgate,
        total_fup,
        total_fdown,
        sum_gin,
        sum_gmid,
        sum_kin,
        sum_kst,
        sum_mix,
        sum_bias,
        sum_rate,
        sum_skip,
    )


def solution(mesh):
    both = P("dp", "tensor")
    in_specs = (
        P(None, ("dp", "tensor"), None),
        P(None, ("dp", "tensor"), None),
        P(),
        P(None, "dp"),
        both,
        both,
        both,
        both,
        both,
        both,
        both,
        P("dp", None),
        both,
        both,
        both,
        both,
        P(),
        P(),
        P(None, "tensor"),
        P(),
        P("tensor"),
        P("tensor"),
        P("tensor"),
        P("tensor"),
    )
    out_specs = (
        P(None, ("dp", "tensor"), None),
        P(None, ("dp", "tensor"), None),
        both,
        both,
        both,
        both,
        both,
        both,
        both,
        P(("dp", "tensor"), None),
        both,
        both,
        both,
        both,
        P(),
        P(),
        P(),
        P(),
        P(),
        P(),
        P(),
        P(),
    )
    return jax.shard_map(local, mesh=mesh, in_specs=in_specs, out_specs=out_specs, check_vma=False)
```

```python
import math

import jax
import jax.numpy as jnp
from jax import lax
from jax.experimental import pallas as pl
from jax.experimental.layout import Layout, with_layout_constraint
from jax.experimental.pallas import tpu as pltpu
from jax.sharding import PartitionSpec as P

HEAD = 128
SH = 48
SHD = 64
NS = 256
CONV = 4
STEP_PAD = 128

epsilon = 1e-05
rope_base = 100000000000.0
f32 = jnp.float32
bf16 = jnp.bfloat16


def project(left, right):
    return jnp.dot(left, right, preferred_element_type=f32)


def project_back(left, right):
    return lax.dot_general(left, right, (((1,), (1,)), ((), ())), preferred_element_type=f32)


def outer_sum(left, right):
    return lax.dot_general(left, right, (((0,), (0,)), ((), ())), preferred_element_type=f32)


def outer_low(left, right):
    return with_layout_constraint(outer_sum(left, right).astype(bf16), Layout(major_to_minor=(0, 1)))


def rms_scale(values):
    return lax.rsqrt(jnp.mean(values * values, axis=-1, keepdims=True) + epsilon)


def rms_back(grad, values, scale, gain):
    weighted = grad * gain
    inner = jnp.sum(weighted * values, axis=-1, keepdims=True)
    return scale * weighted - values * (scale * scale * scale * inner / values.shape[-1])


def shift_down(values, count):
    return jnp.concatenate([jnp.zeros((count, values.shape[1]), values.dtype), values[:-count]], axis=0)


def shift_up(values, count):
    return jnp.concatenate([values[count:], jnp.zeros((count, values.shape[1]), values.dtype)], axis=0)


def conv_sum(signal, kernel, position):
    summed = kernel[CONV][None, :] + signal * kernel[0][None, :]
    for tap in range(1, CONV):
        moved = jnp.where(position >= tap, shift_down(signal, tap), 0.0)
        summed = summed + moved * kernel[tap][None, :]
    return summed


def silu_back(values):
    sig = jax.nn.sigmoid(values)
    return sig * (1.0 + values * (1.0 - sig))


def conv_back(grad, signal, kernel, position):
    grad_sum = grad * silu_back(conv_sum(signal, kernel, position))
    grad_signal = grad_sum * kernel[0][None, :]
    grad_taps = [jnp.sum(grad_sum * signal, axis=0)]
    for tap in range(1, CONV):
        kept = jnp.where(position >= tap, grad_sum, 0.0)
        grad_signal = grad_signal + shift_up(kept, tap) * kernel[tap][None, :]
        grad_taps.append(jnp.sum(kept * shift_down(signal, tap), axis=0))
    grad_taps.append(jnp.sum(grad_sum, axis=0))
    return grad_signal, jnp.stack(grad_taps)


def rope_tables(position):
    half_size = HEAD // 2
    frequency = jnp.exp(jnp.arange(half_size, dtype=f32) * (-2.0 * math.log(rope_base) / HEAD))
    angles = position.astype(f32) * frequency[None, :]
    return jnp.cos(angles)[:, None, :], jnp.sin(angles)[:, None, :]


def rotate(values, cosine, sine):
    half_size = HEAD // 2
    first, second = values[..., :half_size], values[..., half_size:]
    return jnp.concatenate([first * cosine - second * sine, second * cosine + first * sine], axis=-1)


def copy_blocks(order_ref, first_ref, second_ref, first_out_ref, second_out_ref):
    first_out_ref[...] = first_ref[...]
    second_out_ref[...] = second_ref[...]


def pick_halves(values, order, block):
    height, width = values.shape
    count = width // block // 2
    if block % 128:
        mixed = jnp.take(values.reshape(height, -1, block), order, axis=1).reshape(height, width)
        return mixed[:, : width // 2], mixed[:, width // 2 :]
    half = jax.ShapeDtypeStruct((height, width // 2), values.dtype)
    out_spec = pl.BlockSpec((height, block), lambda i, order: (0, i))
    return pl.pallas_call(
        copy_blocks,
        out_shape=(half, half),
        grid_spec=pltpu.PrefetchScalarGridSpec(
            num_scalar_prefetch=1,
            grid=(count,),
            in_specs=[
                pl.BlockSpec((height, block), lambda i, order: (0, order[i])),
                pl.BlockSpec((height, block), lambda i, order: (0, order[i + count])),
            ],
            out_specs=(out_spec, out_spec),
        ),
        cost_estimate=pl.CostEstimate(flops=0, transcendentals=0, bytes_accessed=4 * height * width),
        name="pick_halves",
    )(order, values, values)


def hand_over(values, microseconds):
    def idle(values_ref, out_ref):
        pass

    return pl.pallas_call(
        idle,
        out_shape=jax.ShapeDtypeStruct(values.shape, values.dtype),
        in_specs=[pl.BlockSpec(memory_space=pl.ANY)],
        out_specs=pl.BlockSpec(memory_space=pl.ANY),
        input_output_aliases={0: 0},
        cost_estimate=pl.CostEstimate(flops=microseconds * 1150000000, transcendentals=0, bytes_accessed=0),
        name="hand_over",
    )(values)


def rotate_back(values, cosine, sine):
    return rotate(values, cosine, -sine)


NEGATIVE = -1e30


def sigmoid_of(values):
    return 1.0 / (1.0 + jnp.exp(-values))


def block_mask(rows, segment_col, segment_row):
    row_index = lax.broadcasted_iota(jnp.int32, (rows, rows), 0)
    col_index = lax.broadcasted_iota(jnp.int32, (rows, rows), 1)
    return jnp.where((segment_col == segment_row) & (col_index <= row_index), 0.0, NEGATIVE)


def conv_block(signal, taps_ref, position):
    summed = taps_ref[CONV : CONV + 1, :] + signal * taps_ref[0:1, :]
    moved = []
    for tap in range(1, CONV):
        shifted = jnp.where(position >= tap, pltpu.roll(signal, tap, 0), 0.0)
        moved.append(shifted)
        summed = summed + shifted * taps_ref[tap : tap + 1, :]
    return summed, moved


def conv_block_back(grad_sum, signal, moved, taps_ref, position, sums_ref):
    rows = signal.shape[0]
    grad_signal = grad_sum * taps_ref[0:1, :]
    sums_ref[0, 0:1, :] = jnp.sum(grad_sum * signal, axis=0, keepdims=True)
    for tap in range(1, CONV):
        kept = jnp.where(position >= tap, grad_sum, 0.0)
        grad_signal = grad_signal + pltpu.roll(kept, rows - tap, 0) * taps_ref[tap : tap + 1, :]
        sums_ref[0, tap : tap + 1, :] = jnp.sum(grad_sum * moved[tap - 1], axis=0, keepdims=True)
    sums_ref[0, CONV : CONV + 1, :] = jnp.sum(grad_sum, axis=0, keepdims=True)
    return grad_signal


def mixing_block(inner, mask, run_col, run_row, step_row):
    decay = jnp.exp(run_col - run_row + mask)
    return decay, (inner * decay * step_row).astype(bf16)


def state_forward_kernel(
    signal_ref, gate_ref, taps_ref, skip_ref, state_ref, seg_row_ref, run_row_ref, run_col_ref, step_ref, columns_ref,
    out_ref, square_ref, inner_ref, mask_ref,
):
    rows = signal_ref.shape[0]
    position = columns_ref[:, 1:2]

    @pl.when(pl.program_id(1) == 0)
    def _():
        inner_ref[...] = lax.dot_general(
            state_ref[:, NS:], state_ref[:, :NS], (((1,), (1,)), ((), ())), preferred_element_type=f32
        )
        mask_ref[...] = block_mask(rows, columns_ref[:, 0:1], seg_row_ref[0])
        square_ref[...] = jnp.zeros_like(square_ref)

    summed, _ = conv_block(signal_ref[...], taps_ref, position)
    cols = summed * sigmoid_of(summed)
    cols_low = cols.astype(bf16)
    mixed = []
    for head in range(2):
        _, mixing = mixing_block(
            inner_ref[...], mask_ref[...], run_col_ref[0, 0, :, head : head + 1],
            run_row_ref[0, 0, head : head + 1, :], step_ref[0, 0, head : head + 1, :],
        )
        mixed.append(jnp.dot(mixing, cols_low, preferred_element_type=f32))
    lanes = lax.broadcasted_iota(jnp.int32, cols.shape, 1)
    out = jnp.where(lanes < SHD, mixed[0], mixed[1]) + skip_ref[...] * cols
    out_ref[...] = out
    gate = gate_ref[...]
    gated = out * (gate * sigmoid_of(gate))
    square_ref[...] += gated * gated


def state_backward_kernel(
    grad_ref, out_ref, gate_ref, signal_ref, taps_ref, skip_ref, gain_ref, state_ref, seg_row_ref, run_row_ref, run_col_ref,
    step_ref, columns_ref, state_raw_ref, state_taps_ref, step_all_ref, step_sig_ref, rate_ref, others_ref,
    first_ref, sums_ref, state_sums_ref, head_sums_ref,
    inner_ref, mask_ref, grad_inner_ref, direct_ref, along_ref,
):
    rows = signal_ref.shape[0]
    pair = pl.program_id(1)

    @pl.when(pair == 0)
    def _():
        along_ref[...] = jnp.zeros_like(along_ref)
        inner_ref[...] = lax.dot_general(
            state_ref[:, NS:], state_ref[:, :NS], (((1,), (1,)), ((), ())), preferred_element_type=f32
        )
        mask_ref[...] = block_mask(rows, columns_ref[:, 0:1], seg_row_ref[0])
        grad_inner_ref[...] = jnp.zeros_like(grad_inner_ref)

    grad, out, gate, signal = grad_ref[...], out_ref[...], gate_ref[...], signal_ref[...]
    position, scale, cross = columns_ref[:, 1:2], columns_ref[:, 2:3], columns_ref[:, 3:4]
    here = pl.multiple_of(pair * 2 * SHD, 2 * SHD)
    rest = first_ref.shape[1] // 2 - others_ref.shape[1] // 2 - NS - STEP_PAD // 2
    after_rest = rest + 2 * NS + STEP_PAD
    sig = sigmoid_of(gate)
    silu = gate * sig
    gated = out * silu
    scaled = grad * scale
    grad_gated = scaled * gain_ref[...] - gated * cross
    grad_out = grad_gated * silu
    first_ref[:, pl.ds(here, 2 * SHD)] = (grad_gated * out * (sig * (1.0 + gate * (1.0 - sig)))).astype(bf16)
    summed, moved = conv_block(signal, taps_ref, position)
    sig = sigmoid_of(summed)
    cols = summed * sig
    cols_low = cols.astype(bf16)
    grad_low = grad_out.astype(bf16)
    lanes = lax.broadcasted_iota(jnp.int32, cols.shape, 1)
    zero = jnp.zeros_like(grad_low)
    grad_cols = []
    for head in range(2):
        step_row = step_ref[0, 0, head : head + 1, :]
        inner = inner_ref[...]
        decay, mixing = mixing_block(
            inner, mask_ref[...], run_col_ref[0, 0, :, head : head + 1], run_row_ref[0, 0, head : head + 1, :], step_row
        )
        grad_cols.append(
            lax.dot_general(mixing, grad_low, (((0,), (0,)), ((), ())), preferred_element_type=f32)
        )
        grad_head = jnp.where((lanes < SHD) == (head == 0), grad_low, zero)
        grad_decay = lax.dot_general(
            grad_head, cols_low, (((1,), (1,)), ((), ())), preferred_element_type=f32
        ) * decay
        stepped = grad_decay * step_row
        grad_inner_ref[...] += stepped
        direct_ref[pl.ds(2 * pair + head, 1), :] = jnp.sum(grad_decay * inner, axis=0, keepdims=True)
        along = jnp.sum(stepped * inner, axis=1, keepdims=True)
        along_ref[...] = jnp.where(lanes == 2 * pair + head, along, along_ref[...])
    grad_cols = jnp.where(lanes < SHD, grad_cols[0], grad_cols[1]) + skip_ref[...] * grad_out
    grad_sum = grad_cols * (sig * (1.0 + summed * (1.0 - sig)))
    grad_signal = conv_block_back(grad_sum, signal, moved, taps_ref, position, sums_ref)
    sums_ref[0, CONV + 1 : CONV + 2, :] = jnp.sum(scaled * gated, axis=0, keepdims=True)
    sums_ref[0, CONV + 2 : CONV + 3, :] = jnp.sum(grad_out * cols, axis=0, keepdims=True)
    sums_ref[0, CONV + 3 : CONV + 4, :] = jnp.zeros((1, cols.shape[1]), f32)
    first_ref[:, pl.ds(pl.multiple_of(after_rest + here, 2 * SHD), 2 * SHD)] = grad_signal.astype(bf16)

    @pl.when(pair == pl.num_programs(1) - 1)
    def _():
        inner_low = grad_inner_ref[...].astype(bf16)
        for part, (mine, other) in enumerate((((0, NS), (NS, 2 * NS)), ((NS, 2 * NS), (0, NS)))):
            raw = state_raw_ref[:, mine[0] : mine[1]]
            taps = state_taps_ref.at[:, mine[0] : mine[1]]
            summed, moved = conv_block(raw, taps, position)
            sig = sigmoid_of(summed)
            grad = lax.dot_general(
                inner_low, state_ref[:, other[0] : other[1]], (((part,), (0,)), ((), ())), preferred_element_type=f32
            )
            grad_sum = grad * (sig * (1.0 + summed * (1.0 - sig)))
            back = conv_block_back(grad_sum, raw, moved, taps, position, state_sums_ref.at[:, :, mine[0] : mine[1]])
            first_ref[:, rest + mine[0] : rest + mine[1]] = back.astype(bf16)
        state_sums_ref[0, CONV + 1 :, :] = jnp.zeros((7 - CONV, 2 * NS), f32)
        heads = step_all_ref.shape[1]
        direct, step = direct_ref[...], step_all_ref[0]
        grad_running = along_ref[...].T[:heads] - step * direct
        row_index = lax.broadcasted_iota(jnp.int32, (rows, rows), 0)
        col_index = lax.broadcasted_iota(jnp.int32, (rows, rows), 1)
        lower = jnp.where(col_index <= row_index, 1.0, 0.0)
        grad_product = jnp.dot(
            grad_running, lower, precision=lax.Precision.HIGHEST, preferred_element_type=f32
        )
        grad_raw = (direct + grad_product * rate_ref[...]) * step_sig_ref[0]
        head_sums_ref[0, :, 0:1] = jnp.sum(grad_product * step, axis=1, keepdims=True)
        head_sums_ref[0, :, 1:2] = jnp.sum(grad_raw, axis=1, keepdims=True)
        wide = jnp.concatenate([grad_raw, jnp.zeros((STEP_PAD - heads, rows), f32)], axis=0)
        first_ref[:, rest + 2 * NS : after_rest] = wide.T.astype(bf16)
        first_ref[:, first_ref.shape[1] - others_ref.shape[1] :] = others_ref[...]


def state_specs(rows, pairs):
    block = pl.BlockSpec((rows, 2 * SHD), lambda m, p: (m, p))
    return {
        "block": block,
        "taps": pl.BlockSpec((CONV + 1, 2 * SHD), lambda m, p: (0, p)),
        "vector": pl.BlockSpec((1, 2 * SHD), lambda m, p: (0, p)),
        "state": pl.BlockSpec((rows, 2 * NS), lambda m, p: (m, 0)),
        "columns": pl.BlockSpec((rows, 8), lambda m, p: (m, 0)),
        "row": pl.BlockSpec((1, 1, rows), lambda m, p: (m, 0, 0)),
        "head_row": pl.BlockSpec((1, 1, 2, rows), lambda m, p: (m, p, 0, 0)),
        "head_col": pl.BlockSpec((1, 1, rows, 2), lambda m, p: (m, p, 0, 0)),
    }


def state_forward(signal, gate, taps, skip, state, seg_row, run_row, run_col, step, columns):
    micro, pairs, _, rows = run_row.shape
    spec = state_specs(rows, pairs)
    total, width = signal.shape
    return pl.pallas_call(
        state_forward_kernel,
        out_shape=(jax.ShapeDtypeStruct((total, width), f32), jax.ShapeDtypeStruct((total, 2 * SHD), f32)),
        grid=(micro, pairs),
        in_specs=[spec[name] for name in (
            "block", "block", "taps", "vector", "state", "row", "head_row", "head_col", "head_row", "columns")],
        out_specs=(spec["block"], pl.BlockSpec((rows, 2 * SHD), lambda m, p: (m, 0))),
        scratch_shapes=[pltpu.VMEM((rows, rows), f32), pltpu.VMEM((rows, rows), f32)],
        cost_estimate=pl.CostEstimate(
            flops=8 * total * rows * width // SHD * SHD, transcendentals=total * rows * width // SHD, bytes_accessed=12 * total * width
        ),
        name="state_forward",
    )(signal, gate, taps, skip, state, seg_row, run_row, run_col, step, columns)


def state_backward(
    grad, out, gate, signal, taps, skip, gain, state, seg_row, run_row, run_col, step, columns,
    state_raw, state_taps, step_all, step_sig, rate, others,
):
    micro, pairs, _, rows = run_row.shape
    heads = 2 * pairs
    spec = state_specs(rows, pairs)
    total, width = signal.shape
    joint = 2 * width + 2 * NS + STEP_PAD + others.shape[1]
    heads_block = pl.BlockSpec((1, heads, rows), lambda m, p: (m, 0, 0))
    return pl.pallas_call(
        state_backward_kernel,
        out_shape=(
            jax.ShapeDtypeStruct((total, joint), bf16),
            jax.ShapeDtypeStruct((micro, 8, width), f32),
            jax.ShapeDtypeStruct((micro, 8, 2 * NS), f32),
            jax.ShapeDtypeStruct((micro, heads, 2), f32),
        ),
        grid=(micro, pairs),
        in_specs=[spec[name] for name in (
            "block", "block", "block", "block", "taps", "vector", "vector", "state",
            "row", "head_row", "head_col", "head_row", "columns", "state")]
        + [
            pl.BlockSpec((CONV + 1, 2 * NS), lambda m, p: (0, 0)), heads_block, heads_block,
            pl.BlockSpec((heads, 1), lambda m, p: (0, 0)), pl.BlockSpec((rows, others.shape[1]), lambda m, p: (m, 0)),
        ],
        out_specs=(
            pl.BlockSpec((rows, joint), lambda m, p: (m, 0)), pl.BlockSpec((1, 8, 2 * SHD), lambda m, p: (m, 0, p)),
            pl.BlockSpec((1, 8, 2 * NS), lambda m, p: (m, 0, 0)),
            pl.BlockSpec((1, heads, 2), lambda m, p: (m, 0, 0)),
        ),
        scratch_shapes=[pltpu.VMEM((rows, rows), f32)] * 3 + [pltpu.VMEM((heads, rows), f32), pltpu.VMEM((rows, 2 * SHD), f32)],
        cost_estimate=pl.CostEstimate(
            flops=20 * total * rows * width, transcendentals=total * rows * width // SHD, bytes_accessed=20 * total * width
        ),
        name="state_backward",
    )(
        grad, out, gate, signal, taps, skip, gain, state, seg_row, run_row, run_col, step, columns,
        state_raw, state_taps, step_all, step_sig, rate, others,
    )


def local(
    inputs,
    out_grad,
    deal_order,
    segment,
    query_weight,
    key_weight,
    value_weight,
    attention_out,
    mamba_gate,
    mamba_input,
    step_weight,
    state_weight,
    mamba_out,
    feed_gate,
    feed_up,
    feed_down,
    gain_input,
    gain_middle,
    kernel_inner,
    kernel_state,
    mixer_gain,
    step_bias,
    log_rate,
    skip_gain,
):
    micro, own, width = inputs.shape
    groups = lax.axis_size("dp")
    lanes = lax.axis_size("tensor")
    lane = lax.axis_index("tensor")
    group = lax.axis_index("dp")
    device = group * lanes + lane
    per = own // groups
    rows = own * lanes
    total = micro * rows
    inner_width = SH * SHD
    scale_factor = HEAD ** (-0.5)
    outer_count = groups // 4
    shard = width // groups

    swap_lane = [(0, 1), (1, 0)]

    def other_lane(values):
        return lax.ppermute(values, "tensor", swap_lane)

    def other_group(values, bits):
        return lax.ppermute(values, "dp", [(i, i ^ bits) for i in range(groups)])

    step_padded = jnp.pad(step_weight, ((0, 0), (0, STEP_PAD - step_weight.shape[1])))
    early = dict(
        gate=mamba_gate, state=state_weight, step=step_padded, input=mamba_input, query=query_weight, key=key_weight,
        value=value_weight, mix=mamba_out, attn=attention_out,
    )
    late = dict(fgate=feed_gate, fup=feed_up, fdown=feed_down)
    whole, places_of = {}, {}
    for label, group_weights in (("early", early), ("late", late)):
        start = 0
        for name, weight in group_weights.items():
            places_of[name] = (label, start, weight.shape[1])
            start += weight.shape[1]
        whole[label] = lax.all_gather(jnp.concatenate(list(group_weights.values()), axis=1), "dp", axis=0, tiled=True)

    def full(name):
        label, start, size = places_of[name]
        return lax.slice_in_dim(whole[label], start, start + size, axis=1)

    own_places = jnp.arange(own, dtype=jnp.int32)
    own_order = lax.dynamic_slice_in_dim(deal_order, device * own, own, 1)
    micro_index = jnp.arange(micro, dtype=jnp.int32)[:, None]

    def buffer_place(destination, rank):
        return destination * (micro * per) + micro_index * per + rank

    send_rank = jnp.sum((own_order[:, None, :] < own_order[:, :, None]).astype(jnp.int32), axis=2)
    send_place = buffer_place(send_rank // per, send_rank % per).reshape(-1)
    lane_order = lax.dynamic_index_in_dim(deal_order.reshape(micro, groups, lanes, own), lane, 2, keepdims=False)
    slots = device * own + own_places
    found = lane_order[:, None, :, :] == slots[None, :, None, None]
    source = jnp.sum(
        jnp.where(found, jnp.arange(groups, dtype=jnp.int32)[None, None, :, None], 0), axis=(2, 3)
    )
    recv_rank = jnp.sum(
        ((source[:, None, :] == source[:, :, None]) & (own_places[None, None, :] < own_places[None, :, None])).astype(jnp.int32),
        axis=2,
    )
    recv_place = buffer_place(source, recv_rank).reshape(-1)
    buffer_places = jnp.arange(micro * own, dtype=jnp.int32)
    send_pick = (buffer_places[:, None] == send_place[None, :]).astype(bf16)
    recv_pick = (recv_place[:, None] == buffer_places[None, :]).astype(bf16)

    def exchange(buffer):
        return lax.all_to_all(
            buffer.reshape(groups, micro * per, width), "dp", split_axis=0, concat_axis=0, tiled=True
        ).reshape(micro * own, width)

    def deal(values):
        sent = project(send_pick, values.reshape(micro * own, width)).astype(bf16)
        return project(recv_pick, exchange(sent)).astype(bf16)

    def deal_order_rows(values):
        return outer_sum(recv_pick, values).astype(bf16)

    def deal_take(moved):
        return outer_sum(send_pick, moved).astype(bf16).reshape(micro, own, width)

    def join_lanes(values):
        mine = values.reshape(micro, 1, own, -1)
        theirs = other_lane(values).reshape(micro, 1, own, -1)
        low = jnp.where(lane == 0, mine, theirs)
        high = jnp.where(lane == 0, theirs, mine)
        return jnp.concatenate([low, high], axis=1).reshape(total, -1)

    def lane_rows(values, which):
        return lax.dynamic_index_in_dim(
            values.reshape(micro, lanes, own, -1), which, 1, keepdims=False
        ).reshape(micro * own, -1)

    own_in = deal(inputs)
    own_grad = deal(out_grad)
    whole_in = join_lanes(own_in)
    whole_grad = join_lanes(own_grad)

    before = jnp.sum((segment[:, None, :] < segment[:, :, None]).astype(jnp.int32), axis=2)
    places = jnp.arange(rows, dtype=jnp.int32)
    allowed = (segment[:, :, None] == segment[:, None, :]) & (places[None, None, :] <= places[None, :, None])
    position = (places[None, :] - before).reshape(total, 1)

    masks = [1 << place for place in range(groups.bit_length() - 1)]
    relative = []
    for block in range(groups):
        flip = 0
        for place, mask in enumerate(masks):
            if block >> (len(masks) - 1 - place) & 1:
                flip ^= mask
        relative.append(flip)
    block_order = jnp.bitwise_xor(group.astype(jnp.int32), jnp.array(relative, jnp.int32))

    def split_left(left):
        return pick_halves(left, block_order, shard)

    inner_places = list(range(1, len(masks)))

    def core_send(left_parts, right):
        return outer_low(left_parts[1], right)

    def halve(kept, place):
        return (
            lax.slice_in_dim(kept, 1, 2, axis=place - 1).reshape(-1, kept.shape[-1]),
            lax.slice_in_dim(kept, 0, 1, axis=place - 1),
        )

    class Reduction:
        def __init__(self, first):
            self.places = [place for place in first if place in inner_places]
            self.places += [place for place in inner_places if place not in first]
            self.stage = 0

        def move(self, send, kept):
            self.came = other_group(send, masks[self.places[self.stage]])
            self.kept = kept
            self.stage += 1

        def first(self, left_parts, right, from_core):
            kept = (outer_sum(left_parts[0], right) + from_core.astype(f32)).astype(bf16)
            kept = kept.reshape((2,) * len(inner_places) + (shard, -1))
            return halve(kept, self.places[0])

        def added(self):
            return self.kept.astype(f32) + self.came.reshape(self.kept.shape).astype(f32)

        def next(self):
            return halve(self.added().astype(bf16), self.places[self.stage])

        def last(self):
            return self.added().reshape(shard, -1)

        def step(self):
            return self.next() if self.stage < len(self.places) else self.last()

    order = [deal_order[0, 0] >= 0]

    def unit(work):
        shapes = jax.eval_shape(work)
        results = lax.cond(
            order[0], work, lambda: jax.tree.map(lambda leaf: jnp.zeros(leaf.shape, leaf.dtype), shapes)
        )
        leaves, form = jax.tree.flatten(results)
        least = min(range(len(leaves)), key=lambda place: leaves[place].size)
        leaves[least], order[0] = lax.optimization_barrier((leaves[least], order[0]))
        return jax.tree.unflatten(form, leaves)

    def after(value, *others):
        return lax.optimization_barrier((value, others))[0]

    in32 = whole_in.astype(f32)
    in_scale = rms_scale(in32)
    normed_low = (in32 * in_scale * gain_input).astype(bf16)
    normed_left = split_left(normed_low)
    whole["early"] = after(whole["early"], whole_grad, normed_left)
    gate_z = project(normed_low, full("gate"))
    ssm_in = project(normed_low, full("input"))
    state_raw = project(normed_low, full("state"))
    heads = step_weight.shape[1]
    raw_step = project(normed_low, full("step"))[:, :heads]
    state_low = jax.nn.silu(conv_sum(state_raw, kernel_state, position)).astype(bf16)
    rate = -jnp.exp(log_rate)
    step_size = jax.nn.softplus(raw_step + step_bias)
    step_heads = step_size.reshape(micro, rows, heads).transpose(0, 2, 1)
    lower = (places[None, :] <= places[:, None]).astype(f32)
    running = jnp.einsum(
        "mhj,ij->mhi", step_heads * rate[None, :, None], lower, precision=lax.Precision.HIGHEST, preferred_element_type=f32
    )
    pairs = heads // 2
    run_row = running.reshape(micro, pairs, 2, rows)
    run_col = run_row.transpose(0, 1, 3, 2)
    step_row = step_heads.reshape(micro, pairs, 2, rows)
    skip_wide = jnp.repeat(skip_gain, SHD)[None, :]
    layout = (state_low, segment.reshape(micro, 1, rows).astype(f32), run_row, run_col, step_row)
    row_facts = jnp.concatenate([segment.reshape(total, 1).astype(f32), position.astype(f32)], axis=1)
    ssm_out, squares = state_forward(ssm_in, gate_z, kernel_inner, skip_wide, *layout, jnp.pad(row_facts, ((0, 0), (0, 6))))
    square_own = jnp.sum(squares, axis=1)
    square_sum = square_own + other_lane(square_own)
    inv_rms = lax.rsqrt(square_sum / inner_width + epsilon)[:, None]
    gated_low = (ssm_out * jax.nn.silu(gate_z) * inv_rms * mixer_gain).astype(bf16)

    cosine, sine = rope_tables(position)
    query_low = rotate(project(normed_low, full("query")).reshape(total, -1, HEAD), cosine, sine).astype(bf16)
    key_low = rotate(project(normed_low, full("key")).reshape(total, -1, HEAD), cosine, sine).astype(bf16)
    value_low = project(normed_low, full("value")).astype(bf16)
    kv_here = key_low.shape[1]
    query_low = query_low.reshape(micro, rows, kv_here, -1, HEAD)
    key_low = key_low.reshape(micro, rows, kv_here, HEAD)
    value_low = value_low.reshape(micro, rows, kv_here, HEAD)
    logits = jnp.einsum("migkd,mjgd->mgkij", query_low, key_low, preferred_element_type=f32) * scale_factor
    logits = jnp.where(allowed[:, None, None], logits, -jnp.inf)
    exp_scores = jnp.exp(logits - jnp.max(logits, axis=-1, keepdims=True))
    probs = exp_scores / jnp.sum(exp_scores, axis=-1, keepdims=True)
    probs_low = probs.astype(bf16)
    attended_low = (
        jnp.einsum("mgkij,mjgd->migkd", probs_low, value_low, preferred_element_type=f32).astype(bf16).reshape(total, -1)
    )
    branch_part = (project_back(gated_low, full("mix")) + project_back(attended_low, full("attn"))).astype(bf16)
    branch = branch_part.astype(f32) + other_lane(branch_part).astype(f32)
    whole_mid = (in32 + branch).astype(bf16)
    mid32 = whole_mid.astype(f32)
    mid_scale = rms_scale(mid32)
    mid_low = (mid32 * mid_scale * gain_middle).astype(bf16)
    red_fgate, red_fup, red_low, red_high = [Reduction(places) for places in ((1, 2), (2, 1), (1, 2), (2, 1))]
    feeds = (red_fgate, red_fup)
    ff_cols = feed_gate.shape[1]
    gate_cols = mamba_gate.shape[1]

    def feed_forward():
        gate_ff = project(mid_low, full("fgate"))
        up_ff = project(mid_low, full("fup"))
        sig_ff = jax.nn.sigmoid(gate_ff)
        hidden_low = (gate_ff * sig_ff * up_ff).astype(bf16)
        grad_hidden = project(whole_grad, full("fdown"))
        gate_ff_low = (grad_hidden * up_ff * (sig_ff * (1.0 + gate_ff * (1.0 - sig_ff)))).astype(bf16)
        up_ff_low = (grad_hidden * (gate_ff * sig_ff)).astype(bf16)
        grad_mid_norm = project_back(gate_ff_low, full("fgate")) + project_back(up_ff_low, full("fup"))
        grad_gain_mid = jnp.sum(grad_mid_norm * mid32 * mid_scale, axis=0)
        mid_part = rms_back(grad_mid_norm, mid32, mid_scale, gain_middle).astype(bf16)
        return grad_gain_mid, mid_part, hidden_low, (gate_ff_low, up_ff_low), outer_low(whole_grad, hidden_low)

    grad_gain_mid, mid_part, hidden_low, feed_low, part_fdown = unit(feed_forward)
    sum_fdown = lax.psum_scatter(part_fdown, "dp", scatter_dimension=0, tiled=True)
    mid_other = hand_over(other_lane(mid_part), 45)

    def feed_output():
        ffn_part = project_back(hidden_low, full("fdown")).astype(bf16)
        mid_left = split_left(mid_low)
        return (
            lane_rows(ffn_part, lane), lane_rows(ffn_part, 1 - lane), mid_left[0],
            [core_send(mid_left, right) for right in feed_low],
        )

    ffn_own, ffn_send, mid_keep, send_feed = unit(feed_output)
    feed_came = [other_group(send, 1) for send in send_feed]

    def keep_first(keep, right, came, reductions, sizes):
        kept = (outer_sum(keep, right) + came.astype(f32)).astype(bf16)
        kept = kept.reshape((2,) * len(inner_places) + (shard, -1))
        moves, start = [], 0
        for red, size in zip(reductions, sizes):
            moves.append(halve(kept[..., start : start + size], red.places[0]))
            start += size
        return moves

    def settle(reductions, steps):
        for red, step in zip(reductions, steps):
            if red.stage < len(red.places):
                red.move(*step)
            else:
                red.result = step

    mid_other, feed_came = lax.optimization_barrier((mid_other, feed_came))
    moves = unit(
        lambda: [
            keep_first(mid_keep, right, came, (red,), (ff_cols,))[0] for red, right, came in zip(feeds, feed_low, feed_came)
        ]
    )
    for red, move in zip(feeds, moves):
        red.move(*move)

    def branch_backward():
        grad_middle = whole_grad.astype(f32) + (mid_part.astype(f32) + mid_other.astype(f32))
        whole_branch = grad_middle.astype(bf16)
        grad_gated_norm = project(whole_branch, full("mix"))
        cross_own = jnp.sum(grad_gated_norm * mixer_gain * (ssm_out * jax.nn.silu(gate_z)), axis=1)
        grad_attended = project(whole_branch, full("attn")).astype(bf16).reshape(micro, rows, kv_here, -1, HEAD)
        grad_probs = jnp.einsum("migkd,mjgd->mgkij", grad_attended, value_low, preferred_element_type=f32)
        grad_value = jnp.einsum("mgkij,migkd->mjgd", probs_low, grad_attended, preferred_element_type=f32)
        weighted_sum = jnp.sum(probs * grad_probs, axis=-1, keepdims=True)
        grad_logits = (probs * (grad_probs - weighted_sum)).astype(bf16)
        grad_query_rot = jnp.einsum("mgkij,mjgd->migkd", grad_logits, key_low, preferred_element_type=f32) * scale_factor
        grad_key_rot = jnp.einsum("mgkij,migkd->mjgd", grad_logits, query_low, preferred_element_type=f32) * scale_factor
        query_grad_low = rotate_back(grad_query_rot.reshape(total, -1, HEAD), cosine, sine).astype(bf16).reshape(total, -1)
        key_grad_low = rotate_back(grad_key_rot.reshape(total, -1, HEAD), cosine, sine).astype(bf16).reshape(total, -1)
        value_grad_low = grad_value.astype(bf16).reshape(total, -1)
        return (
            cross_own, lane_rows(grad_middle, lane), grad_gated_norm, whole_branch,
            (query_grad_low, key_grad_low, value_grad_low),
        )

    cross_own, grad_middle_own, grad_gated_norm, whole_branch, qkv_low = unit(branch_backward)
    cross_other = other_lane(cross_own)

    ffn_other = other_lane(ffn_send)

    def branch_partial():
        ffn_out = ffn_own.astype(f32) + ffn_other.astype(f32)
        out_rows = (lane_rows(whole_mid, lane).astype(f32) + ffn_out).astype(bf16)
        return outer_low(whole_branch, jnp.concatenate([gated_low, attended_low], axis=1)), deal_order_rows(out_rows)

    part_branch, out_sent = unit(branch_partial)
    out_moved = exchange(out_sent)
    sum_branch = lax.psum_scatter(part_branch, "dp", scatter_dimension=0, tiled=True)

    def state_space_backward():
        cross = (inv_rms**3) * ((cross_own + cross_other)[:, None] / inner_width)
        step_sig = jax.nn.sigmoid(raw_step + step_bias).reshape(micro, rows, heads).transpose(0, 2, 1)
        columns = jnp.pad(jnp.concatenate([row_facts, inv_rms, cross], axis=1), ((0, 0), (0, 4)))
        first_right, column_sums, state_sums, head_sums = state_backward(
            grad_gated_norm, ssm_out, gate_z, ssm_in, kernel_inner, skip_wide, mixer_gain[None, :], *layout, columns,
            state_raw, kernel_state, step_heads, step_sig, rate[:, None], jnp.concatenate(qkv_low, axis=1),
        )
        return column_sums, state_sums, head_sums, first_right

    column_sums, state_sums, head_sums, first_right = unit(state_space_backward)

    total_fdown_low = [sum_fdown]
    order[0], total_fdown_low = lax.optimization_barrier((order[0], total_fdown_low))
    send_first, steps, block_out = unit(
        lambda: (core_send(normed_left, first_right), [red.step() for red in feeds], deal_take(out_moved))
    )
    settle(feeds, steps)
    first_came = other_group(send_first, 1)

    def input_gradient():
        grad_normed = project_back(first_right, lax.slice_in_dim(whole["early"], 0, first_right.shape[1], axis=1))
        grad_gain_in = jnp.sum(grad_normed * in32 * in_scale, axis=0)
        in_part = rms_back(grad_normed, in32, in_scale, gain_input).astype(bf16)
        return grad_gain_in, lane_rows(in_part, lane), lane_rows(in_part, 1 - lane)

    grad_gain_in, in_own, in_send = unit(input_gradient)

    firsts = (red_low, red_high)
    low_size = gate_cols + 2 * NS + STEP_PAD
    first_sizes = (low_size, first_right.shape[1] - low_size)

    def first_moves():
        moves = keep_first(normed_left[0], first_right, first_came, firsts, first_sizes)
        head_row = (jnp.sum(head_sums, axis=0).T * jnp.stack([rate, jnp.ones_like(rate)])).reshape(1, -1)
        flat = jnp.concatenate(
            [
                jnp.concatenate([jnp.sum(column_sums, axis=0), jnp.sum(state_sums, axis=0)], axis=1),
                grad_gain_in[None, :], grad_gain_mid[None, :], jnp.pad(head_row, ((0, 5), (0, width - head_row.shape[1]))),
            ]
        )
        return moves, lax.optimization_barrier(in_send), [red.step() for red in feeds], flat

    moves, in_send, steps, flat = unit(first_moves)
    flat_moved = other_group(flat, masks[0])
    settle(feeds, steps)
    for red, move in zip(firsts, moves):
        red.move(*move)
    in_other = hand_over(other_lane(in_send), 6)

    flat = unit(lambda: flat + flat_moved)
    flat_moved = other_group(flat, masks[1])

    def send_input():
        in_sum = in_own.astype(f32) + in_other.astype(f32)
        return deal_order_rows((in_sum + grad_middle_own).astype(bf16))

    in_moved = None
    everything = [*feeds, *firsts]
    query_cols, key_cols = query_weight.shape[1], key_weight.shape[1]

    bits = 2

    def finish():
        low, high = red_low.result, red_high.result
        state_rows = low[:, gate_cols : gate_cols + 2 * NS].reshape(lanes, shard // lanes, 2 * NS)
        cut = [0, gate_cols, gate_cols + query_cols, gate_cols + query_cols + key_cols, high.shape[1]]
        pieces = (
            low[:, :gate_cols], low[:, gate_cols + 2 * NS : gate_cols + 2 * NS + heads],
            [high[:, start:stop] for start, stop in zip(cut, cut[1:])],
            [lax.dynamic_index_in_dim(state_rows, which, 0, keepdims=False) for which in (lane, 1 - lane)],
        )
        return pieces, deal_take(in_moved)

    arrived = [red.came for red in feeds] + [sum_branch]
    order[0], arrived = lax.optimization_barrier((order[0], arrived))
    for red, came in zip(feeds, arrived):
        red.came = came
    wides = None
    while pending := [red for red in everything if not hasattr(red, "result")]:
        if in_moved is None:
            pending = list(firsts)
        widen = in_moved is not None and wides is None
        last = all(red.stage == len(red.places) for red in pending) and in_moved is not None

        def round_work():
            steps = [red.step() for red in pending]
            added = flat + flat_moved if bits <= len(masks) else flat
            wide = [arrived[-1].astype(f32), total_fdown_low[0].astype(f32)] if widen else ()
            if last:
                for red, step in zip(pending, steps):
                    red.result = step
                return steps, added, wide, finish()
            return steps, added, wide, send_input() if in_moved is None else ()

        steps, flat, wide, other = unit(round_work)
        if widen:
            wides = wide
        if bits < len(masks):
            flat_moved = other_group(flat, masks[bits])
        bits += 1
        if last:
            break
        settle(pending, steps)
        if in_moved is None:
            in_moved = exchange(other)
    for red, step in zip(pending, steps):
        red.result = step
    (total_gate, total_step, (total_input, total_query, total_key, total_value), states), grad_input = other
    while bits <= len(masks):
        flat = flat + flat_moved
        if bits < len(masks):
            flat_moved = other_group(flat, masks[bits])
        bits += 1
    theirs = other_lane(flat)
    low, high = jnp.where(lane == 0, flat, theirs), jnp.where(lane == 0, theirs, flat)
    both = flat + theirs

    def joined(row, start, count):
        return jnp.concatenate([low[row, start : start + count], high[row, start : start + count]])

    sum_gin, sum_gmid = both[8], both[9]
    sum_kst = both[: CONV + 1, gate_cols : gate_cols + 2 * NS]
    sum_kin = jnp.concatenate([low[: CONV + 1, :gate_cols], high[: CONV + 1, :gate_cols]], axis=1)
    sum_mix = joined(CONV + 1, 0, gate_cols)
    sum_skip = jnp.sum(joined(CONV + 2, 0, gate_cols).reshape(SH, SHD), axis=1)
    sum_bias = joined(10, heads, heads)
    sum_rate = joined(10, 0, heads)

    total_fgate, total_fup = red_fgate.result, red_fup.result
    total_branch, total_fdown = wides
    total_mix, total_attn = total_branch[:, :gate_cols], total_branch[:, gate_cols:]
    state_lane = states[0] + other_lane(states[1])
    return (
        block_out,
        grad_input,
        total_query,
        total_key,
        total_value,
        total_attn,
        total_gate,
        total_input,
        total_step,
        state_lane,
        total_mix,
        total_fgate,
        total_fup,
        total_fdown,
        sum_gin,
        sum_gmid,
        sum_kin,
        sum_kst,
        sum_mix,
        sum_bias,
        sum_rate,
        sum_skip,
    )


def solution(mesh):
    both = P("dp", "tensor")
    in_specs = (
        P(None, ("dp", "tensor"), None),
        P(None, ("dp", "tensor"), None),
        P(),
        P(None, "dp"),
        both,
        both,
        both,
        both,
        both,
        both,
        both,
        P("dp", None),
        both,
        both,
        both,
        both,
        P(),
        P(),
        P(None, "tensor"),
        P(),
        P("tensor"),
        P("tensor"),
        P("tensor"),
        P("tensor"),
    )
    out_specs = (
        P(None, ("dp", "tensor"), None),
        P(None, ("dp", "tensor"), None),
        both,
        both,
        both,
        both,
        both,
        both,
        both,
        P(("dp", "tensor"), None),
        both,
        both,
        both,
        both,
        P(),
        P(),
        P(),
        P(),
        P(),
        P(),
        P(),
        P(),
    )
    return jax.shard_map(local, mesh=mesh, in_specs=in_specs, out_specs=out_specs, check_vma=False)
```

```python
import functools
import math

import jax
import jax.numpy as jnp
from jax import lax
from jax.experimental import pallas as pl
from jax.experimental.layout import Layout, with_layout_constraint
from jax.experimental.pallas import tpu as pltpu
from jax.sharding import PartitionSpec as P

HEAD = 128
SH = 48
SHD = 64
NS = 256
CONV = 4
STEP_PAD = 128

epsilon = 1e-05
rope_base = 100000000000.0
f32 = jnp.float32
bf16 = jnp.bfloat16


def project(left, right):
    return jnp.dot(left, right, preferred_element_type=f32)


def project_back(left, right):
    return lax.dot_general(left, right, (((1,), (1,)), ((), ())), preferred_element_type=f32)


def outer_sum(left, right):
    return lax.dot_general(left, right, (((0,), (0,)), ((), ())), preferred_element_type=f32)


def outer_low(left, right):
    return with_layout_constraint(outer_sum(left, right).astype(bf16), Layout(major_to_minor=(0, 1)))


def rms_scale(values):
    return lax.rsqrt(jnp.mean(values * values, axis=-1, keepdims=True) + epsilon)


def rms_back(grad, values, scale, gain):
    weighted = grad * gain
    inner = jnp.sum(weighted * values, axis=-1, keepdims=True)
    return scale * weighted - values * (scale * scale * scale * inner / values.shape[-1])


def shift_down(values, count):
    return jnp.concatenate([jnp.zeros((count, values.shape[1]), values.dtype), values[:-count]], axis=0)


def shift_up(values, count):
    return jnp.concatenate([values[count:], jnp.zeros((count, values.shape[1]), values.dtype)], axis=0)


def conv_sum(signal, kernel, position):
    summed = kernel[CONV][None, :] + signal * kernel[0][None, :]
    for tap in range(1, CONV):
        moved = jnp.where(position >= tap, shift_down(signal, tap), 0.0)
        summed = summed + moved * kernel[tap][None, :]
    return summed


def silu_back(values):
    sig = jax.nn.sigmoid(values)
    return sig * (1.0 + values * (1.0 - sig))


def conv_back(grad, signal, kernel, position):
    grad_sum = grad * silu_back(conv_sum(signal, kernel, position))
    grad_signal = grad_sum * kernel[0][None, :]
    grad_taps = [jnp.sum(grad_sum * signal, axis=0)]
    for tap in range(1, CONV):
        kept = jnp.where(position >= tap, grad_sum, 0.0)
        grad_signal = grad_signal + shift_up(kept, tap) * kernel[tap][None, :]
        grad_taps.append(jnp.sum(kept * shift_down(signal, tap), axis=0))
    grad_taps.append(jnp.sum(grad_sum, axis=0))
    return grad_signal, jnp.stack(grad_taps)


def rope_tables(position):
    half_size = HEAD // 2
    frequency = jnp.exp(jnp.arange(half_size, dtype=f32) * (-2.0 * math.log(rope_base) / HEAD))
    angles = position.astype(f32) * frequency[None, :]
    cosine, sine = jnp.cos(angles), jnp.sin(angles)
    return jnp.concatenate([cosine, cosine], axis=1), jnp.concatenate([-sine, sine], axis=1)


def copy_blocks(order_ref, first_ref, second_ref, first_out_ref, second_out_ref):
    first_out_ref[...] = first_ref[...]
    second_out_ref[...] = second_ref[...]


def pick_halves(values, order, block):
    height, width = values.shape
    count = width // block // 2
    if block % 128:
        mixed = jnp.take(values.reshape(height, -1, block), order, axis=1).reshape(height, width)
        return mixed[:, : width // 2], mixed[:, width // 2 :]
    half = jax.ShapeDtypeStruct((height, width // 2), values.dtype)
    out_spec = pl.BlockSpec((height, block), lambda i, order: (0, i))
    return pl.pallas_call(
        copy_blocks,
        out_shape=(half, half),
        grid_spec=pltpu.PrefetchScalarGridSpec(
            num_scalar_prefetch=1,
            grid=(count,),
            in_specs=[
                pl.BlockSpec((height, block), lambda i, order: (0, order[i])),
                pl.BlockSpec((height, block), lambda i, order: (0, order[i + count])),
            ],
            out_specs=(out_spec, out_spec),
        ),
        cost_estimate=pl.CostEstimate(flops=0, transcendentals=0, bytes_accessed=4 * height * width),
        name="pick_halves",
    )(order, values, values)


def hand_over(values, microseconds):
    def idle(values_ref, out_ref):
        pass

    return pl.pallas_call(
        idle,
        out_shape=jax.ShapeDtypeStruct(values.shape, values.dtype),
        in_specs=[pl.BlockSpec(memory_space=pl.ANY)],
        out_specs=pl.BlockSpec(memory_space=pl.ANY),
        input_output_aliases={0: 0},
        cost_estimate=pl.CostEstimate(flops=microseconds * 1150000000, transcendentals=0, bytes_accessed=0),
        name="hand_over",
    )(values)


NEGATIVE = -1e30


def sigmoid_of(values):
    return 1.0 / (1.0 + jnp.exp(-values))


def block_mask(rows, segment_col, segment_row):
    row_index = lax.broadcasted_iota(jnp.int32, (rows, rows), 0)
    col_index = lax.broadcasted_iota(jnp.int32, (rows, rows), 1)
    return jnp.where((segment_col == segment_row) & (col_index <= row_index), 0.0, NEGATIVE)


def conv_block(signal, taps_ref, position):
    summed = taps_ref[CONV : CONV + 1, :] + signal * taps_ref[0:1, :]
    moved = []
    for tap in range(1, CONV):
        shifted = jnp.where(position >= tap, pltpu.roll(signal, tap, 0), 0.0)
        moved.append(shifted)
        summed = summed + shifted * taps_ref[tap : tap + 1, :]
    return summed, moved


def conv_block_back(grad_sum, signal, moved, taps_ref, position, sums_ref):
    rows = signal.shape[0]
    grad_signal = grad_sum * taps_ref[0:1, :]
    sums_ref[0, 0:1, :] = jnp.sum(grad_sum * signal, axis=0, keepdims=True)
    for tap in range(1, CONV):
        kept = jnp.where(position >= tap, grad_sum, 0.0)
        grad_signal = grad_signal + pltpu.roll(kept, rows - tap, 0) * taps_ref[tap : tap + 1, :]
        sums_ref[0, tap : tap + 1, :] = jnp.sum(grad_sum * moved[tap - 1], axis=0, keepdims=True)
    sums_ref[0, CONV : CONV + 1, :] = jnp.sum(grad_sum, axis=0, keepdims=True)
    return grad_signal


def mixing_block(inner, mask, run_col, run_row, step_row):
    decay = jnp.exp(run_col - run_row + mask)
    return decay, (inner * decay * step_row).astype(bf16)


def turn(values, cosine_ref, sine_ref, sign):
    return values * cosine_ref[...] + sign * (pltpu.roll(values, HEAD // 2, 1) * sine_ref[...])


def head_probs(query_low, key_low, mask):
    logits = lax.dot_general(query_low, key_low, (((1,), (1,)), ((), ())), preferred_element_type=f32) * HEAD ** (-0.5)
    logits = logits + mask
    weights = jnp.exp(logits - jnp.max(logits, axis=1, keepdims=True))
    return weights / jnp.sum(weights, axis=1, keepdims=True)


def attention_forward_kernel(
    query_ref, key_ref, value_ref, cosine_ref, sine_ref, columns_ref, seg_row_ref,
    attended_ref, query_low_ref, key_low_ref, value_low_ref, mask_ref,
):
    rows = query_ref.shape[0]

    @pl.when(pl.program_id(1) == 0)
    def _():
        mask_ref[...] = block_mask(rows, columns_ref[:, 0:1], seg_row_ref[0])

    query_low = turn(query_ref[...], cosine_ref, sine_ref, 1.0).astype(bf16)
    key_low = turn(key_ref[...], cosine_ref, sine_ref, 1.0).astype(bf16)
    value_low = value_ref[...].astype(bf16)
    probs_low = head_probs(query_low, key_low, mask_ref[...]).astype(bf16)
    attended_ref[...] = jnp.dot(probs_low, value_low, preferred_element_type=f32).astype(bf16)
    query_low_ref[...] = query_low
    key_low_ref[...] = key_low
    value_low_ref[...] = value_low


def attention_backward_kernel(
    grad_ref, query_ref, key_ref, value_ref, cosine_ref, sine_ref, columns_ref, seg_row_ref,
    joint_ref, mask_ref, grad_key_ref, grad_value_ref, *, group, query_cols, key_cols,
):
    rows = query_ref.shape[0]
    head = pl.program_id(1)

    @pl.when(head == 0)
    def _():
        mask_ref[...] = block_mask(rows, columns_ref[:, 0:1], seg_row_ref[0])

    @pl.when(head % group == 0)
    def _():
        grad_key_ref[...] = jnp.zeros_like(grad_key_ref)
        grad_value_ref[...] = jnp.zeros_like(grad_value_ref)

    grad, query_low, key_low = grad_ref[...], query_ref[...], key_ref[...]
    probs = head_probs(query_low, key_low, mask_ref[...])
    grad_probs = lax.dot_general(grad, value_ref[...], (((1,), (1,)), ((), ())), preferred_element_type=f32)
    grad_value_ref[...] += lax.dot_general(
        probs.astype(bf16), grad, (((0,), (0,)), ((), ())), preferred_element_type=f32
    )
    grad_logits = (probs * (grad_probs - jnp.sum(probs * grad_probs, axis=1, keepdims=True))).astype(bf16)
    grad_query = jnp.dot(grad_logits, key_low, preferred_element_type=f32) * HEAD ** (-0.5)
    grad_key_ref[...] += lax.dot_general(
        grad_logits, query_low, (((0,), (0,)), ((), ())), preferred_element_type=f32
    ) * HEAD ** (-0.5)
    joint_ref[:, pl.ds(pl.multiple_of(head * HEAD, HEAD), HEAD)] = turn(
        grad_query, cosine_ref, sine_ref, -1.0
    ).astype(bf16)

    @pl.when(head % group == group - 1)
    def _():
        place = head // group * HEAD
        joint_ref[:, pl.ds(pl.multiple_of(query_cols + place, HEAD), HEAD)] = turn(
            grad_key_ref[...], cosine_ref, sine_ref, -1.0
        ).astype(bf16)
        joint_ref[:, pl.ds(pl.multiple_of(query_cols + key_cols + place, HEAD), HEAD)] = grad_value_ref[...].astype(bf16)


def attention_specs(rows, group):
    table = pl.BlockSpec((rows, HEAD), lambda m, h: (m, 0))
    return (
        lambda start: pl.BlockSpec((rows, HEAD), lambda m, h: (m, start + h)),
        lambda start: pl.BlockSpec((rows, HEAD), lambda m, h: (m, start + h // group)),
        [table, table, pl.BlockSpec((rows, 8), lambda m, h: (m, 0)), pl.BlockSpec((1, 1, rows), lambda m, h: (m, 0, 0))],
    )


def attention_forward(joint, query_cols, key_cols, tables):
    micro, _, rows = tables[3].shape
    total = joint.shape[0]
    heads, kv_heads = query_cols // HEAD, key_cols // HEAD
    by_head, by_kv, table_specs = attention_specs(rows, heads // kv_heads)
    return pl.pallas_call(
        attention_forward_kernel,
        out_shape=tuple(jax.ShapeDtypeStruct((total, size), bf16) for size in (query_cols, query_cols, key_cols, key_cols)),
        grid=(micro, heads),
        in_specs=[by_head(0), by_kv(heads), by_kv(heads + kv_heads)] + table_specs,
        out_specs=(by_head(0), by_head(0), by_kv(0), by_kv(0)),
        scratch_shapes=[pltpu.VMEM((rows, rows), f32)],
        cost_estimate=pl.CostEstimate(
            flops=4 * total * rows * query_cols, transcendentals=total * rows * heads, bytes_accessed=8 * total * query_cols
        ),
        name="attention_forward",
    )(joint, joint, joint, *tables)


def attention_backward(grad, query, key, value, tables):
    micro, _, rows = tables[3].shape
    total, query_cols = query.shape
    key_cols = key.shape[1]
    heads, kv_heads = query_cols // HEAD, key_cols // HEAD
    by_head, by_kv, table_specs = attention_specs(rows, heads // kv_heads)
    joint_cols = query_cols + 2 * key_cols
    return pl.pallas_call(
        functools.partial(
            attention_backward_kernel, group=heads // kv_heads, query_cols=query_cols, key_cols=key_cols
        ),
        out_shape=jax.ShapeDtypeStruct((total, joint_cols), bf16),
        grid=(micro, heads),
        in_specs=[by_head(0), by_head(0), by_kv(0), by_kv(0)] + table_specs,
        out_specs=pl.BlockSpec((rows, joint_cols), lambda m, h: (m, 0)),
        scratch_shapes=[pltpu.VMEM((rows, rows), f32), pltpu.VMEM((rows, HEAD), f32), pltpu.VMEM((rows, HEAD), f32)],
        cost_estimate=pl.CostEstimate(
            flops=10 * total * rows * query_cols, transcendentals=total * rows * heads, bytes_accessed=8 * total * query_cols
        ),
        name="attention_backward",
    )(grad, query, key, value, *tables)


def state_forward_kernel(
    signal_ref, gate_ref, taps_ref, skip_ref, state_ref, seg_row_ref, run_row_ref, run_col_ref, step_ref, columns_ref,
    out_ref, square_ref, inner_ref, mask_ref,
):
    rows = signal_ref.shape[0]
    position = columns_ref[:, 1:2]
    pair = pl.program_id(1)
    here = pl.ds(pl.multiple_of(pair * 2 * SHD, 2 * SHD), 2 * SHD)
    taps_ref, skip_ref = taps_ref.at[:, here], skip_ref.at[:, here]

    @pl.when(pl.program_id(1) == 0)
    def _():
        inner_ref[...] = lax.dot_general(
            state_ref[:, NS:], state_ref[:, :NS], (((1,), (1,)), ((), ())), preferred_element_type=f32
        )
        mask_ref[...] = block_mask(rows, columns_ref[:, 0:1], seg_row_ref[0])
        square_ref[...] = jnp.zeros_like(square_ref)

    summed, _ = conv_block(signal_ref[...], taps_ref, position)
    cols = summed * sigmoid_of(summed)
    cols_low = cols.astype(bf16)
    mixed = []
    for head in range(2):
        _, mixing = mixing_block(
            inner_ref[...], mask_ref[...], run_col_ref[0, pair, :, head : head + 1],
            run_row_ref[0, pair, head : head + 1, :], step_ref[0, pair, head : head + 1, :],
        )
        mixed.append(jnp.dot(mixing, cols_low, preferred_element_type=f32))
    lanes = lax.broadcasted_iota(jnp.int32, cols.shape, 1)
    out = jnp.where(lanes < SHD, mixed[0], mixed[1]) + skip_ref[...] * cols
    out_ref[...] = out
    gate = gate_ref[...]
    gated = out * (gate * sigmoid_of(gate))
    square_ref[...] += gated * gated


def state_backward_kernel(
    grad_ref, out_ref, gate_ref, signal_ref, taps_ref, skip_ref, gain_ref, state_ref, seg_row_ref, run_row_ref, run_col_ref,
    step_ref, columns_ref, state_raw_ref, state_taps_ref, step_all_ref, step_sig_ref, rate_ref, others_ref,
    first_ref, sums_ref, state_sums_ref, head_sums_ref,
    inner_ref, mask_ref, grad_inner_ref, direct_ref, along_ref,
):
    rows = signal_ref.shape[0]
    pair = pl.program_id(1)
    block = pl.ds(pl.multiple_of(pair * 2 * SHD, 2 * SHD), 2 * SHD)
    taps_ref, skip_ref, gain_ref = taps_ref.at[:, block], skip_ref.at[:, block], gain_ref.at[:, block]

    @pl.when(pair == 0)
    def _():
        along_ref[...] = jnp.zeros_like(along_ref)
        inner_ref[...] = lax.dot_general(
            state_ref[:, NS:], state_ref[:, :NS], (((1,), (1,)), ((), ())), preferred_element_type=f32
        )
        mask_ref[...] = block_mask(rows, columns_ref[:, 0:1], seg_row_ref[0])
        grad_inner_ref[...] = jnp.zeros_like(grad_inner_ref)

    grad, out, gate, signal = grad_ref[...], out_ref[...], gate_ref[...], signal_ref[...]
    position, scale, cross = columns_ref[:, 1:2], columns_ref[:, 2:3], columns_ref[:, 3:4]
    here = pl.multiple_of(pair * 2 * SHD, 2 * SHD)
    rest = first_ref.shape[1] // 2 - others_ref.shape[1] // 2 - NS - STEP_PAD // 2
    after_rest = rest + 2 * NS + STEP_PAD
    sig = sigmoid_of(gate)
    silu = gate * sig
    gated = out * silu
    scaled = grad * scale
    grad_gated = scaled * gain_ref[...] - gated * cross
    grad_out = grad_gated * silu
    first_ref[:, pl.ds(here, 2 * SHD)] = (grad_gated * out * (sig * (1.0 + gate * (1.0 - sig)))).astype(bf16)
    summed, moved = conv_block(signal, taps_ref, position)
    sig = sigmoid_of(summed)
    cols = summed * sig
    cols_low = cols.astype(bf16)
    grad_low = grad_out.astype(bf16)
    lanes = lax.broadcasted_iota(jnp.int32, cols.shape, 1)
    zero = jnp.zeros_like(grad_low)
    grad_cols = []
    for head in range(2):
        step_row = step_ref[0, pair, head : head + 1, :]
        inner = inner_ref[...]
        decay, mixing = mixing_block(
            inner, mask_ref[...], run_col_ref[0, pair, :, head : head + 1], run_row_ref[0, pair, head : head + 1, :], step_row
        )
        grad_cols.append(
            lax.dot_general(mixing, grad_low, (((0,), (0,)), ((), ())), preferred_element_type=f32)
        )
        grad_head = jnp.where((lanes < SHD) == (head == 0), grad_low, zero)
        grad_decay = lax.dot_general(
            grad_head, cols_low, (((1,), (1,)), ((), ())), preferred_element_type=f32
        ) * decay
        stepped = grad_decay * step_row
        grad_inner_ref[...] += stepped
        direct_ref[pl.ds(2 * pair + head, 1), :] = jnp.sum(grad_decay * inner, axis=0, keepdims=True)
        along = jnp.sum(stepped * inner, axis=1, keepdims=True)
        along_ref[...] = jnp.where(lanes == 2 * pair + head, along, along_ref[...])
    grad_cols = jnp.where(lanes < SHD, grad_cols[0], grad_cols[1]) + skip_ref[...] * grad_out
    grad_sum = grad_cols * (sig * (1.0 + summed * (1.0 - sig)))
    grad_signal = conv_block_back(grad_sum, signal, moved, taps_ref, position, sums_ref)
    sums_ref[0, CONV + 1 : CONV + 2, :] = jnp.sum(scaled * gated, axis=0, keepdims=True)
    sums_ref[0, CONV + 2 : CONV + 3, :] = jnp.sum(grad_out * cols, axis=0, keepdims=True)
    sums_ref[0, CONV + 3 : CONV + 4, :] = jnp.zeros((1, cols.shape[1]), f32)
    first_ref[:, pl.ds(pl.multiple_of(after_rest + here, 2 * SHD), 2 * SHD)] = grad_signal.astype(bf16)

    @pl.when(pair == pl.num_programs(1) - 1)
    def _():
        inner_low = grad_inner_ref[...].astype(bf16)
        for part, (mine, other) in enumerate((((0, NS), (NS, 2 * NS)), ((NS, 2 * NS), (0, NS)))):
            raw = state_raw_ref[:, mine[0] : mine[1]]
            taps = state_taps_ref.at[:, mine[0] : mine[1]]
            summed, moved = conv_block(raw, taps, position)
            sig = sigmoid_of(summed)
            grad = lax.dot_general(
                inner_low, state_ref[:, other[0] : other[1]], (((part,), (0,)), ((), ())), preferred_element_type=f32
            )
            grad_sum = grad * (sig * (1.0 + summed * (1.0 - sig)))
            back = conv_block_back(grad_sum, raw, moved, taps, position, state_sums_ref.at[:, :, mine[0] : mine[1]])
            first_ref[:, rest + mine[0] : rest + mine[1]] = back.astype(bf16)
        state_sums_ref[0, CONV + 1 :, :] = jnp.zeros((7 - CONV, 2 * NS), f32)
        heads = step_all_ref.shape[1]
        direct, step = direct_ref[...], step_all_ref[0]
        grad_running = along_ref[...].T[:heads] - step * direct
        row_index = lax.broadcasted_iota(jnp.int32, (rows, rows), 0)
        col_index = lax.broadcasted_iota(jnp.int32, (rows, rows), 1)
        lower = jnp.where(col_index <= row_index, 1.0, 0.0)
        grad_product = jnp.dot(
            grad_running, lower, precision=lax.Precision.HIGHEST, preferred_element_type=f32
        )
        grad_raw = (direct + grad_product * rate_ref[...]) * step_sig_ref[0]
        head_sums_ref[0, :, 0:1] = jnp.sum(grad_product * step, axis=1, keepdims=True)
        head_sums_ref[0, :, 1:2] = jnp.sum(grad_raw, axis=1, keepdims=True)
        wide = jnp.concatenate([grad_raw, jnp.zeros((STEP_PAD - heads, rows), f32)], axis=0)
        first_ref[:, rest + 2 * NS : after_rest] = wide.T.astype(bf16)
        first_ref[:, first_ref.shape[1] - others_ref.shape[1] :] = others_ref[...]


def state_specs(rows, pairs):
    block = pl.BlockSpec((rows, 2 * SHD), lambda m, p: (m, p))
    return {
        "block": block,
        "taps": pl.BlockSpec((CONV + 1, 2 * SHD * pairs), lambda m, p: (0, 0)),
        "vector": pl.BlockSpec((1, 2 * SHD * pairs), lambda m, p: (0, 0)),
        "state": pl.BlockSpec((rows, 2 * NS), lambda m, p: (m, 0)),
        "columns": pl.BlockSpec((rows, 8), lambda m, p: (m, 0)),
        "row": pl.BlockSpec((1, 1, rows), lambda m, p: (m, 0, 0)),
        "head_row": pl.BlockSpec((1, pairs, 2, rows), lambda m, p: (m, 0, 0, 0)),
        "head_col": pl.BlockSpec((1, pairs, rows, 2), lambda m, p: (m, 0, 0, 0)),
    }


def state_forward(signal, gate, taps, skip, state, seg_row, run_row, run_col, step, columns):
    micro, pairs, _, rows = run_row.shape
    spec = state_specs(rows, pairs)
    total, width = signal.shape
    return pl.pallas_call(
        state_forward_kernel,
        out_shape=(jax.ShapeDtypeStruct((total, width), f32), jax.ShapeDtypeStruct((total, 2 * SHD), f32)),
        grid=(micro, pairs),
        in_specs=[spec[name] for name in (
            "block", "block", "taps", "vector", "state", "row", "head_row", "head_col", "head_row", "columns")],
        out_specs=(spec["block"], pl.BlockSpec((rows, 2 * SHD), lambda m, p: (m, 0))),
        scratch_shapes=[pltpu.VMEM((rows, rows), f32), pltpu.VMEM((rows, rows), f32)],
        cost_estimate=pl.CostEstimate(
            flops=8 * total * rows * width // SHD * SHD, transcendentals=total * rows * width // SHD, bytes_accessed=12 * total * width
        ),
        name="state_forward",
    )(signal, gate, taps, skip, state, seg_row, run_row, run_col, step, columns)


def state_backward(
    grad, out, gate, signal, taps, skip, gain, state, seg_row, run_row, run_col, step, columns,
    state_raw, state_taps, step_all, step_sig, rate, others,
):
    micro, pairs, _, rows = run_row.shape
    heads = 2 * pairs
    spec = state_specs(rows, pairs)
    total, width = signal.shape
    joint = 2 * width + 2 * NS + STEP_PAD + others.shape[1]
    heads_block = pl.BlockSpec((1, heads, rows), lambda m, p: (m, 0, 0))
    return pl.pallas_call(
        state_backward_kernel,
        out_shape=(
            jax.ShapeDtypeStruct((total, joint), bf16),
            jax.ShapeDtypeStruct((micro, 8, width), f32),
            jax.ShapeDtypeStruct((micro, 8, 2 * NS), f32),
            jax.ShapeDtypeStruct((micro, heads, 2), f32),
        ),
        grid=(micro, pairs),
        in_specs=[spec[name] for name in (
            "block", "block", "block", "block", "taps", "vector", "vector", "state",
            "row", "head_row", "head_col", "head_row", "columns", "state")]
        + [
            pl.BlockSpec((CONV + 1, 2 * NS), lambda m, p: (0, 0)), heads_block, heads_block,
            pl.BlockSpec((heads, 1), lambda m, p: (0, 0)), pl.BlockSpec((rows, others.shape[1]), lambda m, p: (m, 0)),
        ],
        out_specs=(
            pl.BlockSpec((rows, joint), lambda m, p: (m, 0)), pl.BlockSpec((1, 8, 2 * SHD), lambda m, p: (m, 0, p)),
            pl.BlockSpec((1, 8, 2 * NS), lambda m, p: (m, 0, 0)),
            pl.BlockSpec((1, heads, 2), lambda m, p: (m, 0, 0)),
        ),
        scratch_shapes=[pltpu.VMEM((rows, rows), f32)] * 3 + [pltpu.VMEM((heads, rows), f32), pltpu.VMEM((rows, 2 * SHD), f32)],
        cost_estimate=pl.CostEstimate(
            flops=20 * total * rows * width, transcendentals=total * rows * width // SHD, bytes_accessed=20 * total * width
        ),
        name="state_backward",
    )(
        grad, out, gate, signal, taps, skip, gain, state, seg_row, run_row, run_col, step, columns,
        state_raw, state_taps, step_all, step_sig, rate, others,
    )


def local(
    inputs,
    out_grad,
    deal_order,
    segment,
    query_weight,
    key_weight,
    value_weight,
    attention_out,
    mamba_gate,
    mamba_input,
    step_weight,
    state_weight,
    mamba_out,
    feed_gate,
    feed_up,
    feed_down,
    gain_input,
    gain_middle,
    kernel_inner,
    kernel_state,
    mixer_gain,
    step_bias,
    log_rate,
    skip_gain,
):
    micro, own, width = inputs.shape
    groups = lax.axis_size("dp")
    lanes = lax.axis_size("tensor")
    lane = lax.axis_index("tensor")
    group = lax.axis_index("dp")
    device = group * lanes + lane
    per = own // groups
    rows = own * lanes
    total = micro * rows
    inner_width = SH * SHD
    outer_count = groups // 4
    shard = width // groups

    swap_lane = [(0, 1), (1, 0)]

    def other_lane(values):
        return lax.ppermute(values, "tensor", swap_lane)

    def other_group(values, bits):
        return lax.ppermute(values, "dp", [(i, i ^ bits) for i in range(groups)])

    step_padded = jnp.pad(step_weight, ((0, 0), (0, STEP_PAD - step_weight.shape[1])))
    early = dict(
        gate=mamba_gate, state=state_weight, step=step_padded, input=mamba_input, query=query_weight, key=key_weight,
        value=value_weight, mix=mamba_out, attn=attention_out,
    )
    late = dict(fgate=feed_gate, fup=feed_up, fdown=feed_down)
    whole, places_of = {}, {}
    for label, group_weights in (("early", early), ("late", late)):
        start = 0
        for name, weight in group_weights.items():
            places_of[name] = (label, start, weight.shape[1])
            start += weight.shape[1]
        whole[label] = lax.all_gather(jnp.concatenate(list(group_weights.values()), axis=1), "dp", axis=0, tiled=True)

    def full(name):
        label, start, size = places_of[name]
        return lax.slice_in_dim(whole[label], start, start + size, axis=1)

    own_places = jnp.arange(own, dtype=jnp.int32)
    own_order = lax.dynamic_slice_in_dim(deal_order, device * own, own, 1)
    micro_index = jnp.arange(micro, dtype=jnp.int32)[:, None]

    def buffer_place(destination, rank):
        return destination * (micro * per) + micro_index * per + rank

    send_rank = jnp.sum((own_order[:, None, :] < own_order[:, :, None]).astype(jnp.int32), axis=2)
    send_place = buffer_place(send_rank // per, send_rank % per).reshape(-1)
    lane_order = lax.dynamic_index_in_dim(deal_order.reshape(micro, groups, lanes, own), lane, 2, keepdims=False)
    slots = device * own + own_places
    found = lane_order[:, None, :, :] == slots[None, :, None, None]
    source = jnp.sum(
        jnp.where(found, jnp.arange(groups, dtype=jnp.int32)[None, None, :, None], 0), axis=(2, 3)
    )
    recv_rank = jnp.sum(
        ((source[:, None, :] == source[:, :, None]) & (own_places[None, None, :] < own_places[None, :, None])).astype(jnp.int32),
        axis=2,
    )
    recv_place = buffer_place(source, recv_rank).reshape(-1)
    buffer_places = jnp.arange(micro * own, dtype=jnp.int32)
    send_pick = (buffer_places[:, None] == send_place[None, :]).astype(bf16)
    recv_pick = (recv_place[:, None] == buffer_places[None, :]).astype(bf16)

    def exchange(buffer):
        return lax.all_to_all(
            buffer.reshape(groups, micro * per, width), "dp", split_axis=0, concat_axis=0, tiled=True
        ).reshape(micro * own, width)

    def deal(values):
        sent = project(send_pick, values.reshape(micro * own, width)).astype(bf16)
        return project(recv_pick, exchange(sent)).astype(bf16)

    def deal_order_rows(values):
        return outer_sum(recv_pick, values).astype(bf16)

    def deal_take(moved):
        return outer_sum(send_pick, moved).astype(bf16).reshape(micro, own, width)

    def join_lanes(values):
        mine = values.reshape(micro, 1, own, -1)
        theirs = other_lane(values).reshape(micro, 1, own, -1)
        low = jnp.where(lane == 0, mine, theirs)
        high = jnp.where(lane == 0, theirs, mine)
        return jnp.concatenate([low, high], axis=1).reshape(total, -1)

    def lane_rows(values, which):
        return lax.dynamic_index_in_dim(
            values.reshape(micro, lanes, own, -1), which, 1, keepdims=False
        ).reshape(micro * own, -1)

    own_in = deal(inputs)
    own_grad = deal(out_grad)
    whole_in = join_lanes(own_in)
    whole_grad = join_lanes(own_grad)

    before = jnp.sum((segment[:, None, :] < segment[:, :, None]).astype(jnp.int32), axis=2)
    places = jnp.arange(rows, dtype=jnp.int32)
    position = (places[None, :] - before).reshape(total, 1)

    masks = [1 << place for place in range(groups.bit_length() - 1)]
    relative = []
    for block in range(groups):
        flip = 0
        for place, mask in enumerate(masks):
            if block >> (len(masks) - 1 - place) & 1:
                flip ^= mask
        relative.append(flip)
    block_order = jnp.bitwise_xor(group.astype(jnp.int32), jnp.array(relative, jnp.int32))

    def split_left(left):
        return pick_halves(left, block_order, shard)

    inner_places = list(range(1, len(masks)))

    def core_send(left_parts, right):
        return outer_low(left_parts[1], right)

    def halve(kept, place):
        return (
            lax.slice_in_dim(kept, 1, 2, axis=place - 1).reshape(-1, kept.shape[-1]),
            lax.slice_in_dim(kept, 0, 1, axis=place - 1),
        )

    class Reduction:
        def __init__(self, first):
            self.places = [place for place in first if place in inner_places]
            self.places += [place for place in inner_places if place not in first]
            self.stage = 0

        def move(self, send, kept):
            self.came = other_group(send, masks[self.places[self.stage]])
            self.kept = kept
            self.stage += 1

        def first(self, left_parts, right, from_core):
            kept = (outer_sum(left_parts[0], right) + from_core.astype(f32)).astype(bf16)
            kept = kept.reshape((2,) * len(inner_places) + (shard, -1))
            return halve(kept, self.places[0])

        def added(self):
            return self.kept.astype(f32) + self.came.reshape(self.kept.shape).astype(f32)

        def next(self):
            return halve(self.added().astype(bf16), self.places[self.stage])

        def last(self):
            return self.added().reshape(shard, -1)

        def step(self):
            return self.next() if self.stage < len(self.places) else self.last()

    order = [deal_order[0, 0] >= 0]

    def unit(work):
        shapes = jax.eval_shape(work)
        results = lax.cond(
            order[0], work, lambda: jax.tree.map(lambda leaf: jnp.zeros(leaf.shape, leaf.dtype), shapes)
        )
        leaves, form = jax.tree.flatten(results)
        least = min(range(len(leaves)), key=lambda place: leaves[place].size)
        leaves[least], order[0] = lax.optimization_barrier((leaves[least], order[0]))
        return jax.tree.unflatten(form, leaves)

    def after(value, *others):
        return lax.optimization_barrier((value, others))[0]

    in32 = whole_in.astype(f32)
    in_scale = rms_scale(in32)
    normed_low = (in32 * in_scale * gain_input).astype(bf16)
    normed_left = split_left(normed_low)
    whole["early"] = after(whole["early"], whole_grad, normed_left)
    gate_z = project(normed_low, full("gate"))
    ssm_in = project(normed_low, full("input"))
    state_raw = project(normed_low, full("state"))
    heads = step_weight.shape[1]
    raw_step = project(normed_low, full("step"))[:, :heads]
    state_low = jax.nn.silu(conv_sum(state_raw, kernel_state, position)).astype(bf16)
    rate = -jnp.exp(log_rate)
    step_size = jax.nn.softplus(raw_step + step_bias)
    step_heads = step_size.reshape(micro, rows, heads).transpose(0, 2, 1)
    lower = (places[None, :] <= places[:, None]).astype(f32)
    running = jnp.einsum(
        "mhj,ij->mhi", step_heads * rate[None, :, None], lower, precision=lax.Precision.HIGHEST, preferred_element_type=f32
    )
    pairs = heads // 2
    run_row = running.reshape(micro, pairs, 2, rows)
    run_col = run_row.transpose(0, 1, 3, 2)
    step_row = step_heads.reshape(micro, pairs, 2, rows)
    skip_wide = jnp.repeat(skip_gain, SHD)[None, :]
    layout = (state_low, segment.reshape(micro, 1, rows).astype(f32), run_row, run_col, step_row)
    row_facts = jnp.concatenate([segment.reshape(total, 1).astype(f32), position.astype(f32)], axis=1)
    row_columns = jnp.pad(row_facts, ((0, 0), (0, 6)))
    query_cols, key_cols = query_weight.shape[1], key_weight.shape[1]
    attention_tables = (*rope_tables(position), row_columns, layout[1])
    joint_start = places_of["query"][1]
    joint_weight = lax.slice_in_dim(whole["early"], joint_start, joint_start + query_cols + 2 * key_cols, axis=1)
    ssm_out, squares = state_forward(ssm_in, gate_z, kernel_inner, skip_wide, *layout, row_columns)
    attended_low, query_low, key_low, value_low = attention_forward(
        project(normed_low, joint_weight), query_cols, key_cols, attention_tables
    )
    square_own = jnp.sum(squares, axis=1)
    square_sum = square_own + other_lane(square_own)
    inv_rms = lax.rsqrt(square_sum / inner_width + epsilon)[:, None]
    gated_low = (ssm_out * jax.nn.silu(gate_z) * inv_rms * mixer_gain).astype(bf16)

    branch_part = (project_back(gated_low, full("mix")) + project_back(attended_low, full("attn"))).astype(bf16)
    branch = branch_part.astype(f32) + other_lane(branch_part).astype(f32)
    whole_mid = (in32 + branch).astype(bf16)
    mid32 = whole_mid.astype(f32)
    mid_scale = rms_scale(mid32)
    mid_low = (mid32 * mid_scale * gain_middle).astype(bf16)
    red_fgate, red_fup, red_low, red_high = [Reduction(places) for places in ((1, 2), (2, 1), (1, 2), (2, 1))]
    feeds = (red_fgate, red_fup)
    ff_cols = feed_gate.shape[1]
    gate_cols = mamba_gate.shape[1]

    def feed_forward():
        gate_ff = project(mid_low, full("fgate"))
        up_ff = project(mid_low, full("fup"))
        sig_ff = jax.nn.sigmoid(gate_ff)
        hidden_low = (gate_ff * sig_ff * up_ff).astype(bf16)
        grad_hidden = project(whole_grad, full("fdown"))
        gate_ff_low = (grad_hidden * up_ff * (sig_ff * (1.0 + gate_ff * (1.0 - sig_ff)))).astype(bf16)
        up_ff_low = (grad_hidden * (gate_ff * sig_ff)).astype(bf16)
        grad_mid_norm = project_back(gate_ff_low, full("fgate")) + project_back(up_ff_low, full("fup"))
        grad_gain_mid = jnp.sum(grad_mid_norm * mid32 * mid_scale, axis=0)
        mid_part = rms_back(grad_mid_norm, mid32, mid_scale, gain_middle).astype(bf16)
        return grad_gain_mid, mid_part, hidden_low, (gate_ff_low, up_ff_low), outer_low(whole_grad, hidden_low)

    grad_gain_mid, mid_part, hidden_low, feed_low, part_fdown = unit(feed_forward)
    sum_fdown = lax.psum_scatter(part_fdown, "dp", scatter_dimension=0, tiled=True)
    mid_other = hand_over(other_lane(mid_part), 45)

    def feed_output():
        ffn_part = project_back(hidden_low, full("fdown")).astype(bf16)
        mid_left = split_left(mid_low)
        return (
            lane_rows(ffn_part, lane), lane_rows(ffn_part, 1 - lane), mid_left[0],
            [core_send(mid_left, right) for right in feed_low],
        )

    ffn_own, ffn_send, mid_keep, send_feed = unit(feed_output)
    feed_came = [other_group(send, 1) for send in send_feed]

    def keep_first(keep, right, came, reductions, sizes):
        kept = (outer_sum(keep, right) + came.astype(f32)).astype(bf16)
        kept = kept.reshape((2,) * len(inner_places) + (shard, -1))
        moves, start = [], 0
        for red, size in zip(reductions, sizes):
            moves.append(halve(kept[..., start : start + size], red.places[0]))
            start += size
        return moves

    def settle(reductions, steps):
        for red, step in zip(reductions, steps):
            if red.stage < len(red.places):
                red.move(*step)
            else:
                red.result = step

    mid_other, feed_came = lax.optimization_barrier((mid_other, feed_came))
    moves = unit(
        lambda: [
            keep_first(mid_keep, right, came, (red,), (ff_cols,))[0] for red, right, came in zip(feeds, feed_low, feed_came)
        ]
    )
    for red, move in zip(feeds, moves):
        red.move(*move)

    def branch_backward():
        grad_middle = whole_grad.astype(f32) + (mid_part.astype(f32) + mid_other.astype(f32))
        whole_branch = grad_middle.astype(bf16)
        grad_gated_norm = project(whole_branch, full("mix"))
        cross_own = jnp.sum(grad_gated_norm * mixer_gain * (ssm_out * jax.nn.silu(gate_z)), axis=1)
        grad_attended = project(whole_branch, full("attn")).astype(bf16)
        joint_low = attention_backward(grad_attended, query_low, key_low, value_low, attention_tables)
        return (
            cross_own, lane_rows(grad_middle, lane), grad_gated_norm, whole_branch,
            joint_low,
        )

    cross_own, grad_middle_own, grad_gated_norm, whole_branch, joint_low = unit(branch_backward)
    cross_other = other_lane(cross_own)

    ffn_other = other_lane(ffn_send)

    def branch_partial():
        ffn_out = ffn_own.astype(f32) + ffn_other.astype(f32)
        out_rows = (lane_rows(whole_mid, lane).astype(f32) + ffn_out).astype(bf16)
        return outer_low(whole_branch, jnp.concatenate([gated_low, attended_low], axis=1)), deal_order_rows(out_rows)

    part_branch, out_sent = unit(branch_partial)
    out_moved = exchange(out_sent)
    sum_branch = lax.psum_scatter(part_branch, "dp", scatter_dimension=0, tiled=True)

    def state_space_backward():
        cross = (inv_rms**3) * ((cross_own + cross_other)[:, None] / inner_width)
        step_sig = jax.nn.sigmoid(raw_step + step_bias).reshape(micro, rows, heads).transpose(0, 2, 1)
        columns = jnp.pad(jnp.concatenate([row_facts, inv_rms, cross], axis=1), ((0, 0), (0, 4)))
        first_right, column_sums, state_sums, head_sums = state_backward(
            grad_gated_norm, ssm_out, gate_z, ssm_in, kernel_inner, skip_wide, mixer_gain[None, :], *layout, columns,
            state_raw, kernel_state, step_heads, step_sig, rate[:, None], joint_low,
        )
        return column_sums, state_sums, head_sums, first_right

    column_sums, state_sums, head_sums, first_right = unit(state_space_backward)

    total_fdown_low = [sum_fdown]
    order[0], total_fdown_low = lax.optimization_barrier((order[0], total_fdown_low))
    send_first, steps, block_out = unit(
        lambda: (core_send(normed_left, first_right), [red.step() for red in feeds], deal_take(out_moved))
    )
    settle(feeds, steps)
    first_came = other_group(send_first, 1)

    def input_gradient():
        grad_normed = project_back(first_right, lax.slice_in_dim(whole["early"], 0, first_right.shape[1], axis=1))
        grad_gain_in = jnp.sum(grad_normed * in32 * in_scale, axis=0)
        in_part = rms_back(grad_normed, in32, in_scale, gain_input).astype(bf16)
        return grad_gain_in, lane_rows(in_part, lane), lane_rows(in_part, 1 - lane)

    grad_gain_in, in_own, in_send = unit(input_gradient)

    firsts = (red_low, red_high)
    low_size = gate_cols + 2 * NS + STEP_PAD
    first_sizes = (low_size, first_right.shape[1] - low_size)

    def first_moves():
        moves = keep_first(normed_left[0], first_right, first_came, firsts, first_sizes)
        head_row = (jnp.sum(head_sums, axis=0).T * jnp.stack([rate, jnp.ones_like(rate)])).reshape(1, -1)
        flat = jnp.concatenate(
            [
                jnp.concatenate([jnp.sum(column_sums, axis=0), jnp.sum(state_sums, axis=0)], axis=1),
                grad_gain_in[None, :], grad_gain_mid[None, :], jnp.pad(head_row, ((0, 5), (0, width - head_row.shape[1]))),
            ]
        )
        return moves, lax.optimization_barrier(in_send), [red.step() for red in feeds], flat

    moves, in_send, steps, flat = unit(first_moves)
    flat_moved = other_group(flat, masks[0])
    settle(feeds, steps)
    for red, move in zip(firsts, moves):
        red.move(*move)
    in_other = hand_over(other_lane(in_send), 6)

    flat = unit(lambda: flat + flat_moved)
    flat_moved = other_group(flat, masks[1])

    def send_input():
        in_sum = in_own.astype(f32) + in_other.astype(f32)
        return deal_order_rows((in_sum + grad_middle_own).astype(bf16))

    in_moved = None
    everything = [*feeds, *firsts]
    bits = 2

    def finish():
        low, high = red_low.result, red_high.result
        state_rows = low[:, gate_cols : gate_cols + 2 * NS].reshape(lanes, shard // lanes, 2 * NS)
        cut = [0, gate_cols, gate_cols + query_cols, gate_cols + query_cols + key_cols, high.shape[1]]
        pieces = (
            low[:, :gate_cols], low[:, gate_cols + 2 * NS : gate_cols + 2 * NS + heads],
            [high[:, start:stop] for start, stop in zip(cut, cut[1:])],
            [lax.dynamic_index_in_dim(state_rows, which, 0, keepdims=False) for which in (lane, 1 - lane)],
        )
        return pieces, deal_take(in_moved)

    arrived = [red.came for red in feeds] + [sum_branch]
    order[0], arrived = lax.optimization_barrier((order[0], arrived))
    for red, came in zip(feeds, arrived):
        red.came = came
    wides = None
    while pending := [red for red in everything if not hasattr(red, "result")]:
        if in_moved is None:
            pending = list(firsts)
        widen = in_moved is not None and wides is None
        last = all(red.stage == len(red.places) for red in pending) and in_moved is not None

        def round_work():
            steps = [red.step() for red in pending]
            added = flat + flat_moved if bits <= len(masks) else flat
            wide = [arrived[-1].astype(f32), total_fdown_low[0].astype(f32)] if widen else ()
            if last:
                for red, step in zip(pending, steps):
                    red.result = step
                return steps, added, wide, finish()
            return steps, added, wide, send_input() if in_moved is None else ()

        steps, flat, wide, other = unit(round_work)
        if widen:
            wides = wide
        if bits < len(masks):
            flat_moved = other_group(flat, masks[bits])
        bits += 1
        if last:
            break
        settle(pending, steps)
        if in_moved is None:
            in_moved = exchange(other)
    for red, step in zip(pending, steps):
        red.result = step
    (total_gate, total_step, (total_input, total_query, total_key, total_value), states), grad_input = other
    while bits <= len(masks):
        flat = flat + flat_moved
        if bits < len(masks):
            flat_moved = other_group(flat, masks[bits])
        bits += 1
    theirs = other_lane(flat)
    low, high = jnp.where(lane == 0, flat, theirs), jnp.where(lane == 0, theirs, flat)
    both = flat + theirs

    def joined(row, start, count):
        return jnp.concatenate([low[row, start : start + count], high[row, start : start + count]])

    sum_gin, sum_gmid = both[8], both[9]
    sum_kst = both[: CONV + 1, gate_cols : gate_cols + 2 * NS]
    sum_kin = jnp.concatenate([low[: CONV + 1, :gate_cols], high[: CONV + 1, :gate_cols]], axis=1)
    sum_mix = joined(CONV + 1, 0, gate_cols)
    sum_skip = jnp.sum(joined(CONV + 2, 0, gate_cols).reshape(SH, SHD), axis=1)
    sum_bias = joined(10, heads, heads)
    sum_rate = joined(10, 0, heads)

    total_fgate, total_fup = red_fgate.result, red_fup.result
    total_branch, total_fdown = wides
    total_mix, total_attn = total_branch[:, :gate_cols], total_branch[:, gate_cols:]
    state_lane = states[0] + other_lane(states[1])
    return (
        block_out,
        grad_input,
        total_query,
        total_key,
        total_value,
        total_attn,
        total_gate,
        total_input,
        total_step,
        state_lane,
        total_mix,
        total_fgate,
        total_fup,
        total_fdown,
        sum_gin,
        sum_gmid,
        sum_kin,
        sum_kst,
        sum_mix,
        sum_bias,
        sum_rate,
        sum_skip,
    )


def solution(mesh):
    both = P("dp", "tensor")
    in_specs = (
        P(None, ("dp", "tensor"), None),
        P(None, ("dp", "tensor"), None),
        P(),
        P(None, "dp"),
        both,
        both,
        both,
        both,
        both,
        both,
        both,
        P("dp", None),
        both,
        both,
        both,
        both,
        P(),
        P(),
        P(None, "tensor"),
        P(),
        P("tensor"),
        P("tensor"),
        P("tensor"),
        P("tensor"),
    )
    out_specs = (
        P(None, ("dp", "tensor"), None),
        P(None, ("dp", "tensor"), None),
        both,
        both,
        both,
        both,
        both,
        both,
        both,
        P(("dp", "tensor"), None),
        both,
        both,
        both,
        both,
        P(),
        P(),
        P(),
        P(),
        P(),
        P(),
        P(),
        P(),
    )
    return jax.shard_map(local, mesh=mesh, in_specs=in_specs, out_specs=out_specs, check_vma=False)
```

```python
import functools
import math

import jax
import jax.numpy as jnp
from jax import lax
from jax.experimental import pallas as pl
from jax.experimental.layout import Layout, with_layout_constraint
from jax.experimental.pallas import tpu as pltpu
from jax.sharding import PartitionSpec as P

HEAD = 128
SH = 48
SHD = 64
NS = 256
CONV = 4
STEP_PAD = 128

epsilon = 1e-05
rope_base = 100000000000.0
f32 = jnp.float32
bf16 = jnp.bfloat16


def project(left, right):
    return jnp.dot(left, right, preferred_element_type=f32)


def project_back(left, right):
    return lax.dot_general(left, right, (((1,), (1,)), ((), ())), preferred_element_type=f32)


def outer_sum(left, right):
    return lax.dot_general(left, right, (((0,), (0,)), ((), ())), preferred_element_type=f32)


def outer_low(left, right):
    return with_layout_constraint(outer_sum(left, right).astype(bf16), Layout(major_to_minor=(0, 1)))


def rms_scale(values):
    return lax.rsqrt(jnp.mean(values * values, axis=-1, keepdims=True) + epsilon)


def rms_back(grad, values, scale, gain):
    weighted = grad * gain
    inner = jnp.sum(weighted * values, axis=-1, keepdims=True)
    return scale * weighted - values * (scale * scale * scale * inner / values.shape[-1])


def shift_down(values, count):
    return jnp.concatenate([jnp.zeros((count, values.shape[1]), values.dtype), values[:-count]], axis=0)


def shift_up(values, count):
    return jnp.concatenate([values[count:], jnp.zeros((count, values.shape[1]), values.dtype)], axis=0)


def conv_sum(signal, kernel, position):
    summed = kernel[CONV][None, :] + signal * kernel[0][None, :]
    for tap in range(1, CONV):
        moved = jnp.where(position >= tap, shift_down(signal, tap), 0.0)
        summed = summed + moved * kernel[tap][None, :]
    return summed


def silu_back(values):
    sig = jax.nn.sigmoid(values)
    return sig * (1.0 + values * (1.0 - sig))


def conv_back(grad, signal, kernel, position):
    grad_sum = grad * silu_back(conv_sum(signal, kernel, position))
    grad_signal = grad_sum * kernel[0][None, :]
    grad_taps = [jnp.sum(grad_sum * signal, axis=0)]
    for tap in range(1, CONV):
        kept = jnp.where(position >= tap, grad_sum, 0.0)
        grad_signal = grad_signal + shift_up(kept, tap) * kernel[tap][None, :]
        grad_taps.append(jnp.sum(kept * shift_down(signal, tap), axis=0))
    grad_taps.append(jnp.sum(grad_sum, axis=0))
    return grad_signal, jnp.stack(grad_taps)


def rope_tables(position):
    half_size = HEAD // 2
    frequency = jnp.exp(jnp.arange(half_size, dtype=f32) * (-2.0 * math.log(rope_base) / HEAD))
    angles = position.astype(f32) * frequency[None, :]
    cosine, sine = jnp.cos(angles), jnp.sin(angles)
    return jnp.concatenate([cosine, cosine], axis=1), jnp.concatenate([-sine, sine], axis=1)


def copy_blocks(order_ref, first_ref, second_ref, first_out_ref, second_out_ref):
    first_out_ref[...] = first_ref[...]
    second_out_ref[...] = second_ref[...]


def pick_halves(values, order, block):
    height, width = values.shape
    count = width // block // 2
    if block % 128:
        mixed = jnp.take(values.reshape(height, -1, block), order, axis=1).reshape(height, width)
        return mixed[:, : width // 2], mixed[:, width // 2 :]
    half = jax.ShapeDtypeStruct((height, width // 2), values.dtype)
    out_spec = pl.BlockSpec((height, block), lambda i, order: (0, i))
    return pl.pallas_call(
        copy_blocks,
        out_shape=(half, half),
        grid_spec=pltpu.PrefetchScalarGridSpec(
            num_scalar_prefetch=1,
            grid=(count,),
            in_specs=[
                pl.BlockSpec((height, block), lambda i, order: (0, order[i])),
                pl.BlockSpec((height, block), lambda i, order: (0, order[i + count])),
            ],
            out_specs=(out_spec, out_spec),
        ),
        cost_estimate=pl.CostEstimate(flops=0, transcendentals=0, bytes_accessed=4 * height * width),
        name="pick_halves",
    )(order, values, values)


def hand_over(values, microseconds):
    def idle(values_ref, out_ref):
        pass

    return pl.pallas_call(
        idle,
        out_shape=jax.ShapeDtypeStruct(values.shape, values.dtype),
        in_specs=[pl.BlockSpec(memory_space=pl.ANY)],
        out_specs=pl.BlockSpec(memory_space=pl.ANY),
        input_output_aliases={0: 0},
        cost_estimate=pl.CostEstimate(flops=microseconds * 1150000000, transcendentals=0, bytes_accessed=0),
        name="hand_over",
    )(values)


NEGATIVE = -1e30


def sigmoid_of(values):
    return 1.0 / (1.0 + jnp.exp(-values))


def block_mask(rows, segment_col, segment_row):
    row_index = lax.broadcasted_iota(jnp.int32, (rows, rows), 0)
    col_index = lax.broadcasted_iota(jnp.int32, (rows, rows), 1)
    return jnp.where((segment_col == segment_row) & (col_index <= row_index), 0.0, NEGATIVE)


def conv_block(signal, taps_ref, position):
    summed = taps_ref[CONV : CONV + 1, :] + signal * taps_ref[0:1, :]
    moved = []
    for tap in range(1, CONV):
        shifted = jnp.where(position >= tap, pltpu.roll(signal, tap, 0), 0.0)
        moved.append(shifted)
        summed = summed + shifted * taps_ref[tap : tap + 1, :]
    return summed, moved


def conv_block_back(grad_sum, signal, moved, taps_ref, position, sums_ref):
    rows = signal.shape[0]
    grad_signal = grad_sum * taps_ref[0:1, :]
    sums_ref[0, 0:1, :] = jnp.sum(grad_sum * signal, axis=0, keepdims=True)
    for tap in range(1, CONV):
        kept = jnp.where(position >= tap, grad_sum, 0.0)
        grad_signal = grad_signal + pltpu.roll(kept, rows - tap, 0) * taps_ref[tap : tap + 1, :]
        sums_ref[0, tap : tap + 1, :] = jnp.sum(grad_sum * moved[tap - 1], axis=0, keepdims=True)
    sums_ref[0, CONV : CONV + 1, :] = jnp.sum(grad_sum, axis=0, keepdims=True)
    return grad_signal


def mixing_block(inner, mask, run_col, run_row, step_row):
    decay = jnp.exp(run_col - run_row + mask)
    return decay, (inner * decay * step_row).astype(bf16)


def turn(values, cosine_ref, sine_ref, sign):
    return values * cosine_ref[...] + sign * (pltpu.roll(values, HEAD // 2, 1) * sine_ref[...])


def head_probs(query_low, key_low, mask):
    logits = lax.dot_general(query_low, key_low, (((1,), (1,)), ((), ())), preferred_element_type=f32) * HEAD ** (-0.5)
    logits = logits + mask
    weights = jnp.exp(logits - jnp.max(logits, axis=1, keepdims=True))
    return weights / jnp.sum(weights, axis=1, keepdims=True)


def attention_forward_kernel(
    query_ref, key_ref, value_ref, cosine_ref, sine_ref, columns_ref, seg_row_ref,
    attended_ref, query_low_ref, key_low_ref, value_low_ref, mask_ref,
):
    rows = query_ref.shape[0]

    @pl.when(pl.program_id(1) == 0)
    def _():
        mask_ref[...] = block_mask(rows, columns_ref[:, 0:1], seg_row_ref[0])

    query_low = turn(query_ref[...], cosine_ref, sine_ref, 1.0).astype(bf16)
    key_low = turn(key_ref[...], cosine_ref, sine_ref, 1.0).astype(bf16)
    value_low = value_ref[...].astype(bf16)
    probs_low = head_probs(query_low, key_low, mask_ref[...]).astype(bf16)
    attended_ref[...] = jnp.dot(probs_low, value_low, preferred_element_type=f32).astype(bf16)
    query_low_ref[...] = query_low
    key_low_ref[...] = key_low
    value_low_ref[...] = value_low


def attention_backward_kernel(
    grad_ref, query_ref, key_ref, value_ref, cosine_ref, sine_ref, columns_ref, seg_row_ref,
    joint_ref, mask_ref, grad_key_ref, grad_value_ref, *, group, query_cols, key_cols,
):
    rows = query_ref.shape[0]
    head = pl.program_id(1)

    @pl.when(head == 0)
    def _():
        mask_ref[...] = block_mask(rows, columns_ref[:, 0:1], seg_row_ref[0])

    @pl.when(head % group == 0)
    def _():
        grad_key_ref[...] = jnp.zeros_like(grad_key_ref)
        grad_value_ref[...] = jnp.zeros_like(grad_value_ref)

    grad, query_low, key_low = grad_ref[...], query_ref[...], key_ref[...]
    probs = head_probs(query_low, key_low, mask_ref[...])
    grad_probs = lax.dot_general(grad, value_ref[...], (((1,), (1,)), ((), ())), preferred_element_type=f32)
    grad_value_ref[...] += lax.dot_general(
        probs.astype(bf16), grad, (((0,), (0,)), ((), ())), preferred_element_type=f32
    )
    grad_logits = (probs * (grad_probs - jnp.sum(probs * grad_probs, axis=1, keepdims=True))).astype(bf16)
    grad_query = jnp.dot(grad_logits, key_low, preferred_element_type=f32) * HEAD ** (-0.5)
    grad_key_ref[...] += lax.dot_general(
        grad_logits, query_low, (((0,), (0,)), ((), ())), preferred_element_type=f32
    ) * HEAD ** (-0.5)
    joint_ref[:, pl.ds(pl.multiple_of(head * HEAD, HEAD), HEAD)] = turn(
        grad_query, cosine_ref, sine_ref, -1.0
    ).astype(bf16)

    @pl.when(head % group == group - 1)
    def _():
        place = head // group * HEAD
        joint_ref[:, pl.ds(pl.multiple_of(query_cols + place, HEAD), HEAD)] = turn(
            grad_key_ref[...], cosine_ref, sine_ref, -1.0
        ).astype(bf16)
        joint_ref[:, pl.ds(pl.multiple_of(query_cols + key_cols + place, HEAD), HEAD)] = grad_value_ref[...].astype(bf16)


def attention_specs(rows, group):
    table = pl.BlockSpec((rows, HEAD), lambda m, h: (m, 0))
    return (
        lambda start: pl.BlockSpec((rows, HEAD), lambda m, h: (m, start + h)),
        lambda start: pl.BlockSpec((rows, HEAD), lambda m, h: (m, start + h // group)),
        [table, table, pl.BlockSpec((rows, 8), lambda m, h: (m, 0)), pl.BlockSpec((1, 1, rows), lambda m, h: (m, 0, 0))],
    )


def attention_forward(joint, query_cols, key_cols, tables):
    micro, _, rows = tables[3].shape
    total = joint.shape[0]
    heads, kv_heads = query_cols // HEAD, key_cols // HEAD
    by_head, by_kv, table_specs = attention_specs(rows, heads // kv_heads)
    return pl.pallas_call(
        attention_forward_kernel,
        out_shape=tuple(jax.ShapeDtypeStruct((total, size), bf16) for size in (query_cols, query_cols, key_cols, key_cols)),
        grid=(micro, heads),
        in_specs=[by_head(0), by_kv(heads), by_kv(heads + kv_heads)] + table_specs,
        out_specs=(by_head(0), by_head(0), by_kv(0), by_kv(0)),
        scratch_shapes=[pltpu.VMEM((rows, rows), f32)],
        cost_estimate=pl.CostEstimate(
            flops=4 * total * rows * query_cols, transcendentals=total * rows * heads, bytes_accessed=8 * total * query_cols
        ),
        name="attention_forward",
    )(joint, joint, joint, *tables)


def attention_backward(grad, query, key, value, tables):
    micro, _, rows = tables[3].shape
    total, query_cols = query.shape
    key_cols = key.shape[1]
    heads, kv_heads = query_cols // HEAD, key_cols // HEAD
    by_head, by_kv, table_specs = attention_specs(rows, heads // kv_heads)
    joint_cols = query_cols + 2 * key_cols
    return pl.pallas_call(
        functools.partial(
            attention_backward_kernel, group=heads // kv_heads, query_cols=query_cols, key_cols=key_cols
        ),
        out_shape=jax.ShapeDtypeStruct((total, joint_cols), bf16),
        grid=(micro, heads),
        in_specs=[by_head(0), by_head(0), by_kv(0), by_kv(0)] + table_specs,
        out_specs=pl.BlockSpec((rows, joint_cols), lambda m, h: (m, 0)),
        scratch_shapes=[pltpu.VMEM((rows, rows), f32), pltpu.VMEM((rows, HEAD), f32), pltpu.VMEM((rows, HEAD), f32)],
        cost_estimate=pl.CostEstimate(
            flops=10 * total * rows * query_cols, transcendentals=total * rows * heads, bytes_accessed=8 * total * query_cols
        ),
        name="attention_backward",
    )(grad, query, key, value, *tables)


def state_forward_kernel(
    signal_ref, gate_ref, taps_ref, skip_ref, state_ref, seg_row_ref, run_row_ref, run_col_ref, step_ref, columns_ref,
    out_ref, square_ref, inner_ref, mask_ref,
):
    rows = signal_ref.shape[0]
    position = columns_ref[:, 1:2]
    pair = pl.program_id(1)
    here = pl.ds(pl.multiple_of(pair * 2 * SHD, 2 * SHD), 2 * SHD)
    taps_ref, skip_ref = taps_ref.at[:, here], skip_ref.at[:, here]

    @pl.when(pl.program_id(1) == 0)
    def _():
        inner_ref[...] = lax.dot_general(
            state_ref[:, NS:], state_ref[:, :NS], (((1,), (1,)), ((), ())), preferred_element_type=f32
        )
        mask_ref[...] = block_mask(rows, columns_ref[:, 0:1], seg_row_ref[0])
        square_ref[...] = jnp.zeros_like(square_ref)

    summed, _ = conv_block(signal_ref[...], taps_ref, position)
    cols = summed * sigmoid_of(summed)
    cols_low = cols.astype(bf16)
    mixed = []
    for head in range(2):
        _, mixing = mixing_block(
            inner_ref[...], mask_ref[...], run_col_ref[0, pair, :, head : head + 1],
            run_row_ref[0, pair, head : head + 1, :], step_ref[0, pair, head : head + 1, :],
        )
        mixed.append(jnp.dot(mixing, cols_low, preferred_element_type=f32))
    lanes = lax.broadcasted_iota(jnp.int32, cols.shape, 1)
    out = jnp.where(lanes < SHD, mixed[0], mixed[1]) + skip_ref[...] * cols
    out_ref[...] = out
    gate = gate_ref[...]
    gated = out * (gate * sigmoid_of(gate))
    square_ref[...] += gated * gated


def state_backward_kernel(
    grad_ref, out_ref, gate_ref, signal_ref, taps_ref, skip_ref, gain_ref, state_ref, seg_row_ref, run_row_ref, run_col_ref,
    step_ref, columns_ref, state_raw_ref, state_taps_ref, step_all_ref, step_sig_ref, rate_ref, others_ref,
    first_ref, sums_ref, state_sums_ref, head_sums_ref,
    inner_ref, mask_ref, grad_inner_ref, direct_ref, along_ref,
):
    rows = signal_ref.shape[0]
    pair = pl.program_id(1)
    block = pl.ds(pl.multiple_of(pair * 2 * SHD, 2 * SHD), 2 * SHD)
    taps_ref, skip_ref, gain_ref = taps_ref.at[:, block], skip_ref.at[:, block], gain_ref.at[:, block]

    @pl.when(pair == 0)
    def _():
        along_ref[...] = jnp.zeros_like(along_ref)
        inner_ref[...] = lax.dot_general(
            state_ref[:, NS:], state_ref[:, :NS], (((1,), (1,)), ((), ())), preferred_element_type=f32
        )
        mask_ref[...] = block_mask(rows, columns_ref[:, 0:1], seg_row_ref[0])
        grad_inner_ref[...] = jnp.zeros_like(grad_inner_ref)

    grad, out, gate, signal = grad_ref[...], out_ref[...], gate_ref[...], signal_ref[...]
    position, scale, cross = columns_ref[:, 1:2], columns_ref[:, 2:3], columns_ref[:, 3:4]
    here = pl.multiple_of(pair * 2 * SHD, 2 * SHD)
    rest = first_ref.shape[1] // 2 - others_ref.shape[1] // 2 - NS - STEP_PAD // 2
    after_rest = rest + 2 * NS + STEP_PAD
    sig = sigmoid_of(gate)
    silu = gate * sig
    gated = out * silu
    scaled = grad * scale
    grad_gated = scaled * gain_ref[...] - gated * cross
    grad_out = grad_gated * silu
    first_ref[:, pl.ds(here, 2 * SHD)] = (grad_gated * out * (sig * (1.0 + gate * (1.0 - sig)))).astype(bf16)
    summed, moved = conv_block(signal, taps_ref, position)
    sig = sigmoid_of(summed)
    cols = summed * sig
    cols_low = cols.astype(bf16)
    grad_low = grad_out.astype(bf16)
    lanes = lax.broadcasted_iota(jnp.int32, cols.shape, 1)
    zero = jnp.zeros_like(grad_low)
    grad_cols = []
    for head in range(2):
        step_row = step_ref[0, pair, head : head + 1, :]
        inner = inner_ref[...]
        decay, mixing = mixing_block(
            inner, mask_ref[...], run_col_ref[0, pair, :, head : head + 1], run_row_ref[0, pair, head : head + 1, :], step_row
        )
        grad_cols.append(
            lax.dot_general(mixing, grad_low, (((0,), (0,)), ((), ())), preferred_element_type=f32)
        )
        grad_head = jnp.where((lanes < SHD) == (head == 0), grad_low, zero)
        grad_decay = lax.dot_general(
            grad_head, cols_low, (((1,), (1,)), ((), ())), preferred_element_type=f32
        ) * decay
        stepped = grad_decay * step_row
        grad_inner_ref[...] += stepped
        direct_ref[pl.ds(2 * pair + head, 1), :] = jnp.sum(grad_decay * inner, axis=0, keepdims=True)
        along = jnp.sum(stepped * inner, axis=1, keepdims=True)
        along_ref[...] = jnp.where(lanes == 2 * pair + head, along, along_ref[...])
    grad_cols = jnp.where(lanes < SHD, grad_cols[0], grad_cols[1]) + skip_ref[...] * grad_out
    grad_sum = grad_cols * (sig * (1.0 + summed * (1.0 - sig)))
    grad_signal = conv_block_back(grad_sum, signal, moved, taps_ref, position, sums_ref)
    sums_ref[0, CONV + 1 : CONV + 2, :] = jnp.sum(scaled * gated, axis=0, keepdims=True)
    sums_ref[0, CONV + 2 : CONV + 3, :] = jnp.sum(grad_out * cols, axis=0, keepdims=True)
    sums_ref[0, CONV + 3 : CONV + 4, :] = jnp.zeros((1, cols.shape[1]), f32)
    first_ref[:, pl.ds(pl.multiple_of(after_rest + here, 2 * SHD), 2 * SHD)] = grad_signal.astype(bf16)

    @pl.when(pair == pl.num_programs(1) - 1)
    def _():
        inner_low = grad_inner_ref[...].astype(bf16)
        for part, (mine, other) in enumerate((((0, NS), (NS, 2 * NS)), ((NS, 2 * NS), (0, NS)))):
            raw = state_raw_ref[:, mine[0] : mine[1]]
            taps = state_taps_ref.at[:, mine[0] : mine[1]]
            summed, moved = conv_block(raw, taps, position)
            sig = sigmoid_of(summed)
            grad = lax.dot_general(
                inner_low, state_ref[:, other[0] : other[1]], (((part,), (0,)), ((), ())), preferred_element_type=f32
            )
            grad_sum = grad * (sig * (1.0 + summed * (1.0 - sig)))
            back = conv_block_back(grad_sum, raw, moved, taps, position, state_sums_ref.at[:, :, mine[0] : mine[1]])
            first_ref[:, rest + mine[0] : rest + mine[1]] = back.astype(bf16)
        state_sums_ref[0, CONV + 1 :, :] = jnp.zeros((7 - CONV, 2 * NS), f32)
        heads = step_all_ref.shape[1]
        direct, step = direct_ref[...], step_all_ref[0]
        grad_running = along_ref[...].T[:heads] - step * direct
        row_index = lax.broadcasted_iota(jnp.int32, (rows, rows), 0)
        col_index = lax.broadcasted_iota(jnp.int32, (rows, rows), 1)
        lower = jnp.where(col_index <= row_index, 1.0, 0.0)
        grad_product = jnp.dot(
            grad_running, lower, precision=lax.Precision.HIGHEST, preferred_element_type=f32
        )
        grad_raw = (direct + grad_product * rate_ref[...]) * step_sig_ref[0]
        head_sums_ref[0, :, 0:1] = jnp.sum(grad_product * step, axis=1, keepdims=True)
        head_sums_ref[0, :, 1:2] = jnp.sum(grad_raw, axis=1, keepdims=True)
        wide = jnp.concatenate([grad_raw, jnp.zeros((STEP_PAD - heads, rows), f32)], axis=0)
        first_ref[:, rest + 2 * NS : after_rest] = wide.T.astype(bf16)
        first_ref[:, first_ref.shape[1] - others_ref.shape[1] :] = others_ref[...]


def state_specs(rows, pairs):
    block = pl.BlockSpec((rows, 2 * SHD), lambda m, p: (m, p))
    return {
        "block": block,
        "taps": pl.BlockSpec((CONV + 1, 2 * SHD * pairs), lambda m, p: (0, 0)),
        "vector": pl.BlockSpec((1, 2 * SHD * pairs), lambda m, p: (0, 0)),
        "state": pl.BlockSpec((rows, 2 * NS), lambda m, p: (m, 0)),
        "columns": pl.BlockSpec((rows, 8), lambda m, p: (m, 0)),
        "row": pl.BlockSpec((1, 1, rows), lambda m, p: (m, 0, 0)),
        "head_row": pl.BlockSpec((1, pairs, 2, rows), lambda m, p: (m, 0, 0, 0)),
        "head_col": pl.BlockSpec((1, pairs, rows, 2), lambda m, p: (m, 0, 0, 0)),
    }


def state_forward(signal, gate, taps, skip, state, seg_row, run_row, run_col, step, columns):
    micro, pairs, _, rows = run_row.shape
    spec = state_specs(rows, pairs)
    total, width = signal.shape
    return pl.pallas_call(
        state_forward_kernel,
        out_shape=(jax.ShapeDtypeStruct((total, width), f32), jax.ShapeDtypeStruct((total, 2 * SHD), f32)),
        grid=(micro, pairs),
        in_specs=[spec[name] for name in (
            "block", "block", "taps", "vector", "state", "row", "head_row", "head_col", "head_row", "columns")],
        out_specs=(spec["block"], pl.BlockSpec((rows, 2 * SHD), lambda m, p: (m, 0))),
        scratch_shapes=[pltpu.VMEM((rows, rows), f32), pltpu.VMEM((rows, rows), f32)],
        cost_estimate=pl.CostEstimate(
            flops=8 * total * rows * width // SHD * SHD, transcendentals=total * rows * width // SHD, bytes_accessed=12 * total * width
        ),
        name="state_forward",
    )(signal, gate, taps, skip, state, seg_row, run_row, run_col, step, columns)


def state_backward(
    grad, out, gate, signal, taps, skip, gain, state, seg_row, run_row, run_col, step, columns,
    state_raw, state_taps, step_all, step_sig, rate, others,
):
    micro, pairs, _, rows = run_row.shape
    heads = 2 * pairs
    spec = state_specs(rows, pairs)
    total, width = signal.shape
    joint = 2 * width + 2 * NS + STEP_PAD + others.shape[1]
    heads_block = pl.BlockSpec((1, heads, rows), lambda m, p: (m, 0, 0))
    return pl.pallas_call(
        state_backward_kernel,
        out_shape=(
            jax.ShapeDtypeStruct((total, joint), bf16),
            jax.ShapeDtypeStruct((micro, 8, width), f32),
            jax.ShapeDtypeStruct((micro, 8, 2 * NS), f32),
            jax.ShapeDtypeStruct((micro, heads, 2), f32),
        ),
        grid=(micro, pairs),
        in_specs=[spec[name] for name in (
            "block", "block", "block", "block", "taps", "vector", "vector", "state",
            "row", "head_row", "head_col", "head_row", "columns", "state")]
        + [
            pl.BlockSpec((CONV + 1, 2 * NS), lambda m, p: (0, 0)), heads_block, heads_block,
            pl.BlockSpec((heads, 1), lambda m, p: (0, 0)), pl.BlockSpec((rows, others.shape[1]), lambda m, p: (m, 0)),
        ],
        out_specs=(
            pl.BlockSpec((rows, joint), lambda m, p: (m, 0)), pl.BlockSpec((1, 8, 2 * SHD), lambda m, p: (m, 0, p)),
            pl.BlockSpec((1, 8, 2 * NS), lambda m, p: (m, 0, 0)),
            pl.BlockSpec((1, heads, 2), lambda m, p: (m, 0, 0)),
        ),
        scratch_shapes=[pltpu.VMEM((rows, rows), f32)] * 3 + [pltpu.VMEM((heads, rows), f32), pltpu.VMEM((rows, 2 * SHD), f32)],
        cost_estimate=pl.CostEstimate(
            flops=20 * total * rows * width, transcendentals=total * rows * width // SHD, bytes_accessed=20 * total * width
        ),
        name="state_backward",
    )(
        grad, out, gate, signal, taps, skip, gain, state, seg_row, run_row, run_col, step, columns,
        state_raw, state_taps, step_all, step_sig, rate, others,
    )


def local(
    inputs,
    out_grad,
    deal_order,
    segment,
    query_weight,
    key_weight,
    value_weight,
    attention_out,
    mamba_gate,
    mamba_input,
    step_weight,
    state_weight,
    mamba_out,
    feed_gate,
    feed_up,
    feed_down,
    gain_input,
    gain_middle,
    kernel_inner,
    kernel_state,
    mixer_gain,
    step_bias,
    log_rate,
    skip_gain,
):
    micro, own, width = inputs.shape
    groups = lax.axis_size("dp")
    lanes = lax.axis_size("tensor")
    lane = lax.axis_index("tensor")
    group = lax.axis_index("dp")
    device = group * lanes + lane
    per = own // groups
    rows = own * lanes
    total = micro * rows
    inner_width = SH * SHD
    outer_count = groups // 4
    shard = width // groups

    swap_lane = [(0, 1), (1, 0)]

    def other_lane(values):
        return lax.ppermute(values, "tensor", swap_lane)

    def other_group(values, bits):
        return lax.ppermute(values, "dp", [(i, i ^ bits) for i in range(groups)])

    step_padded = jnp.pad(step_weight, ((0, 0), (0, STEP_PAD - step_weight.shape[1])))
    early = dict(
        gate=mamba_gate, state=state_weight, step=step_padded, input=mamba_input, query=query_weight, key=key_weight,
        value=value_weight, mix=mamba_out, attn=attention_out,
    )
    late = dict(fgate=feed_gate, fup=feed_up, fdown=feed_down)
    whole, places_of = {}, {}
    for label, group_weights in (("early", early), ("late", late)):
        start = 0
        for name, weight in group_weights.items():
            places_of[name] = (label, start, weight.shape[1])
            start += weight.shape[1]
        whole[label] = lax.all_gather(jnp.concatenate(list(group_weights.values()), axis=1), "dp", axis=0, tiled=True)

    def full(name):
        label, start, size = places_of[name]
        return lax.slice_in_dim(whole[label], start, start + size, axis=1)

    own_places = jnp.arange(own, dtype=jnp.int32)
    own_order = lax.dynamic_slice_in_dim(deal_order, device * own, own, 1)
    micro_index = jnp.arange(micro, dtype=jnp.int32)[:, None]

    def buffer_place(destination, rank):
        return destination * (micro * per) + micro_index * per + rank

    send_rank = jnp.sum((own_order[:, None, :] < own_order[:, :, None]).astype(jnp.int32), axis=2)
    send_place = buffer_place(send_rank // per, send_rank % per).reshape(-1)
    lane_order = lax.dynamic_index_in_dim(deal_order.reshape(micro, groups, lanes, own), lane, 2, keepdims=False)
    slots = device * own + own_places
    found = lane_order[:, None, :, :] == slots[None, :, None, None]
    source = jnp.sum(
        jnp.where(found, jnp.arange(groups, dtype=jnp.int32)[None, None, :, None], 0), axis=(2, 3)
    )
    recv_rank = jnp.sum(
        ((source[:, None, :] == source[:, :, None]) & (own_places[None, None, :] < own_places[None, :, None])).astype(jnp.int32),
        axis=2,
    )
    recv_place = buffer_place(source, recv_rank).reshape(-1)
    buffer_places = jnp.arange(micro * own, dtype=jnp.int32)
    send_pick = (buffer_places[:, None] == send_place[None, :]).astype(bf16)
    recv_pick = (recv_place[:, None] == buffer_places[None, :]).astype(bf16)

    def exchange(buffer):
        return lax.all_to_all(
            buffer.reshape(groups, micro * per, width), "dp", split_axis=0, concat_axis=0, tiled=True
        ).reshape(micro * own, width)

    def deal(values):
        sent = project(send_pick, values.reshape(micro * own, width)).astype(bf16)
        return project(recv_pick, exchange(sent)).astype(bf16)

    def deal_order_rows(values):
        return outer_sum(recv_pick, values).astype(bf16)

    def deal_take(moved):
        return outer_sum(send_pick, moved).astype(bf16).reshape(micro, own, width)

    def join_lanes(values):
        mine = values.reshape(micro, 1, own, -1)
        theirs = other_lane(values).reshape(micro, 1, own, -1)
        low = jnp.where(lane == 0, mine, theirs)
        high = jnp.where(lane == 0, theirs, mine)
        return jnp.concatenate([low, high], axis=1).reshape(total, -1)

    def lane_rows(values, which):
        return lax.dynamic_index_in_dim(
            values.reshape(micro, lanes, own, -1), which, 1, keepdims=False
        ).reshape(micro * own, -1)

    own_in = deal(inputs)
    own_grad = deal(out_grad)
    whole_in = join_lanes(own_in)
    whole_grad = join_lanes(own_grad)

    before = jnp.sum((segment[:, None, :] < segment[:, :, None]).astype(jnp.int32), axis=2)
    places = jnp.arange(rows, dtype=jnp.int32)
    position = (places[None, :] - before).reshape(total, 1)

    masks = [1 << place for place in range(groups.bit_length() - 1)]
    relative = []
    for block in range(groups):
        flip = 0
        for place, mask in enumerate(masks):
            if block >> (len(masks) - 1 - place) & 1:
                flip ^= mask
        relative.append(flip)
    block_order = jnp.bitwise_xor(group.astype(jnp.int32), jnp.array(relative, jnp.int32))

    def split_left(left):
        return pick_halves(left, block_order, shard)

    inner_places = list(range(1, len(masks)))

    def core_send(left_parts, right):
        return outer_low(left_parts[1], right)

    def halve(kept, place):
        return (
            lax.slice_in_dim(kept, 1, 2, axis=place - 1).reshape(-1, kept.shape[-1]),
            lax.slice_in_dim(kept, 0, 1, axis=place - 1),
        )

    class Reduction:
        def __init__(self, first):
            self.places = [place for place in first if place in inner_places]
            self.places += [place for place in inner_places if place not in first]
            self.stage = 0

        def move(self, send, kept):
            self.came = other_group(send, masks[self.places[self.stage]])
            self.kept = kept
            self.stage += 1

        def first(self, left_parts, right, from_core):
            kept = (outer_sum(left_parts[0], right) + from_core.astype(f32)).astype(bf16)
            kept = kept.reshape((2,) * len(inner_places) + (shard, -1))
            return halve(kept, self.places[0])

        def added(self):
            return self.kept.astype(f32) + self.came.reshape(self.kept.shape).astype(f32)

        def next(self):
            return halve(self.added().astype(bf16), self.places[self.stage])

        def last(self):
            return self.added().reshape(shard, -1)

        def step(self):
            return self.next() if self.stage < len(self.places) else self.last()

    order = [deal_order[0, 0] >= 0]

    def unit(work):
        shapes = jax.eval_shape(work)
        results = lax.cond(
            order[0], work, lambda: jax.tree.map(lambda leaf: jnp.zeros(leaf.shape, leaf.dtype), shapes)
        )
        leaves, form = jax.tree.flatten(results)
        least = min(range(len(leaves)), key=lambda place: leaves[place].size)
        leaves[least], order[0] = lax.optimization_barrier((leaves[least], order[0]))
        return jax.tree.unflatten(form, leaves)

    def after(value, *others):
        return lax.optimization_barrier((value, others))[0]

    in32 = whole_in.astype(f32)
    in_scale = rms_scale(in32)
    normed_low = (in32 * in_scale * gain_input).astype(bf16)
    normed_left = split_left(normed_low)
    whole["early"] = after(whole["early"], whole_grad, normed_left)
    gate_z = project(normed_low, full("gate"))
    ssm_in = project(normed_low, full("input"))
    state_raw = project(normed_low, full("state"))
    heads = step_weight.shape[1]
    raw_step = project(normed_low, full("step"))[:, :heads]
    state_low = jax.nn.silu(conv_sum(state_raw, kernel_state, position)).astype(bf16)
    rate = -jnp.exp(log_rate)
    step_size = jax.nn.softplus(raw_step + step_bias)
    step_heads = step_size.reshape(micro, rows, heads).transpose(0, 2, 1)
    lower = (places[None, :] <= places[:, None]).astype(f32)
    running = jnp.einsum(
        "mhj,ij->mhi", step_heads * rate[None, :, None], lower, precision=lax.Precision.HIGHEST, preferred_element_type=f32
    )
    pairs = heads // 2
    run_row = running.reshape(micro, pairs, 2, rows)
    run_col = run_row.transpose(0, 1, 3, 2)
    step_row = step_heads.reshape(micro, pairs, 2, rows)
    skip_wide = jnp.repeat(skip_gain, SHD)[None, :]
    layout = (state_low, segment.reshape(micro, 1, rows).astype(f32), run_row, run_col, step_row)
    row_facts = jnp.concatenate([segment.reshape(total, 1).astype(f32), position.astype(f32)], axis=1)
    row_columns = jnp.pad(row_facts, ((0, 0), (0, 6)))
    query_cols, key_cols = query_weight.shape[1], key_weight.shape[1]
    attention_tables = (*rope_tables(position), row_columns, layout[1])
    joint_start = places_of["query"][1]
    joint_weight = lax.slice_in_dim(whole["early"], joint_start, joint_start + query_cols + 2 * key_cols, axis=1)
    ssm_out, squares = state_forward(ssm_in, gate_z, kernel_inner, skip_wide, *layout, row_columns)
    attended_low, query_low, key_low, value_low = attention_forward(
        project(normed_low, joint_weight), query_cols, key_cols, attention_tables
    )
    square_own = jnp.sum(squares, axis=1)
    square_sum = square_own + other_lane(square_own)
    inv_rms = lax.rsqrt(square_sum / inner_width + epsilon)[:, None]
    gated_low = (ssm_out * jax.nn.silu(gate_z) * inv_rms * mixer_gain).astype(bf16)

    branch_part = (project_back(gated_low, full("mix")) + project_back(attended_low, full("attn"))).astype(bf16)
    branch = branch_part.astype(f32) + other_lane(branch_part).astype(f32)
    whole_mid = (in32 + branch).astype(bf16)
    mid32 = whole_mid.astype(f32)
    mid_scale = rms_scale(mid32)
    mid_low = (mid32 * mid_scale * gain_middle).astype(bf16)
    red_fgate, red_fup, red_low, red_high = [Reduction(places) for places in ((1, 2), (2, 1), (1, 2), (2, 1))]
    feeds = (red_fgate, red_fup)
    ff_cols = feed_gate.shape[1]
    gate_cols = mamba_gate.shape[1]

    def feed_forward():
        gate_ff = project(mid_low, full("fgate"))
        up_ff = project(mid_low, full("fup"))
        sig_ff = jax.nn.sigmoid(gate_ff)
        hidden_low = (gate_ff * sig_ff * up_ff).astype(bf16)
        grad_hidden = project(whole_grad, full("fdown"))
        gate_ff_low = (grad_hidden * up_ff * (sig_ff * (1.0 + gate_ff * (1.0 - sig_ff)))).astype(bf16)
        up_ff_low = (grad_hidden * (gate_ff * sig_ff)).astype(bf16)
        grad_mid_norm = project_back(gate_ff_low, full("fgate")) + project_back(up_ff_low, full("fup"))
        grad_gain_mid = jnp.sum(grad_mid_norm * mid32 * mid_scale, axis=0)
        mid_part = rms_back(grad_mid_norm, mid32, mid_scale, gain_middle).astype(bf16)
        return grad_gain_mid, mid_part, hidden_low, (gate_ff_low, up_ff_low), outer_low(whole_grad, hidden_low)

    grad_gain_mid, mid_part, hidden_low, feed_low, part_fdown = unit(feed_forward)
    sum_fdown = lax.psum_scatter(part_fdown, "dp", scatter_dimension=0, tiled=True)
    mid_other = hand_over(other_lane(mid_part), 45)

    def feed_output():
        ffn_part = project_back(hidden_low, full("fdown")).astype(bf16)
        mid_left = split_left(mid_low)
        return (
            lane_rows(ffn_part, lane), lane_rows(ffn_part, 1 - lane), mid_left[0],
            [core_send(mid_left, right) for right in feed_low],
        )

    ffn_own, ffn_send, mid_keep, send_feed = unit(feed_output)
    feed_came = [other_group(send, 1) for send in send_feed]

    def keep_first(keep, right, came, reductions, sizes):
        kept = (outer_sum(keep, right) + came.astype(f32)).astype(bf16)
        kept = kept.reshape((2,) * len(inner_places) + (shard, -1))
        moves, start = [], 0
        for red, size in zip(reductions, sizes):
            moves.append(halve(kept[..., start : start + size], red.places[0]))
            start += size
        return moves

    def settle(reductions, steps):
        for red, step in zip(reductions, steps):
            if red.stage < len(red.places):
                red.move(*step)
            else:
                red.result = step

    mid_other, feed_came = lax.optimization_barrier((mid_other, feed_came))
    moves = unit(
        lambda: [
            keep_first(mid_keep, right, came, (red,), (ff_cols,))[0] for red, right, came in zip(feeds, feed_low, feed_came)
        ]
    )
    for red, move in zip(feeds, moves):
        red.move(*move)

    def branch_backward():
        grad_middle = whole_grad.astype(f32) + (mid_part.astype(f32) + mid_other.astype(f32))
        whole_branch = grad_middle.astype(bf16)
        grad_gated_norm = project(whole_branch, full("mix"))
        cross_own = jnp.sum(grad_gated_norm * mixer_gain * (ssm_out * jax.nn.silu(gate_z)), axis=1)
        grad_attended = project(whole_branch, full("attn")).astype(bf16)
        joint_low = attention_backward(grad_attended, query_low, key_low, value_low, attention_tables)
        return (
            cross_own, lane_rows(grad_middle, lane), grad_gated_norm, whole_branch,
            joint_low,
        )

    cross_own, grad_middle_own, grad_gated_norm, whole_branch, joint_low = unit(branch_backward)
    cross_other = other_lane(cross_own)

    ffn_other = other_lane(ffn_send)

    def branch_partial():
        ffn_out = ffn_own.astype(f32) + ffn_other.astype(f32)
        out_rows = (lane_rows(whole_mid, lane).astype(f32) + ffn_out).astype(bf16)
        return outer_low(whole_branch, jnp.concatenate([gated_low, attended_low], axis=1)), deal_order_rows(out_rows)

    part_branch, out_sent = unit(branch_partial)
    out_moved = exchange(out_sent)
    sum_branch = lax.psum_scatter(part_branch, "dp", scatter_dimension=0, tiled=True)
    step_sig = jax.nn.sigmoid(raw_step + step_bias).reshape(micro, rows, heads).transpose(0, 2, 1)
    gain_row, rate_column = mixer_gain[None, :], rate[:, None]

    def state_space_backward():
        cross = (inv_rms**3) * ((cross_own + cross_other)[:, None] / inner_width)
        columns = jnp.pad(jnp.concatenate([row_facts, inv_rms, cross], axis=1), ((0, 0), (0, 4)))
        first_right, column_sums, state_sums, head_sums = state_backward(
            grad_gated_norm, ssm_out, gate_z, ssm_in, kernel_inner, skip_wide, gain_row, *layout, columns,
            state_raw, kernel_state, step_heads, step_sig, rate_column, joint_low,
        )
        return column_sums, state_sums, head_sums, first_right

    column_sums, state_sums, head_sums, first_right = unit(state_space_backward)

    total_fdown_low = [sum_fdown]
    order[0], total_fdown_low = lax.optimization_barrier((order[0], total_fdown_low))
    send_first, steps, block_out = unit(
        lambda: (core_send(normed_left, first_right), [red.step() for red in feeds], deal_take(out_moved))
    )
    settle(feeds, steps)
    first_came = other_group(send_first, 1)

    def input_gradient():
        grad_normed = project_back(first_right, lax.slice_in_dim(whole["early"], 0, first_right.shape[1], axis=1))
        grad_gain_in = jnp.sum(grad_normed * in32 * in_scale, axis=0)
        in_part = rms_back(grad_normed, in32, in_scale, gain_input).astype(bf16)
        return grad_gain_in, lane_rows(in_part, lane), lane_rows(in_part, 1 - lane)

    grad_gain_in, in_own, in_send = unit(input_gradient)

    firsts = (red_low, red_high)
    low_size = gate_cols + 2 * NS + STEP_PAD
    first_sizes = (low_size, first_right.shape[1] - low_size)

    def first_moves():
        moves = keep_first(normed_left[0], first_right, first_came, firsts, first_sizes)
        return moves, lax.optimization_barrier(in_send), [red.step() for red in feeds]

    moves, in_send, steps = unit(first_moves)
    settle(feeds, steps)
    for red, move in zip(firsts, moves):
        red.move(*move)
    in_other = hand_over(other_lane(in_send), 6)

    def small_block():
        head_row = (jnp.sum(head_sums, axis=0).T * jnp.stack([rate, jnp.ones_like(rate)])).reshape(1, -1)
        return jnp.concatenate(
            [
                jnp.concatenate([jnp.sum(column_sums, axis=0), jnp.sum(state_sums, axis=0)], axis=1),
                grad_gain_in[None, :], grad_gain_mid[None, :], jnp.pad(head_row, ((0, 5), (0, width - head_row.shape[1]))),
            ]
        )
    flat = unit(small_block)
    flat_moved = other_group(flat, masks[0])

    def send_input():
        in_sum = in_own.astype(f32) + in_other.astype(f32)
        return deal_order_rows((in_sum + grad_middle_own).astype(bf16))

    bits = 1

    def finish():
        low, high = red_low.result, red_high.result
        state_rows = low[:, gate_cols : gate_cols + 2 * NS].reshape(lanes, shard // lanes, 2 * NS)
        cut = [0, gate_cols, gate_cols + query_cols, gate_cols + query_cols + key_cols, high.shape[1]]
        pieces = (
            low[:, :gate_cols], low[:, gate_cols + 2 * NS : gate_cols + 2 * NS + heads],
            [high[:, start:stop] for start, stop in zip(cut, cut[1:])],
            [lax.dynamic_index_in_dim(state_rows, which, 0, keepdims=False) for which in (lane, 1 - lane)],
        )
        return pieces, deal_take(in_moved)

    arrived = [red.came for red in feeds] + [sum_branch]
    order[0], arrived = lax.optimization_barrier((order[0], arrived))
    for red, came in zip(feeds, arrived):
        red.came = came
    sum_branch = arrived[-1]
    in_moved = None
    while red_low.stage < len(red_low.places):
        moving = [red for red in (*firsts, *feeds) if red.stage < len(red.places)]
        steps, flat, sent = unit(
            lambda: (
                [red.next() for red in moving],
                flat + flat_moved if flat_moved is not None else flat,
                send_input() if in_moved is None else (),
            )
        )
        settle(moving, steps)
        flat_moved = other_group(flat, masks[bits]) if bits < len(masks) else None
        bits += 1
        if in_moved is None:
            in_moved = exchange(sent)
    totals, flat = unit(
        lambda: (
            [red.last() for red in feeds] + [sum_branch.astype(f32), total_fdown_low[0].astype(f32)],
            flat + flat_moved if flat_moved is not None else flat,
        )
    )
    total_fgate, total_fup, total_branch, total_fdown = totals
    flat_moved = other_group(flat, masks[bits]) if bits < len(masks) else None
    bits += 1

    def last_work():
        red_low.result, red_high.result = red_low.last(), red_high.last()
        return finish(), flat + flat_moved if flat_moved is not None else flat

    ((total_gate, total_step, (total_input, total_query, total_key, total_value), states), grad_input), flat = unit(last_work)
    while bits < len(masks):
        flat = flat + other_group(flat, masks[bits])
        bits += 1
    theirs = other_lane(flat)
    low, high = jnp.where(lane == 0, flat, theirs), jnp.where(lane == 0, theirs, flat)
    both = flat + theirs

    def joined(row, start, count):
        return jnp.concatenate([low[row, start : start + count], high[row, start : start + count]])

    sum_gin, sum_gmid = both[8], both[9]
    sum_kst = both[: CONV + 1, gate_cols : gate_cols + 2 * NS]
    sum_kin = jnp.concatenate([low[: CONV + 1, :gate_cols], high[: CONV + 1, :gate_cols]], axis=1)
    sum_mix = joined(CONV + 1, 0, gate_cols)
    sum_skip = jnp.sum(joined(CONV + 2, 0, gate_cols).reshape(SH, SHD), axis=1)
    sum_bias = joined(10, heads, heads)
    sum_rate = joined(10, 0, heads)

    total_mix, total_attn = total_branch[:, :gate_cols], total_branch[:, gate_cols:]
    state_lane = states[0] + other_lane(states[1])
    return (
        block_out,
        grad_input,
        total_query,
        total_key,
        total_value,
        total_attn,
        total_gate,
        total_input,
        total_step,
        state_lane,
        total_mix,
        total_fgate,
        total_fup,
        total_fdown,
        sum_gin,
        sum_gmid,
        sum_kin,
        sum_kst,
        sum_mix,
        sum_bias,
        sum_rate,
        sum_skip,
    )


def solution(mesh):
    both = P("dp", "tensor")
    in_specs = (
        P(None, ("dp", "tensor"), None),
        P(None, ("dp", "tensor"), None),
        P(),
        P(None, "dp"),
        both,
        both,
        both,
        both,
        both,
        both,
        both,
        P("dp", None),
        both,
        both,
        both,
        both,
        P(),
        P(),
        P(None, "tensor"),
        P(),
        P("tensor"),
        P("tensor"),
        P("tensor"),
        P("tensor"),
    )
    out_specs = (
        P(None, ("dp", "tensor"), None),
        P(None, ("dp", "tensor"), None),
        both,
        both,
        both,
        both,
        both,
        both,
        both,
        P(("dp", "tensor"), None),
        both,
        both,
        both,
        both,
        P(),
        P(),
        P(),
        P(),
        P(),
        P(),
        P(),
        P(),
    )
    return jax.shard_map(local, mesh=mesh, in_specs=in_specs, out_specs=out_specs, check_vma=False)
```

```python
import functools
import math

import jax
import jax.numpy as jnp
from jax import lax
from jax.experimental import pallas as pl
from jax.experimental.layout import Layout, with_layout_constraint
from jax.experimental.pallas import tpu as pltpu
from jax.sharding import PartitionSpec as P

HEAD = 128
SH = 48
SHD = 64
NS = 256
CONV = 4
STEP_PAD = 128

epsilon = 1e-05
rope_base = 100000000000.0
f32 = jnp.float32
bf16 = jnp.bfloat16


def project(left, right):
    return jnp.dot(left, right, preferred_element_type=f32)


def project_back(left, right):
    return lax.dot_general(left, right, (((1,), (1,)), ((), ())), preferred_element_type=f32)


def outer_sum(left, right):
    return lax.dot_general(left, right, (((0,), (0,)), ((), ())), preferred_element_type=f32)


def outer_low(left, right):
    return with_layout_constraint(outer_sum(left, right).astype(bf16), Layout(major_to_minor=(0, 1)))


def rms_scale(values):
    return lax.rsqrt(jnp.mean(values * values, axis=-1, keepdims=True) + epsilon)


def rms_back(grad, values, scale, gain):
    weighted = grad * gain
    inner = jnp.sum(weighted * values, axis=-1, keepdims=True)
    return scale * weighted - values * (scale * scale * scale * inner / values.shape[-1])


def shift_down(values, count):
    return jnp.concatenate([jnp.zeros((count, values.shape[1]), values.dtype), values[:-count]], axis=0)


def shift_up(values, count):
    return jnp.concatenate([values[count:], jnp.zeros((count, values.shape[1]), values.dtype)], axis=0)


def conv_sum(signal, kernel, position):
    summed = kernel[CONV][None, :] + signal * kernel[0][None, :]
    for tap in range(1, CONV):
        moved = jnp.where(position >= tap, shift_down(signal, tap), 0.0)
        summed = summed + moved * kernel[tap][None, :]
    return summed


def silu_back(values):
    sig = jax.nn.sigmoid(values)
    return sig * (1.0 + values * (1.0 - sig))


def conv_back(grad, signal, kernel, position):
    grad_sum = grad * silu_back(conv_sum(signal, kernel, position))
    grad_signal = grad_sum * kernel[0][None, :]
    grad_taps = [jnp.sum(grad_sum * signal, axis=0)]
    for tap in range(1, CONV):
        kept = jnp.where(position >= tap, grad_sum, 0.0)
        grad_signal = grad_signal + shift_up(kept, tap) * kernel[tap][None, :]
        grad_taps.append(jnp.sum(kept * shift_down(signal, tap), axis=0))
    grad_taps.append(jnp.sum(grad_sum, axis=0))
    return grad_signal, jnp.stack(grad_taps)


def rope_tables(position):
    half_size = HEAD // 2
    frequency = jnp.exp(jnp.arange(half_size, dtype=f32) * (-2.0 * math.log(rope_base) / HEAD))
    angles = position.astype(f32) * frequency[None, :]
    cosine, sine = jnp.cos(angles), jnp.sin(angles)
    return jnp.concatenate([cosine, cosine], axis=1), jnp.concatenate([-sine, sine], axis=1)


def copy_blocks(order_ref, first_ref, second_ref, first_out_ref, second_out_ref):
    first_out_ref[...] = first_ref[...]
    second_out_ref[...] = second_ref[...]


def pick_halves(values, order, block):
    height, width = values.shape
    count = width // block // 2
    if block % 128:
        mixed = jnp.take(values.reshape(height, -1, block), order, axis=1).reshape(height, width)
        return mixed[:, : width // 2], mixed[:, width // 2 :]
    half = jax.ShapeDtypeStruct((height, width // 2), values.dtype)
    out_spec = pl.BlockSpec((height, block), lambda i, order: (0, i))
    return pl.pallas_call(
        copy_blocks,
        out_shape=(half, half),
        grid_spec=pltpu.PrefetchScalarGridSpec(
            num_scalar_prefetch=1,
            grid=(count,),
            in_specs=[
                pl.BlockSpec((height, block), lambda i, order: (0, order[i])),
                pl.BlockSpec((height, block), lambda i, order: (0, order[i + count])),
            ],
            out_specs=(out_spec, out_spec),
        ),
        cost_estimate=pl.CostEstimate(flops=0, transcendentals=0, bytes_accessed=4 * height * width),
        name="pick_halves",
    )(order, values, values)


def join_columns(pieces):
    height = pieces[0].shape[0]
    width = sum(piece.shape[1] for piece in pieces)

    def put_all(*refs):
        start = 0
        for source in refs[:-1]:
            refs[-1][:, start : start + source.shape[1]] = source[...]
            start += source.shape[1]

    return pl.pallas_call(
        put_all,
        out_shape=jax.ShapeDtypeStruct((height, width), pieces[0].dtype),
        cost_estimate=pl.CostEstimate(flops=0, transcendentals=0, bytes_accessed=4 * height * width),
        name="join_columns",
    )(*pieces)


def hand_over(values, microseconds):
    def idle(values_ref, out_ref):
        pass

    return pl.pallas_call(
        idle,
        out_shape=jax.ShapeDtypeStruct(values.shape, values.dtype),
        in_specs=[pl.BlockSpec(memory_space=pl.ANY)],
        out_specs=pl.BlockSpec(memory_space=pl.ANY),
        input_output_aliases={0: 0},
        cost_estimate=pl.CostEstimate(flops=microseconds * 1150000000, transcendentals=0, bytes_accessed=0),
        name="hand_over",
    )(values)


NEGATIVE = -1e30


def sigmoid_of(values):
    return 1.0 / (1.0 + jnp.exp(-values))


def block_mask(rows, segment_col, segment_row):
    row_index = lax.broadcasted_iota(jnp.int32, (rows, rows), 0)
    col_index = lax.broadcasted_iota(jnp.int32, (rows, rows), 1)
    return jnp.where((segment_col == segment_row) & (col_index <= row_index), 0.0, NEGATIVE)


def conv_block(signal, taps_ref, position):
    summed = taps_ref[CONV : CONV + 1, :] + signal * taps_ref[0:1, :]
    moved = []
    for tap in range(1, CONV):
        shifted = jnp.where(position >= tap, pltpu.roll(signal, tap, 0), 0.0)
        moved.append(shifted)
        summed = summed + shifted * taps_ref[tap : tap + 1, :]
    return summed, moved


def conv_block_back(grad_sum, signal, moved, taps_ref, position, sums_ref):
    rows = signal.shape[0]
    grad_signal = grad_sum * taps_ref[0:1, :]
    sums_ref[0, 0:1, :] = jnp.sum(grad_sum * signal, axis=0, keepdims=True)
    for tap in range(1, CONV):
        kept = jnp.where(position >= tap, grad_sum, 0.0)
        grad_signal = grad_signal + pltpu.roll(kept, rows - tap, 0) * taps_ref[tap : tap + 1, :]
        sums_ref[0, tap : tap + 1, :] = jnp.sum(grad_sum * moved[tap - 1], axis=0, keepdims=True)
    sums_ref[0, CONV : CONV + 1, :] = jnp.sum(grad_sum, axis=0, keepdims=True)
    return grad_signal


def mixing_block(inner, mask, run_col, run_row, step_row):
    decay = jnp.exp(run_col - run_row + mask)
    return decay, (inner * decay * step_row).astype(bf16)


def turn(values, cosine_ref, sine_ref, sign):
    return values * cosine_ref[...] + sign * (pltpu.roll(values, HEAD // 2, 1) * sine_ref[...])


def head_probs(query_low, key_low, mask):
    logits = lax.dot_general(query_low, key_low, (((1,), (1,)), ((), ())), preferred_element_type=f32) * HEAD ** (-0.5)
    logits = logits + mask
    weights = jnp.exp(logits - jnp.max(logits, axis=1, keepdims=True))
    return weights / jnp.sum(weights, axis=1, keepdims=True)


def attention_forward_kernel(
    query_ref, key_ref, value_ref, cosine_ref, sine_ref, columns_ref, seg_row_ref,
    attended_ref, query_low_ref, key_low_ref, value_low_ref, mask_ref,
):
    rows = query_ref.shape[0]

    @pl.when(pl.program_id(1) == 0)
    def _():
        mask_ref[...] = block_mask(rows, columns_ref[:, 0:1], seg_row_ref[0])

    query_low = turn(query_ref[...], cosine_ref, sine_ref, 1.0).astype(bf16)
    key_low = turn(key_ref[...], cosine_ref, sine_ref, 1.0).astype(bf16)
    value_low = value_ref[...].astype(bf16)
    probs_low = head_probs(query_low, key_low, mask_ref[...]).astype(bf16)
    attended_ref[...] = jnp.dot(probs_low, value_low, preferred_element_type=f32).astype(bf16)
    query_low_ref[...] = query_low
    key_low_ref[...] = key_low
    value_low_ref[...] = value_low


def attention_backward_kernel(
    grad_ref, query_ref, key_ref, value_ref, cosine_ref, sine_ref, columns_ref, seg_row_ref,
    joint_ref, mask_ref, grad_key_ref, grad_value_ref, *, group, query_cols, key_cols,
):
    rows = query_ref.shape[0]
    head = pl.program_id(1)

    @pl.when(head == 0)
    def _():
        mask_ref[...] = block_mask(rows, columns_ref[:, 0:1], seg_row_ref[0])

    @pl.when(head % group == 0)
    def _():
        grad_key_ref[...] = jnp.zeros_like(grad_key_ref)
        grad_value_ref[...] = jnp.zeros_like(grad_value_ref)

    grad, query_low, key_low = grad_ref[...], query_ref[...], key_ref[...]
    probs = head_probs(query_low, key_low, mask_ref[...])
    grad_probs = lax.dot_general(grad, value_ref[...], (((1,), (1,)), ((), ())), preferred_element_type=f32)
    grad_value_ref[...] += lax.dot_general(
        probs.astype(bf16), grad, (((0,), (0,)), ((), ())), preferred_element_type=f32
    )
    grad_logits = (probs * (grad_probs - jnp.sum(probs * grad_probs, axis=1, keepdims=True))).astype(bf16)
    grad_query = jnp.dot(grad_logits, key_low, preferred_element_type=f32) * HEAD ** (-0.5)
    grad_key_ref[...] += lax.dot_general(
        grad_logits, query_low, (((0,), (0,)), ((), ())), preferred_element_type=f32
    ) * HEAD ** (-0.5)
    joint_ref[:, pl.ds(pl.multiple_of(head * HEAD, HEAD), HEAD)] = turn(
        grad_query, cosine_ref, sine_ref, -1.0
    ).astype(bf16)

    @pl.when(head % group == group - 1)
    def _():
        place = head // group * HEAD
        joint_ref[:, pl.ds(pl.multiple_of(query_cols + place, HEAD), HEAD)] = turn(
            grad_key_ref[...], cosine_ref, sine_ref, -1.0
        ).astype(bf16)
        joint_ref[:, pl.ds(pl.multiple_of(query_cols + key_cols + place, HEAD), HEAD)] = grad_value_ref[...].astype(bf16)


def attention_specs(rows, group):
    table = pl.BlockSpec((rows, HEAD), lambda m, h: (m, 0))
    return (
        lambda start: pl.BlockSpec((rows, HEAD), lambda m, h: (m, start + h)),
        lambda start: pl.BlockSpec((rows, HEAD), lambda m, h: (m, start + h // group)),
        [table, table, pl.BlockSpec((rows, 8), lambda m, h: (m, 0)), pl.BlockSpec((1, 1, rows), lambda m, h: (m, 0, 0))],
    )


def attention_forward(joint, query_cols, key_cols, tables):
    micro, _, rows = tables[3].shape
    total = joint.shape[0]
    heads, kv_heads = query_cols // HEAD, key_cols // HEAD
    by_head, by_kv, table_specs = attention_specs(rows, heads // kv_heads)
    return pl.pallas_call(
        attention_forward_kernel,
        out_shape=tuple(jax.ShapeDtypeStruct((total, size), bf16) for size in (query_cols, query_cols, key_cols, key_cols)),
        grid=(micro, heads),
        in_specs=[by_head(0), by_kv(heads), by_kv(heads + kv_heads)] + table_specs,
        out_specs=(by_head(0), by_head(0), by_kv(0), by_kv(0)),
        scratch_shapes=[pltpu.VMEM((rows, rows), f32)],
        cost_estimate=pl.CostEstimate(
            flops=4 * total * rows * query_cols, transcendentals=total * rows * heads, bytes_accessed=8 * total * query_cols
        ),
        name="attention_forward",
    )(joint, joint, joint, *tables)


def attention_backward(grad, query, key, value, tables):
    micro, _, rows = tables[3].shape
    total, query_cols = query.shape
    key_cols = key.shape[1]
    heads, kv_heads = query_cols // HEAD, key_cols // HEAD
    by_head, by_kv, table_specs = attention_specs(rows, heads // kv_heads)
    joint_cols = query_cols + 2 * key_cols
    return pl.pallas_call(
        functools.partial(
            attention_backward_kernel, group=heads // kv_heads, query_cols=query_cols, key_cols=key_cols
        ),
        out_shape=jax.ShapeDtypeStruct((total, joint_cols), bf16),
        grid=(micro, heads),
        in_specs=[by_head(0), by_head(0), by_kv(0), by_kv(0)] + table_specs,
        out_specs=pl.BlockSpec((rows, joint_cols), lambda m, h: (m, 0)),
        scratch_shapes=[pltpu.VMEM((rows, rows), f32), pltpu.VMEM((rows, HEAD), f32), pltpu.VMEM((rows, HEAD), f32)],
        cost_estimate=pl.CostEstimate(
            flops=10 * total * rows * query_cols, transcendentals=total * rows * heads, bytes_accessed=8 * total * query_cols
        ),
        name="attention_backward",
    )(grad, query, key, value, *tables)


def state_forward_kernel(
    signal_ref, gate_ref, taps_ref, skip_ref, state_ref, seg_row_ref, run_row_ref, run_col_ref, step_ref, columns_ref,
    out_ref, square_ref, inner_ref, mask_ref,
):
    rows = signal_ref.shape[0]
    position = columns_ref[:, 1:2]
    pair = pl.program_id(1)
    here = pl.ds(pl.multiple_of(pair * 2 * SHD, 2 * SHD), 2 * SHD)
    taps_ref, skip_ref = taps_ref.at[:, here], skip_ref.at[:, here]

    @pl.when(pl.program_id(1) == 0)
    def _():
        inner_ref[...] = lax.dot_general(
            state_ref[:, NS:], state_ref[:, :NS], (((1,), (1,)), ((), ())), preferred_element_type=f32
        )
        mask_ref[...] = block_mask(rows, columns_ref[:, 0:1], seg_row_ref[0])
        square_ref[...] = jnp.zeros_like(square_ref)

    summed, _ = conv_block(signal_ref[...], taps_ref, position)
    cols = summed * sigmoid_of(summed)
    cols_low = cols.astype(bf16)
    mixed = []
    for head in range(2):
        _, mixing = mixing_block(
            inner_ref[...], mask_ref[...], run_col_ref[0, pair, :, head : head + 1],
            run_row_ref[0, pair, head : head + 1, :], step_ref[0, pair, head : head + 1, :],
        )
        mixed.append(jnp.dot(mixing, cols_low, preferred_element_type=f32))
    lanes = lax.broadcasted_iota(jnp.int32, cols.shape, 1)
    out = jnp.where(lanes < SHD, mixed[0], mixed[1]) + skip_ref[...] * cols
    out_ref[...] = out
    gate = gate_ref[...]
    gated = out * (gate * sigmoid_of(gate))
    square_ref[...] += gated * gated


def state_backward_kernel(
    grad_ref, out_ref, gate_ref, signal_ref, taps_ref, skip_ref, gain_ref, state_ref, seg_row_ref, run_row_ref, run_col_ref,
    step_ref, columns_ref, state_raw_ref, state_taps_ref, step_all_ref, step_sig_ref, rate_ref, others_ref,
    first_ref, sums_ref, state_sums_ref, head_sums_ref,
    inner_ref, mask_ref, grad_inner_ref, direct_ref, along_ref,
):
    rows = signal_ref.shape[0]
    pair = pl.program_id(1)
    block = pl.ds(pl.multiple_of(pair * 2 * SHD, 2 * SHD), 2 * SHD)
    taps_ref, skip_ref, gain_ref = taps_ref.at[:, block], skip_ref.at[:, block], gain_ref.at[:, block]

    @pl.when(pair == 0)
    def _():
        along_ref[...] = jnp.zeros_like(along_ref)
        inner_ref[...] = lax.dot_general(
            state_ref[:, NS:], state_ref[:, :NS], (((1,), (1,)), ((), ())), preferred_element_type=f32
        )
        mask_ref[...] = block_mask(rows, columns_ref[:, 0:1], seg_row_ref[0])
        grad_inner_ref[...] = jnp.zeros_like(grad_inner_ref)

    grad, out, gate, signal = grad_ref[...], out_ref[...], gate_ref[...], signal_ref[...]
    position, scale, cross = columns_ref[:, 1:2], columns_ref[:, 2:3], columns_ref[:, 3:4]
    here = pl.multiple_of(pair * 2 * SHD, 2 * SHD)
    rest = first_ref.shape[1] // 2 - others_ref.shape[1] // 2 - NS - STEP_PAD // 2
    after_rest = rest + 2 * NS + STEP_PAD
    sig = sigmoid_of(gate)
    silu = gate * sig
    gated = out * silu
    scaled = grad * scale
    grad_gated = scaled * gain_ref[...] - gated * cross
    grad_out = grad_gated * silu
    first_ref[:, pl.ds(here, 2 * SHD)] = (grad_gated * out * (sig * (1.0 + gate * (1.0 - sig)))).astype(bf16)
    summed, moved = conv_block(signal, taps_ref, position)
    sig = sigmoid_of(summed)
    cols = summed * sig
    cols_low = cols.astype(bf16)
    grad_low = grad_out.astype(bf16)
    lanes = lax.broadcasted_iota(jnp.int32, cols.shape, 1)
    zero = jnp.zeros_like(grad_low)
    grad_cols = []
    for head in range(2):
        step_row = step_ref[0, pair, head : head + 1, :]
        inner = inner_ref[...]
        decay, mixing = mixing_block(
            inner, mask_ref[...], run_col_ref[0, pair, :, head : head + 1], run_row_ref[0, pair, head : head + 1, :], step_row
        )
        grad_cols.append(
            lax.dot_general(mixing, grad_low, (((0,), (0,)), ((), ())), preferred_element_type=f32)
        )
        grad_head = jnp.where((lanes < SHD) == (head == 0), grad_low, zero)
        grad_decay = lax.dot_general(
            grad_head, cols_low, (((1,), (1,)), ((), ())), preferred_element_type=f32
        ) * decay
        stepped = grad_decay * step_row
        grad_inner_ref[...] += stepped
        direct_ref[pl.ds(2 * pair + head, 1), :] = jnp.sum(grad_decay * inner, axis=0, keepdims=True)
        along = jnp.sum(stepped * inner, axis=1, keepdims=True)
        along_ref[...] = jnp.where(lanes == 2 * pair + head, along, along_ref[...])
    grad_cols = jnp.where(lanes < SHD, grad_cols[0], grad_cols[1]) + skip_ref[...] * grad_out
    grad_sum = grad_cols * (sig * (1.0 + summed * (1.0 - sig)))
    grad_signal = conv_block_back(grad_sum, signal, moved, taps_ref, position, sums_ref)
    sums_ref[0, CONV + 1 : CONV + 2, :] = jnp.sum(scaled * gated, axis=0, keepdims=True)
    sums_ref[0, CONV + 2 : CONV + 3, :] = jnp.sum(grad_out * cols, axis=0, keepdims=True)
    sums_ref[0, CONV + 3 : CONV + 4, :] = jnp.zeros((1, cols.shape[1]), f32)
    first_ref[:, pl.ds(pl.multiple_of(after_rest + here, 2 * SHD), 2 * SHD)] = grad_signal.astype(bf16)

    @pl.when(pair == pl.num_programs(1) - 1)
    def _():
        inner_low = grad_inner_ref[...].astype(bf16)
        for part, (mine, other) in enumerate((((0, NS), (NS, 2 * NS)), ((NS, 2 * NS), (0, NS)))):
            raw = state_raw_ref[:, mine[0] : mine[1]]
            taps = state_taps_ref.at[:, mine[0] : mine[1]]
            summed, moved = conv_block(raw, taps, position)
            sig = sigmoid_of(summed)
            grad = lax.dot_general(
                inner_low, state_ref[:, other[0] : other[1]], (((part,), (0,)), ((), ())), preferred_element_type=f32
            )
            grad_sum = grad * (sig * (1.0 + summed * (1.0 - sig)))
            back = conv_block_back(grad_sum, raw, moved, taps, position, state_sums_ref.at[:, :, mine[0] : mine[1]])
            first_ref[:, rest + mine[0] : rest + mine[1]] = back.astype(bf16)
        state_sums_ref[0, CONV + 1 :, :] = jnp.zeros((7 - CONV, 2 * NS), f32)
        heads = step_all_ref.shape[1]
        direct, step = direct_ref[...], step_all_ref[0]
        grad_running = along_ref[...].T[:heads] - step * direct
        row_index = lax.broadcasted_iota(jnp.int32, (rows, rows), 0)
        col_index = lax.broadcasted_iota(jnp.int32, (rows, rows), 1)
        lower = jnp.where(col_index <= row_index, 1.0, 0.0)
        grad_product = jnp.dot(
            grad_running, lower, precision=lax.Precision.HIGHEST, preferred_element_type=f32
        )
        grad_raw = (direct + grad_product * rate_ref[...]) * step_sig_ref[0]
        head_sums_ref[0, :, 0:1] = jnp.sum(grad_product * step, axis=1, keepdims=True)
        head_sums_ref[0, :, 1:2] = jnp.sum(grad_raw, axis=1, keepdims=True)
        wide = jnp.concatenate([grad_raw, jnp.zeros((STEP_PAD - heads, rows), f32)], axis=0)
        first_ref[:, rest + 2 * NS : after_rest] = wide.T.astype(bf16)
        first_ref[:, first_ref.shape[1] - others_ref.shape[1] :] = others_ref[...]


def state_specs(rows, pairs):
    block = pl.BlockSpec((rows, 2 * SHD), lambda m, p: (m, p))
    return {
        "block": block,
        "taps": pl.BlockSpec((CONV + 1, 2 * SHD * pairs), lambda m, p: (0, 0)),
        "vector": pl.BlockSpec((1, 2 * SHD * pairs), lambda m, p: (0, 0)),
        "state": pl.BlockSpec((rows, 2 * NS), lambda m, p: (m, 0)),
        "columns": pl.BlockSpec((rows, 8), lambda m, p: (m, 0)),
        "row": pl.BlockSpec((1, 1, rows), lambda m, p: (m, 0, 0)),
        "head_row": pl.BlockSpec((1, pairs, 2, rows), lambda m, p: (m, 0, 0, 0)),
        "head_col": pl.BlockSpec((1, pairs, rows, 2), lambda m, p: (m, 0, 0, 0)),
    }


def state_forward(signal, gate, taps, skip, state, seg_row, run_row, run_col, step, columns):
    micro, pairs, _, rows = run_row.shape
    spec = state_specs(rows, pairs)
    total, width = signal.shape
    return pl.pallas_call(
        state_forward_kernel,
        out_shape=(jax.ShapeDtypeStruct((total, width), f32), jax.ShapeDtypeStruct((total, 2 * SHD), f32)),
        grid=(micro, pairs),
        in_specs=[spec[name] for name in (
            "block", "block", "taps", "vector", "state", "row", "head_row", "head_col", "head_row", "columns")],
        out_specs=(spec["block"], pl.BlockSpec((rows, 2 * SHD), lambda m, p: (m, 0))),
        scratch_shapes=[pltpu.VMEM((rows, rows), f32), pltpu.VMEM((rows, rows), f32)],
        cost_estimate=pl.CostEstimate(
            flops=8 * total * rows * width // SHD * SHD, transcendentals=total * rows * width // SHD, bytes_accessed=12 * total * width
        ),
        name="state_forward",
    )(signal, gate, taps, skip, state, seg_row, run_row, run_col, step, columns)


def state_backward(
    grad, out, gate, signal, taps, skip, gain, state, seg_row, run_row, run_col, step, columns,
    state_raw, state_taps, step_all, step_sig, rate, others,
):
    micro, pairs, _, rows = run_row.shape
    heads = 2 * pairs
    spec = state_specs(rows, pairs)
    total, width = signal.shape
    joint = 2 * width + 2 * NS + STEP_PAD + others.shape[1]
    heads_block = pl.BlockSpec((1, heads, rows), lambda m, p: (m, 0, 0))
    return pl.pallas_call(
        state_backward_kernel,
        out_shape=(
            jax.ShapeDtypeStruct((total, joint), bf16),
            jax.ShapeDtypeStruct((micro, 8, width), f32),
            jax.ShapeDtypeStruct((micro, 8, 2 * NS), f32),
            jax.ShapeDtypeStruct((micro, heads, 2), f32),
        ),
        grid=(micro, pairs),
        in_specs=[spec[name] for name in (
            "block", "block", "block", "block", "taps", "vector", "vector", "state",
            "row", "head_row", "head_col", "head_row", "columns", "state")]
        + [
            pl.BlockSpec((CONV + 1, 2 * NS), lambda m, p: (0, 0)), heads_block, heads_block,
            pl.BlockSpec((heads, 1), lambda m, p: (0, 0)), pl.BlockSpec((rows, others.shape[1]), lambda m, p: (m, 0)),
        ],
        out_specs=(
            pl.BlockSpec((rows, joint), lambda m, p: (m, 0)), pl.BlockSpec((1, 8, 2 * SHD), lambda m, p: (m, 0, p)),
            pl.BlockSpec((1, 8, 2 * NS), lambda m, p: (m, 0, 0)),
            pl.BlockSpec((1, heads, 2), lambda m, p: (m, 0, 0)),
        ),
        scratch_shapes=[pltpu.VMEM((rows, rows), f32)] * 3 + [pltpu.VMEM((heads, rows), f32), pltpu.VMEM((rows, 2 * SHD), f32)],
        cost_estimate=pl.CostEstimate(
            flops=20 * total * rows * width, transcendentals=total * rows * width // SHD, bytes_accessed=20 * total * width
        ),
        name="state_backward",
    )(
        grad, out, gate, signal, taps, skip, gain, state, seg_row, run_row, run_col, step, columns,
        state_raw, state_taps, step_all, step_sig, rate, others,
    )


def local(
    inputs,
    out_grad,
    deal_order,
    segment,
    query_weight,
    key_weight,
    value_weight,
    attention_out,
    mamba_gate,
    mamba_input,
    step_weight,
    state_weight,
    mamba_out,
    feed_gate,
    feed_up,
    feed_down,
    gain_input,
    gain_middle,
    kernel_inner,
    kernel_state,
    mixer_gain,
    step_bias,
    log_rate,
    skip_gain,
):
    micro, own, width = inputs.shape
    groups = lax.axis_size("dp")
    lanes = lax.axis_size("tensor")
    lane = lax.axis_index("tensor")
    group = lax.axis_index("dp")
    device = group * lanes + lane
    per = own // groups
    rows = own * lanes
    total = micro * rows
    inner_width = SH * SHD
    outer_count = groups // 4
    shard = width // groups

    swap_lane = [(0, 1), (1, 0)]

    def other_lane(values):
        return lax.ppermute(values, "tensor", swap_lane)

    def other_group(values, bits):
        return lax.ppermute(values, "dp", [(i, i ^ bits) for i in range(groups)])

    def after(value, *others):
        return lax.optimization_barrier((value, others))[0]

    step_padded = jnp.pad(step_weight, ((0, 0), (0, STEP_PAD - step_weight.shape[1])))
    early = dict(
        gate=mamba_gate, state=state_weight, step=step_padded, input=mamba_input, query=query_weight, key=key_weight,
        value=value_weight, mix=mamba_out, attn=attention_out,
    )
    late = dict(fgate=feed_gate, fup=feed_up, fdown=feed_down)
    whole, places_of = {}, {}
    for label, group_weights in (("early", early), ("late", late)):
        start = 0
        for name, weight in group_weights.items():
            places_of[name] = (label, start, weight.shape[1])
            start += weight.shape[1]
        whole[label] = lax.all_gather(join_columns(list(group_weights.values())), "dp", axis=0, tiled=True)

    def full(name):
        label, start, size = places_of[name]
        return lax.slice_in_dim(whole[label], start, start + size, axis=1)

    own_places = jnp.arange(own, dtype=jnp.int32)
    own_order = lax.dynamic_slice_in_dim(deal_order, device * own, own, 1)
    micro_index = jnp.arange(micro, dtype=jnp.int32)[:, None]

    def buffer_place(destination, rank):
        return destination * (micro * per) + micro_index * per + rank

    send_rank = jnp.sum((own_order[:, None, :] < own_order[:, :, None]).astype(jnp.int32), axis=2)
    send_place = buffer_place(send_rank // per, send_rank % per).reshape(-1)
    lane_order = lax.dynamic_index_in_dim(deal_order.reshape(micro, groups, lanes, own), lane, 2, keepdims=False)
    slots = device * own + own_places
    found = lane_order[:, None, :, :] == slots[None, :, None, None]
    source = jnp.sum(
        jnp.where(found, jnp.arange(groups, dtype=jnp.int32)[None, None, :, None], 0), axis=(2, 3)
    )
    recv_rank = jnp.sum(
        ((source[:, None, :] == source[:, :, None]) & (own_places[None, None, :] < own_places[None, :, None])).astype(jnp.int32),
        axis=2,
    )
    recv_place = buffer_place(source, recv_rank).reshape(-1)
    buffer_places = jnp.arange(micro * own, dtype=jnp.int32)
    send_pick = (buffer_places[:, None] == send_place[None, :]).astype(bf16)
    recv_pick = (recv_place[:, None] == buffer_places[None, :]).astype(bf16)

    def exchange(buffer):
        return lax.all_to_all(
            buffer.reshape(groups, micro * per, width), "dp", split_axis=0, concat_axis=0, tiled=True
        ).reshape(micro * own, width)

    def deal(values):
        sent = project(send_pick, values.reshape(micro * own, width)).astype(bf16)
        return project(recv_pick, exchange(sent)).astype(bf16)

    def deal_order_rows(values):
        return outer_sum(recv_pick, values).astype(bf16)

    def deal_take(moved):
        return outer_sum(send_pick, moved).astype(bf16).reshape(micro, own, width)

    def join_lanes(values):
        mine = values.reshape(micro, 1, own, -1)
        theirs = other_lane(values).reshape(micro, 1, own, -1)
        low = jnp.where(lane == 0, mine, theirs)
        high = jnp.where(lane == 0, theirs, mine)
        return jnp.concatenate([low, high], axis=1).reshape(total, -1)

    def lane_rows(values, which):
        return lax.dynamic_index_in_dim(
            values.reshape(micro, lanes, own, -1), which, 1, keepdims=False
        ).reshape(micro * own, -1)

    own_in = deal(inputs)
    own_grad = deal(out_grad)
    whole_in = join_lanes(own_in)
    whole_grad = join_lanes(own_grad)

    before = jnp.sum((segment[:, None, :] < segment[:, :, None]).astype(jnp.int32), axis=2)
    places = jnp.arange(rows, dtype=jnp.int32)
    position = (places[None, :] - before).reshape(total, 1)

    masks = [1 << place for place in range(groups.bit_length() - 1)]
    relative = []
    for block in range(groups):
        flip = 0
        for place, mask in enumerate(masks):
            if block >> (len(masks) - 1 - place) & 1:
                flip ^= mask
        relative.append(flip)
    block_order = jnp.bitwise_xor(group.astype(jnp.int32), jnp.array(relative, jnp.int32))

    def split_left(left):
        return pick_halves(left, block_order, shard)

    inner_places = list(range(1, len(masks)))

    def core_send(left_parts, right):
        return outer_low(left_parts[1], right)

    def halve(kept, place):
        return (
            lax.slice_in_dim(kept, 1, 2, axis=place - 1).reshape(-1, kept.shape[-1]),
            lax.slice_in_dim(kept, 0, 1, axis=place - 1),
        )

    class Reduction:
        def __init__(self, first):
            self.places = [place for place in first if place in inner_places]
            self.places += [place for place in inner_places if place not in first]
            self.stage = 0

        def move(self, send, kept):
            self.came = other_group(send, masks[self.places[self.stage]])
            self.kept = kept
            self.stage += 1

        def first(self, left_parts, right, from_core):
            kept = (outer_sum(left_parts[0], right) + from_core.astype(f32)).astype(bf16)
            kept = kept.reshape((2,) * len(inner_places) + (shard, -1))
            return halve(kept, self.places[0])

        def added(self):
            return self.kept.astype(f32) + self.came.reshape(self.kept.shape).astype(f32)

        def next(self):
            return halve(self.added().astype(bf16), self.places[self.stage])

        def last(self):
            return self.added().reshape(shard, -1)

        def step(self):
            return self.next() if self.stage < len(self.places) else self.last()

    order = [deal_order[0, 0] >= 0]

    def unit(work):
        shapes = jax.eval_shape(work)
        results = lax.cond(
            order[0], work, lambda: jax.tree.map(lambda leaf: jnp.zeros(leaf.shape, leaf.dtype), shapes)
        )
        leaves, form = jax.tree.flatten(results)
        least = min(range(len(leaves)), key=lambda place: leaves[place].size)
        leaves[least], order[0] = lax.optimization_barrier((leaves[least], order[0]))
        return jax.tree.unflatten(form, leaves)

    in32 = whole_in.astype(f32)
    in_scale = rms_scale(in32)
    normed_low = (in32 * in_scale * gain_input).astype(bf16)
    normed_left = split_left(normed_low)
    whole["early"] = after(whole["early"], whole_grad, normed_left)
    gate_z = project(normed_low, full("gate"))
    ssm_in = project(normed_low, full("input"))
    state_raw = project(normed_low, full("state"))
    heads = step_weight.shape[1]
    raw_step = project(normed_low, full("step"))[:, :heads]
    state_low = jax.nn.silu(conv_sum(state_raw, kernel_state, position)).astype(bf16)
    rate = -jnp.exp(log_rate)
    step_size = jax.nn.softplus(raw_step + step_bias)
    step_heads = step_size.reshape(micro, rows, heads).transpose(0, 2, 1)
    lower = (places[None, :] <= places[:, None]).astype(f32)
    running = jnp.einsum(
        "mhj,ij->mhi", step_heads * rate[None, :, None], lower, precision=lax.Precision.HIGHEST, preferred_element_type=f32
    )
    pairs = heads // 2
    run_row = running.reshape(micro, pairs, 2, rows)
    run_col = run_row.transpose(0, 1, 3, 2)
    step_row = step_heads.reshape(micro, pairs, 2, rows)
    skip_wide = jnp.repeat(skip_gain, SHD)[None, :]
    layout = (state_low, segment.reshape(micro, 1, rows).astype(f32), run_row, run_col, step_row)
    row_facts = jnp.concatenate([segment.reshape(total, 1).astype(f32), position.astype(f32)], axis=1)
    row_columns = jnp.pad(row_facts, ((0, 0), (0, 6)))
    query_cols, key_cols = query_weight.shape[1], key_weight.shape[1]
    attention_tables = (*rope_tables(position), row_columns, layout[1])
    joint_start = places_of["query"][1]
    joint_weight = lax.slice_in_dim(whole["early"], joint_start, joint_start + query_cols + 2 * key_cols, axis=1)
    ssm_out, squares = state_forward(ssm_in, gate_z, kernel_inner, skip_wide, *layout, row_columns)
    attended_low, query_low, key_low, value_low = attention_forward(
        project(normed_low, joint_weight), query_cols, key_cols, attention_tables
    )
    square_own = jnp.sum(squares, axis=1)
    square_sum = square_own + other_lane(square_own)
    inv_rms = lax.rsqrt(square_sum / inner_width + epsilon)[:, None]
    gated_low = (ssm_out * jax.nn.silu(gate_z) * inv_rms * mixer_gain).astype(bf16)

    branch_part = (project_back(gated_low, full("mix")) + project_back(attended_low, full("attn"))).astype(bf16)
    branch = branch_part.astype(f32) + other_lane(branch_part).astype(f32)
    whole_mid = (in32 + branch).astype(bf16)
    mid32 = whole_mid.astype(f32)
    mid_scale = rms_scale(mid32)
    mid_low = (mid32 * mid_scale * gain_middle).astype(bf16)
    red_fgate, red_fup, red_low, red_high = [Reduction(places) for places in ((1, 2), (2, 1), (1, 2), (2, 1))]
    feeds = (red_fgate, red_fup)
    ff_cols = feed_gate.shape[1]
    gate_cols = mamba_gate.shape[1]

    def feed_forward():
        gate_ff = project(mid_low, full("fgate"))
        up_ff = project(mid_low, full("fup"))
        sig_ff = jax.nn.sigmoid(gate_ff)
        hidden_low = (gate_ff * sig_ff * up_ff).astype(bf16)
        grad_hidden = project(whole_grad, full("fdown"))
        gate_ff_low = (grad_hidden * up_ff * (sig_ff * (1.0 + gate_ff * (1.0 - sig_ff)))).astype(bf16)
        up_ff_low = (grad_hidden * (gate_ff * sig_ff)).astype(bf16)
        feed_low = (gate_ff_low, up_ff_low)
        return hidden_low, feed_low, feed_back(feed_low, 0), outer_low(whole_grad, hidden_low)

    half = total // 2

    def feed_back(feed_low, start):
        gate_part, up_part, values, scale = [
            lax.slice_in_dim(array, start, start + half) for array in (*feed_low, mid32, mid_scale)
        ]
        grad_mid_norm = project_back(gate_part, full("fgate")) + project_back(up_part, full("fup"))
        grad_gain = jnp.sum(grad_mid_norm * values * scale, axis=0)
        return rms_back(grad_mid_norm, values, scale, gain_middle).astype(bf16), grad_gain

    hidden_low, feed_low, (mid_part_low, gain_mid_low), part_fdown = unit(feed_forward)
    mid_other_low = hand_over(other_lane(mid_part_low), 2)
    mid_part_high, gain_mid_high = unit(lambda: feed_back(feed_low, half))
    mid_other_high = hand_over(other_lane(mid_part_high), 45)
    sum_fdown = lax.psum_scatter(part_fdown, "dp", scatter_dimension=0, tiled=True)
    grad_gain_mid = gain_mid_low + gain_mid_high

    def feed_output():
        ffn_part = project_back(hidden_low, full("fdown")).astype(bf16)
        return lane_rows(ffn_part, lane), lane_rows(ffn_part, 1 - lane)

    def feed_sends():
        mid_left = split_left(mid_low)
        return mid_left[0], [core_send(mid_left, right) for right in feed_low]

    mid_keep, send_feed = unit(feed_sends)
    order[0], mid_other_low = lax.optimization_barrier((order[0], mid_other_low))
    ffn_own, ffn_send = unit(feed_output)
    feed_came = [other_group(send, 1) for send in send_feed]

    def keep_first(keep, right, came, reductions, sizes):
        kept = (outer_sum(keep, right) + came.astype(f32)).astype(bf16)
        kept = kept.reshape((2,) * len(inner_places) + (shard, -1))
        moves, start = [], 0
        for red, size in zip(reductions, sizes):
            moves.append(halve(kept[..., start : start + size], red.places[0]))
            start += size
        return moves

    def settle(reductions, steps):
        for red, step in zip(reductions, steps):
            if red.stage < len(red.places):
                red.move(*step)
            else:
                red.result = step

    mid_other_high, feed_came = lax.optimization_barrier((mid_other_high, feed_came))
    moves = unit(
        lambda: [
            keep_first(mid_keep, right, came, (red,), (ff_cols,))[0] for red, right, came in zip(feeds, feed_low, feed_came)
        ]
    )
    for red, move in zip(feeds, moves):
        red.move(*move)

    def branch_backward():
        mid_sums = [
            mine.astype(f32) + other.astype(f32)
            for mine, other in ((mid_part_low, mid_other_low), (mid_part_high, mid_other_high))
        ]
        grad_middle = whole_grad.astype(f32) + jnp.concatenate(mid_sums)
        whole_branch = grad_middle.astype(bf16)
        grad_gated_norm = project(whole_branch, full("mix"))
        cross_own = jnp.sum(grad_gated_norm * mixer_gain * (ssm_out * jax.nn.silu(gate_z)), axis=1)
        grad_attended = project(whole_branch, full("attn")).astype(bf16)
        joint_low = attention_backward(grad_attended, query_low, key_low, value_low, attention_tables)
        return (
            cross_own, lane_rows(grad_middle, lane), grad_gated_norm, whole_branch,
            joint_low,
        )

    cross_own, grad_middle_own, grad_gated_norm, whole_branch, joint_low = unit(branch_backward)
    cross_other = other_lane(cross_own)

    ffn_other = other_lane(ffn_send)

    def branch_partial():
        ffn_out = ffn_own.astype(f32) + ffn_other.astype(f32)
        out_rows = (lane_rows(whole_mid, lane).astype(f32) + ffn_out).astype(bf16)
        return outer_low(whole_branch, jnp.concatenate([gated_low, attended_low], axis=1)), deal_order_rows(out_rows)

    part_branch, out_sent = unit(branch_partial)
    out_moved = exchange(out_sent)
    sum_branch = lax.psum_scatter(part_branch, "dp", scatter_dimension=0, tiled=True)
    step_sig = jax.nn.sigmoid(raw_step + step_bias).reshape(micro, rows, heads).transpose(0, 2, 1)
    gain_row, rate_column = mixer_gain[None, :], rate[:, None]

    def state_space_backward():
        cross = (inv_rms**3) * ((cross_own + cross_other)[:, None] / inner_width)
        columns = jnp.pad(jnp.concatenate([row_facts, inv_rms, cross], axis=1), ((0, 0), (0, 4)))
        first_right, column_sums, state_sums, head_sums = state_backward(
            grad_gated_norm, ssm_out, gate_z, ssm_in, kernel_inner, skip_wide, gain_row, *layout, columns,
            state_raw, kernel_state, step_heads, step_sig, rate_column, joint_low,
        )
        return column_sums, state_sums, head_sums, first_right

    column_sums, state_sums, head_sums, first_right = unit(state_space_backward)

    total_fdown_low = [sum_fdown]
    order[0], total_fdown_low = lax.optimization_barrier((order[0], total_fdown_low))
    send_first, steps, block_out = unit(
        lambda: (core_send(normed_left, first_right), [red.step() for red in feeds], deal_take(out_moved))
    )
    settle(feeds, steps)
    first_came = other_group(send_first, 1)

    def input_gradient():
        grad_normed = project_back(first_right, lax.slice_in_dim(whole["early"], 0, first_right.shape[1], axis=1))
        grad_gain_in = jnp.sum(grad_normed * in32 * in_scale, axis=0)
        in_part = rms_back(grad_normed, in32, in_scale, gain_input).astype(bf16)
        return grad_gain_in, lane_rows(in_part, lane), lane_rows(in_part, 1 - lane)

    grad_gain_in, in_own, in_send = unit(input_gradient)

    firsts = (red_low, red_high)
    low_size = gate_cols + 2 * NS + STEP_PAD
    first_sizes = (low_size, first_right.shape[1] - low_size)

    def first_moves():
        moves = keep_first(normed_left[0], first_right, first_came, firsts, first_sizes)
        return moves, lax.optimization_barrier(in_send), [red.step() for red in feeds]

    moves, in_send, steps = unit(first_moves)
    settle(feeds, steps)
    for red, move in zip(firsts, moves):
        red.move(*move)
    in_other = hand_over(other_lane(in_send), 6)

    def small_block():
        head_row = (jnp.sum(head_sums, axis=0).T * jnp.stack([rate, jnp.ones_like(rate)])).reshape(1, -1)
        return jnp.concatenate(
            [
                jnp.concatenate([jnp.sum(column_sums, axis=0), jnp.sum(state_sums, axis=0)], axis=1),
                grad_gain_in[None, :], grad_gain_mid[None, :], jnp.pad(head_row, ((0, 5), (0, width - head_row.shape[1]))),
            ]
        )
    flat = unit(small_block)
    flat_moved = other_group(flat, masks[0])

    def send_input():
        in_sum = in_own.astype(f32) + in_other.astype(f32)
        return deal_order_rows((in_sum + grad_middle_own).astype(bf16))

    bits = 1

    def finish():
        low, high = red_low.result, red_high.result
        state_rows = low[:, gate_cols : gate_cols + 2 * NS].reshape(lanes, shard // lanes, 2 * NS)
        cut = [0, gate_cols, gate_cols + query_cols, gate_cols + query_cols + key_cols, high.shape[1]]
        pieces = (
            low[:, :gate_cols], low[:, gate_cols + 2 * NS : gate_cols + 2 * NS + heads],
            [high[:, start:stop] for start, stop in zip(cut, cut[1:])],
            [lax.dynamic_index_in_dim(state_rows, which, 0, keepdims=False) for which in (lane, 1 - lane)],
        )
        return pieces, deal_take(in_moved)

    arrived = [red.came for red in feeds] + [sum_branch]
    order[0], arrived = lax.optimization_barrier((order[0], arrived))
    for red, came in zip(feeds, arrived):
        red.came = came
    sum_branch = arrived[-1]
    in_moved = None
    while red_low.stage < len(red_low.places):
        moving = [red for red in (*firsts, *feeds) if red.stage < len(red.places)]
        steps, flat, sent = unit(
            lambda: (
                [red.next() for red in moving],
                flat + flat_moved if flat_moved is not None else flat,
                send_input() if in_moved is None else (),
            )
        )
        settle(moving, steps)
        flat_moved = other_group(flat, masks[bits]) if bits < len(masks) else None
        bits += 1
        if in_moved is None:
            in_moved = exchange(sent)
    totals, flat = unit(
        lambda: (
            [red.last() for red in feeds] + [sum_branch.astype(f32), total_fdown_low[0].astype(f32)],
            flat + flat_moved if flat_moved is not None else flat,
        )
    )
    total_fgate, total_fup, total_branch, total_fdown = totals
    flat_moved = other_group(flat, masks[bits]) if bits < len(masks) else None
    bits += 1

    def last_work():
        red_low.result, red_high.result = red_low.last(), red_high.last()
        return finish(), flat + flat_moved if flat_moved is not None else flat

    ((total_gate, total_step, (total_input, total_query, total_key, total_value), states), grad_input), flat = unit(last_work)
    while bits < len(masks):
        flat = flat + other_group(flat, masks[bits])
        bits += 1
    theirs = other_lane(flat)
    low, high = jnp.where(lane == 0, flat, theirs), jnp.where(lane == 0, theirs, flat)
    both = flat + theirs

    def joined(row, start, count):
        return jnp.concatenate([low[row, start : start + count], high[row, start : start + count]])

    sum_gin, sum_gmid = both[8], both[9]
    sum_kst = both[: CONV + 1, gate_cols : gate_cols + 2 * NS]
    sum_kin = jnp.concatenate([low[: CONV + 1, :gate_cols], high[: CONV + 1, :gate_cols]], axis=1)
    sum_mix = joined(CONV + 1, 0, gate_cols)
    sum_skip = jnp.sum(joined(CONV + 2, 0, gate_cols).reshape(SH, SHD), axis=1)
    sum_bias = joined(10, heads, heads)
    sum_rate = joined(10, 0, heads)

    total_mix, total_attn = total_branch[:, :gate_cols], total_branch[:, gate_cols:]
    state_lane = states[0] + other_lane(states[1])
    return (
        block_out,
        grad_input,
        total_query,
        total_key,
        total_value,
        total_attn,
        total_gate,
        total_input,
        total_step,
        state_lane,
        total_mix,
        total_fgate,
        total_fup,
        total_fdown,
        sum_gin,
        sum_gmid,
        sum_kin,
        sum_kst,
        sum_mix,
        sum_bias,
        sum_rate,
        sum_skip,
    )


def solution(mesh):
    both = P("dp", "tensor")
    in_specs = (
        P(None, ("dp", "tensor"), None),
        P(None, ("dp", "tensor"), None),
        P(),
        P(None, "dp"),
        both,
        both,
        both,
        both,
        both,
        both,
        both,
        P("dp", None),
        both,
        both,
        both,
        both,
        P(),
        P(),
        P(None, "tensor"),
        P(),
        P("tensor"),
        P("tensor"),
        P("tensor"),
        P("tensor"),
    )
    out_specs = (
        P(None, ("dp", "tensor"), None),
        P(None, ("dp", "tensor"), None),
        both,
        both,
        both,
        both,
        both,
        both,
        both,
        P(("dp", "tensor"), None),
        both,
        both,
        both,
        both,
        P(),
        P(),
        P(),
        P(),
        P(),
        P(),
        P(),
        P(),
    )
    return jax.shard_map(local, mesh=mesh, in_specs=in_specs, out_specs=out_specs, check_vma=False)
```

```python
import functools
import math

import jax
import jax.numpy as jnp
from jax import lax
from jax.experimental import pallas as pl
from jax.experimental.layout import Layout, with_layout_constraint
from jax.experimental.pallas import tpu as pltpu
from jax.sharding import PartitionSpec as P

HEAD = 128
SH = 48
SHD = 64
NS = 256
CONV = 4
STEP_PAD = 128

epsilon = 1e-05
rope_base = 100000000000.0
f32 = jnp.float32
bf16 = jnp.bfloat16


def project(left, right):
    return jnp.dot(left, right, preferred_element_type=f32)


def project_back(left, right):
    return lax.dot_general(left, right, (((1,), (1,)), ((), ())), preferred_element_type=f32)


def outer_sum(left, right):
    return lax.dot_general(left, right, (((0,), (0,)), ((), ())), preferred_element_type=f32)


def outer_low(left, right):
    return with_layout_constraint(outer_sum(left, right).astype(bf16), Layout(major_to_minor=(0, 1)))


def rms_scale(values):
    return lax.rsqrt(jnp.mean(values * values, axis=-1, keepdims=True) + epsilon)


def rms_back(grad, values, scale, gain):
    weighted = grad * gain
    inner = jnp.sum(weighted * values, axis=-1, keepdims=True)
    return scale * weighted - values * (scale * scale * scale * inner / values.shape[-1])


def shift_down(values, count):
    return jnp.concatenate([jnp.zeros((count, values.shape[1]), values.dtype), values[:-count]], axis=0)


def shift_up(values, count):
    return jnp.concatenate([values[count:], jnp.zeros((count, values.shape[1]), values.dtype)], axis=0)


def conv_sum(signal, kernel, position):
    summed = kernel[CONV][None, :] + signal * kernel[0][None, :]
    for tap in range(1, CONV):
        moved = jnp.where(position >= tap, shift_down(signal, tap), 0.0)
        summed = summed + moved * kernel[tap][None, :]
    return summed


def silu_back(values):
    sig = jax.nn.sigmoid(values)
    return sig * (1.0 + values * (1.0 - sig))


def conv_back(grad, signal, kernel, position):
    grad_sum = grad * silu_back(conv_sum(signal, kernel, position))
    grad_signal = grad_sum * kernel[0][None, :]
    grad_taps = [jnp.sum(grad_sum * signal, axis=0)]
    for tap in range(1, CONV):
        kept = jnp.where(position >= tap, grad_sum, 0.0)
        grad_signal = grad_signal + shift_up(kept, tap) * kernel[tap][None, :]
        grad_taps.append(jnp.sum(kept * shift_down(signal, tap), axis=0))
    grad_taps.append(jnp.sum(grad_sum, axis=0))
    return grad_signal, jnp.stack(grad_taps)


def rope_tables(position):
    half_size = HEAD // 2
    frequency = jnp.exp(jnp.arange(half_size, dtype=f32) * (-2.0 * math.log(rope_base) / HEAD))
    angles = position.astype(f32) * frequency[None, :]
    cosine, sine = jnp.cos(angles), jnp.sin(angles)
    return jnp.concatenate([cosine, cosine], axis=1), jnp.concatenate([-sine, sine], axis=1)


def copy_blocks(order_ref, first_ref, second_ref, first_out_ref, second_out_ref):
    first_out_ref[...] = first_ref[...]
    second_out_ref[...] = second_ref[...]


def pick_halves(values, order, block):
    height, width = values.shape
    count = width // block // 2
    if block % 128:
        mixed = jnp.take(values.reshape(height, -1, block), order, axis=1).reshape(height, width)
        return mixed[:, : width // 2], mixed[:, width // 2 :]
    half = jax.ShapeDtypeStruct((height, width // 2), values.dtype)
    out_spec = pl.BlockSpec((height, block), lambda i, order: (0, i))
    return pl.pallas_call(
        copy_blocks,
        out_shape=(half, half),
        grid_spec=pltpu.PrefetchScalarGridSpec(
            num_scalar_prefetch=1,
            grid=(count,),
            in_specs=[
                pl.BlockSpec((height, block), lambda i, order: (0, order[i])),
                pl.BlockSpec((height, block), lambda i, order: (0, order[i + count])),
            ],
            out_specs=(out_spec, out_spec),
        ),
        cost_estimate=pl.CostEstimate(flops=0, transcendentals=0, bytes_accessed=4 * height * width),
        name="pick_halves",
    )(order, values, values)


def join_columns(pieces):
    height = pieces[0].shape[0]
    width = sum(piece.shape[1] for piece in pieces)

    def put_all(*refs):
        start = 0
        for source in refs[:-1]:
            refs[-1][:, start : start + source.shape[1]] = source[...]
            start += source.shape[1]

    return pl.pallas_call(
        put_all,
        out_shape=jax.ShapeDtypeStruct((height, width), pieces[0].dtype),
        cost_estimate=pl.CostEstimate(flops=0, transcendentals=0, bytes_accessed=4 * height * width),
        name="join_columns",
    )(*pieces)


def hand_over(values, microseconds):
    def idle(values_ref, out_ref):
        pass

    return pl.pallas_call(
        idle,
        out_shape=jax.ShapeDtypeStruct(values.shape, values.dtype),
        in_specs=[pl.BlockSpec(memory_space=pl.ANY)],
        out_specs=pl.BlockSpec(memory_space=pl.ANY),
        input_output_aliases={0: 0},
        cost_estimate=pl.CostEstimate(flops=microseconds * 1150000000, transcendentals=0, bytes_accessed=0),
        name="hand_over",
    )(values)


NEGATIVE = -1e30


def sigmoid_of(values):
    return 1.0 / (1.0 + jnp.exp(-values))


def block_mask(rows, segment_col, segment_row):
    row_index = lax.broadcasted_iota(jnp.int32, (rows, rows), 0)
    col_index = lax.broadcasted_iota(jnp.int32, (rows, rows), 1)
    return jnp.where((segment_col == segment_row) & (col_index <= row_index), 0.0, NEGATIVE)


def conv_block(signal, taps_ref, position):
    summed = taps_ref[CONV : CONV + 1, :] + signal * taps_ref[0:1, :]
    moved = []
    for tap in range(1, CONV):
        shifted = jnp.where(position >= tap, pltpu.roll(signal, tap, 0), 0.0)
        moved.append(shifted)
        summed = summed + shifted * taps_ref[tap : tap + 1, :]
    return summed, moved


def conv_block_back(grad_sum, signal, moved, taps_ref, position, sums_ref):
    rows = signal.shape[0]
    grad_signal = grad_sum * taps_ref[0:1, :]
    sums_ref[0, 0:1, :] = jnp.sum(grad_sum * signal, axis=0, keepdims=True)
    for tap in range(1, CONV):
        kept = jnp.where(position >= tap, grad_sum, 0.0)
        grad_signal = grad_signal + pltpu.roll(kept, rows - tap, 0) * taps_ref[tap : tap + 1, :]
        sums_ref[0, tap : tap + 1, :] = jnp.sum(grad_sum * moved[tap - 1], axis=0, keepdims=True)
    sums_ref[0, CONV : CONV + 1, :] = jnp.sum(grad_sum, axis=0, keepdims=True)
    return grad_signal


def mixing_block(inner, mask, run_col, run_row, step_row):
    decay = jnp.exp(run_col - run_row + mask)
    return decay, (inner * decay * step_row).astype(bf16)


def turn(values, cosine_ref, sine_ref, sign):
    return values * cosine_ref[...] + sign * (pltpu.roll(values, HEAD // 2, 1) * sine_ref[...])


def head_probs(query_low, key_low, mask):
    logits = lax.dot_general(query_low, key_low, (((1,), (1,)), ((), ())), preferred_element_type=f32) * HEAD ** (-0.5)
    logits = logits + mask
    weights = jnp.exp(logits - jnp.max(logits, axis=1, keepdims=True))
    return weights / jnp.sum(weights, axis=1, keepdims=True)


def attention_forward_kernel(
    query_ref, key_ref, value_ref, cosine_ref, sine_ref, columns_ref, seg_row_ref,
    attended_ref, query_low_ref, key_low_ref, value_low_ref, mask_ref,
):
    rows = query_ref.shape[0]

    @pl.when(pl.program_id(1) == 0)
    def _():
        mask_ref[...] = block_mask(rows, columns_ref[:, 0:1], seg_row_ref[0])

    query_low = turn(query_ref[...], cosine_ref, sine_ref, 1.0).astype(bf16)
    key_low = turn(key_ref[...], cosine_ref, sine_ref, 1.0).astype(bf16)
    value_low = value_ref[...].astype(bf16)
    probs_low = head_probs(query_low, key_low, mask_ref[...]).astype(bf16)
    attended_ref[...] = jnp.dot(probs_low, value_low, preferred_element_type=f32).astype(bf16)
    query_low_ref[...] = query_low
    key_low_ref[...] = key_low
    value_low_ref[...] = value_low


def attention_backward_kernel(
    grad_ref, query_ref, key_ref, value_ref, cosine_ref, sine_ref, columns_ref, seg_row_ref,
    joint_ref, mask_ref, grad_key_ref, grad_value_ref, *, group, query_cols, key_cols,
):
    rows = query_ref.shape[0]
    head = pl.program_id(1)

    @pl.when(head == 0)
    def _():
        mask_ref[...] = block_mask(rows, columns_ref[:, 0:1], seg_row_ref[0])

    @pl.when(head % group == 0)
    def _():
        grad_key_ref[...] = jnp.zeros_like(grad_key_ref)
        grad_value_ref[...] = jnp.zeros_like(grad_value_ref)

    grad, query_low, key_low = grad_ref[...], query_ref[...], key_ref[...]
    probs = head_probs(query_low, key_low, mask_ref[...])
    grad_probs = lax.dot_general(grad, value_ref[...], (((1,), (1,)), ((), ())), preferred_element_type=f32)
    grad_value_ref[...] += lax.dot_general(
        probs.astype(bf16), grad, (((0,), (0,)), ((), ())), preferred_element_type=f32
    )
    grad_logits = (probs * (grad_probs - jnp.sum(probs * grad_probs, axis=1, keepdims=True))).astype(bf16)
    grad_query = jnp.dot(grad_logits, key_low, preferred_element_type=f32) * HEAD ** (-0.5)
    grad_key_ref[...] += lax.dot_general(
        grad_logits, query_low, (((0,), (0,)), ((), ())), preferred_element_type=f32
    ) * HEAD ** (-0.5)
    joint_ref[:, pl.ds(pl.multiple_of(head * HEAD, HEAD), HEAD)] = turn(
        grad_query, cosine_ref, sine_ref, -1.0
    ).astype(bf16)

    @pl.when(head % group == group - 1)
    def _():
        place = head // group * HEAD
        joint_ref[:, pl.ds(pl.multiple_of(query_cols + place, HEAD), HEAD)] = turn(
            grad_key_ref[...], cosine_ref, sine_ref, -1.0
        ).astype(bf16)
        joint_ref[:, pl.ds(pl.multiple_of(query_cols + key_cols + place, HEAD), HEAD)] = grad_value_ref[...].astype(bf16)


def attention_specs(rows, group):
    table = pl.BlockSpec((rows, HEAD), lambda m, h: (m, 0))
    return (
        lambda start: pl.BlockSpec((rows, HEAD), lambda m, h: (m, start + h)),
        lambda start: pl.BlockSpec((rows, HEAD), lambda m, h: (m, start + h // group)),
        [table, table, pl.BlockSpec((rows, 8), lambda m, h: (m, 0)), pl.BlockSpec((1, 1, rows), lambda m, h: (m, 0, 0))],
    )


def attention_forward(query, key_value, tables):
    micro, _, rows = tables[3].shape
    total, query_cols = query.shape
    key_cols = key_value.shape[1] // 2
    heads, kv_heads = query_cols // HEAD, key_cols // HEAD
    by_head, by_kv, table_specs = attention_specs(rows, heads // kv_heads)
    return pl.pallas_call(
        attention_forward_kernel,
        out_shape=tuple(jax.ShapeDtypeStruct((total, size), bf16) for size in (query_cols, query_cols, key_cols, key_cols)),
        grid=(micro, heads),
        in_specs=[by_head(0), by_kv(0), by_kv(kv_heads)] + table_specs,
        out_specs=(by_head(0), by_head(0), by_kv(0), by_kv(0)),
        scratch_shapes=[pltpu.VMEM((rows, rows), f32)],
        cost_estimate=pl.CostEstimate(
            flops=4 * total * rows * query_cols, transcendentals=total * rows * heads, bytes_accessed=8 * total * query_cols
        ),
        name="attention_forward",
    )(query, key_value, key_value, *tables)


def attention_backward(grad, query, key, value, tables):
    micro, _, rows = tables[3].shape
    total, query_cols = query.shape
    key_cols = key.shape[1]
    heads, kv_heads = query_cols // HEAD, key_cols // HEAD
    by_head, by_kv, table_specs = attention_specs(rows, heads // kv_heads)
    joint_cols = query_cols + 2 * key_cols
    return pl.pallas_call(
        functools.partial(
            attention_backward_kernel, group=heads // kv_heads, query_cols=query_cols, key_cols=key_cols
        ),
        out_shape=jax.ShapeDtypeStruct((total, joint_cols), bf16),
        grid=(micro, heads),
        in_specs=[by_head(0), by_head(0), by_kv(0), by_kv(0)] + table_specs,
        out_specs=pl.BlockSpec((rows, joint_cols), lambda m, h: (m, 0)),
        scratch_shapes=[pltpu.VMEM((rows, rows), f32), pltpu.VMEM((rows, HEAD), f32), pltpu.VMEM((rows, HEAD), f32)],
        cost_estimate=pl.CostEstimate(
            flops=10 * total * rows * query_cols, transcendentals=total * rows * heads, bytes_accessed=8 * total * query_cols
        ),
        name="attention_backward",
    )(grad, query, key, value, *tables)


def state_forward_kernel(
    signal_ref, gate_ref, taps_ref, skip_ref, state_ref, seg_row_ref, run_row_ref, run_col_ref, step_ref, columns_ref,
    out_ref, square_ref, inner_ref, mask_ref,
):
    rows = signal_ref.shape[0]
    position = columns_ref[:, 1:2]
    pair = pl.program_id(1)
    here = pl.ds(pl.multiple_of(pair * 2 * SHD, 2 * SHD), 2 * SHD)
    taps_ref, skip_ref = taps_ref.at[:, here], skip_ref.at[:, here]

    @pl.when(pl.program_id(1) == 0)
    def _():
        inner_ref[...] = lax.dot_general(
            state_ref[:, NS:], state_ref[:, :NS], (((1,), (1,)), ((), ())), preferred_element_type=f32
        )
        mask_ref[...] = block_mask(rows, columns_ref[:, 0:1], seg_row_ref[0])
        square_ref[...] = jnp.zeros_like(square_ref)

    summed, _ = conv_block(signal_ref[...], taps_ref, position)
    cols = summed * sigmoid_of(summed)
    cols_low = cols.astype(bf16)
    mixed = []
    for head in range(2):
        _, mixing = mixing_block(
            inner_ref[...], mask_ref[...], run_col_ref[0, pair, :, head : head + 1],
            run_row_ref[0, pair, head : head + 1, :], step_ref[0, pair, head : head + 1, :],
        )
        mixed.append(jnp.dot(mixing, cols_low, preferred_element_type=f32))
    lanes = lax.broadcasted_iota(jnp.int32, cols.shape, 1)
    out = jnp.where(lanes < SHD, mixed[0], mixed[1]) + skip_ref[...] * cols
    out_ref[...] = out
    gate = gate_ref[...]
    gated = out * (gate * sigmoid_of(gate))
    square_ref[...] += gated * gated


def state_backward_kernel(
    grad_ref, out_ref, gate_ref, signal_ref, taps_ref, skip_ref, gain_ref, state_ref, seg_row_ref, run_row_ref, run_col_ref,
    step_ref, columns_ref, state_raw_ref, state_taps_ref, step_all_ref, step_sig_ref, rate_ref, others_ref,
    first_ref, sums_ref, state_sums_ref, head_sums_ref,
    inner_ref, mask_ref, grad_inner_ref, direct_ref, along_ref, *, query_cols,
):
    rows = signal_ref.shape[0]
    rest = taps_ref.shape[1]
    after_rest = rest + 2 * NS + STEP_PAD
    input_start = after_rest + query_cols
    pair = pl.program_id(1)
    block = pl.ds(pl.multiple_of(pair * 2 * SHD, 2 * SHD), 2 * SHD)
    taps_ref, skip_ref, gain_ref = taps_ref.at[:, block], skip_ref.at[:, block], gain_ref.at[:, block]

    @pl.when(pair == 0)
    def _():
        along_ref[...] = jnp.zeros_like(along_ref)
        inner_ref[...] = lax.dot_general(
            state_ref[:, NS:], state_ref[:, :NS], (((1,), (1,)), ((), ())), preferred_element_type=f32
        )
        mask_ref[...] = block_mask(rows, columns_ref[:, 0:1], seg_row_ref[0])
        grad_inner_ref[...] = jnp.zeros_like(grad_inner_ref)

    grad, out, gate, signal = grad_ref[...], out_ref[...], gate_ref[...], signal_ref[...]
    position, scale, cross = columns_ref[:, 1:2], columns_ref[:, 2:3], columns_ref[:, 3:4]
    here = pl.multiple_of(pair * 2 * SHD, 2 * SHD)
    sig = sigmoid_of(gate)
    silu = gate * sig
    gated = out * silu
    scaled = grad * scale
    grad_gated = scaled * gain_ref[...] - gated * cross
    grad_out = grad_gated * silu
    first_ref[:, pl.ds(here, 2 * SHD)] = (grad_gated * out * (sig * (1.0 + gate * (1.0 - sig)))).astype(bf16)
    summed, moved = conv_block(signal, taps_ref, position)
    sig = sigmoid_of(summed)
    cols = summed * sig
    cols_low = cols.astype(bf16)
    grad_low = grad_out.astype(bf16)
    lanes = lax.broadcasted_iota(jnp.int32, cols.shape, 1)
    zero = jnp.zeros_like(grad_low)
    grad_cols = []
    for head in range(2):
        step_row = step_ref[0, pair, head : head + 1, :]
        inner = inner_ref[...]
        decay, mixing = mixing_block(
            inner, mask_ref[...], run_col_ref[0, pair, :, head : head + 1], run_row_ref[0, pair, head : head + 1, :], step_row
        )
        grad_cols.append(
            lax.dot_general(mixing, grad_low, (((0,), (0,)), ((), ())), preferred_element_type=f32)
        )
        grad_head = jnp.where((lanes < SHD) == (head == 0), grad_low, zero)
        grad_decay = lax.dot_general(
            grad_head, cols_low, (((1,), (1,)), ((), ())), preferred_element_type=f32
        ) * decay
        stepped = grad_decay * step_row
        grad_inner_ref[...] += stepped
        direct_ref[pl.ds(2 * pair + head, 1), :] = jnp.sum(grad_decay * inner, axis=0, keepdims=True)
        along = jnp.sum(stepped * inner, axis=1, keepdims=True)
        along_ref[...] = jnp.where(lanes == 2 * pair + head, along, along_ref[...])
    grad_cols = jnp.where(lanes < SHD, grad_cols[0], grad_cols[1]) + skip_ref[...] * grad_out
    grad_sum = grad_cols * (sig * (1.0 + summed * (1.0 - sig)))
    grad_signal = conv_block_back(grad_sum, signal, moved, taps_ref, position, sums_ref)
    sums_ref[0, CONV + 1 : CONV + 2, :] = jnp.sum(scaled * gated, axis=0, keepdims=True)
    sums_ref[0, CONV + 2 : CONV + 3, :] = jnp.sum(grad_out * cols, axis=0, keepdims=True)
    sums_ref[0, CONV + 3 : CONV + 4, :] = jnp.zeros((1, cols.shape[1]), f32)
    first_ref[:, pl.ds(pl.multiple_of(input_start + here, 2 * SHD), 2 * SHD)] = grad_signal.astype(bf16)

    @pl.when(pair == pl.num_programs(1) - 1)
    def _():
        inner_low = grad_inner_ref[...].astype(bf16)
        for part, (mine, other) in enumerate((((0, NS), (NS, 2 * NS)), ((NS, 2 * NS), (0, NS)))):
            raw = state_raw_ref[:, mine[0] : mine[1]]
            taps = state_taps_ref.at[:, mine[0] : mine[1]]
            summed, moved = conv_block(raw, taps, position)
            sig = sigmoid_of(summed)
            grad = lax.dot_general(
                inner_low, state_ref[:, other[0] : other[1]], (((part,), (0,)), ((), ())), preferred_element_type=f32
            )
            grad_sum = grad * (sig * (1.0 + summed * (1.0 - sig)))
            back = conv_block_back(grad_sum, raw, moved, taps, position, state_sums_ref.at[:, :, mine[0] : mine[1]])
            first_ref[:, rest + mine[0] : rest + mine[1]] = back.astype(bf16)
        state_sums_ref[0, CONV + 1 :, :] = jnp.zeros((7 - CONV, 2 * NS), f32)
        heads = step_all_ref.shape[1]
        direct, step = direct_ref[...], step_all_ref[0]
        grad_running = along_ref[...].T[:heads] - step * direct
        row_index = lax.broadcasted_iota(jnp.int32, (rows, rows), 0)
        col_index = lax.broadcasted_iota(jnp.int32, (rows, rows), 1)
        lower = jnp.where(col_index <= row_index, 1.0, 0.0)
        grad_product = jnp.dot(
            grad_running, lower, precision=lax.Precision.HIGHEST, preferred_element_type=f32
        )
        grad_raw = (direct + grad_product * rate_ref[...]) * step_sig_ref[0]
        head_sums_ref[0, :, 0:1] = jnp.sum(grad_product * step, axis=1, keepdims=True)
        head_sums_ref[0, :, 1:2] = jnp.sum(grad_raw, axis=1, keepdims=True)
        wide = jnp.concatenate([grad_raw, jnp.zeros((STEP_PAD - heads, rows), f32)], axis=0)
        first_ref[:, rest + 2 * NS : after_rest] = wide.T.astype(bf16)
        first_ref[:, after_rest:input_start] = others_ref[:, :query_cols]
        first_ref[:, input_start + rest :] = others_ref[:, query_cols:]


def state_specs(rows, pairs):
    block = pl.BlockSpec((rows, 2 * SHD), lambda m, p: (m, p))
    return {
        "block": block,
        "taps": pl.BlockSpec((CONV + 1, 2 * SHD * pairs), lambda m, p: (0, 0)),
        "vector": pl.BlockSpec((1, 2 * SHD * pairs), lambda m, p: (0, 0)),
        "state": pl.BlockSpec((rows, 2 * NS), lambda m, p: (m, 0)),
        "columns": pl.BlockSpec((rows, 8), lambda m, p: (m, 0)),
        "row": pl.BlockSpec((1, 1, rows), lambda m, p: (m, 0, 0)),
        "head_row": pl.BlockSpec((1, pairs, 2, rows), lambda m, p: (m, 0, 0, 0)),
        "head_col": pl.BlockSpec((1, pairs, rows, 2), lambda m, p: (m, 0, 0, 0)),
    }


def state_forward(signal, gate, taps, skip, state, seg_row, run_row, run_col, step, columns):
    micro, pairs, _, rows = run_row.shape
    spec = state_specs(rows, pairs)
    total, width = signal.shape
    return pl.pallas_call(
        state_forward_kernel,
        out_shape=(jax.ShapeDtypeStruct((total, width), f32), jax.ShapeDtypeStruct((total, 2 * SHD), f32)),
        grid=(micro, pairs),
        in_specs=[spec[name] for name in (
            "block", "block", "taps", "vector", "state", "row", "head_row", "head_col", "head_row", "columns")],
        out_specs=(spec["block"], pl.BlockSpec((rows, 2 * SHD), lambda m, p: (m, 0))),
        scratch_shapes=[pltpu.VMEM((rows, rows), f32), pltpu.VMEM((rows, rows), f32)],
        cost_estimate=pl.CostEstimate(
            flops=8 * total * rows * width // SHD * SHD, transcendentals=total * rows * width // SHD, bytes_accessed=12 * total * width
        ),
        name="state_forward",
    )(signal, gate, taps, skip, state, seg_row, run_row, run_col, step, columns)


def state_backward(
    grad, out, gate, signal, taps, skip, gain, state, seg_row, run_row, run_col, step, columns,
    state_raw, state_taps, step_all, step_sig, rate, others, query_cols,
):
    micro, pairs, _, rows = run_row.shape
    heads = 2 * pairs
    spec = state_specs(rows, pairs)
    total, width = signal.shape
    joint = 2 * width + 2 * NS + STEP_PAD + others.shape[1]
    heads_block = pl.BlockSpec((1, heads, rows), lambda m, p: (m, 0, 0))
    return pl.pallas_call(
        functools.partial(state_backward_kernel, query_cols=query_cols),
        out_shape=(
            jax.ShapeDtypeStruct((total, joint), bf16),
            jax.ShapeDtypeStruct((micro, 8, width), f32),
            jax.ShapeDtypeStruct((micro, 8, 2 * NS), f32),
            jax.ShapeDtypeStruct((micro, heads, 2), f32),
        ),
        grid=(micro, pairs),
        in_specs=[spec[name] for name in (
            "block", "block", "block", "block", "taps", "vector", "vector", "state",
            "row", "head_row", "head_col", "head_row", "columns", "state")]
        + [
            pl.BlockSpec((CONV + 1, 2 * NS), lambda m, p: (0, 0)), heads_block, heads_block,
            pl.BlockSpec((heads, 1), lambda m, p: (0, 0)), pl.BlockSpec((rows, others.shape[1]), lambda m, p: (m, 0)),
        ],
        out_specs=(
            pl.BlockSpec((rows, joint), lambda m, p: (m, 0)), pl.BlockSpec((1, 8, 2 * SHD), lambda m, p: (m, 0, p)),
            pl.BlockSpec((1, 8, 2 * NS), lambda m, p: (m, 0, 0)),
            pl.BlockSpec((1, heads, 2), lambda m, p: (m, 0, 0)),
        ),
        scratch_shapes=[pltpu.VMEM((rows, rows), f32)] * 3 + [pltpu.VMEM((heads, rows), f32), pltpu.VMEM((rows, 2 * SHD), f32)],
        cost_estimate=pl.CostEstimate(
            flops=20 * total * rows * width, transcendentals=total * rows * width // SHD, bytes_accessed=20 * total * width
        ),
        name="state_backward",
    )(
        grad, out, gate, signal, taps, skip, gain, state, seg_row, run_row, run_col, step, columns,
        state_raw, state_taps, step_all, step_sig, rate, others,
    )


def local(
    inputs,
    out_grad,
    deal_order,
    segment,
    query_weight,
    key_weight,
    value_weight,
    attention_out,
    mamba_gate,
    mamba_input,
    step_weight,
    state_weight,
    mamba_out,
    feed_gate,
    feed_up,
    feed_down,
    gain_input,
    gain_middle,
    kernel_inner,
    kernel_state,
    mixer_gain,
    step_bias,
    log_rate,
    skip_gain,
):
    micro, own, width = inputs.shape
    groups = lax.axis_size("dp")
    lanes = lax.axis_size("tensor")
    lane = lax.axis_index("tensor")
    group = lax.axis_index("dp")
    device = group * lanes + lane
    per = own // groups
    rows = own * lanes
    total = micro * rows
    inner_width = SH * SHD
    outer_count = groups // 4
    shard = width // groups

    swap_lane = [(0, 1), (1, 0)]

    def other_lane(values):
        return lax.ppermute(values, "tensor", swap_lane)

    def other_group(values, bits):
        return lax.ppermute(values, "dp", [(i, i ^ bits) for i in range(groups)])

    def after(value, *others):
        return lax.optimization_barrier((value, others))[0]

    step_padded = jnp.pad(step_weight, ((0, 0), (0, STEP_PAD - step_weight.shape[1])))
    early = dict(
        gate=mamba_gate, state=state_weight, step=step_padded, query=query_weight, input=mamba_input, key=key_weight,
        value=value_weight, mix=mamba_out, attn=attention_out,
    )
    late = dict(fgate=feed_gate, fup=feed_up, fdown=feed_down)
    whole, places_of = {}, {}
    for label, group_weights in (("early", early), ("late", late)):
        start = 0
        for name, weight in group_weights.items():
            places_of[name] = (label, start, weight.shape[1])
            start += weight.shape[1]
        whole[label] = lax.all_gather(join_columns(list(group_weights.values())), "dp", axis=0, tiled=True)

    def full(name):
        label, start, size = places_of[name]
        return lax.slice_in_dim(whole[label], start, start + size, axis=1)

    own_places = jnp.arange(own, dtype=jnp.int32)
    own_order = lax.dynamic_slice_in_dim(deal_order, device * own, own, 1)
    micro_index = jnp.arange(micro, dtype=jnp.int32)[:, None]

    def buffer_place(destination, rank):
        return destination * (micro * per) + micro_index * per + rank

    send_rank = jnp.sum((own_order[:, None, :] < own_order[:, :, None]).astype(jnp.int32), axis=2)
    send_place = buffer_place(send_rank // per, send_rank % per).reshape(-1)
    lane_order = lax.dynamic_index_in_dim(deal_order.reshape(micro, groups, lanes, own), lane, 2, keepdims=False)
    slots = device * own + own_places
    found = lane_order[:, None, :, :] == slots[None, :, None, None]
    source = jnp.sum(
        jnp.where(found, jnp.arange(groups, dtype=jnp.int32)[None, None, :, None], 0), axis=(2, 3)
    )
    recv_rank = jnp.sum(
        ((source[:, None, :] == source[:, :, None]) & (own_places[None, None, :] < own_places[None, :, None])).astype(jnp.int32),
        axis=2,
    )
    recv_place = buffer_place(source, recv_rank).reshape(-1)
    buffer_places = jnp.arange(micro * own, dtype=jnp.int32)
    send_pick = (buffer_places[:, None] == send_place[None, :]).astype(bf16)
    recv_pick = (recv_place[:, None] == buffer_places[None, :]).astype(bf16)

    def exchange(buffer):
        return lax.all_to_all(
            buffer.reshape(groups, micro * per, width), "dp", split_axis=0, concat_axis=0, tiled=True
        ).reshape(micro * own, width)

    def deal(values):
        sent = project(send_pick, values.reshape(micro * own, width)).astype(bf16)
        return project(recv_pick, exchange(sent)).astype(bf16)

    def deal_order_rows(values):
        return outer_sum(recv_pick, values).astype(bf16)

    def deal_take(moved):
        return outer_sum(send_pick, moved).astype(bf16).reshape(micro, own, width)

    def join_lanes(values):
        mine = values.reshape(micro, 1, own, -1)
        theirs = other_lane(values).reshape(micro, 1, own, -1)
        low = jnp.where(lane == 0, mine, theirs)
        high = jnp.where(lane == 0, theirs, mine)
        return jnp.concatenate([low, high], axis=1).reshape(total, -1)

    def lane_rows(values, which):
        return lax.dynamic_index_in_dim(
            values.reshape(micro, lanes, own, -1), which, 1, keepdims=False
        ).reshape(micro * own, -1)

    own_in = deal(inputs)
    own_grad = deal(out_grad)
    whole_in = join_lanes(own_in)
    whole_grad = join_lanes(own_grad)

    before = jnp.sum((segment[:, None, :] < segment[:, :, None]).astype(jnp.int32), axis=2)
    places = jnp.arange(rows, dtype=jnp.int32)
    position = (places[None, :] - before).reshape(total, 1)

    masks = [1 << place for place in range(groups.bit_length() - 1)]
    relative = []
    for block in range(groups):
        flip = 0
        for place, mask in enumerate(masks):
            if block >> (len(masks) - 1 - place) & 1:
                flip ^= mask
        relative.append(flip)
    block_order = jnp.bitwise_xor(group.astype(jnp.int32), jnp.array(relative, jnp.int32))

    def split_left(left):
        return pick_halves(left, block_order, shard)

    inner_places = list(range(1, len(masks)))

    def core_send(left_parts, right):
        return outer_low(left_parts[1], right)

    def halve(kept, place):
        return (
            lax.slice_in_dim(kept, 1, 2, axis=place - 1).reshape(-1, kept.shape[-1]),
            lax.slice_in_dim(kept, 0, 1, axis=place - 1),
        )

    class Reduction:
        def __init__(self, first):
            self.places = [place for place in first if place in inner_places]
            self.places += [place for place in inner_places if place not in first]
            self.stage = 0

        def move(self, send, kept):
            self.came = other_group(send, masks[self.places[self.stage]])
            self.kept = kept
            self.stage += 1

        def first(self, left_parts, right, from_core):
            kept = (outer_sum(left_parts[0], right) + from_core.astype(f32)).astype(bf16)
            kept = kept.reshape((2,) * len(inner_places) + (shard, -1))
            return halve(kept, self.places[0])

        def added(self):
            return self.kept.astype(f32) + self.came.reshape(self.kept.shape).astype(f32)

        def next(self):
            return halve(self.added().astype(bf16), self.places[self.stage])

        def last(self):
            return self.added().reshape(shard, -1)

        def step(self):
            return self.next() if self.stage < len(self.places) else self.last()

    order = [deal_order[0, 0] >= 0]

    def unit(work):
        shapes = jax.eval_shape(work)
        results = lax.cond(
            order[0], work, lambda: jax.tree.map(lambda leaf: jnp.zeros(leaf.shape, leaf.dtype), shapes)
        )
        leaves, form = jax.tree.flatten(results)
        least = min(range(len(leaves)), key=lambda place: leaves[place].size)
        leaves[least], order[0] = lax.optimization_barrier((leaves[least], order[0]))
        return jax.tree.unflatten(form, leaves)

    in32 = whole_in.astype(f32)
    in_scale = rms_scale(in32)
    normed_low = (in32 * in_scale * gain_input).astype(bf16)
    normed_left = split_left(normed_low)
    whole["early"] = after(whole["early"], whole_grad, normed_left)
    gate_z = project(normed_low, full("gate"))
    ssm_in = project(normed_low, full("input"))
    state_raw = project(normed_low, full("state"))
    heads = step_weight.shape[1]
    raw_step = project(normed_low, full("step"))[:, :heads]
    state_low = jax.nn.silu(conv_sum(state_raw, kernel_state, position)).astype(bf16)
    rate = -jnp.exp(log_rate)
    step_size = jax.nn.softplus(raw_step + step_bias)
    step_heads = step_size.reshape(micro, rows, heads).transpose(0, 2, 1)
    lower = (places[None, :] <= places[:, None]).astype(f32)
    running = jnp.einsum(
        "mhj,ij->mhi", step_heads * rate[None, :, None], lower, precision=lax.Precision.HIGHEST, preferred_element_type=f32
    )
    pairs = heads // 2
    run_row = running.reshape(micro, pairs, 2, rows)
    run_col = run_row.transpose(0, 1, 3, 2)
    step_row = step_heads.reshape(micro, pairs, 2, rows)
    skip_wide = jnp.repeat(skip_gain, SHD)[None, :]
    layout = (state_low, segment.reshape(micro, 1, rows).astype(f32), run_row, run_col, step_row)
    row_facts = jnp.concatenate([segment.reshape(total, 1).astype(f32), position.astype(f32)], axis=1)
    row_columns = jnp.pad(row_facts, ((0, 0), (0, 6)))
    query_cols, key_cols = query_weight.shape[1], key_weight.shape[1]
    attention_tables = (*rope_tables(position), row_columns, layout[1])
    pair_start = places_of["key"][1]
    pair_weight = lax.slice_in_dim(whole["early"], pair_start, pair_start + 2 * key_cols, axis=1)
    ssm_out, squares = state_forward(ssm_in, gate_z, kernel_inner, skip_wide, *layout, row_columns)
    attended_low, query_low, key_low, value_low = attention_forward(
        project(normed_low, full("query")), project(normed_low, pair_weight), attention_tables
    )
    square_own = jnp.sum(squares, axis=1)
    square_sum = square_own + other_lane(square_own)
    inv_rms = lax.rsqrt(square_sum / inner_width + epsilon)[:, None]
    gated_low = (ssm_out * jax.nn.silu(gate_z) * inv_rms * mixer_gain).astype(bf16)

    branch_part = (project_back(gated_low, full("mix")) + project_back(attended_low, full("attn"))).astype(bf16)
    branch = branch_part.astype(f32) + other_lane(branch_part).astype(f32)
    whole_mid = (in32 + branch).astype(bf16)
    mid32 = whole_mid.astype(f32)
    mid_scale = rms_scale(mid32)
    mid_low = (mid32 * mid_scale * gain_middle).astype(bf16)
    red_fgate, red_fup, red_low, red_high = [Reduction(places) for places in ((1, 2), (2, 1), (1, 2), (2, 1))]
    feeds = (red_fgate, red_fup)
    ff_cols = feed_gate.shape[1]
    gate_cols = mamba_gate.shape[1]

    def feed_forward():
        gate_ff = project(mid_low, full("fgate"))
        up_ff = project(mid_low, full("fup"))
        sig_ff = jax.nn.sigmoid(gate_ff)
        hidden_low = (gate_ff * sig_ff * up_ff).astype(bf16)
        grad_hidden = project(whole_grad, full("fdown"))
        gate_ff_low = (grad_hidden * up_ff * (sig_ff * (1.0 + gate_ff * (1.0 - sig_ff)))).astype(bf16)
        up_ff_low = (grad_hidden * (gate_ff * sig_ff)).astype(bf16)
        feed_low = (gate_ff_low, up_ff_low)
        return hidden_low, feed_low, feed_back(feed_low, 0), outer_low(whole_grad, hidden_low)

    half = total // 2

    def feed_back(feed_low, start):
        gate_part, up_part, values, scale = [
            lax.slice_in_dim(array, start, start + half) for array in (*feed_low, mid32, mid_scale)
        ]
        grad_mid_norm = project_back(gate_part, full("fgate")) + project_back(up_part, full("fup"))
        grad_gain = jnp.sum(grad_mid_norm * values * scale, axis=0)
        return rms_back(grad_mid_norm, values, scale, gain_middle).astype(bf16), grad_gain

    hidden_low, feed_low, (mid_part_low, gain_mid_low), part_fdown = unit(feed_forward)
    mid_other_low = hand_over(other_lane(mid_part_low), 2)
    mid_part_high, gain_mid_high = unit(lambda: feed_back(feed_low, half))
    mid_other_high = hand_over(other_lane(mid_part_high), 45)
    sum_fdown = lax.psum_scatter(part_fdown, "dp", scatter_dimension=0, tiled=True)
    grad_gain_mid = gain_mid_low + gain_mid_high

    def feed_output():
        ffn_part = project_back(hidden_low, full("fdown")).astype(bf16)
        return lane_rows(ffn_part, lane), lane_rows(ffn_part, 1 - lane)

    def feed_sends():
        mid_left = split_left(mid_low)
        return mid_left[0], [core_send(mid_left, right) for right in feed_low]

    mid_keep, send_feed = unit(feed_sends)
    order[0], mid_other_low = lax.optimization_barrier((order[0], mid_other_low))
    ffn_own, ffn_send = unit(feed_output)
    feed_came = [other_group(send, 1) for send in send_feed]

    def keep_first(keep, right, came, reductions, sizes):
        kept = (outer_sum(keep, right) + came.astype(f32)).astype(bf16)
        kept = kept.reshape((2,) * len(inner_places) + (shard, -1))
        moves, start = [], 0
        for red, size in zip(reductions, sizes):
            moves.append(halve(kept[..., start : start + size], red.places[0]))
            start += size
        return moves

    def settle(reductions, steps):
        for red, step in zip(reductions, steps):
            if red.stage < len(red.places):
                red.move(*step)
            else:
                red.result = step

    mid_other_high, feed_came = lax.optimization_barrier((mid_other_high, feed_came))
    moves = unit(
        lambda: [
            keep_first(mid_keep, right, came, (red,), (ff_cols,))[0] for red, right, came in zip(feeds, feed_low, feed_came)
        ]
    )
    for red, move in zip(feeds, moves):
        red.move(*move)

    def branch_backward():
        mid_sums = [
            mine.astype(f32) + other.astype(f32)
            for mine, other in ((mid_part_low, mid_other_low), (mid_part_high, mid_other_high))
        ]
        grad_middle = whole_grad.astype(f32) + jnp.concatenate(mid_sums)
        whole_branch = grad_middle.astype(bf16)
        grad_gated_norm = project(whole_branch, full("mix"))
        cross_own = jnp.sum(grad_gated_norm * mixer_gain * (ssm_out * jax.nn.silu(gate_z)), axis=1)
        grad_attended = project(whole_branch, full("attn")).astype(bf16)
        joint_low = attention_backward(grad_attended, query_low, key_low, value_low, attention_tables)
        return (
            cross_own, lane_rows(grad_middle, lane), grad_gated_norm, whole_branch,
            joint_low,
        )

    cross_own, grad_middle_own, grad_gated_norm, whole_branch, joint_low = unit(branch_backward)
    cross_other = other_lane(cross_own)

    ffn_other = other_lane(ffn_send)

    def branch_partial():
        ffn_out = ffn_own.astype(f32) + ffn_other.astype(f32)
        out_rows = (lane_rows(whole_mid, lane).astype(f32) + ffn_out).astype(bf16)
        return outer_low(whole_branch, jnp.concatenate([gated_low, attended_low], axis=1)), deal_order_rows(out_rows)

    part_branch, out_sent = unit(branch_partial)
    out_moved = exchange(out_sent)
    sum_branch = lax.psum_scatter(part_branch, "dp", scatter_dimension=0, tiled=True)
    step_sig = jax.nn.sigmoid(raw_step + step_bias).reshape(micro, rows, heads).transpose(0, 2, 1)
    gain_row, rate_column = mixer_gain[None, :], rate[:, None]

    def state_space_backward():
        cross = (inv_rms**3) * ((cross_own + cross_other)[:, None] / inner_width)
        columns = jnp.pad(jnp.concatenate([row_facts, inv_rms, cross], axis=1), ((0, 0), (0, 4)))
        first_right, column_sums, state_sums, head_sums = state_backward(
            grad_gated_norm, ssm_out, gate_z, ssm_in, kernel_inner, skip_wide, gain_row, *layout, columns,
            state_raw, kernel_state, step_heads, step_sig, rate_column, joint_low, query_cols,
        )
        return column_sums, state_sums, head_sums, first_right

    column_sums, state_sums, head_sums, first_right = unit(state_space_backward)

    total_fdown_low = [sum_fdown]
    order[0], total_fdown_low = lax.optimization_barrier((order[0], total_fdown_low))
    send_first, steps, block_out = unit(
        lambda: (core_send(normed_left, first_right), [red.step() for red in feeds], deal_take(out_moved))
    )
    settle(feeds, steps)
    first_came = other_group(send_first, 1)

    def input_gradient():
        grad_normed = project_back(first_right, lax.slice_in_dim(whole["early"], 0, first_right.shape[1], axis=1))
        grad_gain_in = jnp.sum(grad_normed * in32 * in_scale, axis=0)
        in_part = rms_back(grad_normed, in32, in_scale, gain_input).astype(bf16)
        return grad_gain_in, lane_rows(in_part, lane), lane_rows(in_part, 1 - lane)

    grad_gain_in, in_own, in_send = unit(input_gradient)

    firsts = (red_low, red_high)
    low_size = gate_cols + 2 * NS + STEP_PAD + query_cols
    first_sizes = (low_size, first_right.shape[1] - low_size)

    def first_moves():
        moves = keep_first(normed_left[0], first_right, first_came, firsts, first_sizes)
        return moves, lax.optimization_barrier(in_send), [red.step() for red in feeds]

    moves, in_send, steps = unit(first_moves)
    settle(feeds, steps)
    for red, move in zip(firsts, moves):
        red.move(*move)
    in_other = hand_over(other_lane(in_send), 6)

    def small_block():
        head_row = (jnp.sum(head_sums, axis=0).T * jnp.stack([rate, jnp.ones_like(rate)])).reshape(1, -1)
        return jnp.concatenate(
            [
                jnp.concatenate([jnp.sum(column_sums, axis=0), jnp.sum(state_sums, axis=0)], axis=1),
                grad_gain_in[None, :], grad_gain_mid[None, :], jnp.pad(head_row, ((0, 5), (0, width - head_row.shape[1]))),
            ]
        )
    flat = unit(small_block)
    flat_moved = other_group(flat, masks[0])

    def send_input():
        in_sum = in_own.astype(f32) + in_other.astype(f32)
        return deal_order_rows((in_sum + grad_middle_own).astype(bf16))

    bits = 1

    def finish():
        low, high = red_low.result, red_high.result
        state_rows = low[:, gate_cols : gate_cols + 2 * NS].reshape(lanes, shard // lanes, 2 * NS)
        cut = [0, gate_cols, gate_cols + key_cols, high.shape[1]]
        pieces = (
            low[:, :gate_cols], low[:, gate_cols + 2 * NS : gate_cols + 2 * NS + heads],
            low[:, gate_cols + 2 * NS + STEP_PAD :], [high[:, start:stop] for start, stop in zip(cut, cut[1:])],
            [lax.dynamic_index_in_dim(state_rows, which, 0, keepdims=False) for which in (lane, 1 - lane)],
        )
        return pieces, deal_take(in_moved)

    arrived = [red.came for red in feeds] + [sum_branch]
    order[0], arrived = lax.optimization_barrier((order[0], arrived))
    for red, came in zip(feeds, arrived):
        red.came = came
    sum_branch = arrived[-1]
    in_moved = None
    while red_low.stage < len(red_low.places):
        moving = [red for red in (*firsts, *feeds) if red.stage < len(red.places)]
        steps, flat, sent = unit(
            lambda: (
                [red.next() for red in moving],
                flat + flat_moved if flat_moved is not None else flat,
                send_input() if in_moved is None else (),
            )
        )
        settle(moving, steps)
        flat_moved = other_group(flat, masks[bits]) if bits < len(masks) else None
        bits += 1
        if in_moved is None:
            in_moved = exchange(sent)
    totals, flat = unit(
        lambda: (
            [red.last() for red in feeds] + [sum_branch.astype(f32), total_fdown_low[0].astype(f32)],
            flat + flat_moved if flat_moved is not None else flat,
        )
    )
    total_fgate, total_fup, total_branch, total_fdown = totals
    flat_moved = other_group(flat, masks[bits]) if bits < len(masks) else None
    bits += 1

    def last_work():
        red_low.result, red_high.result = red_low.last(), red_high.last()
        return finish(), flat + flat_moved if flat_moved is not None else flat

    ((total_gate, total_step, total_query, (total_input, total_key, total_value), states), grad_input), flat = unit(last_work)
    while bits < len(masks):
        flat = flat + other_group(flat, masks[bits])
        bits += 1
    theirs = other_lane(flat)
    low, high = jnp.where(lane == 0, flat, theirs), jnp.where(lane == 0, theirs, flat)
    both = flat + theirs

    def joined(row, start, count):
        return jnp.concatenate([low[row, start : start + count], high[row, start : start + count]])

    sum_gin, sum_gmid = both[8], both[9]
    sum_kst = both[: CONV + 1, gate_cols : gate_cols + 2 * NS]
    sum_kin = jnp.concatenate([low[: CONV + 1, :gate_cols], high[: CONV + 1, :gate_cols]], axis=1)
    sum_mix = joined(CONV + 1, 0, gate_cols)
    sum_skip = jnp.sum(joined(CONV + 2, 0, gate_cols).reshape(SH, SHD), axis=1)
    sum_bias = joined(10, heads, heads)
    sum_rate = joined(10, 0, heads)

    total_mix, total_attn = total_branch[:, :gate_cols], total_branch[:, gate_cols:]
    state_lane = states[0] + other_lane(states[1])
    return (
        block_out,
        grad_input,
        total_query,
        total_key,
        total_value,
        total_attn,
        total_gate,
        total_input,
        total_step,
        state_lane,
        total_mix,
        total_fgate,
        total_fup,
        total_fdown,
        sum_gin,
        sum_gmid,
        sum_kin,
        sum_kst,
        sum_mix,
        sum_bias,
        sum_rate,
        sum_skip,
    )


def solution(mesh):
    both = P("dp", "tensor")
    in_specs = (
        P(None, ("dp", "tensor"), None),
        P(None, ("dp", "tensor"), None),
        P(),
        P(None, "dp"),
        both,
        both,
        both,
        both,
        both,
        both,
        both,
        P("dp", None),
        both,
        both,
        both,
        both,
        P(),
        P(),
        P(None, "tensor"),
        P(),
        P("tensor"),
        P("tensor"),
        P("tensor"),
        P("tensor"),
    )
    out_specs = (
        P(None, ("dp", "tensor"), None),
        P(None, ("dp", "tensor"), None),
        both,
        both,
        both,
        both,
        both,
        both,
        both,
        P(("dp", "tensor"), None),
        both,
        both,
        both,
        both,
        P(),
        P(),
        P(),
        P(),
        P(),
        P(),
        P(),
        P(),
    )
    return jax.shard_map(local, mesh=mesh, in_specs=in_specs, out_specs=out_specs, check_vma=False)
```

```python
import functools
import math

import jax
import jax.numpy as jnp
from jax import lax
from jax.experimental import pallas as pl
from jax.experimental.layout import Layout, with_layout_constraint
from jax.experimental.pallas import tpu as pltpu
from jax.sharding import PartitionSpec as P

HEAD = 128
SH = 48
SHD = 64
NS = 256
CONV = 4
STEP_PAD = 128

epsilon = 1e-05
rope_base = 100000000000.0
f32 = jnp.float32
bf16 = jnp.bfloat16


def project(left, right):
    return jnp.dot(left, right, preferred_element_type=f32)


def project_back(left, right):
    return lax.dot_general(left, right, (((1,), (1,)), ((), ())), preferred_element_type=f32)


def outer_sum(left, right):
    return lax.dot_general(left, right, (((0,), (0,)), ((), ())), preferred_element_type=f32)


def outer_low(left, right):
    return with_layout_constraint(outer_sum(left, right).astype(bf16), Layout(major_to_minor=(0, 1)))


def rms_scale(values):
    return lax.rsqrt(jnp.mean(values * values, axis=-1, keepdims=True) + epsilon)


def rms_back(grad, values, scale, gain):
    weighted = grad * gain
    inner = jnp.sum(weighted * values, axis=-1, keepdims=True)
    return scale * weighted - values * (scale * scale * scale * inner / values.shape[-1])


def shift_down(values, count):
    return jnp.concatenate([jnp.zeros((count, values.shape[1]), values.dtype), values[:-count]], axis=0)


def shift_up(values, count):
    return jnp.concatenate([values[count:], jnp.zeros((count, values.shape[1]), values.dtype)], axis=0)


def conv_sum(signal, kernel, position):
    summed = kernel[CONV][None, :] + signal * kernel[0][None, :]
    for tap in range(1, CONV):
        moved = jnp.where(position >= tap, shift_down(signal, tap), 0.0)
        summed = summed + moved * kernel[tap][None, :]
    return summed


def silu_back(values):
    sig = jax.nn.sigmoid(values)
    return sig * (1.0 + values * (1.0 - sig))


def conv_back(grad, signal, kernel, position):
    grad_sum = grad * silu_back(conv_sum(signal, kernel, position))
    grad_signal = grad_sum * kernel[0][None, :]
    grad_taps = [jnp.sum(grad_sum * signal, axis=0)]
    for tap in range(1, CONV):
        kept = jnp.where(position >= tap, grad_sum, 0.0)
        grad_signal = grad_signal + shift_up(kept, tap) * kernel[tap][None, :]
        grad_taps.append(jnp.sum(kept * shift_down(signal, tap), axis=0))
    grad_taps.append(jnp.sum(grad_sum, axis=0))
    return grad_signal, jnp.stack(grad_taps)


def rope_tables(position):
    half_size = HEAD // 2
    frequency = jnp.exp(jnp.arange(half_size, dtype=f32) * (-2.0 * math.log(rope_base) / HEAD))
    angles = position.astype(f32) * frequency[None, :]
    cosine, sine = jnp.cos(angles), jnp.sin(angles)
    return jnp.concatenate([cosine, cosine], axis=1), jnp.concatenate([-sine, sine], axis=1)


def copy_blocks(order_ref, first_ref, second_ref, first_out_ref, second_out_ref):
    first_out_ref[...] = first_ref[...]
    second_out_ref[...] = second_ref[...]


def pick_halves(values, order, block):
    height, width = values.shape
    count = width // block // 2
    if block % 128:
        mixed = jnp.take(values.reshape(height, -1, block), order, axis=1).reshape(height, width)
        return mixed[:, : width // 2], mixed[:, width // 2 :]
    half = jax.ShapeDtypeStruct((height, width // 2), values.dtype)
    out_spec = pl.BlockSpec((height, block), lambda i, order: (0, i))
    return pl.pallas_call(
        copy_blocks,
        out_shape=(half, half),
        grid_spec=pltpu.PrefetchScalarGridSpec(
            num_scalar_prefetch=1,
            grid=(count,),
            in_specs=[
                pl.BlockSpec((height, block), lambda i, order: (0, order[i])),
                pl.BlockSpec((height, block), lambda i, order: (0, order[i + count])),
            ],
            out_specs=(out_spec, out_spec),
        ),
        cost_estimate=pl.CostEstimate(flops=0, transcendentals=0, bytes_accessed=4 * height * width),
        name="pick_halves",
    )(order, values, values)


def join_columns(pieces):
    height = pieces[0].shape[0]
    width = sum(piece.shape[1] for piece in pieces)

    def put_all(*refs):
        start = 0
        for source in refs[:-1]:
            refs[-1][:, start : start + source.shape[1]] = source[...]
            start += source.shape[1]

    return pl.pallas_call(
        put_all,
        out_shape=jax.ShapeDtypeStruct((height, width), pieces[0].dtype),
        cost_estimate=pl.CostEstimate(flops=0, transcendentals=0, bytes_accessed=4 * height * width),
        name="join_columns",
    )(*pieces)


def hand_over(values, microseconds):
    def idle(values_ref, out_ref):
        pass

    return pl.pallas_call(
        idle,
        out_shape=jax.ShapeDtypeStruct(values.shape, values.dtype),
        in_specs=[pl.BlockSpec(memory_space=pl.ANY)],
        out_specs=pl.BlockSpec(memory_space=pl.ANY),
        input_output_aliases={0: 0},
        cost_estimate=pl.CostEstimate(flops=microseconds * 1150000000, transcendentals=0, bytes_accessed=0),
        name="hand_over",
    )(values)


NEGATIVE = -1e30


def sigmoid_of(values):
    return 1.0 / (1.0 + jnp.exp(-values))


def block_mask(rows, segment_col, segment_row):
    row_index = lax.broadcasted_iota(jnp.int32, (rows, rows), 0)
    col_index = lax.broadcasted_iota(jnp.int32, (rows, rows), 1)
    return jnp.where((segment_col == segment_row) & (col_index <= row_index), 0.0, NEGATIVE)


def conv_block(signal, taps_ref, position):
    summed = taps_ref[CONV : CONV + 1, :] + signal * taps_ref[0:1, :]
    moved = []
    for tap in range(1, CONV):
        shifted = jnp.where(position >= tap, pltpu.roll(signal, tap, 0), 0.0)
        moved.append(shifted)
        summed = summed + shifted * taps_ref[tap : tap + 1, :]
    return summed, moved


def conv_block_back(grad_sum, signal, moved, taps_ref, position, sums_ref):
    rows = signal.shape[0]
    grad_signal = grad_sum * taps_ref[0:1, :]
    sums_ref[0, 0:1, :] = jnp.sum(grad_sum * signal, axis=0, keepdims=True)
    for tap in range(1, CONV):
        kept = jnp.where(position >= tap, grad_sum, 0.0)
        grad_signal = grad_signal + pltpu.roll(kept, rows - tap, 0) * taps_ref[tap : tap + 1, :]
        sums_ref[0, tap : tap + 1, :] = jnp.sum(grad_sum * moved[tap - 1], axis=0, keepdims=True)
    sums_ref[0, CONV : CONV + 1, :] = jnp.sum(grad_sum, axis=0, keepdims=True)
    return grad_signal


def mixing_block(inner, mask, run_col, run_row, step_row):
    decay = jnp.exp(run_col - run_row + mask)
    return decay, (inner * decay * step_row).astype(bf16)


def turn(values, cosine_ref, sine_ref, sign):
    return values * cosine_ref[...] + sign * (pltpu.roll(values, HEAD // 2, 1) * sine_ref[...])


def head_probs(query_low, key_low, mask):
    logits = lax.dot_general(query_low, key_low, (((1,), (1,)), ((), ())), preferred_element_type=f32) * HEAD ** (-0.5)
    logits = logits + mask
    weights = jnp.exp(logits - jnp.max(logits, axis=1, keepdims=True))
    return weights / jnp.sum(weights, axis=1, keepdims=True)


def attention_forward_kernel(
    query_ref, key_ref, value_ref, cosine_ref, sine_ref, columns_ref, seg_row_ref,
    attended_ref, query_low_ref, key_low_ref, value_low_ref, mask_ref,
):
    rows = query_ref.shape[0]

    @pl.when(pl.program_id(1) == 0)
    def _():
        mask_ref[...] = block_mask(rows, columns_ref[:, 0:1], seg_row_ref[0])

    query_low = turn(query_ref[...], cosine_ref, sine_ref, 1.0).astype(bf16)
    key_low = turn(key_ref[...], cosine_ref, sine_ref, 1.0).astype(bf16)
    value_low = value_ref[...].astype(bf16)
    probs_low = head_probs(query_low, key_low, mask_ref[...]).astype(bf16)
    attended_ref[...] = jnp.dot(probs_low, value_low, preferred_element_type=f32).astype(bf16)
    query_low_ref[...] = query_low
    key_low_ref[...] = key_low
    value_low_ref[...] = value_low


def attention_backward_kernel(
    grad_ref, query_ref, key_ref, value_ref, cosine_ref, sine_ref, columns_ref, seg_row_ref,
    joint_ref, mask_ref, grad_key_ref, grad_value_ref, *, group, query_cols, key_cols,
):
    rows = query_ref.shape[0]
    head = pl.program_id(1)

    @pl.when(head == 0)
    def _():
        mask_ref[...] = block_mask(rows, columns_ref[:, 0:1], seg_row_ref[0])

    @pl.when(head % group == 0)
    def _():
        grad_key_ref[...] = jnp.zeros_like(grad_key_ref)
        grad_value_ref[...] = jnp.zeros_like(grad_value_ref)

    grad, query_low, key_low = grad_ref[...], query_ref[...], key_ref[...]
    probs = head_probs(query_low, key_low, mask_ref[...])
    grad_probs = lax.dot_general(grad, value_ref[...], (((1,), (1,)), ((), ())), preferred_element_type=f32)
    grad_value_ref[...] += lax.dot_general(
        probs.astype(bf16), grad, (((0,), (0,)), ((), ())), preferred_element_type=f32
    )
    grad_logits = (probs * (grad_probs - jnp.sum(probs * grad_probs, axis=1, keepdims=True))).astype(bf16)
    grad_query = jnp.dot(grad_logits, key_low, preferred_element_type=f32) * HEAD ** (-0.5)
    grad_key_ref[...] += lax.dot_general(
        grad_logits, query_low, (((0,), (0,)), ((), ())), preferred_element_type=f32
    ) * HEAD ** (-0.5)
    joint_ref[:, pl.ds(pl.multiple_of(head * HEAD, HEAD), HEAD)] = turn(
        grad_query, cosine_ref, sine_ref, -1.0
    ).astype(bf16)

    @pl.when(head % group == group - 1)
    def _():
        place = head // group * HEAD
        joint_ref[:, pl.ds(pl.multiple_of(query_cols + place, HEAD), HEAD)] = turn(
            grad_key_ref[...], cosine_ref, sine_ref, -1.0
        ).astype(bf16)
        joint_ref[:, pl.ds(pl.multiple_of(query_cols + key_cols + place, HEAD), HEAD)] = grad_value_ref[...].astype(bf16)


def attention_specs(rows, group):
    table = pl.BlockSpec((rows, HEAD), lambda m, h: (m, 0))
    return (
        lambda start: pl.BlockSpec((rows, HEAD), lambda m, h: (m, start + h)),
        lambda start: pl.BlockSpec((rows, HEAD), lambda m, h: (m, start + h // group)),
        [table, table, pl.BlockSpec((rows, 8), lambda m, h: (m, 0)), pl.BlockSpec((1, 1, rows), lambda m, h: (m, 0, 0))],
    )


def attention_forward(query, key_value, tables):
    micro, _, rows = tables[3].shape
    total, query_cols = query.shape
    key_cols = key_value.shape[1] // 2
    heads, kv_heads = query_cols // HEAD, key_cols // HEAD
    by_head, by_kv, table_specs = attention_specs(rows, heads // kv_heads)
    return pl.pallas_call(
        attention_forward_kernel,
        out_shape=tuple(jax.ShapeDtypeStruct((total, size), bf16) for size in (query_cols, query_cols, key_cols, key_cols)),
        grid=(micro, heads),
        in_specs=[by_head(0), by_kv(0), by_kv(kv_heads)] + table_specs,
        out_specs=(by_head(0), by_head(0), by_kv(0), by_kv(0)),
        scratch_shapes=[pltpu.VMEM((rows, rows), f32)],
        cost_estimate=pl.CostEstimate(
            flops=4 * total * rows * query_cols, transcendentals=total * rows * heads, bytes_accessed=8 * total * query_cols
        ),
        name="attention_forward",
    )(query, key_value, key_value, *tables)


def attention_backward(grad, query, key, value, tables):
    micro, _, rows = tables[3].shape
    total, query_cols = query.shape
    key_cols = key.shape[1]
    heads, kv_heads = query_cols // HEAD, key_cols // HEAD
    by_head, by_kv, table_specs = attention_specs(rows, heads // kv_heads)
    joint_cols = query_cols + 2 * key_cols
    return pl.pallas_call(
        functools.partial(
            attention_backward_kernel, group=heads // kv_heads, query_cols=query_cols, key_cols=key_cols
        ),
        out_shape=jax.ShapeDtypeStruct((total, joint_cols), bf16),
        grid=(micro, heads),
        in_specs=[by_head(0), by_head(0), by_kv(0), by_kv(0)] + table_specs,
        out_specs=pl.BlockSpec((rows, joint_cols), lambda m, h: (m, 0)),
        scratch_shapes=[pltpu.VMEM((rows, rows), f32), pltpu.VMEM((rows, HEAD), f32), pltpu.VMEM((rows, HEAD), f32)],
        cost_estimate=pl.CostEstimate(
            flops=10 * total * rows * query_cols, transcendentals=total * rows * heads, bytes_accessed=8 * total * query_cols
        ),
        name="attention_backward",
    )(grad, query, key, value, *tables)


def state_forward_kernel(
    signal_ref, gate_ref, taps_ref, skip_ref, state_ref, seg_row_ref, run_row_ref, run_col_ref, step_ref, columns_ref,
    out_ref, square_ref, inner_ref, mask_ref,
):
    rows = signal_ref.shape[0]
    position = columns_ref[:, 1:2]
    pair = pl.program_id(1)
    here = pl.ds(pl.multiple_of(pair * 2 * SHD, 2 * SHD), 2 * SHD)
    taps_ref, skip_ref = taps_ref.at[:, here], skip_ref.at[:, here]

    @pl.when(pl.program_id(1) == 0)
    def _():
        inner_ref[...] = lax.dot_general(
            state_ref[:, NS:], state_ref[:, :NS], (((1,), (1,)), ((), ())), preferred_element_type=f32
        )
        mask_ref[...] = block_mask(rows, columns_ref[:, 0:1], seg_row_ref[0])
        square_ref[...] = jnp.zeros_like(square_ref)

    summed, _ = conv_block(signal_ref[...], taps_ref, position)
    cols = summed * sigmoid_of(summed)
    cols_low = cols.astype(bf16)
    mixed = []
    for head in range(2):
        _, mixing = mixing_block(
            inner_ref[...], mask_ref[...], run_col_ref[0, pair, :, head : head + 1],
            run_row_ref[0, pair, head : head + 1, :], step_ref[0, pair, head : head + 1, :],
        )
        mixed.append(jnp.dot(mixing, cols_low, preferred_element_type=f32))
    lanes = lax.broadcasted_iota(jnp.int32, cols.shape, 1)
    out = jnp.where(lanes < SHD, mixed[0], mixed[1]) + skip_ref[...] * cols
    out_ref[...] = out
    gate = gate_ref[...]
    gated = out * (gate * sigmoid_of(gate))
    square_ref[...] += gated * gated


def state_backward_kernel(
    grad_ref, out_ref, gate_ref, signal_ref, taps_ref, skip_ref, gain_ref, state_ref, seg_row_ref, run_row_ref, run_col_ref,
    step_ref, columns_ref, state_raw_ref, state_taps_ref, step_all_ref, step_sig_ref, rate_ref, others_ref,
    first_ref, sums_ref, state_sums_ref, head_sums_ref,
    inner_ref, mask_ref, grad_inner_ref, direct_ref, along_ref, *, query_cols,
):
    rows = signal_ref.shape[0]
    rest = taps_ref.shape[1]
    after_rest = rest + 2 * NS + STEP_PAD
    input_start = after_rest + query_cols
    pair = pl.program_id(1)
    block = pl.ds(pl.multiple_of(pair * 2 * SHD, 2 * SHD), 2 * SHD)
    taps_ref, skip_ref, gain_ref = taps_ref.at[:, block], skip_ref.at[:, block], gain_ref.at[:, block]

    @pl.when(pair == 0)
    def _():
        along_ref[...] = jnp.zeros_like(along_ref)
        inner_ref[...] = lax.dot_general(
            state_ref[:, NS:], state_ref[:, :NS], (((1,), (1,)), ((), ())), preferred_element_type=f32
        )
        mask_ref[...] = block_mask(rows, columns_ref[:, 0:1], seg_row_ref[0])
        grad_inner_ref[...] = jnp.zeros_like(grad_inner_ref)

    grad, out, gate, signal = grad_ref[...], out_ref[...], gate_ref[...], signal_ref[...]
    position, scale, cross = columns_ref[:, 1:2], columns_ref[:, 2:3], columns_ref[:, 3:4]
    here = pl.multiple_of(pair * 2 * SHD, 2 * SHD)
    sig = sigmoid_of(gate)
    silu = gate * sig
    gated = out * silu
    scaled = grad * scale
    grad_gated = scaled * gain_ref[...] - gated * cross
    grad_out = grad_gated * silu
    first_ref[:, pl.ds(here, 2 * SHD)] = (grad_gated * out * (sig * (1.0 + gate * (1.0 - sig)))).astype(bf16)
    summed, moved = conv_block(signal, taps_ref, position)
    sig = sigmoid_of(summed)
    cols = summed * sig
    cols_low = cols.astype(bf16)
    grad_low = grad_out.astype(bf16)
    lanes = lax.broadcasted_iota(jnp.int32, cols.shape, 1)
    zero = jnp.zeros_like(grad_low)
    grad_cols = []
    cut = rows // 2
    for head in range(2):
        grad_head = jnp.where((lanes < SHD) == (head == 0), grad_low, zero)
        partial_cols, directs, alongs = [], [], []
        for start, stop in ((0, cut), (cut, rows)):
            step_row = step_ref[0, pair, head : head + 1, :stop]
            inner = inner_ref[start:stop, :stop]
            decay, mixing = mixing_block(
                inner, mask_ref[start:stop, :stop], run_col_ref[0, pair, start:stop, head : head + 1],
                run_row_ref[0, pair, head : head + 1, :stop], step_row,
            )
            partial_cols.append(
                lax.dot_general(mixing, grad_low[start:stop], (((0,), (0,)), ((), ())), preferred_element_type=f32)
            )
            grad_decay = lax.dot_general(
                grad_head[start:stop], cols_low[:stop], (((1,), (1,)), ((), ())), preferred_element_type=f32
            ) * decay
            stepped = grad_decay * step_row
            grad_inner_ref[start:stop, :stop] += stepped
            directs.append(jnp.sum(grad_decay * inner, axis=0, keepdims=True))
            alongs.append(jnp.sum(stepped * inner, axis=1, keepdims=True))
        grad_cols.append(jnp.concatenate([partial_cols[0] + partial_cols[1][:cut], partial_cols[1][cut:]], axis=0))
        direct_ref[pl.ds(2 * pair + head, 1), :] = jnp.concatenate(
            [directs[0] + directs[1][:, :cut], directs[1][:, cut:]], axis=1
        )
        along = jnp.concatenate(alongs, axis=0)
        along_ref[...] = jnp.where(lanes == 2 * pair + head, along, along_ref[...])
    grad_cols = jnp.where(lanes < SHD, grad_cols[0], grad_cols[1]) + skip_ref[...] * grad_out
    grad_sum = grad_cols * (sig * (1.0 + summed * (1.0 - sig)))
    grad_signal = conv_block_back(grad_sum, signal, moved, taps_ref, position, sums_ref)
    sums_ref[0, CONV + 1 : CONV + 2, :] = jnp.sum(scaled * gated, axis=0, keepdims=True)
    sums_ref[0, CONV + 2 : CONV + 3, :] = jnp.sum(grad_out * cols, axis=0, keepdims=True)
    sums_ref[0, CONV + 3 : CONV + 4, :] = jnp.zeros((1, cols.shape[1]), f32)
    first_ref[:, pl.ds(pl.multiple_of(input_start + here, 2 * SHD), 2 * SHD)] = grad_signal.astype(bf16)

    @pl.when(pair == pl.num_programs(1) - 1)
    def _():
        inner_low = grad_inner_ref[...].astype(bf16)
        for part, (mine, other) in enumerate((((0, NS), (NS, 2 * NS)), ((NS, 2 * NS), (0, NS)))):
            raw = state_raw_ref[:, mine[0] : mine[1]]
            taps = state_taps_ref.at[:, mine[0] : mine[1]]
            summed, moved = conv_block(raw, taps, position)
            sig = sigmoid_of(summed)
            grad = lax.dot_general(
                inner_low, state_ref[:, other[0] : other[1]], (((part,), (0,)), ((), ())), preferred_element_type=f32
            )
            grad_sum = grad * (sig * (1.0 + summed * (1.0 - sig)))
            back = conv_block_back(grad_sum, raw, moved, taps, position, state_sums_ref.at[:, :, mine[0] : mine[1]])
            first_ref[:, rest + mine[0] : rest + mine[1]] = back.astype(bf16)
        state_sums_ref[0, CONV + 1 :, :] = jnp.zeros((7 - CONV, 2 * NS), f32)
        heads = step_all_ref.shape[1]
        direct, step = direct_ref[...], step_all_ref[0]
        grad_running = along_ref[...].T[:heads] - step * direct
        row_index = lax.broadcasted_iota(jnp.int32, (rows, rows), 0)
        col_index = lax.broadcasted_iota(jnp.int32, (rows, rows), 1)
        lower = jnp.where(col_index <= row_index, 1.0, 0.0)
        grad_product = jnp.dot(
            grad_running, lower, precision=lax.Precision.HIGHEST, preferred_element_type=f32
        )
        grad_raw = (direct + grad_product * rate_ref[...]) * step_sig_ref[0]
        head_sums_ref[0, :, 0:1] = jnp.sum(grad_product * step, axis=1, keepdims=True)
        head_sums_ref[0, :, 1:2] = jnp.sum(grad_raw, axis=1, keepdims=True)
        wide = jnp.concatenate([grad_raw, jnp.zeros((STEP_PAD - heads, rows), f32)], axis=0)
        first_ref[:, rest + 2 * NS : after_rest] = wide.T.astype(bf16)
        first_ref[:, after_rest:input_start] = others_ref[:, :query_cols]
        first_ref[:, input_start + rest :] = others_ref[:, query_cols:]


def state_specs(rows, pairs):
    block = pl.BlockSpec((rows, 2 * SHD), lambda m, p: (m, p))
    return {
        "block": block,
        "taps": pl.BlockSpec((CONV + 1, 2 * SHD * pairs), lambda m, p: (0, 0)),
        "vector": pl.BlockSpec((1, 2 * SHD * pairs), lambda m, p: (0, 0)),
        "state": pl.BlockSpec((rows, 2 * NS), lambda m, p: (m, 0)),
        "columns": pl.BlockSpec((rows, 8), lambda m, p: (m, 0)),
        "row": pl.BlockSpec((1, 1, rows), lambda m, p: (m, 0, 0)),
        "head_row": pl.BlockSpec((1, pairs, 2, rows), lambda m, p: (m, 0, 0, 0)),
        "head_col": pl.BlockSpec((1, pairs, rows, 2), lambda m, p: (m, 0, 0, 0)),
    }


def state_forward(signal, gate, taps, skip, state, seg_row, run_row, run_col, step, columns):
    micro, pairs, _, rows = run_row.shape
    spec = state_specs(rows, pairs)
    total, width = signal.shape
    return pl.pallas_call(
        state_forward_kernel,
        out_shape=(jax.ShapeDtypeStruct((total, width), f32), jax.ShapeDtypeStruct((total, 2 * SHD), f32)),
        grid=(micro, pairs),
        in_specs=[spec[name] for name in (
            "block", "block", "taps", "vector", "state", "row", "head_row", "head_col", "head_row", "columns")],
        out_specs=(spec["block"], pl.BlockSpec((rows, 2 * SHD), lambda m, p: (m, 0))),
        scratch_shapes=[pltpu.VMEM((rows, rows), f32), pltpu.VMEM((rows, rows), f32)],
        cost_estimate=pl.CostEstimate(
            flops=8 * total * rows * width // SHD * SHD, transcendentals=total * rows * width // SHD, bytes_accessed=12 * total * width
        ),
        name="state_forward",
    )(signal, gate, taps, skip, state, seg_row, run_row, run_col, step, columns)


def state_backward(
    grad, out, gate, signal, taps, skip, gain, state, seg_row, run_row, run_col, step, columns,
    state_raw, state_taps, step_all, step_sig, rate, others, query_cols,
):
    micro, pairs, _, rows = run_row.shape
    heads = 2 * pairs
    spec = state_specs(rows, pairs)
    total, width = signal.shape
    joint = 2 * width + 2 * NS + STEP_PAD + others.shape[1]
    heads_block = pl.BlockSpec((1, heads, rows), lambda m, p: (m, 0, 0))
    return pl.pallas_call(
        functools.partial(state_backward_kernel, query_cols=query_cols),
        out_shape=(
            jax.ShapeDtypeStruct((total, joint), bf16),
            jax.ShapeDtypeStruct((micro, 8, width), f32),
            jax.ShapeDtypeStruct((micro, 8, 2 * NS), f32),
            jax.ShapeDtypeStruct((micro, heads, 2), f32),
        ),
        grid=(micro, pairs),
        in_specs=[spec[name] for name in (
            "block", "block", "block", "block", "taps", "vector", "vector", "state",
            "row", "head_row", "head_col", "head_row", "columns", "state")]
        + [
            pl.BlockSpec((CONV + 1, 2 * NS), lambda m, p: (0, 0)), heads_block, heads_block,
            pl.BlockSpec((heads, 1), lambda m, p: (0, 0)), pl.BlockSpec((rows, others.shape[1]), lambda m, p: (m, 0)),
        ],
        out_specs=(
            pl.BlockSpec((rows, joint), lambda m, p: (m, 0)), pl.BlockSpec((1, 8, 2 * SHD), lambda m, p: (m, 0, p)),
            pl.BlockSpec((1, 8, 2 * NS), lambda m, p: (m, 0, 0)),
            pl.BlockSpec((1, heads, 2), lambda m, p: (m, 0, 0)),
        ),
        scratch_shapes=[pltpu.VMEM((rows, rows), f32)] * 3 + [pltpu.VMEM((heads, rows), f32), pltpu.VMEM((rows, 2 * SHD), f32)],
        cost_estimate=pl.CostEstimate(
            flops=20 * total * rows * width, transcendentals=total * rows * width // SHD, bytes_accessed=20 * total * width
        ),
        name="state_backward",
    )(
        grad, out, gate, signal, taps, skip, gain, state, seg_row, run_row, run_col, step, columns,
        state_raw, state_taps, step_all, step_sig, rate, others,
    )


def local(
    inputs,
    out_grad,
    deal_order,
    segment,
    query_weight,
    key_weight,
    value_weight,
    attention_out,
    mamba_gate,
    mamba_input,
    step_weight,
    state_weight,
    mamba_out,
    feed_gate,
    feed_up,
    feed_down,
    gain_input,
    gain_middle,
    kernel_inner,
    kernel_state,
    mixer_gain,
    step_bias,
    log_rate,
    skip_gain,
):
    micro, own, width = inputs.shape
    groups = lax.axis_size("dp")
    lanes = lax.axis_size("tensor")
    lane = lax.axis_index("tensor")
    group = lax.axis_index("dp")
    device = group * lanes + lane
    per = own // groups
    rows = own * lanes
    total = micro * rows
    inner_width = SH * SHD
    outer_count = groups // 4
    shard = width // groups

    swap_lane = [(0, 1), (1, 0)]

    def other_lane(values):
        return lax.ppermute(values, "tensor", swap_lane)

    def other_group(values, bits):
        return lax.ppermute(values, "dp", [(i, i ^ bits) for i in range(groups)])

    def after(value, *others):
        return lax.optimization_barrier((value, others))[0]

    step_padded = jnp.pad(step_weight, ((0, 0), (0, STEP_PAD - step_weight.shape[1])))
    early = dict(
        gate=mamba_gate, state=state_weight, step=step_padded, query=query_weight, input=mamba_input, key=key_weight,
        value=value_weight, mix=mamba_out, attn=attention_out,
    )
    late = dict(fgate=feed_gate, fup=feed_up, fdown=feed_down)
    whole, places_of = {}, {}
    for label, group_weights in (("early", early), ("late", late)):
        start = 0
        for name, weight in group_weights.items():
            places_of[name] = (label, start, weight.shape[1])
            start += weight.shape[1]
        whole[label] = lax.all_gather(join_columns(list(group_weights.values())), "dp", axis=0, tiled=True)

    def full(name):
        label, start, size = places_of[name]
        return lax.slice_in_dim(whole[label], start, start + size, axis=1)

    own_places = jnp.arange(own, dtype=jnp.int32)
    own_order = lax.dynamic_slice_in_dim(deal_order, device * own, own, 1)
    micro_index = jnp.arange(micro, dtype=jnp.int32)[:, None]

    def buffer_place(destination, rank):
        return destination * (micro * per) + micro_index * per + rank

    send_rank = jnp.sum((own_order[:, None, :] < own_order[:, :, None]).astype(jnp.int32), axis=2)
    send_place = buffer_place(send_rank // per, send_rank % per).reshape(-1)
    lane_order = lax.dynamic_index_in_dim(deal_order.reshape(micro, groups, lanes, own), lane, 2, keepdims=False)
    slots = device * own + own_places
    found = lane_order[:, None, :, :] == slots[None, :, None, None]
    source = jnp.sum(
        jnp.where(found, jnp.arange(groups, dtype=jnp.int32)[None, None, :, None], 0), axis=(2, 3)
    )
    recv_rank = jnp.sum(
        ((source[:, None, :] == source[:, :, None]) & (own_places[None, None, :] < own_places[None, :, None])).astype(jnp.int32),
        axis=2,
    )
    recv_place = buffer_place(source, recv_rank).reshape(-1)
    buffer_places = jnp.arange(micro * own, dtype=jnp.int32)
    send_pick = (buffer_places[:, None] == send_place[None, :]).astype(bf16)
    recv_pick = (recv_place[:, None] == buffer_places[None, :]).astype(bf16)

    def exchange(buffer):
        return lax.all_to_all(
            buffer.reshape(groups, micro * per, width), "dp", split_axis=0, concat_axis=0, tiled=True
        ).reshape(micro * own, width)

    def deal(values):
        sent = project(send_pick, values.reshape(micro * own, width)).astype(bf16)
        return project(recv_pick, exchange(sent)).astype(bf16)

    def deal_order_rows(values):
        return outer_sum(recv_pick, values).astype(bf16)

    def deal_take(moved):
        return outer_sum(send_pick, moved).astype(bf16).reshape(micro, own, width)

    def join_lanes(values):
        mine = values.reshape(micro, 1, own, -1)
        theirs = other_lane(values).reshape(micro, 1, own, -1)
        low = jnp.where(lane == 0, mine, theirs)
        high = jnp.where(lane == 0, theirs, mine)
        return jnp.concatenate([low, high], axis=1).reshape(total, -1)

    def lane_rows(values, which):
        return lax.dynamic_index_in_dim(
            values.reshape(micro, lanes, own, -1), which, 1, keepdims=False
        ).reshape(micro * own, -1)

    own_in = deal(inputs)
    own_grad = deal(out_grad)
    whole_in = join_lanes(own_in)
    whole_grad = join_lanes(own_grad)

    before = jnp.sum((segment[:, None, :] < segment[:, :, None]).astype(jnp.int32), axis=2)
    places = jnp.arange(rows, dtype=jnp.int32)
    position = (places[None, :] - before).reshape(total, 1)

    masks = [1 << place for place in range(groups.bit_length() - 1)]
    relative = []
    for block in range(groups):
        flip = 0
        for place, mask in enumerate(masks):
            if block >> (len(masks) - 1 - place) & 1:
                flip ^= mask
        relative.append(flip)
    block_order = jnp.bitwise_xor(group.astype(jnp.int32), jnp.array(relative, jnp.int32))

    def split_left(left):
        return pick_halves(left, block_order, shard)

    inner_places = list(range(1, len(masks)))

    def core_send(left_parts, right):
        return outer_low(left_parts[1], right)

    def halve(kept, place):
        return (
            lax.slice_in_dim(kept, 1, 2, axis=place - 1).reshape(-1, kept.shape[-1]),
            lax.slice_in_dim(kept, 0, 1, axis=place - 1),
        )

    class Reduction:
        def __init__(self, first):
            self.places = [place for place in first if place in inner_places]
            self.places += [place for place in inner_places if place not in first]
            self.stage = 0

        def move(self, send, kept):
            self.came = other_group(send, masks[self.places[self.stage]])
            self.kept = kept
            self.stage += 1

        def first(self, left_parts, right, from_core):
            kept = (outer_sum(left_parts[0], right) + from_core.astype(f32)).astype(bf16)
            kept = kept.reshape((2,) * len(inner_places) + (shard, -1))
            return halve(kept, self.places[0])

        def added(self):
            return self.kept.astype(f32) + self.came.reshape(self.kept.shape).astype(f32)

        def next(self):
            return halve(self.added().astype(bf16), self.places[self.stage])

        def last(self):
            return self.added().reshape(shard, -1)

        def step(self):
            return self.next() if self.stage < len(self.places) else self.last()

    order = [deal_order[0, 0] >= 0]

    def unit(work):
        shapes = jax.eval_shape(work)
        results = lax.cond(
            order[0], work, lambda: jax.tree.map(lambda leaf: jnp.zeros(leaf.shape, leaf.dtype), shapes)
        )
        leaves, form = jax.tree.flatten(results)
        least = min(range(len(leaves)), key=lambda place: leaves[place].size)
        leaves[least], order[0] = lax.optimization_barrier((leaves[least], order[0]))
        return jax.tree.unflatten(form, leaves)

    in32 = whole_in.astype(f32)
    in_scale = rms_scale(in32)
    normed_low = (in32 * in_scale * gain_input).astype(bf16)
    normed_left = split_left(normed_low)
    whole["early"] = after(whole["early"], whole_grad, normed_left)
    gate_z = project(normed_low, full("gate"))
    ssm_in = project(normed_low, full("input"))
    state_raw = project(normed_low, full("state"))
    heads = step_weight.shape[1]
    raw_step = project(normed_low, full("step"))[:, :heads]
    state_low = jax.nn.silu(conv_sum(state_raw, kernel_state, position)).astype(bf16)
    rate = -jnp.exp(log_rate)
    step_size = jax.nn.softplus(raw_step + step_bias)
    step_heads = step_size.reshape(micro, rows, heads).transpose(0, 2, 1)
    lower = (places[None, :] <= places[:, None]).astype(f32)
    running = jnp.einsum(
        "mhj,ij->mhi", step_heads * rate[None, :, None], lower, precision=lax.Precision.HIGHEST, preferred_element_type=f32
    )
    pairs = heads // 2
    run_row = running.reshape(micro, pairs, 2, rows)
    run_col = run_row.transpose(0, 1, 3, 2)
    step_row = step_heads.reshape(micro, pairs, 2, rows)
    skip_wide = jnp.repeat(skip_gain, SHD)[None, :]
    layout = (state_low, segment.reshape(micro, 1, rows).astype(f32), run_row, run_col, step_row)
    row_facts = jnp.concatenate([segment.reshape(total, 1).astype(f32), position.astype(f32)], axis=1)
    row_columns = jnp.pad(row_facts, ((0, 0), (0, 6)))
    query_cols, key_cols = query_weight.shape[1], key_weight.shape[1]
    attention_tables = (*rope_tables(position), row_columns, layout[1])
    pair_start = places_of["key"][1]
    pair_weight = lax.slice_in_dim(whole["early"], pair_start, pair_start + 2 * key_cols, axis=1)
    ssm_out, squares = state_forward(ssm_in, gate_z, kernel_inner, skip_wide, *layout, row_columns)
    attended_low, query_low, key_low, value_low = attention_forward(
        project(normed_low, full("query")), project(normed_low, pair_weight), attention_tables
    )
    square_own = jnp.sum(squares, axis=1)
    square_sum = square_own + other_lane(square_own)
    inv_rms = lax.rsqrt(square_sum / inner_width + epsilon)[:, None]
    gated_low = (ssm_out * jax.nn.silu(gate_z) * inv_rms * mixer_gain).astype(bf16)

    branch_part = (project_back(gated_low, full("mix")) + project_back(attended_low, full("attn"))).astype(bf16)
    branch = branch_part.astype(f32) + other_lane(branch_part).astype(f32)
    whole_mid = (in32 + branch).astype(bf16)
    mid32 = whole_mid.astype(f32)
    mid_scale = rms_scale(mid32)
    mid_low = (mid32 * mid_scale * gain_middle).astype(bf16)
    red_fgate, red_fup, red_low, red_high = [Reduction(places) for places in ((1, 2), (2, 1), (1, 2), (2, 1))]
    feeds = (red_fgate, red_fup)
    ff_cols = feed_gate.shape[1]
    gate_cols = mamba_gate.shape[1]

    def feed_forward():
        gate_ff = project(mid_low, full("fgate"))
        up_ff = project(mid_low, full("fup"))
        sig_ff = jax.nn.sigmoid(gate_ff)
        hidden_low = (gate_ff * sig_ff * up_ff).astype(bf16)
        grad_hidden = project(whole_grad, full("fdown"))
        gate_ff_low = (grad_hidden * up_ff * (sig_ff * (1.0 + gate_ff * (1.0 - sig_ff)))).astype(bf16)
        up_ff_low = (grad_hidden * (gate_ff * sig_ff)).astype(bf16)
        feed_low = (gate_ff_low, up_ff_low)
        return hidden_low, feed_low, feed_back(feed_low, 0), outer_low(whole_grad, hidden_low)

    half = total // 2

    def feed_back(feed_low, start):
        gate_part, up_part, values, scale = [
            lax.slice_in_dim(array, start, start + half) for array in (*feed_low, mid32, mid_scale)
        ]
        grad_mid_norm = project_back(gate_part, full("fgate")) + project_back(up_part, full("fup"))
        grad_gain = jnp.sum(grad_mid_norm * values * scale, axis=0)
        return rms_back(grad_mid_norm, values, scale, gain_middle).astype(bf16), grad_gain

    hidden_low, feed_low, (mid_part_low, gain_mid_low), part_fdown = unit(feed_forward)
    mid_other_low = hand_over(other_lane(mid_part_low), 2)
    mid_part_high, gain_mid_high = unit(lambda: feed_back(feed_low, half))
    mid_other_high = hand_over(other_lane(mid_part_high), 45)
    sum_fdown = lax.psum_scatter(part_fdown, "dp", scatter_dimension=0, tiled=True)
    grad_gain_mid = gain_mid_low + gain_mid_high

    def feed_output():
        ffn_part = project_back(hidden_low, full("fdown")).astype(bf16)
        return lane_rows(ffn_part, lane), lane_rows(ffn_part, 1 - lane)

    def feed_sends():
        mid_left = split_left(mid_low)
        return mid_left[0], [core_send(mid_left, right) for right in feed_low]

    mid_keep, send_feed = unit(feed_sends)
    order[0], mid_other_low = lax.optimization_barrier((order[0], mid_other_low))
    ffn_own, ffn_send = unit(feed_output)
    feed_came = [other_group(send, 1) for send in send_feed]

    def keep_first(keep, right, came, reductions, sizes):
        kept = (outer_sum(keep, right) + came.astype(f32)).astype(bf16)
        kept = kept.reshape((2,) * len(inner_places) + (shard, -1))
        moves, start = [], 0
        for red, size in zip(reductions, sizes):
            moves.append(halve(kept[..., start : start + size], red.places[0]))
            start += size
        return moves

    def settle(reductions, steps):
        for red, step in zip(reductions, steps):
            if red.stage < len(red.places):
                red.move(*step)
            else:
                red.result = step

    mid_other_high, feed_came = lax.optimization_barrier((mid_other_high, feed_came))
    moves = unit(
        lambda: [
            keep_first(mid_keep, right, came, (red,), (ff_cols,))[0] for red, right, came in zip(feeds, feed_low, feed_came)
        ]
    )
    for red, move in zip(feeds, moves):
        red.move(*move)

    def branch_backward():
        mid_sums = [
            mine.astype(f32) + other.astype(f32)
            for mine, other in ((mid_part_low, mid_other_low), (mid_part_high, mid_other_high))
        ]
        grad_middle = whole_grad.astype(f32) + jnp.concatenate(mid_sums)
        whole_branch = grad_middle.astype(bf16)
        grad_gated_norm = project(whole_branch, full("mix"))
        cross_own = jnp.sum(grad_gated_norm * mixer_gain * (ssm_out * jax.nn.silu(gate_z)), axis=1)
        grad_attended = project(whole_branch, full("attn")).astype(bf16)
        joint_low = attention_backward(grad_attended, query_low, key_low, value_low, attention_tables)
        return (
            cross_own, lane_rows(grad_middle, lane), grad_gated_norm, whole_branch,
            joint_low,
        )

    cross_own, grad_middle_own, grad_gated_norm, whole_branch, joint_low = unit(branch_backward)
    cross_other = other_lane(cross_own)

    ffn_other = other_lane(ffn_send)

    def branch_partial():
        ffn_out = ffn_own.astype(f32) + ffn_other.astype(f32)
        out_rows = (lane_rows(whole_mid, lane).astype(f32) + ffn_out).astype(bf16)
        return outer_low(whole_branch, jnp.concatenate([gated_low, attended_low], axis=1)), deal_order_rows(out_rows)

    part_branch, out_sent = unit(branch_partial)
    out_moved = exchange(out_sent)
    sum_branch = lax.psum_scatter(part_branch, "dp", scatter_dimension=0, tiled=True)
    step_sig = jax.nn.sigmoid(raw_step + step_bias).reshape(micro, rows, heads).transpose(0, 2, 1)
    gain_row, rate_column = mixer_gain[None, :], rate[:, None]

    def state_space_backward():
        cross = (inv_rms**3) * ((cross_own + cross_other)[:, None] / inner_width)
        columns = jnp.pad(jnp.concatenate([row_facts, inv_rms, cross], axis=1), ((0, 0), (0, 4)))
        first_right, column_sums, state_sums, head_sums = state_backward(
            grad_gated_norm, ssm_out, gate_z, ssm_in, kernel_inner, skip_wide, gain_row, *layout, columns,
            state_raw, kernel_state, step_heads, step_sig, rate_column, joint_low, query_cols,
        )
        return column_sums, state_sums, head_sums, first_right

    column_sums, state_sums, head_sums, first_right = unit(state_space_backward)

    total_fdown_low = [sum_fdown]
    order[0], total_fdown_low, out_moved = lax.optimization_barrier((order[0], total_fdown_low, out_moved))
    send_first, steps = unit(lambda: (core_send(normed_left, first_right), [red.step() for red in feeds]))
    settle(feeds, steps)
    first_came = other_group(send_first, 1)

    def input_gradient():
        grad_normed = project_back(first_right, lax.slice_in_dim(whole["early"], 0, first_right.shape[1], axis=1))
        grad_gain_in = jnp.sum(grad_normed * in32 * in_scale, axis=0)
        in_part = rms_back(grad_normed, in32, in_scale, gain_input).astype(bf16)
        return grad_gain_in, lane_rows(in_part, lane), lane_rows(in_part, 1 - lane)

    grad_gain_in, in_own, in_send = unit(input_gradient)

    firsts = (red_low, red_high)
    low_size = gate_cols + 2 * NS + STEP_PAD + query_cols
    first_sizes = (low_size, first_right.shape[1] - low_size)

    def first_moves():
        moves = keep_first(normed_left[0], first_right, first_came, firsts, first_sizes)
        return moves, lax.optimization_barrier(in_send), [red.step() for red in feeds]

    moves, in_send, steps = unit(first_moves)
    settle(feeds, steps)
    for red, move in zip(firsts, moves):
        red.move(*move)
    in_other = hand_over(other_lane(in_send), 6)

    def small_block():
        head_row = (jnp.sum(head_sums, axis=0).T * jnp.stack([rate, jnp.ones_like(rate)])).reshape(1, -1)
        return jnp.concatenate(
            [
                jnp.concatenate([jnp.sum(column_sums, axis=0), jnp.sum(state_sums, axis=0)], axis=1),
                grad_gain_in[None, :], grad_gain_mid[None, :], jnp.pad(head_row, ((0, 5), (0, width - head_row.shape[1]))),
            ]
        )
    flat = unit(small_block)
    flat_moved = other_group(flat, masks[0])

    def send_input():
        in_sum = in_own.astype(f32) + in_other.astype(f32)
        return deal_order_rows((in_sum + grad_middle_own).astype(bf16))

    bits = 1

    def finish():
        low, high = red_low.result, red_high.result
        state_rows = low[:, gate_cols : gate_cols + 2 * NS].reshape(lanes, shard // lanes, 2 * NS)
        cut = [0, gate_cols, gate_cols + key_cols, high.shape[1]]
        pieces = (
            low[:, :gate_cols], low[:, gate_cols + 2 * NS : gate_cols + 2 * NS + heads],
            low[:, gate_cols + 2 * NS + STEP_PAD :], [high[:, start:stop] for start, stop in zip(cut, cut[1:])],
            [lax.dynamic_index_in_dim(state_rows, which, 0, keepdims=False) for which in (lane, 1 - lane)],
        )
        return pieces, deal_take(in_moved)

    arrived = [red.came for red in feeds] + [sum_branch]
    order[0], arrived = lax.optimization_barrier((order[0], arrived))
    for red, came in zip(feeds, arrived):
        red.came = came
    sum_branch = arrived[-1]
    in_moved = None
    while red_low.stage < len(red_low.places):
        moving = [red for red in (*firsts, *feeds) if red.stage < len(red.places)]
        steps, flat, sent = unit(
            lambda: (
                [red.next() for red in moving],
                flat + flat_moved if flat_moved is not None else flat,
                send_input() if in_moved is None else (),
            )
        )
        settle(moving, steps)
        flat_moved = other_group(flat, masks[bits]) if bits < len(masks) else None
        bits += 1
        if in_moved is None:
            in_moved = exchange(sent)
    totals, block_out, flat = unit(
        lambda: (
            [red.last() for red in feeds] + [sum_branch.astype(f32), total_fdown_low[0].astype(f32)],
            deal_take(out_moved),
            flat + flat_moved if flat_moved is not None else flat,
        )
    )
    total_fgate, total_fup, total_branch, total_fdown = totals
    flat_moved = other_group(flat, masks[bits]) if bits < len(masks) else None
    bits += 1

    def last_work():
        red_low.result, red_high.result = red_low.last(), red_high.last()
        return finish(), flat + flat_moved if flat_moved is not None else flat

    ((total_gate, total_step, total_query, (total_input, total_key, total_value), states), grad_input), flat = unit(last_work)
    while bits < len(masks):
        flat = flat + other_group(flat, masks[bits])
        bits += 1
    theirs = other_lane(flat)
    low, high = jnp.where(lane == 0, flat, theirs), jnp.where(lane == 0, theirs, flat)
    both = flat + theirs

    def joined(row, start, count):
        return jnp.concatenate([low[row, start : start + count], high[row, start : start + count]])

    sum_gin, sum_gmid = both[8], both[9]
    sum_kst = both[: CONV + 1, gate_cols : gate_cols + 2 * NS]
    sum_kin = jnp.concatenate([low[: CONV + 1, :gate_cols], high[: CONV + 1, :gate_cols]], axis=1)
    sum_mix = joined(CONV + 1, 0, gate_cols)
    sum_skip = jnp.sum(joined(CONV + 2, 0, gate_cols).reshape(SH, SHD), axis=1)
    sum_bias = joined(10, heads, heads)
    sum_rate = joined(10, 0, heads)

    total_mix, total_attn = total_branch[:, :gate_cols], total_branch[:, gate_cols:]
    state_lane = states[0] + other_lane(states[1])
    return (
        block_out,
        grad_input,
        total_query,
        total_key,
        total_value,
        total_attn,
        total_gate,
        total_input,
        total_step,
        state_lane,
        total_mix,
        total_fgate,
        total_fup,
        total_fdown,
        sum_gin,
        sum_gmid,
        sum_kin,
        sum_kst,
        sum_mix,
        sum_bias,
        sum_rate,
        sum_skip,
    )


def solution(mesh):
    both = P("dp", "tensor")
    in_specs = (
        P(None, ("dp", "tensor"), None),
        P(None, ("dp", "tensor"), None),
        P(),
        P(None, "dp"),
        both,
        both,
        both,
        both,
        both,
        both,
        both,
        P("dp", None),
        both,
        both,
        both,
        both,
        P(),
        P(),
        P(None, "tensor"),
        P(),
        P("tensor"),
        P("tensor"),
        P("tensor"),
        P("tensor"),
    )
    out_specs = (
        P(None, ("dp", "tensor"), None),
        P(None, ("dp", "tensor"), None),
        both,
        both,
        both,
        both,
        both,
        both,
        both,
        P(("dp", "tensor"), None),
        both,
        both,
        both,
        both,
        P(),
        P(),
        P(),
        P(),
        P(),
        P(),
        P(),
        P(),
    )
    return jax.shard_map(local, mesh=mesh, in_specs=in_specs, out_specs=out_specs, check_vma=False)
```
